32 devices in a mesh: dp: 2 (over core), row: 4 (over y, x), col: 4 (over z).
Axes of the slice: x: 2, y: 2, z: 4, core: 2. Of those that a mesh axis runs over, the one named last changes fastest.
Arguments:
- inputs: bfloat16 [768, 8192], P('row', ('dp', 'col')), may hold values from -6 to 6
- doc_ids: int32 [8192], P(('dp', 'row')), may hold values from 0 to 31, as said below
- qkv_weight: bfloat16 [768, 2304], P('row', 'col'), may hold values from -0.625 to 0.625
- qkv_bias: bfloat16 [2304], P('col'), may hold values from -3 to 3
- proj_weight: bfloat16 [768, 768], P('col', 'row'), may hold values from -0.3125 to 0.3125
- proj_bias: bfloat16 [768], P('row'), may hold values from -2 to 2
- first_gain: float32 [768], P('row'), may hold values from 0.5 to 1.5
- first_shift: float32 [768], P('row'), may hold values from -2 to 2
- ffn_up: bfloat16 [768, 3072], P('row', 'col'), may hold values from -0.21875 to 0.21875
- ffn_up_bias: bfloat16 [3072], P('col'), may hold values from -3 to 3
- ffn_down: bfloat16 [768, 3072], P('row', 'col'), may hold values from -0.109375 to 0.109375
- ffn_down_bias: bfloat16 [768], P('row'), may hold values from -2 to 2
- second_gain: float32 [768], P('row'), may hold values from 0.5 to 1.5
- second_shift: float32 [768], P('row'), may hold values from -2 to 2
- conv_kernel: float32 [12, 33], P('col'), may hold values from -0.75 to 0.75
- cotangent: float32 [768, 8192], P('row', ('dp', 'col')), may hold values from -6 to 6
Outputs:
- output: float32 [768, 8192], P('row', ('dp', 'col'))
- grad_inputs: float32 [768, 8192], P('row', ('dp', 'col'))
- grad_qkv_weight: float32 [768, 2304], P('row', 'col')
- grad_qkv_bias: float32 [2304], P('col')
- grad_proj_weight: float32 [768, 768], P('col', 'row')
- grad_proj_bias: float32 [768], P('row')
- grad_first_gain: float32 [768], P('row')
- grad_first_shift: float32 [768], P('row')
- grad_ffn_up: float32 [768, 3072], P('row', 'col')
- grad_ffn_up_bias: float32 [3072], P('col')
- grad_ffn_down: float32 [768, 3072], P('row', 'col')
- grad_ffn_down_bias: float32 [768], P('row')
- grad_second_gain: float32 [768], P('row')
- grad_second_shift: float32 [768], P('row')
- grad_conv_kernel: float32 [12, 33], P('col')
The draws below stay inside these ranges and needn't reach their ends.
Inputs may be any that keep to these rules, and one draw needn't show every extreme that they name: `doc_ids`: within each sequence of 1024 consecutive tokens the document numbers start at 0, never fall and rise by at most one from token to token; every document has 16 or more tokens.
All inputs are finite; a program needn't handle non-finite values.
Results may differ from the reference program's by a relative error of at most 0.013.
The reference program's roundings to bfloat16 on the way count: a program that leaves them out, or rounds other values in their place, can miss the bound.
Values may be sent and summed in bfloat16 or wider, within the bound.
A program may use at most 256 MiB of HBM per device.

```python
import math
import jax
import jax.numpy as jnp
from jax import lax

D = 768
HEADS = 12
FF = 3072
HEAD_DIM = 64
SEQ_LEN = 1024
SEG = 16
CONV = 33
ITERS = 6
TOKENS = 8192


def draw_doc_ids(key, part):
    sequence_count = TOKENS // SEQ_LEN
    slot_count = SEQ_LEN // 32
    level_key, keep_key, jitter_key, full_key = jax.random.split(jax.random.fold_in(key, 11), 4)
    levels = jax.random.randint(level_key, (sequence_count, 1), 0, 9)
    full_seq = jax.random.randint(full_key, (), 0, sequence_count)
    seq_index = jnp.arange(sequence_count, dtype=jnp.int32)[:, None]
    levels = jnp.where(seq_index == full_seq, 8, levels)
    kept = jax.random.randint(keep_key, (sequence_count, slot_count), 0, 8) < levels
    slots = jnp.arange(slot_count, dtype=jnp.int32)
    kept = kept & (slots[None, :] > 0)
    jitter = jax.random.randint(jitter_key, (sequence_count, slot_count), -8, 8)
    bounds = 32 * slots[None, :] + jitter
    positions = jnp.arange(SEQ_LEN, dtype=jnp.int32)
    crossed = (positions[None, :, None] >= bounds[:, None, :]) & kept[:, None, :]
    return jnp.sum(crossed.astype(jnp.int32), axis=2).reshape(TOKENS).astype(jnp.int32)


def block_scale(rng, extent, cuts, least, high):
    gain = 1.0
    for position, parts in cuts:
        heights = jax.random.uniform(jax.random.fold_in(jax.random.fold_in(rng, 6), position), (parts,), jnp.float32, least / len(cuts), high / len(cuts))
        gain = gain * jnp.repeat(jnp.exp(heights), extent[position] // parts).reshape((-1,) + (1,) * (len(extent) - 1 - position))
    return gain


def scatter_about(stream_key, shape, scale, reach, cuts=(), kind=jnp.bfloat16):
    entries = scale * jax.random.normal(stream_key, shape, jnp.float32)
    if cuts:
        entries = entries * block_scale(stream_key, shape, cuts, -0.22, 0.18)
    return jnp.clip(entries, -reach, reach).astype(kind)


def setup_inputs(seed: int = 0) -> dict:
    streams_of = jax.random.split(jax.random.key(seed), 17)
    inputs = scatter_about(streams_of[0], (D, TOKENS), 1.0, 6.0, ((0, 4), (1, 8)))
    doc_ids = draw_doc_ids(jax.random.fold_in(streams_of[16], 71), 0)
    qkv_weight = scatter_about(streams_of[2], (D, 3 * D), (D // 8) ** -0.5, 0.625, ((0, 4), (1, 4)))
    qkv_bias = scatter_about(streams_of[3], (3 * D,), 0.5, 3.0, ((0, 4),))
    proj_weight = scatter_about(streams_of[4], (D, D), (D // 2) ** -0.5, 0.3125, ((0, 4), (1, 4)))
    proj_bias = scatter_about(streams_of[5], (D,), 0.3, 2.0, ((0, 4),))
    first_gain = jnp.clip(1.0 + 0.1 * jax.random.normal(streams_of[6], (D,), jnp.float32), 0.5, 1.5)
    first_shift = scatter_about(streams_of[7], (D,), 0.3, 2.0, ((0, 4),), jnp.float32)
    ffn_up = scatter_about(streams_of[8], (D, FF), D ** -0.5, 0.21875, ((0, 4), (1, 4)))
    ffn_up_bias = scatter_about(streams_of[9], (FF,), 0.5, 3.0, ((0, 4),))
    ffn_down = scatter_about(streams_of[10], (D, FF), FF ** -0.5, 0.109375, ((0, 4), (1, 4)))
    ffn_down_bias = scatter_about(streams_of[11], (D,), 0.3, 2.0, ((0, 4),))
    second_gain = jnp.clip(1.0 + 0.1 * jax.random.normal(streams_of[12], (D,), jnp.float32), 0.5, 1.5)
    second_shift = scatter_about(streams_of[13], (D,), 0.3, 2.0, ((0, 4),), jnp.float32)
    conv_kernel = scatter_about(streams_of[14], (HEADS, CONV), (2 * CONV) ** -0.5, 0.75, ((0, 4),), jnp.float32)
    cotangent = scatter_about(streams_of[15], (D, TOKENS), 1.0, 6.0, ((0, 4), (1, 8)), jnp.float32)
    return dict(inputs=inputs, doc_ids=doc_ids, qkv_weight=qkv_weight, qkv_bias=qkv_bias, proj_weight=proj_weight, proj_bias=proj_bias, first_gain=first_gain, first_shift=first_shift, ffn_up=ffn_up, ffn_up_bias=ffn_up_bias, ffn_down=ffn_down, ffn_down_bias=ffn_down_bias, second_gain=second_gain, second_shift=second_shift, conv_kernel=conv_kernel, cotangent=cotangent)


EPSILON = 1e-05
HIGHEST_PRECISION = lax.Precision.HIGHEST
MASKED_SCORE = -1000000000.0

@jax.custom_vjp
def low(v):
    return lax.optimization_barrier(v.astype(jnp.bfloat16)).astype(jnp.float32)

@jax.custom_vjp
def low_back(v):
    return v

def low_keep(v):
    return (low(v), None)

def low_pass(kept, grad):
    return (grad,)

def back_keep(v):
    return (v, None)

def back_low(kept, grad):
    return (low(grad),)
low.defvjp(low_keep, low_pass)
low_back.defvjp(back_keep, back_low)

def matmul(left_side, right_side):
    return jnp.dot(left_side, right_side, precision=HIGHEST_PRECISION, preferred_element_type=jnp.float32)

def batched(formula, left_side, right_side):
    return jnp.einsum(formula, left_side, right_side, precision=HIGHEST_PRECISION, preferred_element_type=jnp.float32)

def masked_softmax(scores, keep_mask):
    scores = jnp.where(keep_mask, scores, MASKED_SCORE)
    largest = lax.optimization_barrier(jnp.max(scores, axis=-1, keepdims=True))
    weights = jnp.exp(scores - largest)
    return weights / lax.optimization_barrier(jnp.sum(weights, axis=-1, keepdims=True))

def newton_pinv(kernel):
    land_total = kernel.shape[-1]
    identity = jnp.eye(land_total, dtype=jnp.float32)
    estimate = jnp.swapaxes(kernel, -1, -2) / land_total
    for iteration in range(ITERS):
        product = batched('hij,hjk->hik', kernel, estimate)
        nested = 7.0 * identity - product
        nested = 15.0 * identity - batched('hij,hjk->hik', product, nested)
        nested = 13.0 * identity - batched('hij,hjk->hik', product, nested)
        estimate = batched('hij,hjk->hik', 0.25 * estimate, nested)
    return estimate

def doc_conv(values, documents, kernel):
    half_width = CONV // 2
    length = values.shape[0]
    padded = jnp.pad(values, ((half_width, half_width), (0, 0), (0, 0)))
    padded_docs = jnp.pad(documents, (half_width, half_width), constant_values=-1)
    running = jnp.zeros(values.shape, jnp.float32)
    for offset in range(CONV):
        same_doc = (padded_docs[offset:offset + length] == documents)[:, None, None]
        shifted = padded[offset:offset + length]
        running = running + jnp.where(same_doc, shifted, 0.0) * kernel[:, offset][None, :, None]
    return running

def nystrom(qkv_seq, documents, kernel):
    length = qkv_seq.shape[0]
    head_count = qkv_seq.shape[1]
    land_count = length // SEG
    root_scale = HEAD_DIM ** (-0.25)
    queries = qkv_seq[:, :, 0] * root_scale
    key_rows = qkv_seq[:, :, 1] * root_scale
    values = qkv_seq[:, :, 2]
    query_land = lax.optimization_barrier(jnp.mean(queries.reshape(land_count, SEG, head_count, HEAD_DIM), axis=1))
    key_land = lax.optimization_barrier(jnp.mean(key_rows.reshape(land_count, SEG, head_count, HEAD_DIM), axis=1))
    land_docs = documents.reshape(land_count, SEG)[:, 0]
    kernel_one = masked_softmax(batched('thd,jhd->htj', queries, key_land), (documents[:, None] == land_docs[None, :])[None])
    kernel_two = masked_softmax(batched('ihd,jhd->hij', query_land, key_land), (land_docs[:, None] == land_docs[None, :])[None])
    kernel_three = masked_softmax(batched('ihd,thd->hit', query_land, key_rows), (land_docs[:, None] == documents[None, :])[None])
    inverse = newton_pinv(kernel_two)
    summary = batched('hit,thd->hid', kernel_three, values)
    mixed_rows = batched('hij,hjd->hid', inverse, summary)
    result = batched('htj,hjd->thd', kernel_one, mixed_rows)
    return result + doc_conv(values, documents, kernel)

def layer_norm(residual, gain_vec, bias_vec):
    average = lax.optimization_barrier(jnp.mean(residual, axis=-1, keepdims=True))
    spread = lax.optimization_barrier(jnp.mean(residual * residual, axis=-1, keepdims=True)) - average * average
    return (residual - average) * lax.rsqrt(spread + EPSILON) * gain_vec + bias_vec

def layer_rows(row_block, documents, params):
    qkv_weight, qkv_bias, proj_weight, proj_bias, first_gain, first_shift, ffn_up, ffn_up_bias, ffn_down, ffn_down_bias, second_gain, second_shift, conv_kernel = params
    row_total = row_block.shape[0]
    qkv_rounded = low(low_back(matmul(row_block, qkv_weight) + qkv_bias))
    sequences = qkv_rounded.reshape(row_total // SEQ_LEN, SEQ_LEN, HEADS, 3, HEAD_DIM)
    seq_docs = documents.reshape(row_total // SEQ_LEN, SEQ_LEN)
    attended = jax.vmap(nystrom, in_axes=(0, 0, None))(sequences, seq_docs, conv_kernel)
    attended = low(attended.reshape(row_total, D))
    first_residual = row_block + low_back(matmul(attended, proj_weight) + proj_bias)
    hidden = layer_norm(first_residual, first_gain, first_shift)
    pre_gelu = low_back(matmul(low(hidden), ffn_up) + ffn_up_bias)
    active = low(jax.nn.gelu(pre_gelu, approximate=False))
    second_residual = hidden + low_back(matmul(active, jnp.transpose(ffn_down)) + ffn_down_bias)
    return layer_norm(second_residual, second_gain, second_shift)

def reference(inputs, doc_ids, qkv_weight, qkv_bias, proj_weight, proj_bias, first_gain, first_shift, ffn_up, ffn_up_bias, ffn_down, ffn_down_bias, second_gain, second_shift, conv_kernel, cotangent):
    params = tuple((entry.astype(jnp.float32) for entry in (qkv_weight, qkv_bias, proj_weight, proj_bias, first_gain, first_shift, ffn_up, ffn_up_bias, ffn_down, ffn_down_bias, second_gain, second_shift, conv_kernel)))
    seq_total = TOKENS // SEQ_LEN
    group_size = math.gcd(seq_total, max(1, 4096 // SEQ_LEN))
    block_docs = doc_ids.reshape(seq_total // group_size, group_size * SEQ_LEN)

    def one_block(block_pair, weights):
        return layer_rows(block_pair[0], block_pair[1], weights)
    checked = jax.checkpoint(one_block)

    def forward(columns_all, weights):
        rows_all = jnp.transpose(columns_all)
        blocks = rows_all.reshape(seq_total // group_size, group_size * SEQ_LEN, D)
        mapped = lax.map(lambda block_pair: checked(block_pair, weights), (blocks, block_docs))
        return jnp.transpose(mapped.reshape(TOKENS, D))
    output, pullback = jax.vjp(forward, inputs.astype(jnp.float32), params)
    grad_inputs, gradients = pullback(cotangent)
    return (output, grad_inputs) + tuple(gradients)
```

```python
import functools

import jax
import jax.numpy as jnp
from jax import lax
from jax.experimental import pallas as pl
from jax.experimental.pallas import tpu as pltpu
from jax.sharding import PartitionSpec as P

D = 768
HEAD_DIM = 64
SEQ_LEN = 1024
EPSILON = 1e-05
F32=jnp.float32; BF=jnp.bfloat16
HD=64; SEQ=1024; SEG=16; CONV=33; ITERS=6; L=64
NEG=-1e9

def dg(a,b,ca,cb):
    return lax.dot_general(a,b,(((ca,),(cb,)),((),())),preferred_element_type=F32)
def nn(a,b): return dg(a,b,1,0)
def nt(a,b): return dg(a,b,1,1)
def tn(a,b): return dg(a,b,0,0)
def split(x):
    hi=x.astype(BF); lo=(x-hi.astype(F32)).astype(BF)
    return hi,lo
def cat(hl): return jnp.concatenate(hl,axis=0)
def halves(x):
    n=x.shape[0]//2
    return x[:n]+x[n:]
def nn2(a,b): return halves(nn(cat(split(a)),b))
def nt2(a,b): return halves(nt(cat(split(a)),b))
def nn3(a,b):
    ah,al=split(a); bh,bl=split(b)
    return halves(nn(cat((ah,al)),bh))+nn(ah,bl)
def nt3(a,b):
    ah,al=split(a); bh,bl=split(b)
    return halves(nt(cat((ah,al)),bh))+nt(ah,bl)

def iota(shape,dim): return lax.broadcasted_iota(jnp.int32,shape,dim)
def avg_mat():
    return jnp.where((iota((L,SEQ),1)//SEG)==iota((L,SEQ),0),F32(1.0/SEG),F32(0)).astype(BF)
def pick_mat():
    return jnp.where(iota((L,SEQ),1)==iota((L,SEQ),0)*SEG,F32(1),F32(0)).astype(BF)

def doc_parts(doc_ref):
    row=doc_ref[...]
    rowb=jnp.broadcast_to(row.astype(F32),(8,SEQ)).astype(BF)
    pick=pick_mat()
    land_row=nt(rowb,pick)[0:1]
    land_col=nt(pick,rowb)[:,0:1]
    return row.astype(F32),land_row,land_col

def conv_masks(doc_row,mask_ref):
    t=iota((1,SEQ),1)
    for o in range(CONV):
        s=o-CONV//2
        rolled=pltpu.roll(doc_row,(-s)%SEQ,1) if s else doc_row
        ok=(rolled==doc_row)&(t+s>=0)&(t+s<SEQ)
        mask_ref[pl.ds(o,1),:]=jnp.where(ok,F32(1),F32(0))

def head_scores(h,qkv_ref,doc_row,land_row,land_col,k1_ref,k3_ref,k2_ref,ql_ref,kl_ref,sum_ref):
    b=h*3*HD
    q=qkv_ref[b:b+HD,:]; k=qkv_ref[b+HD:b+2*HD,:]; v=qkv_ref[b+2*HD:b+3*HD,:]
    at=avg_mat()
    ql=nt(at,q); kl=nt(at,k)
    ql_ref[h]=ql; kl_ref[h]=kl
    keep=land_col==doc_row
    s1=jnp.where(keep,nn2(kl,q)*0.125,NEG)
    e1=jnp.exp(s1-jnp.max(s1,axis=0,keepdims=True))
    k1_ref[h]=e1/jnp.sum(e1,axis=0,keepdims=True)
    s3=jnp.where(keep,nn2(ql,k)*0.125,NEG)
    e3=jnp.exp(s3-jnp.max(s3,axis=1,keepdims=True))
    k3=e3/jnp.sum(e3,axis=1,keepdims=True)
    k3_ref[h]=k3
    s2=jnp.where(land_col==land_row,nt3(ql,kl)*0.125,NEG)
    e2=jnp.exp(s2-jnp.max(s2,axis=1,keepdims=True))
    k2_ref[h]=e2/jnp.sum(e2,axis=1,keepdims=True)
    sum_ref[h]=nt2(k3,v)

def eye(): return jnp.where(iota((L,L),0)==iota((L,L),1),F32(1),F32(0))

def newton(nh,k2_ref,v_ref,p_ref,n1_ref,n2_ref,n3_ref):
    for h in range(nh):
        v_ref[0,h]=k2_ref[h].T*(1.0/L)
    def step(i,_):
        I=eye()
        P=[nn3(k2_ref[h],v_ref[i,h]) for h in range(nh)]
        N1=[7.0*I-P[h] for h in range(nh)]
        N2=[15.0*I-nn3(P[h],N1[h]) for h in range(nh)]
        N3=[13.0*I-nn3(P[h],N2[h]) for h in range(nh)]
        for h in range(nh):
            p_ref[i,h]=P[h]; n1_ref[i,h]=N1[h]; n2_ref[i,h]=N2[h]; n3_ref[i,h]=N3[h]
            v_ref[i+1,h]=nn3(0.25*v_ref[i,h],N3[h])
        return 0
    lax.fori_loop(0,ITERS,step,0)

def conv_fwd(nh,qkv_ref,mask_ref,w_ref,acc_ref):
    for h in range(nh):
        def group(g,_):
            r=pl.multiple_of(h*3*HD+2*HD+g*16,16)
            v=qkv_ref[pl.ds(r,16),:].astype(F32)
            acc=jnp.zeros((16,SEQ),F32)
            for o in range(CONV):
                s=o-CONV//2
                c=mask_ref[pl.ds(o,1),:]*w_ref[h,o]
                acc=acc+(pltpu.roll(v,(-s)%SEQ,1) if s else v)*c
            ro=pl.multiple_of(h*HD+g*16,16)
            acc_ref[pl.ds(ro,16),:]=acc
            return 0
        lax.fori_loop(0,HD//16,group,0)

def head_out(h,k1_ref,inv,sum_ref,mix_ref,acc_ref,att_ref):
    mixed=nn3(inv,sum_ref[h])
    mix_ref[h]=mixed
    mt=mixed.T
    k1=k1_ref[h]
    res=nn3(mt,k1)
    att_ref[h*HD:(h+1)*HD,:]=(res+acc_ref[h*HD:(h+1)*HD,:]).astype(BF)

def attn_fwd_body(nh,qkv_ref,doc_ref,w_ref,att_ref,k1_ref,k3_ref,k2_ref,ql_ref,kl_ref,sum_ref,mix_ref,v_ref,p_ref,n1_ref,n2_ref,n3_ref,mask_ref,acc_ref):
    doc_row,land_row,land_col=doc_parts(doc_ref)
    for h in range(nh):
        head_scores(h,qkv_ref,doc_row,land_row,land_col,k1_ref,k3_ref,k2_ref,ql_ref,kl_ref,sum_ref)
    newton(nh,k2_ref,v_ref,p_ref,n1_ref,n2_ref,n3_ref)
    conv_masks(doc_row,mask_ref)
    conv_fwd(nh,qkv_ref,mask_ref,w_ref,acc_ref)
    for h in range(nh):
        head_out(h,k1_ref,v_ref[ITERS,h],sum_ref,mix_ref,acc_ref,att_ref)

def save_shapes(nh):
    S=jax.ShapeDtypeStruct
    sm=S((nh,L,L),F32)
    return [S((nh,L,SEQ),F32),S((nh,L,SEQ),F32),sm,sm,sm,sm,sm,S((ITERS+1,nh,L,L),F32)]+[S((ITERS,nh,L,L),F32)]*4+[S((40,SEQ),F32)]

def attn_fwd(qkvT,doc,w):
    nh=w.shape[0]
    V=pl.BlockSpec(memory_space=pltpu.VMEM)
    outs=[jax.ShapeDtypeStruct((nh*HD,SEQ),BF)]+save_shapes(nh)
    return pl.pallas_call(functools.partial(attn_fwd_body,nh),out_shape=outs,
        in_specs=[V,V,pl.BlockSpec(memory_space=pltpu.SMEM)],out_specs=[V]*len(outs),
        scratch_shapes=[pltpu.VMEM((nh*HD,SEQ),F32)],
        compiler_params=pltpu.CompilerParams(vmem_limit_bytes=50<<20),name="attn_fwd")(qkvT,doc,w)

def newton_bwd(nh,k2_ref,v_ref,p_ref,n1_ref,n2_ref,n3_ref,gv_ref,gk_ref):
    for h in range(nh):
        gk_ref[h]=jnp.zeros((L,L),F32)
    def step(j,_):
        i=ITERS-1-j
        H=range(nh)
        gV=[gv_ref[h] for h in H]; V=[v_ref[i,h] for h in H]
        VT=[V[h].T for h in H]; PT=[p_ref[i,h].T for h in H]
        gN3=[0.25*nn3(VT[h],gV[h]) for h in H]
        gVn=[0.25*nt3(gV[h],n3_ref[i,h]) for h in H]
        gN2=[-nn3(PT[h],gN3[h]) for h in H]
        gN1=[-nn3(PT[h],gN2[h]) for h in H]
        gP=[-nt3(gN3[h],n2_ref[i,h])-nt3(gN2[h],n1_ref[i,h])-gN1[h] for h in H]
        for h in H:
            gk_ref[h]+=nt3(gP[h],V[h])
            gv_ref[h]=gVn[h]+nn3(k2_ref[h].T,gP[h])
        return 0
    lax.fori_loop(0,ITERS,step,0)
    for h in range(nh):
        gk_ref[h]+=gv_ref[h].T*(1.0/L)

def conv_bwd(nh,qkv_ref,g_ref,mask_ref,w_ref,gacc_ref,gw_ref):
    for h in range(nh):
        gw_ref[h]=jnp.zeros((40,8,128),F32)
        def group(g,_):
            r=pl.multiple_of(h*3*HD+2*HD+g*16,16)
            ro=pl.multiple_of(h*HD+g*16,16)
            v=qkv_ref[pl.ds(r,16),:].astype(F32)
            gg=g_ref[pl.ds(ro,16),:].astype(F32)
            acc=jnp.zeros((16,SEQ),F32)
            for o in range(CONV):
                s=o-CONV//2
                m=mask_ref[pl.ds(CONV-1-o,1),:]
                R=(pltpu.roll(gg,s%SEQ,1) if s else gg)*m
                acc=acc+R*w_ref[h,o]
                pr=v*R
                x=pr[0:8]+pr[8:16]
                y=x[:,0:128]
                for c in range(1,SEQ//128): y=y+x[:,c*128:(c+1)*128]
                gw_ref[h,o]+=y
            gacc_ref[pl.ds(ro,16),:]=acc
            return 0
        lax.fori_loop(0,HD//16,group,0)

def head_bwd1(h,qkv_ref,g_ref,k1_ref,k3_ref,sum_ref,mix_ref,inv,gv_ref,gs1_ref,gs3_ref,gacc_ref):
    b=h*3*HD
    v=qkv_ref[b+2*HD:b+3*HD,:]
    g=g_ref[h*HD:(h+1)*HD,:]
    k1=k1_ref[h]
    gmix=nt2(k1,g)
    gk1=nn2(mix_ref[h],g)
    gs1_ref[h]=k1*(gk1-jnp.sum(k1*gk1,axis=0,keepdims=True))
    gv_ref[h]=nt3(gmix,sum_ref[h])
    gsum=nn3(inv.T,gmix)
    k3=k3_ref[h]
    gk3=nn2(gsum,v)
    gs3_ref[h]=k3*(gk3-jnp.sum(k3*gk3,axis=1,keepdims=True))
    gacc_ref[h*HD:(h+1)*HD,:]+=nn3(gsum.T,k3)

def head_bwd2(h,qkv_ref,k2_ref,gk_ref,ql_ref,kl_ref,gs1_ref,gs3_ref,gacc_ref,out_ref):
    b=h*3*HD
    q=qkv_ref[b:b+HD,:]; k=qkv_ref[b+HD:b+2*HD,:]
    k2=k2_ref[h]; gk2=gk_ref[h]
    gs2=k2*(gk2-jnp.sum(k2*gk2,axis=1,keepdims=True))
    ql=ql_ref[h]; kl=kl_ref[h]
    gs1=gs1_ref[h]; gs3=gs3_ref[h]
    gkl=nt2(gs1,q)+nn3(gs2.T,ql)
    gql=nt2(gs3,k)+nn3(gs2,kl)
    at=avg_mat()
    gq=(nn3(kl.T,gs1)+nn2(gql.T,at))*0.125
    gk=(nn3(ql.T,gs3)+nn2(gkl.T,at))*0.125
    out_ref[b:b+HD,:]=gq.astype(BF)
    out_ref[b+HD:b+2*HD,:]=gk.astype(BF)
    out_ref[b+2*HD:b+3*HD,:]=gacc_ref[h*HD:(h+1)*HD,:].astype(BF)

def attn_bwd_body(nh,qkv_ref,g_ref,w_ref,k1_ref,k3_ref,k2_ref,ql_ref,kl_ref,sum_ref,mix_ref,v_ref,p_ref,n1_ref,n2_ref,n3_ref,mask_ref,out_ref,gw_ref,gv_ref,gk_ref,gs1_ref,gs3_ref,gacc_ref):
    conv_bwd(nh,qkv_ref,g_ref,mask_ref,w_ref,gacc_ref,gw_ref)
    for h in range(nh):
        head_bwd1(h,qkv_ref,g_ref,k1_ref,k3_ref,sum_ref,mix_ref,v_ref[ITERS,h],gv_ref,gs1_ref,gs3_ref,gacc_ref)
    newton_bwd(nh,k2_ref,v_ref,p_ref,n1_ref,n2_ref,n3_ref,gv_ref,gk_ref)
    for h in range(nh):
        head_bwd2(h,qkv_ref,k2_ref,gk_ref,ql_ref,kl_ref,gs1_ref,gs3_ref,gacc_ref,out_ref)

def attn_bwd(qkvT,g,w,saved):
    nh=w.shape[0]
    V=pl.BlockSpec(memory_space=pltpu.VMEM)
    outs=[jax.ShapeDtypeStruct((nh*3*HD,SEQ),BF),jax.ShapeDtypeStruct((nh,40,8,128),F32)]
    sm=pltpu.VMEM((nh,L,L),F32); bg=pltpu.VMEM((nh,L,SEQ),F32)
    return pl.pallas_call(functools.partial(attn_bwd_body,nh),out_shape=outs,
        in_specs=[V,V,pl.BlockSpec(memory_space=pltpu.SMEM)]+[V]*len(saved),out_specs=[V]*2,
        scratch_shapes=[sm,sm,bg,bg,pltpu.VMEM((nh*HD,SEQ),F32)],
        compiler_params=pltpu.CompilerParams(vmem_limit_bytes=50<<20),name="attn_bwd")(qkvT,g,w,*saved)
MESH = pl.DeviceIdType.MESH
ANY = pl.BlockSpec(memory_space=pl.ANY)


def struct(shape, dtype):
    return jax.ShapeDtypeStruct(shape, dtype)


def comm_call(body, name, cid, ins, outs, sems):
    return pl.pallas_call(
        body,
        out_shape=outs,
        in_specs=[ANY] * len(ins),
        out_specs=[ANY] * len(outs),
        scratch_shapes=[pltpu.SemaphoreType.DMA((n,)) for n in sems],
        compiler_params=pltpu.CompilerParams(collective_id=cid, has_side_effects=True),
        name=name,
    )(*ins)


def remote(src, dst, ss, rs, dev):
    return pltpu.make_async_remote_copy(
        src_ref=src, dst_ref=dst, send_sem=ss, recv_sem=rs, device_id=dev, device_id_type=MESH
    )


def greet_row(rows, r):
    bar = pltpu.get_barrier_semaphore()
    for k in range(1, rows):
        pl.semaphore_signal(bar, inc=1, device_id={"row": lax.rem(r + k, rows)}, device_id_type=MESH)
    pl.semaphore_wait(bar, rows - 1)


def greet(axis, size, me):
    bar = pltpu.get_barrier_semaphore()
    for k in range(1, size):
        pl.semaphore_signal(bar, inc=1, device_id={axis: lax.rem(me + k, size)}, device_id_type=MESH)
    pl.semaphore_wait(bar, size - 1)


def axis_exchange(axis, size, cid, name, arrays, outs, src_of, dst_of):
    n = len(arrays)

    def body(*refs):
        ins, dsts, (ss, rs, ls) = refs[:n], refs[n : 2 * n], refs[2 * n :]
        me = lax.axis_index(axis)
        greet(axis, size, me)
        copies = []
        for k in range(1, size):
            peer = lax.rem(me + k, size)
            for i in range(n):
                slot = (k - 1) * n + i
                cp = remote(src_of(i, ins[i], peer), dst_of(i, dsts[i], me), ss.at[slot], rs.at[slot], {axis: peer})
                cp.start()
                copies.append(cp)
        local = [pltpu.make_async_copy(src_of(i, ins[i], me), dst_of(i, dsts[i], me), ls.at[i]) for i in range(n)]
        for cp in local:
            cp.start()
        for cp in copies:
            cp.wait()
        for cp in local:
            cp.wait()

    m = (size - 1) * n
    return comm_call(body, name, cid, arrays, outs, (m, m, n))


def gather_front(R, C, S, fb, inputs, cot, docs, wqkv):
    HB = R // S
    QT = SEQ_LEN // HB
    ext = wqkv.shape[0]

    def body(x_ref, g_ref, d_ref, w_ref, xg_ref, gg_ref, dg_ref, wg_ref, ss, rs, ws, wr, ls, ds, dr):
        r = lax.axis_index("row")
        c = lax.axis_index("col")
        a, h = r // HB, lax.rem(r, HB)
        bar = pltpu.get_barrier_semaphore()
        for k in range(1, R):
            pl.semaphore_signal(bar, inc=1, device_id={"row": lax.rem(r + k, R)}, device_id_type=MESH)
        own_w = c == h
        for q in range(R):
            @pl.when(jnp.logical_not(own_w & (r == q)))
            def _():
                pl.semaphore_signal(bar, inc=1, device_id={"row": q, "col": h}, device_id_type=MESH)
        doc_row = c * S + a
        doc_self = (doc_row == r) & own_w
        @pl.when(jnp.logical_not(doc_self))
        def _():
            pl.semaphore_signal(bar, inc=1, device_id={"row": doc_row, "col": h}, device_id_type=MESH)
        dst_row, dst_col = lax.rem(r, S) * HB + c, r // S
        send_self = (dst_row == r) & (dst_col == c)
        extra = jnp.where(own_w, 0, 1) + jnp.where(send_self, 0, 1)
        pl.semaphore_wait(bar, R - 1 + S * C - 1 + extra)

        def rows_at(ref, q):
            return ref.at[pl.ds(pl.multiple_of(q * fb, fb), fb), :]

        doc_cp = remote(d_ref, dg_ref, ds.at[0], dr.at[0], {"row": dst_row, "col": dst_col})
        doc_in = remote(d_ref, dg_ref, ds.at[0], dr.at[0], {"row": doc_row, "col": h})
        doc_local = pltpu.make_async_copy(d_ref, dg_ref, ls.at[3])
        @pl.when(jnp.logical_not(send_self))
        def _():
            doc_cp.start()
        @pl.when(send_self)
        def _():
            doc_local.start()
        copies = []
        for k in range(1, R):
            p = lax.rem(r + k, R)
            ap, hp = p // HB, lax.rem(p, HB)
            cp = remote(
                x_ref.at[:, pl.ds(pl.multiple_of(ap * SEQ_LEN, SEQ_LEN), SEQ_LEN)],
                rows_at(xg_ref, r), ss.at[2 * k - 2], rs.at[2 * k - 2], {"row": p})
            cp.start()
            copies.append(cp)
        for ap in range(S):
            for cq in range(C):
                t = ap * HB + c
                me = (t == r) & (c == cq)
                cp = remote(w_ref, wg_ref.at[r], ws.at[ap * C + cq], wr.at[r], {"row": t, "col": cq})
                @pl.when(jnp.logical_not(me))
                def _():
                    cp.start()
        for k in range(1, R):
            p = lax.rem(r + k, R)
            ap, hp = p // HB, lax.rem(p, HB)
            cp = remote(
                g_ref.at[:, pl.ds(pl.multiple_of(ap * SEQ_LEN + hp * QT, QT), QT)],
                rows_at(gg_ref, r), ss.at[2 * k - 1], rs.at[2 * k - 1], {"row": p})
            cp.start()
            copies.append(cp)
        local = [
            pltpu.make_async_copy(x_ref.at[:, pl.ds(pl.multiple_of(a * SEQ_LEN, SEQ_LEN), SEQ_LEN)], rows_at(xg_ref, r), ls.at[0]),
            pltpu.make_async_copy(g_ref.at[:, pl.ds(pl.multiple_of(a * SEQ_LEN + h * QT, QT), QT)], rows_at(gg_ref, r), ls.at[1]),
        ]
        for cp in local:
            cp.start()
        w_local = pltpu.make_async_copy(w_ref, wg_ref.at[r], ls.at[2])
        @pl.when(own_w)
        def _():
            w_local.start()
        for cp in copies:
            cp.wait()
        for cp in local:
            cp.wait()
        @pl.when(own_w)
        def _():
            w_local.wait()
        for ap in range(S):
            for cq in range(C):
                t = ap * HB + c
                me = (t == r) & (c == cq)
                cp = remote(w_ref, wg_ref.at[r], ws.at[ap * C + cq], wr.at[r], {"row": t, "col": cq})
                @pl.when(jnp.logical_not(me))
                def _():
                    cp.wait_send()
        for q in range(R):
            cp = remote(w_ref, wg_ref.at[q], ws.at[0], wr.at[q], {"row": q, "col": h})
            @pl.when(jnp.logical_not(own_w & (r == q)))
            def _():
                cp.wait_recv()
        @pl.when(jnp.logical_not(send_self))
        def _():
            doc_cp.wait_send()
        @pl.when(send_self)
        def _():
            doc_local.wait()
        @pl.when(jnp.logical_not(doc_self))
        def _():
            doc_in.wait_recv()

    outs = [
        struct((D, SEQ_LEN), BF),
        struct((D, QT), BF),
        struct(docs.shape, docs.dtype),
        struct((R,) + wqkv.shape, BF),
    ]
    return comm_call(body, "gather_front", 1, (inputs, cot, docs, wqkv), outs,
                     (2 * R - 2, 2 * R - 2, S * C, R, 4, 1, 1))


def gather_weights(R, C, fb, proj, up, down):
    pb, fc = proj.shape[0], up.shape[1]
    ph, fh = pb // 2, fc // 2
    FF = fc * C

    def body(p_ref, u_ref, d_ref, po_ref, uo_ref, do_ref, zs, zr, rs_, rr, xs, xr, ls):
        d = lax.axis_index("dp")
        r = lax.axis_index("row")
        c = lax.axis_index("col")
        bar = pltpu.get_barrier_semaphore()
        for k in range(1, C):
            pl.semaphore_signal(bar, inc=1, device_id={"col": lax.rem(c + k, C)}, device_id_type=MESH)
        for k in range(1, R):
            pl.semaphore_signal(bar, inc=1, device_id={"row": lax.rem(r + k, R)}, device_id_type=MESH)
        pl.semaphore_signal(bar, inc=1, device_id={"dp": 1 - d}, device_id_type=MESH)
        pl.semaphore_wait(bar, C + R - 1)

        def wide(ref, row, col):
            return ref.at[pl.ds(pl.multiple_of(row * fb, fb), fb), pl.ds(pl.multiple_of(col * fc + d * fh, fh), fh)]

        def narrow(ref, row, col):
            return ref.at[row, pl.ds(pl.multiple_of(col * pb + d * ph, ph), ph), :]

        srcs = (p_ref.at[pl.ds(pl.multiple_of(d * ph, ph), ph), :],
                u_ref.at[:, pl.ds(pl.multiple_of(d * fh, fh), fh)],
                d_ref.at[:, pl.ds(pl.multiple_of(d * fh, fh), fh)])

        def places(row, col):
            return (narrow(po_ref, row, col), wide(uo_ref, row, col), wide(do_ref, row, col))

        mine = places(r, c)
        local = [pltpu.make_async_copy(srcs[i], mine[i], ls.at[i]) for i in range(3)]
        for cp in local:
            cp.start()
        zc = []
        for k in range(1, C):
            q = lax.rem(c + k, C)
            for i in range(3):
                cp = remote(srcs[i], mine[i], zs.at[(k - 1) * 3 + i], zr.at[(k - 1) * 3 + i], {"col": q})
                cp.start()
                zc.append(cp)
        for cp in local:
            cp.wait()
        sent = []

        def spread(step, col):
            here = places(r, col)
            for k in range(1, R):
                p = lax.rem(r + k, R)
                for i in range(3):
                    slot = (step * (R - 1) + k - 1) * 3 + i
                    cp = remote(here[i], here[i], rs_.at[slot], rr.at[slot], {"row": p})
                    cp.start()
                    sent.append(cp)

        spread(0, c)
        for k in range(1, C):
            for i in range(3):
                zc[(k - 1) * 3 + i].wait()
            spread(k, lax.rem(c + C - k, C))
        for cp in sent:
            cp.wait()
        cross = []
        for q in range(C):
            for i, ref in enumerate((uo_ref, do_ref)):
                part = ref.at[:, pl.ds(pl.multiple_of(q * fc + d * fh, fh), fh)]
                cp = remote(part, part, xs.at[q * 3 + i], xr.at[q * 3 + i], {"dp": 1 - d})
                cp.start()
                cross.append(cp)
            part = po_ref.at[:, pl.ds(pl.multiple_of(q * pb + d * ph, ph), ph), :]
            cp = remote(part, part, xs.at[q * 3 + 2], xr.at[q * 3 + 2], {"dp": 1 - d})
            cp.start()
            cross.append(cp)
        for cp in cross:
            cp.wait()

    outs = [struct((R, D, fb), BF), struct((D, FF), BF), struct((D, FF), BF)]
    nz, nr = 3 * (C - 1), 3 * C * (R - 1)
    return comm_call(body, "gather_weights", 2, (proj, up, down), outs, (nz, nz, nr, nr, 3 * C, 3 * C, 3))


def group_exchange(R, S, cid, name, x, out, src_of, dst_of):
    HB = R // S

    def body(x_ref, o_ref, ss, rs, ls):
        r = lax.axis_index("row")
        a, h = r // HB, lax.rem(r, HB)
        bar = pltpu.get_barrier_semaphore()
        for k in range(1, HB):
            pl.semaphore_signal(bar, inc=1, device_id={"row": a * HB + lax.rem(h + k, HB)}, device_id_type=MESH)
        pl.semaphore_wait(bar, HB - 1)
        copies = []
        for k in range(1, HB):
            p = lax.rem(h + k, HB)
            cp = remote(src_of(x_ref, p), dst_of(o_ref, h), ss.at[k - 1], rs.at[k - 1], {"row": a * HB + p})
            cp.start()
            copies.append(cp)
        local = pltpu.make_async_copy(src_of(x_ref, h), dst_of(o_ref, h), ls.at[0])
        local.start()
        for cp in copies:
            cp.wait()
        local.wait()

    return comm_call(body, name, cid, (x,), [out], (HB - 1, HB - 1, 1))[0]


def send_qkv_grad(R, C, S, fb, blocks):
    HB = R // S

    def body(b_ref, o_ref, ss, rs, ls):
        r = lax.axis_index("row")
        c = lax.axis_index("col")
        a, h = r // HB, lax.rem(r, HB)
        own = c == h
        bar = pltpu.get_barrier_semaphore()
        for ap in range(S):
            for cq in range(C):
                t = ap * HB + c
                @pl.when(jnp.logical_not((t == r) & (c == cq)))
                def _():
                    pl.semaphore_signal(bar, inc=1, device_id={"row": t, "col": cq}, device_id_type=MESH)
        pl.semaphore_wait(bar, R - 1 + jnp.where(own, 0, 1))
        slot = a * C + c
        for q in range(R):
            cp = remote(b_ref.at[q], o_ref.at[slot], ss.at[q], rs.at[slot], {"row": q, "col": h})
            @pl.when(jnp.logical_not(own & (r == q)))
            def _():
                cp.start()
        local = pltpu.make_async_copy(b_ref.at[r], o_ref.at[slot], ls.at[0])
        @pl.when(own)
        def _():
            local.start()
            local.wait()
        for q in range(R):
            cp = remote(b_ref.at[q], o_ref.at[slot], ss.at[q], rs.at[slot], {"row": q, "col": h})
            @pl.when(jnp.logical_not(own & (r == q)))
            def _():
                cp.wait_send()
        for ap in range(S):
            for cq in range(C):
                t = ap * HB + c
                cp = remote(b_ref.at[0], o_ref.at[ap * C + cq], ss.at[0], rs.at[ap * C + cq], {"row": t, "col": cq})
                @pl.when(jnp.logical_not((t == r) & (c == cq)))
                def _():
                    cp.wait_recv()

    out = struct((S * C,) + blocks.shape[1:], blocks.dtype)
    return comm_call(body, "send_qkv_grad", 9, (blocks,), [out], (R, S * C, 1))[0]


def exact_gelu(values):
    return jax.nn.gelu(values, approximate=False)


def col_vec(v):
    return v.astype(F32)[:, None]


def norm_forward(residual, gain, shift):
    average = jnp.mean(residual, axis=0, keepdims=True)
    spread = jnp.mean(residual * residual, axis=0, keepdims=True) - average * average
    scaling = lax.rsqrt(spread + EPSILON)
    normed = (residual - average) * scaling
    return normed * gain + shift, normed, scaling


def norm_backward(upstream, gain, normed, scaling):
    scaled = upstream * gain
    mean_scaled = jnp.mean(scaled, axis=0, keepdims=True)
    crossed = jnp.mean(scaled * normed, axis=0, keepdims=True)
    return scaling * (scaled - mean_scaled - normed * crossed)


def other_core(x):
    return lax.ppermute(x, "dp", [(0, 1), (1, 0)])


def make_shards(R, C):
    def shards(inputs, doc_ids, qkv_weight, qkv_bias, proj_weight, proj_bias, first_gain, first_shift,
               ffn_up, ffn_up_bias, ffn_down, ffn_down_bias, second_gain, second_shift, conv_kernel, cotangent):
        S = inputs.shape[1] // SEQ_LEN
        HB = R // S
        QT = SEQ_LEN // HB
        fb = inputs.shape[0]
        nh = conv_kernel.shape[0]
        qw = qkv_weight.shape[1]
        fc = ffn_up.shape[1]
        fh = fc // 2
        pb = proj_weight.shape[0]
        ph = pb // 2
        FF = fc * C
        dp = lax.axis_index("dp")
        r = lax.axis_index("row")
        c = lax.axis_index("col")
        a, h = r // HB, r % HB

        small = jnp.concatenate([first_gain, first_shift, second_gain, second_shift,
                                 proj_bias.astype(F32), ffn_down_bias.astype(F32)]).reshape(6, fb)
        row_params = lax.all_gather(small, "row", axis=1, tiled=True)
        col_params = lax.all_gather(jnp.concatenate([ffn_up_bias.astype(F32), conv_kernel.reshape(-1)]), "col", axis=0)
        gain1, shift1, gain2, shift2, bias_p, bias_d = [row_params[i][:, None] for i in range(6)]
        bias_u = col_params[:, :fc].reshape(FF)[:, None]
        taps = lax.dynamic_index_in_dim(col_params[:, fc:], h, 0, keepdims=False).reshape(nh, CONV)

        bias_rows = jnp.concatenate([qkv_bias[None], jnp.zeros((15, qw), BF)], axis=0)
        wext = jnp.concatenate([qkv_weight, bias_rows], axis=0)
        xg, cg, docs, wg = gather_front(R, C, S, fb, inputs, cotangent.astype(BF), doc_ids[None], wext)
        wp, wu, wd = gather_weights(R, C, fb, proj_weight, ffn_up, ffn_down)
        wq = wg[:, :fb].reshape(D, qw)
        qkv = (tn(wq, xg) + wg[0, fb].astype(F32)[:, None]).astype(BF)
        fwd = attn_fwd(qkv, docs, taps)
        att, saved = fwd[0], fwd[1:]
        hb = nh * HEAD_DIM

        def my_rows(ref, k):
            return ref.at[pl.ds(pl.multiple_of(k * hb, hb), hb), :]

        def my_cols(ref, k):
            return ref.at[:, pl.ds(pl.multiple_of(k * QT, QT), QT)]

        attq = group_exchange(R, S, 3, "spread_attended", att, struct((D, QT), BF), my_cols, my_rows)

        rows = lax.dynamic_slice_in_dim(xg, h * QT, QT, 1).astype(F32)
        proj_out = jnp.concatenate([tn(wp[q], attq) for q in range(R)], axis=0)
        res1 = rows + (proj_out + bias_p)
        hidden, normed1, scale1 = norm_forward(res1, gain1, shift1)
        hid = hidden.astype(BF)
        pre = tn(wu, hid) + bias_u
        active, gelu_back = jax.vjp(exact_gelu, pre)
        act = active.astype(BF)
        res2 = hidden + (nn(wd, act) + bias_d)
        out, normed2, scale2 = norm_forward(res2, gain2, shift2)
        ups = cg.astype(F32)
        gres2 = norm_backward(ups, gain2, normed2, scale2)
        gdown = gres2.astype(BF)
        gpre = gelu_back(tn(wd, gdown))[0].astype(BF)
        ghid = gres2 + nn(wu, gpre)
        gres1 = norm_backward(ghid, gain1, normed1, scale1)
        gatt_out = gres1.astype(BF)
        gattq = sum(nn(wp[q], gatt_out[q * fb:(q + 1) * fb]) for q in range(R)).astype(BF)
        gatt = group_exchange(R, S, 4, "spread_grad", gattq, struct((hb, SEQ_LEN), BF), my_rows, my_cols)
        gqkv, gtaps = attn_bwd(qkv, gatt, taps, saved)

        part = nn(wq, gqkv)
        part = lax.dynamic_update_slice_in_dim(part, lax.dynamic_slice_in_dim(part, h * QT, QT, 1) + gres1, h * QT, 1).astype(BF)

        def feat(ref, q):
            return ref.at[pl.ds(pl.multiple_of(q * fb, fb), fb), :]

        def slot(ref, q):
            return ref.at[q]

        def place(i, ref, q):
            return ref.at[:, pl.ds(pl.multiple_of(q * QT, QT), QT)]

        terms, out_block = axis_exchange(
            "row", R, 5, "spread_input_grad", (part, out.astype(BF)),
            [struct((R, fb, SEQ_LEN), BF), struct((fb, S * SEQ_LEN), BF)],
            lambda i, ref, q: feat(ref, q),
            lambda i, ref, q: slot(ref, q) if i == 0 else place(i, ref, q))
        gin = jnp.sum(terms.reshape(S, HB, fb, SEQ_LEN).astype(F32), axis=1)
        grad_inputs = jnp.swapaxes(gin, 0, 1).reshape(fb, S * SEQ_LEN)

        def half(x, n, k):
            return lax.dynamic_index_in_dim(x.reshape(C, 2, n, QT), k, 1, keepdims=False).reshape(C * n, QT)

        gives = (hid, gdown, gatt_out, half(act, fh, 1 - dp), half(gpre, fh, 1 - dp), half(attq, ph, 1 - dp))
        got = [other_core(x) for x in gives]
        keep = (hid, gdown, gatt_out, half(act, fh, dp), half(gpre, fh, dp), half(attq, ph, dp))
        hid2, gdown2, gatt2, act2, gpre2, attq2 = [jnp.concatenate([x, y], axis=1) for x, y in zip(keep, got)]
        gu = nt(hid2, gpre2).astype(BF)
        gd = nt(gdown2, act2).astype(BF)
        gp = nt(attq2, gatt2).astype(BF)
        gp = jnp.swapaxes(gp.reshape(C * ph, R, fb), 0, 1)
        tu, td, tp = axis_exchange(
            "row", R, 6, "reduce_rows", (gu, gd, gp),
            [struct((R, fb, C * fh), BF)] * 2 + [struct((R, C * ph, fb), BF)],
            lambda i, ref, q: slot(ref, q) if i == 2 else feat(ref, q),
            lambda i, ref, q: slot(ref, q))
        su, sd, sp = [jnp.sum(t.astype(F32), axis=0).astype(BF) for t in (tu, td, tp)]

        def hcols(ref, q):
            return ref.at[:, pl.ds(pl.multiple_of(q * fh, fh), fh)]

        def prows(ref, q):
            return ref.at[pl.ds(pl.multiple_of(q * ph, ph), ph), :]

        zu, zd, zp = axis_exchange(
            "col", C, 7, "reduce_cols", (su, sd, sp),
            [struct((C, fb, fh), BF)] * 2 + [struct((C, ph, fb), BF)],
            lambda i, ref, q: prows(ref, q) if i == 2 else hcols(ref, q),
            lambda i, ref, q: slot(ref, q))
        fu, fd, fp = [jnp.sum(t.astype(F32), axis=0) for t in (zu, zd, zp)]

        def both(x, axis):
            y = other_core(x)
            return jnp.concatenate([jnp.where(dp == 0, x, y), jnp.where(dp == 0, y, x)], axis=axis)

        grad_up, grad_down, grad_proj = both(fu, 1), both(fd, 1), both(fp, 0)

        gq = nt(xg, gqkv).astype(BF).reshape(R, fb, qw)
        pair = gq.reshape(R // 2, 2, fb, qw)
        mine = lax.dynamic_index_in_dim(pair, dp, 1, keepdims=False)
        theirs = other_core(lax.dynamic_index_in_dim(pair, 1 - dp, 1, keepdims=False))
        summed = (mine.astype(F32) + theirs.astype(F32)).astype(BF)
        full = jnp.stack([summed, summed], axis=1).reshape(R, fb, qw)
        qterms = send_qkv_grad(R, C, S, fb, full)
        qsum = jnp.sum(qterms.astype(F32), axis=0)
        qother = other_core(qsum)
        grad_qkv = jnp.where((r % 2) == dp, qsum, qother)

        def total(x):
            return jnp.sum(x.astype(F32), axis=1)

        def at(x, size, index):
            return lax.dynamic_update_slice_in_dim(jnp.zeros((size,), F32), x, index * x.shape[0], 0)

        vec = jnp.concatenate([
            total(ghid * normed1), total(ghid), total(ups * normed2),
            total(gatt_out), total(gdown), total(gpre),
            at(total(cotangent), D, r), at(total(gqkv), C * qw, h),
            at(jnp.sum(gtaps, axis=(2, 3))[:, :CONV].reshape(-1), C * nh * CONV, h)])
        vec = lax.psum(vec, ("dp", "row", "col"))
        sizes = [D] * 5 + [FF, D, C * qw, C * nh * CONV]
        pieces = []
        offset = 0
        for n in sizes:
            pieces.append(vec[offset:offset + n])
            offset += n
        g1, b1, g2, pbias, dbias, ubias, b2, qbias, tgrad = pieces

        def my_part(x, n, index):
            return lax.dynamic_slice_in_dim(x, index * n, n, 0)

        return (out_block.astype(F32), grad_inputs, grad_qkv, my_part(qbias, qw, c), grad_proj, my_part(pbias, fb, r),
                my_part(g1, fb, r), my_part(b1, fb, r), grad_up, my_part(ubias, fc, c), grad_down,
                my_part(dbias, fb, r), my_part(g2, fb, r), my_part(b2, fb, r),
                my_part(tgrad, nh * CONV, c).reshape(nh, CONV))
    return shards


def solution(mesh):
    in_specs = (P("row", ("dp", "col")), P(("dp", "row")), P("row", "col"), P("col"), P("col", "row"), P("row"),
                P("row"), P("row"), P("row", "col"), P("col"), P("row", "col"), P("row"), P("row"), P("row"),
                P("col", None), P("row", ("dp", "col")))
    out_specs = (P("row", ("dp", "col")), P("row", ("dp", "col")), P("row", "col"), P("col"), P("col", "row"), P("row"),
                 P("row"), P("row"), P("row", "col"), P("col"), P("row", "col"), P("row"), P("row"), P("row"),
                 P("col", None))
    fn = make_shards(mesh.shape["row"], mesh.shape["col"])
    return jax.shard_map(fn, mesh=mesh, in_specs=in_specs, out_specs=out_specs, check_vma=False)
```

```python
import functools

import jax
import jax.numpy as jnp
from jax import lax
from jax.experimental import pallas as pl
from jax.experimental.pallas import tpu as pltpu
from jax.sharding import PartitionSpec as P

D = 768
HEAD_DIM = 64
SEQ_LEN = 1024
EPSILON = 1e-05
F32=jnp.float32; BF=jnp.bfloat16
HD=64; SEQ=1024; SEG=16; CONV=33; ITERS=6; L=64
NEG=-1e9

def dg(a,b,ca,cb):
    return lax.dot_general(a,b,(((ca,),(cb,)),((),())),preferred_element_type=F32)
def nn(a,b): return dg(a,b,1,0)
def nt(a,b): return dg(a,b,1,1)
def tn(a,b): return dg(a,b,0,0)
def split(x):
    hi=x.astype(BF); lo=(x-hi.astype(F32)).astype(BF)
    return hi,lo
def cat(hl): return jnp.concatenate(hl,axis=0)
def halves(x):
    n=x.shape[0]//2
    return x[:n]+x[n:]
def nn2(a,b): return halves(nn(cat(split(a)),b))
def nt2(a,b): return halves(nt(cat(split(a)),b))
def nn3(a,b):
    ah,al=split(a); bh,bl=split(b)
    return halves(nn(cat((ah,al)),bh))+nn(ah,bl)
def nt3(a,b):
    ah,al=split(a); bh,bl=split(b)
    return halves(nt(cat((ah,al)),bh))+nt(ah,bl)

def iota(shape,dim): return lax.broadcasted_iota(jnp.int32,shape,dim)
def avg_mat():
    return jnp.where((iota((L,SEQ),1)//SEG)==iota((L,SEQ),0),F32(1.0/SEG),F32(0)).astype(BF)
def pick_mat():
    return jnp.where(iota((L,SEQ),1)==iota((L,SEQ),0)*SEG,F32(1),F32(0)).astype(BF)

def conv_masks(doc_row,mask_ref):
    t=iota((1,SEQ),1)
    for o in range(CONV):
        s=o-CONV//2
        rolled=pltpu.roll(doc_row,(-s)%SEQ,1) if s else doc_row
        ok=(rolled==doc_row)&(t+s>=0)&(t+s<SEQ)
        mask_ref[pl.ds(o,1),:]=jnp.where(ok,F32(1),F32(0))

def head_scores(h,qkv_ref,doc_row,land_row,land_col,k1_ref,k3_ref,k2_ref,ql_ref,kl_ref,sum_ref):
    b=h*3*HD
    q=qkv_ref[b:b+HD,:]; k=qkv_ref[b+HD:b+2*HD,:]; v=qkv_ref[b+2*HD:b+3*HD,:]
    at=avg_mat()
    ql=nt(at,q); kl=nt(at,k)
    ql_ref[h]=ql; kl_ref[h]=kl
    keep=land_col==doc_row
    s1=jnp.where(keep,nn2(kl,q)*0.125,NEG)
    e1=jnp.exp(s1-jnp.max(s1,axis=0,keepdims=True))
    k1_ref[h]=e1/jnp.sum(e1,axis=0,keepdims=True)
    s3=jnp.where(keep,nn2(ql,k)*0.125,NEG)
    e3=jnp.exp(s3-jnp.max(s3,axis=1,keepdims=True))
    k3=e3/jnp.sum(e3,axis=1,keepdims=True)
    k3_ref[h]=k3
    s2=jnp.where(land_col==land_row,nt3(ql,kl)*0.125,NEG)
    e2=jnp.exp(s2-jnp.max(s2,axis=1,keepdims=True))
    k2_ref[h]=e2/jnp.sum(e2,axis=1,keepdims=True)
    sum_ref[h]=nt2(k3,v)

def eye(): return jnp.where(iota((L,L),0)==iota((L,L),1),F32(1),F32(0))

def newton(nh,k2_ref,v_ref,p_ref,n1_ref,n2_ref,n3_ref):
    for h in range(nh):
        v_ref[0,h]=k2_ref[h].T*(1.0/L)
    def step(i,_):
        I=eye()
        P=[nn3(k2_ref[h],v_ref[i,h]) for h in range(nh)]
        N1=[7.0*I-P[h] for h in range(nh)]
        N2=[15.0*I-nn3(P[h],N1[h]) for h in range(nh)]
        N3=[13.0*I-nn3(P[h],N2[h]) for h in range(nh)]
        for h in range(nh):
            p_ref[i,h]=P[h]; n1_ref[i,h]=N1[h]; n2_ref[i,h]=N2[h]; n3_ref[i,h]=N3[h]
            v_ref[i+1,h]=nn3(0.25*v_ref[i,h],N3[h])
        return 0
    lax.fori_loop(0,ITERS,step,0)

def conv_fwd(nh,qkv_ref,mask_ref,w_ref,acc_ref):
    for h in range(nh):
        def group(g,_):
            r=pl.multiple_of(h*3*HD+2*HD+g*16,16)
            v=qkv_ref[pl.ds(r,16),:].astype(F32)
            acc=jnp.zeros((16,SEQ),F32)
            for o in range(CONV):
                s=o-CONV//2
                c=mask_ref[pl.ds(o,1),:]*w_ref[1+h,o]
                acc=acc+(pltpu.roll(v,(-s)%SEQ,1) if s else v)*c
            ro=pl.multiple_of(h*HD+g*16,16)
            acc_ref[pl.ds(ro,16),:]=acc
            return 0
        lax.fori_loop(0,HD//16,group,0)

def head_out(h,k1_ref,inv,sum_ref,mix_ref,acc_ref,att_ref):
    mixed=nn3(inv,sum_ref[h])
    mix_ref[h]=mixed
    mt=mixed.T
    k1=k1_ref[h]
    res=nn3(mt,k1)
    att_ref[h*HD:(h+1)*HD,:]=(res+acc_ref[h*HD:(h+1)*HD,:]).astype(BF)

def newton_bwd(nh,k2_ref,v_ref,p_ref,n1_ref,n2_ref,n3_ref,gv_ref,gk_ref):
    for h in range(nh):
        gk_ref[h]=jnp.zeros((L,L),F32)
    def step(j,_):
        i=ITERS-1-j
        H=range(nh)
        gV=[gv_ref[h] for h in H]; V=[v_ref[i,h] for h in H]
        VT=[V[h].T for h in H]; PT=[p_ref[i,h].T for h in H]
        gN3=[0.25*nn3(VT[h],gV[h]) for h in H]
        gVn=[0.25*nt3(gV[h],n3_ref[i,h]) for h in H]
        gN2=[-nn3(PT[h],gN3[h]) for h in H]
        gN1=[-nn3(PT[h],gN2[h]) for h in H]
        gP=[-nt3(gN3[h],n2_ref[i,h])-nt3(gN2[h],n1_ref[i,h])-gN1[h] for h in H]
        for h in H:
            gk_ref[h]+=nt3(gP[h],V[h])
            gv_ref[h]=gVn[h]+nn3(k2_ref[h].T,gP[h])
        return 0
    lax.fori_loop(0,ITERS,step,0)
    for h in range(nh):
        gk_ref[h]+=gv_ref[h].T*(1.0/L)

def conv_bwd(nh,qkv_ref,g_ref,mask_ref,w_ref,gacc_ref,gw_ref):
    for h in range(nh):
        gw_ref[h]=jnp.zeros((40,8,128),F32)
        def group(g,_):
            r=pl.multiple_of(h*3*HD+2*HD+g*16,16)
            ro=pl.multiple_of(h*HD+g*16,16)
            v=qkv_ref[pl.ds(r,16),:].astype(F32)
            gg=g_ref[pl.ds(ro,16),:].astype(F32)
            acc=jnp.zeros((16,SEQ),F32)
            for o in range(CONV):
                s=o-CONV//2
                m=mask_ref[pl.ds(CONV-1-o,1),:]
                R=(pltpu.roll(gg,s%SEQ,1) if s else gg)*m
                acc=acc+R*w_ref[1+h,o]
                pr=v*R
                x=pr[0:8]+pr[8:16]
                y=x[:,0:128]
                for c in range(1,SEQ//128): y=y+x[:,c*128:(c+1)*128]
                gw_ref[h,o]+=y
            gacc_ref[pl.ds(ro,16),:]=acc
            return 0
        lax.fori_loop(0,HD//16,group,0)

def head_bwd1(h,qkv_ref,g_ref,k1_ref,k3_ref,sum_ref,mix_ref,inv,gv_ref,gs1_ref,gs3_ref,gacc_ref):
    b=h*3*HD
    v=qkv_ref[b+2*HD:b+3*HD,:]
    g=g_ref[h*HD:(h+1)*HD,:]
    k1=k1_ref[h]
    gmix=nt2(k1,g)
    gk1=nn2(mix_ref[h],g)
    gs1_ref[h]=k1*(gk1-jnp.sum(k1*gk1,axis=0,keepdims=True))
    gv_ref[h]=nt3(gmix,sum_ref[h])
    gsum=nn3(inv.T,gmix)
    k3=k3_ref[h]
    gk3=nn2(gsum,v)
    gs3_ref[h]=k3*(gk3-jnp.sum(k3*gk3,axis=1,keepdims=True))
    gacc_ref[h*HD:(h+1)*HD,:]+=nn3(gsum.T,k3)

def head_bwd2(h,qkv_ref,k2_ref,gk_ref,ql_ref,kl_ref,gs1_ref,gs3_ref,gacc_ref,out_ref):
    b=h*3*HD
    q=qkv_ref[b:b+HD,:]; k=qkv_ref[b+HD:b+2*HD,:]
    k2=k2_ref[h]; gk2=gk_ref[h]
    gs2=k2*(gk2-jnp.sum(k2*gk2,axis=1,keepdims=True))
    ql=ql_ref[h]; kl=kl_ref[h]
    gs1=gs1_ref[h]; gs3=gs3_ref[h]
    gkl=nt2(gs1,q)+nn3(gs2.T,ql)
    gql=nt2(gs3,k)+nn3(gs2,kl)
    at=avg_mat()
    gq=(nn3(kl.T,gs1)+nn2(gql.T,at))*0.125
    gk=(nn3(ql.T,gs3)+nn2(gkl.T,at))*0.125
    out_ref[b:b+HD,:]=gq.astype(BF)
    out_ref[b+HD:b+2*HD,:]=gk.astype(BF)
    out_ref[b+2*HD:b+3*HD,:]=gacc_ref[h*HD:(h+1)*HD,:].astype(BF)

MESH = pl.DeviceIdType.MESH
QUERY = 256


def struct(shape, dtype):
    return jax.ShapeDtypeStruct(shape, dtype)


def remote(src, dst, ss, rs, dev):
    return pltpu.make_async_remote_copy(
        src_ref=src, dst_ref=dst, send_sem=ss, recv_sem=rs, device_id=dev, device_id_type=MESH
    )


def run(*copies):
    for cp in copies:
        cp.start()


def al(x, n):
    return pl.multiple_of(x, n)


def erf(x):
    x = jnp.clip(x, -4.0, 4.0)
    y = x * x
    p = jnp.float32(-2.72614225801306e-10)
    for k in (2.77068142495902e-08, -2.10102402082508e-06, -5.69250639462346e-05,
              -7.34990630326855e-04, -2.95459980854025e-03, -1.60960333262415e-02):
        p = p * y + jnp.float32(k)
    q = jnp.float32(-1.45660718464996e-05)
    for k in (-2.13374055278905e-04, -1.68282697438203e-03, -7.37332916720468e-03, -1.42647390514189e-02):
        q = q * y + jnp.float32(k)
    return x * p / q


def norm_forward(residual, gain, shift):
    average = jnp.mean(residual, axis=1, keepdims=True)
    spread = jnp.mean(residual * residual, axis=1, keepdims=True) - average * average
    scaling = lax.rsqrt(spread + EPSILON)
    normed = (residual - average) * scaling
    return normed * gain + shift, normed, scaling


def norm_backward(upstream, gain, normed, scaling):
    scaled = upstream * gain
    mean_scaled = jnp.mean(scaled, axis=1, keepdims=True)
    crossed = jnp.mean(scaled * normed, axis=1, keepdims=True)
    return scaling * (scaled - mean_scaled - normed * crossed)


def tsum(x):
    return jnp.sum(x, axis=0, keepdims=True)


def layer_call(R, C, S, fb, nh, fc, pb, qw, args):
    HB = R // S
    QT = SEQ_LEN // HB
    FF = fc * C
    fh, ph = fc // 2, pb // 2
    hb = nh * HD
    fbp = args["rowp"].shape[1]
    NV = 24
    CH = 256
    V = pltpu.VMEM
    small = (nh, L, L)
    names_in = ["x", "cot", "wq", "wp", "wu", "wd", "meta", "rowp", "colp"]
    outs = dict(
        out=((fb, S * SEQ_LEN), F32), gin=((fb, S * SEQ_LEN), F32), gqw=((fb, qw), F32), gup=((fb, fc), F32),
        gdn=((fb, fc), F32), gpj=((pb, fb), F32), sv=((NV, D), F32))
    bufs = dict(
        xg=((D, SEQ_LEN), BF), wg=((R, fb, qw), BF), mt=((8, SEQ_LEN), F32), rp=((R, 8, fbp), F32), cp=((C, 8, fc), F32),
        cg=((D, QT), BF), wpf=((R, D, fb), BF), wuf=((D, FF), BF), wdf=((D, FF), BF),
        qkv=((3 * hb, SEQ_LEN), BF), k1=((nh, L, SEQ_LEN), F32), k3=((nh, L, SEQ_LEN), F32), k2=(small, F32),
        ql=(small, F32), kl=(small, F32), sm=(small, F32), mix=(small, F32), nv=((ITERS + 1,) + small, F32),
        np_=((ITERS,) + small, F32), n1=((ITERS,) + small, F32), n2=((ITERS,) + small, F32), n3=((ITERS,) + small, F32),
        mask=((40, SEQ_LEN), F32), acc=((hb, SEQ_LEN), F32), att=((hb, SEQ_LEN), BF), attq=((D, QT), BF),
        resT=((D, QT), F32), prow=((8, D), F32), hidden=((QT, D), F32), hid=((QT, D), BF), nm1=((QT, D), F32),
        sc1=((QT, 1), F32), act=((QT, FF), BF), dact=((QT, FF), F32), res2=((QT, D), F32), gdown=((QT, D), BF),
        gpre=((QT, FF), BF), gattoT=((D, QT), BF), outT=((D, QT), BF),
        gatt=((hb, SEQ_LEN), BF),
        hid_o=((QT, D), BF), gdown_o=((QT, D), BF), gattoT_o=((D, QT), BF), att_o=((C * ph, QT), BF),
        act_o=((QT, C * fh), BF), gpre_o=((QT, C * fh), BF),
        gu=((D, C * fh), BF), gd=((D, C * fh), BF), gp=((R, C * ph, fb), BF),
        ru=((R - 1, fb, C * fh), BF), rd=((R - 1, fb, C * fh), BF), rpj=((R - 1, C * ph, fb), BF),

        zu=((C - 1, fb, fh), BF), zd=((C - 1, fb, fh), BF), zp=((C - 1, ph, fb), BF),
        gv=(small, F32), gk=(small, F32),
        gw=((nh, 40, 8, 128), F32), gqkv=((3 * hb, SEQ_LEN), BF),
        part=((D, SEQ_LEN), BF), pr=((R - 1, fb, SEQ_LEN), BF), outr=((fb, S * SEQ_LEN), BF),
        gq=((R, fb, qw), BF), gqo=((R // 2, fb, qw), BF), gqr=((R, fb, qw), BF),
        gqz=((C, fb, qw), BF), svr=((R - 1, NV, D), F32), svz=((C - 1, NV, D), F32), svo=((NV, D), F32),
        sv1=((NV, D), F32), sv2=((NV, D), F32), sv0=((NV, D), F32), tmp=((8, D), F32))
    sems = dict(
        x=R - 1, cot=R - 1, rowp=R - 1, colp=C - 1, meta=1, ws=S * C, wr=R, wd2=R, z=3 * (C - 1), row=3 * C * (R - 1),
        cross=3 * C, att=HB - 1, gatt=HB - 1, ex=3 + 3 * C, rrow=3 * (R - 1), rcol=3 * (C - 1), part=R - 1, outx=R - 1,
        gqd=R // 2, gqrow=R, gqcol=C, gqf=1, svrow=R - 1, svcol=C - 1, svd=1, fin=3, loc=12)

    def body(*refs):
        n = len(names_in)
        i = dict(zip(names_in, refs[:n]))
        o = dict(zip(outs, refs[n:n + len(outs)]))
        k = n + len(outs)
        b = dict(zip(bufs, refs[k:k + len(bufs)]))
        k += len(bufs)
        ss = dict(zip(sems, refs[k:k + len(sems)]))
        k += len(sems)
        rs = dict(zip(sems, refs[k:k + len(sems)]))
        k += len(sems)
        tap_ref = refs[k]
        d = lax.axis_index("dp")
        r = lax.axis_index("row")
        c = lax.axis_index("col")
        a, h = r // HB, lax.rem(r, HB)
        core = {"dp": 1 - d}

        def snd(group, slot, src, dst, dev):
            return remote(src, dst, ss[group].at[slot], rs[group].at[slot], dev)

        def loc(slot, src, dst):
            return pltpu.make_async_copy(src, dst, ss["loc"].at[slot])

        def fr(ref, q):
            return ref.at[pl.ds(al(q * fb, fb), fb), :]

        own = c == h
        bar = pltpu.get_barrier_semaphore()
        for k in range(1, R):
            pl.semaphore_signal(bar, inc=1, device_id={"row": lax.rem(r + k, R)}, device_id_type=MESH)
        for k in range(1, C):
            pl.semaphore_signal(bar, inc=1, device_id={"col": lax.rem(c + k, C)}, device_id_type=MESH)
        pl.semaphore_signal(bar, inc=1, device_id=core, device_id_type=MESH)
        for q in range(R):
            @pl.when(jnp.logical_not(own & (r == q)))
            def _():
                pl.semaphore_signal(bar, inc=1, device_id={"row": q, "col": h}, device_id_type=MESH)
        pl.semaphore_wait(bar, R - 1 + C - 1 + 1 + S * C - jnp.where(own, 1, 0))

        def xcols(q):
            return i["x"].at[:, pl.ds(al(q // HB * SEQ_LEN, SEQ_LEN), SEQ_LEN)]

        def peer(k):
            return lax.rem(r + k, R)

        xs = [snd("x", k - 1, xcols(peer(k)), fr(b["xg"], r), {"row": peer(k)}) for k in range(1, R)]
        run(*xs)
        x_loc = loc(0, xcols(r), fr(b["xg"], r))
        x_loc.start()
        par = lax.rem(r, 2) == d
        w_out = []
        for ap in range(S):
            for cq in range(C):
                t = ap * HB + c
                go = par & jnp.logical_not((t == r) & (c == cq))
                cp = remote(i["wq"], b["wg"].at[r], ss["ws"].at[ap * C + cq], rs["wr"].at[r], {"row": t, "col": cq})
                w_out.append((go, cp))
        for go, cp in w_out:
            @pl.when(go)
            def _():
                cp.start()
        w_loc = loc(1, i["wq"], b["wg"].at[r])
        @pl.when(own & par)
        def _():
            w_loc.start()
        dst_row, dst_col = lax.rem(r, S) * HB + c, r // S
        meta_self = (dst_row == r) & (dst_col == c)
        src_row = c * S + a
        meta_out = snd("meta", 0, i["meta"], b["mt"], {"row": dst_row, "col": dst_col})
        meta_in = snd("meta", 0, i["meta"], b["mt"], {"row": src_row, "col": h})
        meta_loc = loc(2, i["meta"], b["mt"])
        @pl.when(jnp.logical_not(meta_self))
        def _():
            meta_out.start()
        @pl.when(meta_self)
        def _():
            meta_loc.start()
        def wide(ref, row, col):
            return ref.at[pl.ds(al(row * fb, fb), fb), pl.ds(al(col * fc + d * fh, fh), fh)]

        def narrow(ref, row, col):
            return ref.at[row, pl.ds(al(col * pb + d * ph, ph), ph), :]

        srcs = (i["wp"].at[pl.ds(al(d * ph, ph), ph), :], i["wu"].at[:, pl.ds(al(d * fh, fh), fh)],
                i["wd"].at[:, pl.ds(al(d * fh, fh), fh)])

        def places(row, col):
            return narrow(b["wpf"], row, col), wide(b["wuf"], row, col), wide(b["wdf"], row, col)

        mine = places(r, c)
        bulk_loc = [loc(3 + j, srcs[j], mine[j]) for j in range(3)]
        run(*bulk_loc)
        zc = []
        for k in range(1, C):
            for j in range(3):
                zc.append(snd("z", (k - 1) * 3 + j, srcs[j], mine[j], {"col": lax.rem(c + k, C)}))
        run(*zc)
        row_out = []
        for step in range(C):
            here = places(r, lax.rem(c + C - step, C))
            row_out.append([
                snd("row", (step * (R - 1) + k - 1) * 3 + j, here[j], here[j], {"row": peer(k)})
                for k in range(1, R) for j in range(3)])

        def spread(step):
            if step:
                for j in range(3):
                    zc[(step - 1) * 3 + j].wait_recv()
            run(*row_out[step])

        for cp in xs:
            cp.wait()
        for cp in bulk_loc:
            cp.wait()
        gs = [snd("cot", k - 1, i["cot"].at[:, pl.ds(al(peer(k) // HB * SEQ_LEN + lax.rem(peer(k), HB) * QT, QT), QT)],
                  fr(b["cg"], r), {"row": peer(k)}) for k in range(1, R)]
        run(*gs)
        g_loc = loc(6, i["cot"].at[:, pl.ds(al(a * SEQ_LEN + h * QT, QT), QT)], fr(b["cg"], r))
        g_loc.start()
        ps = [snd("rowp", k - 1, i["rowp"], b["rp"].at[r], {"row": peer(k)}) for k in range(1, R)]
        run(*ps)
        p_loc = loc(7, i["rowp"], b["rp"].at[r])
        p_loc.start()
        cs = [snd("colp", k - 1, i["colp"], b["cp"].at[c], {"col": lax.rem(c + k, C)}) for k in range(1, C)]
        run(*cs)
        c_loc = loc(8, i["colp"], b["cp"].at[c])
        c_loc.start()
        spread(0)
        w_fwd = [snd("wd2", q, b["wg"].at[q], b["wg"].at[q], core) for q in range(R)]
        for q in range(R):
            mine_q = (q % 2) == d
            here_q = own & (r == q)
            w_in = remote(i["wq"], b["wg"].at[q], ss["ws"].at[0], rs["wr"].at[q], {"row": q, "col": h})
            @pl.when(mine_q & here_q)
            def _():
                w_loc.wait()
            @pl.when(mine_q & jnp.logical_not(here_q))
            def _():
                w_in.wait_recv()
            @pl.when(mine_q)
            def _():
                w_fwd[q].start()
        for q in range(R):
            @pl.when((q % 2) != d)
            def _():
                w_fwd[q].wait_recv()
        x_loc.wait()
        @pl.when(jnp.logical_not(meta_self))
        def _():
            meta_in.wait_recv()
        @pl.when(meta_self)
        def _():
            meta_loc.wait()
        tap_cp = loc(9, b["mt"], tap_ref)
        tap_cp.start()
        qb = jnp.where(iota((8, qw), 0) == 1 + nh, b["mt"][:, 0:qw], 0.0).astype(BF)
        ones8 = jnp.ones((8, SEQ_LEN), BF)
        acc = tn(qb, ones8)
        for q in range(R):
            acc = acc + tn(b["wg"][q], b["xg"][q * fb:(q + 1) * fb, :])
        b["qkv"][...] = acc.astype(BF)
        tap_cp.wait()

        doc_row = b["mt"][0:1, :]
        rowb = jnp.broadcast_to(doc_row, (8, SEQ_LEN)).astype(BF)
        pick = pick_mat()
        land_row = nt(rowb, pick)[0:1]
        land_col = nt(pick, rowb)[:, 0:1]
        spread(1)
        for hh in range(nh):
            head_scores(hh, b["qkv"], doc_row, land_row, land_col, b["k1"], b["k3"], b["k2"], b["ql"], b["kl"], b["sm"])
        spread(2)
        newton(nh, b["k2"], b["nv"], b["np_"], b["n1"], b["n2"], b["n3"])
        for step in range(3, C):
            spread(step)
        conv_masks(doc_row, b["mask"])
        conv_fwd(nh, b["qkv"], b["mask"], tap_ref, b["acc"])
        for hh in range(nh):
            head_out(hh, b["k1"], b["nv"][ITERS, hh], b["sm"], b["mix"], b["acc"], b["att"])

        def group(k):
            return lax.rem(h + k, HB)

        def hrows(ref, q):
            return ref.at[pl.ds(al(q * hb, hb), hb), :]

        def tcols(ref, q):
            return ref.at[:, pl.ds(al(q * QT, QT), QT)]

        at = [snd("att", k - 1, tcols(b["att"], group(k)), hrows(b["attq"], h), {"row": a * HB + group(k)})
              for k in range(1, HB)]
        run(*at)
        at_loc = loc(0, tcols(b["att"], h), hrows(b["attq"], h))
        at_loc.start()
        for cp in ps + cs + gs:
            cp.wait()
        for cp in (p_loc, c_loc, g_loc):
            cp.wait()
        prow = jnp.zeros((8, D), F32)
        for q in range(R):
            piece = jnp.concatenate([b["rp"][q], jnp.zeros((8, D - fbp), F32)], axis=1)
            prow = prow + (pltpu.roll(piece, q * fb, 1) if q else piece)
        b["prow"][...] = prow
        cross = []
        for step in range(C):
            for cp in row_out[step]:
                cp.wait()
            q = lax.rem(c + C - step, C)
            pc = b["wpf"].at[:, pl.ds(al(q * pb + d * ph, ph), ph), :]
            cols = pl.ds(al(q * fc + d * fh, fh), fh)
            cross += [snd("cross", step * 3, pc, pc, core),
                      snd("cross", step * 3 + 1, b["wuf"].at[:, cols], b["wuf"].at[:, cols], core),
                      snd("cross", step * 3 + 2, b["wdf"].at[:, cols], b["wdf"].at[:, cols], core)]
            run(*cross[-3:])
        for cp in zc:
            cp.wait_send()
        for cp in at:
            cp.wait()
        at_loc.wait()
        for cp in cross:
            cp.wait()

        for q in range(R):
            t = tn(b["wpf"][q], b["attq"][...])
            b["resT"][q * fb:(q + 1) * fb, :] = t + b["xg"][q * fb:(q + 1) * fb, pl.ds(al(h * QT, QT), QT)].astype(F32)
        res1 = b["resT"][...].T + b["prow"][4:5, :]
        hidden, nm1, sc1 = norm_forward(res1, b["prow"][0:1, :], b["prow"][1:2, :])
        b["hidden"][...] = hidden
        b["nm1"][...] = nm1
        b["sc1"][...] = sc1
        b["hid"][...] = hidden.astype(BF)
        exch = [snd("ex", 0, b["hid"], b["hid_o"], core)]
        exch[0].start()

        def up(j, _):
            cols = pl.ds(al(j * CH, CH), CH)
            per = fc // CH
            bias = b["cp"][j // per, 0:1, pl.ds(al(lax.rem(j, per) * CH, CH), CH)]
            pre = nn(b["hid"][...], b["wuf"][:, cols]) + bias
            cdf = 0.5 + 0.5 * erf(pre * 0.7071067811865476)
            b["act"][:, cols] = (pre * cdf).astype(BF)
            b["dact"][:, cols] = cdf + pre * (jnp.exp(-0.5 * pre * pre) * 0.3989422804014327)
            return 0

        lax.fori_loop(0, FF // CH, up, 0)
        for q in range(C):
            e = snd("ex", 3 + q, b["act"].at[:, pl.ds(al(q * fc + (1 - d) * fh, fh), fh)],
                    b["act_o"].at[:, q * fh:(q + 1) * fh], core)
            e.start()
            exch.append(e)

        def down(j, _):
            cols = pl.ds(al(j * CH, CH), CH)
            b["res2"][:, cols] = b["hidden"][:, cols] + nt(b["act"][...], b["wdf"][cols, :]) + b["prow"][5:6, cols]
            return 0

        lax.fori_loop(0, D // CH, down, 0)
        gain2 = b["prow"][2:3, :]
        out, nm2, sc2 = norm_forward(b["res2"][...], gain2, b["prow"][3:4, :])
        ups = b["cg"][...].astype(F32).T
        sv = b["sv0"]
        sv[...] = jnp.zeros((NV, D), F32)
        sv[2:3, :] = tsum(ups * nm2)
        sv[5:6, :] = tsum(ups)
        gres2 = norm_backward(ups, gain2, nm2, sc2)
        b["res2"][...] = gres2
        b["gdown"][...] = gres2.astype(BF)
        sv[4:5, :] = tsum(b["gdown"][...].astype(F32))
        e = snd("ex", 1, b["gdown"], b["gdown_o"], core)
        e.start()
        exch.append(e)
        b["outT"][...] = out.T.astype(BF)
        ox = [snd("outx", k - 1, fr(b["outT"], peer(k)), tcols(b["outr"], a * HB + h), {"row": peer(k)}) for k in range(1, R)]
        run(*ox)
        o_loc = loc(1, fr(b["outT"], r), tcols(b["outr"], a * HB + h))
        o_loc.start()

        def gact(j, _):
            cols = pl.ds(al(j * CH, CH), CH)
            g = nn(b["gdown"][...], b["wdf"][:, cols])
            gp = (g * b["dact"][:, cols]).astype(BF)
            b["gpre"][:, cols] = gp
            per = D // CH
            sv[pl.ds(8 + j // per, 1), pl.ds(al(lax.rem(j, per) * CH, CH), CH)] = tsum(gp.astype(F32))
            return 0

        lax.fori_loop(0, FF // CH, gact, 0)
        for q in range(C):
            e = snd("ex", 3 + C + q, b["gpre"].at[:, pl.ds(al(q * fc + (1 - d) * fh, fh), fh)],
                    b["gpre_o"].at[:, q * fh:(q + 1) * fh], core)
            e.start()
            exch.append(e)

        def ghid_step(j, _):
            cols = pl.ds(al(j * CH, CH), CH)
            b["hidden"][:, cols] = b["res2"][:, cols] + nt(b["gpre"][...], b["wuf"][cols, :])
            return 0

        lax.fori_loop(0, D // CH, ghid_step, 0)
        ghid = b["hidden"][...]
        nm1 = b["nm1"][...]
        sv[0:1, :] = tsum(ghid * nm1)
        sv[1:2, :] = tsum(ghid)
        gres1 = norm_backward(ghid, b["prow"][0:1, :], nm1, b["sc1"][...])
        sv[3:4, :] = tsum(gres1.astype(BF).astype(F32))
        b["resT"][...] = gres1.T
        b["gattoT"][...] = b["resT"][...].astype(BF)
        ga = jnp.zeros((D, QT), F32)
        for q in range(R):
            ga = ga + nn(b["wpf"][q], b["gattoT"][q * fb:(q + 1) * fb, :])
        b["cg"][...] = ga.astype(BF)
        gt = [snd("gatt", k - 1, hrows(b["cg"], group(k)), tcols(b["gatt"], h), {"row": a * HB + group(k)})
              for k in range(1, HB)]
        run(*gt)
        gt_loc = loc(2, hrows(b["cg"], h), tcols(b["gatt"], h))
        gt_loc.start()
        e = snd("ex", 2, b["gattoT"], b["gattoT_o"], core)
        e.start()
        exch.append(e)
        for q in range(C):
            e = snd("ex", 3 + 2 * C + q, b["attq"].at[pl.ds(al(q * pb + (1 - d) * ph, ph), ph), :],
                    b["att_o"].at[q * ph:(q + 1) * ph, :], core)
            e.start()
            exch.append(e)
        for cp in exch:
            cp.wait()

        for q in range(C):
            cols = pl.ds(al(q * fc + d * fh, fh), fh)
            to = slice(q * fh, (q + 1) * fh)
            b["gd"][:, to] = (tn(b["gdown"][...], b["act"][:, cols]) + tn(b["gdown_o"][...], b["act_o"][:, to])).astype(BF)
            b["gu"][:, to] = (tn(b["hid"][...], b["gpre"][:, cols]) + tn(b["hid_o"][...], b["gpre_o"][:, to])).astype(BF)
            rows = pl.ds(al(q * pb + d * ph, ph), ph)
            tp = slice(q * ph, (q + 1) * ph)
            for p in range(R):
                f = slice(p * fb, (p + 1) * fb)
                b["gp"][p, tp, :] = (nt(b["attq"][rows, :], b["gattoT"][f, :])
                                     + nt(b["att_o"][tp, :], b["gattoT_o"][f, :])).astype(BF)
        rr = []
        for k in range(1, R):
            p = peer(k)
            rr += [snd("rrow", (k - 1) * 3, fr(b["gd"], p), b["rd"].at[k - 1], {"row": p}),
                   snd("rrow", (k - 1) * 3 + 1, fr(b["gu"], p), b["ru"].at[k - 1], {"row": p}),
                   snd("rrow", (k - 1) * 3 + 2, b["gp"].at[p], b["rpj"].at[k - 1], {"row": p})]
        for cp in gt:
            cp.wait()
        gt_loc.wait()
        run(*rr)

        conv_bwd(nh, b["qkv"], b["gatt"], b["mask"], tap_ref, b["acc"], b["gw"])
        for hh in range(nh):
            head_bwd1(hh, b["qkv"], b["gatt"], b["k1"], b["k3"], b["sm"], b["mix"], b["nv"][ITERS, hh], b["gv"], b["k1"], b["k3"], b["acc"])
        newton_bwd(nh, b["k2"], b["nv"], b["np_"], b["n1"], b["n2"], b["n3"], b["gv"], b["gk"])
        for hh in range(nh):
            head_bwd2(hh, b["qkv"], b["k2"], b["gk"], b["ql"], b["kl"], b["k1"], b["k3"], b["acc"], b["gqkv"])

        for q in range(R):
            f = slice(q * fb, (q + 1) * fb)
            b["part"][f, :] = nn(b["wg"][q], b["gqkv"][...]).astype(BF)
            mine_cols = pl.ds(al(h * QT, QT), QT)
            b["part"][f, mine_cols] = (nn(b["wg"][q], b["gqkv"][:, mine_cols]) + b["resT"][f, :]).astype(BF)
        pt = [snd("part", k - 1, fr(b["part"], peer(k)), b["pr"].at[k - 1], {"row": peer(k)}) for k in range(1, R)]
        run(*pt)
        for q in range(R):
            b["gq"][q] = nt(b["xg"][q * fb:(q + 1) * fb, :], b["gqkv"][...]).astype(BF)
        gqd = [snd("gqd", j, b["gq"].at[2 * j + 1 - d], b["gqo"].at[j], core) for j in range(R // 2)]
        run(*gqd)
        qsum = nt(jnp.ones((8, SEQ_LEN), BF), b["gqkv"][...])[0:1]
        tg = jnp.sum(b["gw"][...], axis=2).reshape(nh * 40, 128)
        thi, tlo = split(tg)
        one = jnp.ones((8, 128), BF)
        trow = (nt(one, thi) + nt(one, tlo))[0:1]
        b["tmp"][...] = jnp.zeros((8, D), F32)
        b["tmp"][0:1, 0:qw] = qsum
        b["tmp"][1:2, 0:nh * 40] = trow
        sv[pl.ds(12 + 2 * h, 1), :] = b["tmp"][0:1, :]
        sv[pl.ds(13 + 2 * h, 1), :] = b["tmp"][1:2, :]
        sr = [snd("svrow", k - 1, sv, b["svr"].at[k - 1], {"row": peer(k)}) for k in range(1, R)]
        run(*sr)
        for cp in gqd:
            cp.wait()
        gq_out = []
        for j in range(R // 2):
            b["gq"][2 * j + d] = (b["gq"][2 * j + d].astype(F32) + b["gqo"][j].astype(F32)).astype(BF)
            q = 2 * j + d
            cp = remote(b["gq"].at[2 * j + d], b["gqr"].at[r], ss["gqrow"].at[j], rs["gqrow"].at[r], {"row": q})
            lc = loc(3, b["gq"].at[2 * j + d], b["gqr"].at[r])
            gq_out.append((q, cp, lc))
            @pl.when(q != r)
            def _():
                cp.start()
            @pl.when(q == r)
            def _():
                lc.start()
        for cp in rr:
            cp.wait()
        own_rows = pl.ds(al(r * fb, fb), fb)

        def added(own_part, buf):
            t = own_part.astype(F32)
            for k in range(R - 1):
                t = t + buf[k].astype(F32)
            return t.astype(BF)

        b["gd"][own_rows, :] = added(b["gd"][own_rows, :], b["rd"])
        b["gu"][own_rows, :] = added(b["gu"][own_rows, :], b["ru"])
        b["gp"][r] = added(b["gp"][r], b["rpj"])
        rc = []
        for k in range(1, C):
            q = lax.rem(c + k, C)
            cols = pl.ds(al(q * fh, fh), fh)
            rc += [snd("rcol", (k - 1) * 3, b["gd"].at[own_rows, cols], b["zd"].at[k - 1], {"col": q}),
                   snd("rcol", (k - 1) * 3 + 1, b["gu"].at[own_rows, cols], b["zu"].at[k - 1], {"col": q}),
                   snd("rcol", (k - 1) * 3 + 2, b["gp"].at[r, pl.ds(al(q * ph, ph), ph), :], b["zp"].at[k - 1], {"col": q})]
        run(*rc)
        for cp in sr:
            cp.wait()
        t = sv[...]
        for k in range(R - 1):
            t = t + b["svr"][k]
        b["sv1"][...] = t
        sc = [snd("svcol", k - 1, b["sv1"], b["svz"].at[k - 1], {"col": lax.rem(c + k, C)}) for k in range(1, C)]
        run(*sc)
        gq_col = []
        for hp in range(HB):
            cp = remote(b["gqr"].at[hp], b["gqz"].at[c], ss["gqcol"].at[hp], rs["gqcol"].at[c], {"col": hp})
            lc = loc(4, b["gqr"].at[hp], b["gqz"].at[c])
            gq_col.append((hp, cp, lc))
        @pl.when(par)
        def _():
            for q in range(R):
                cp = remote(b["gq"].at[0], b["gqr"].at[q], ss["gqrow"].at[0], rs["gqrow"].at[q], {"row": q})
                @pl.when(q != r)
                def _():
                    cp.wait_recv()
        for q, cp, lc in gq_out:
            @pl.when(q != r)
            def _():
                cp.wait_send()
            @pl.when(q == r)
            def _():
                lc.wait()
        @pl.when(par)
        def _():
            for ap in range(1, S):
                for hp in range(HB):
                    b["gqr"][hp] = (b["gqr"][hp].astype(F32) + b["gqr"][ap * HB + hp].astype(F32)).astype(BF)
            for hp, cp, lc in gq_col:
                @pl.when(hp != c)
                def _():
                    cp.start()
                @pl.when(hp == c)
                def _():
                    lc.start()
        for cp in rc:
            cp.wait()

        def ended(own_part, buf):
            t = own_part.astype(F32)
            for k in range(C - 1):
                t = t + buf[k].astype(F32)
            return t

        mycols = pl.ds(al(c * fh, fh), fh)
        half_cols = pl.ds(al(d * fh, fh), fh)
        half_rows = pl.ds(al(d * ph, ph), ph)
        o["gdn"][:, half_cols] = ended(b["gd"][own_rows, mycols], b["zd"])
        o["gup"][:, half_cols] = ended(b["gu"][own_rows, mycols], b["zu"])
        o["gpj"][half_rows, :] = ended(b["gp"][r, pl.ds(al(c * ph, ph), ph), :], b["zp"])
        fin = [snd("fin", 0, o["gdn"].at[:, half_cols], o["gdn"].at[:, half_cols], core),
               snd("fin", 1, o["gup"].at[:, half_cols], o["gup"].at[:, half_cols], core),
               snd("fin", 2, o["gpj"].at[half_rows, :], o["gpj"].at[half_rows, :], core)]
        run(*fin)
        for cp in sc:
            cp.wait()
        t = b["sv1"][...]
        for k in range(C - 1):
            t = t + b["svz"][k]
        b["sv2"][...] = t
        sd = snd("svd", 0, b["sv2"], b["svo"], core)
        sd.start()
        gqf = snd("gqf", 0, o["gqw"], o["gqw"], core)
        @pl.when(par)
        def _():
            for hp, cp, lc in gq_col:
                @pl.when(hp != c)
                def _():
                    cp.wait_send()
                @pl.when(hp == c)
                def _():
                    lc.wait()
                inn = remote(b["gqr"].at[0], b["gqz"].at[hp], ss["gqcol"].at[0], rs["gqcol"].at[hp], {"col": hp})
                @pl.when(hp != c)
                def _():
                    inn.wait_recv()
            t = b["gqz"][0].astype(F32)
            for q in range(1, C):
                t = t + b["gqz"][q].astype(F32)
            o["gqw"][...] = t
            gqf.start()
        for cp in pt:
            cp.wait()
        if S == 1:
            t = b["part"][own_rows, :].astype(F32)
            for k in range(R - 1):
                t = t + b["pr"][k].astype(F32)
            o["gin"][...] = t
        else:
            o["gin"][...] = jnp.zeros((fb, S * SEQ_LEN), F32)
            o["gin"][:, pl.ds(al(a * SEQ_LEN, SEQ_LEN), SEQ_LEN)] = b["part"][own_rows, :].astype(F32)
            for k in range(1, R):
                q = lax.rem(r + R - k, R) // HB
                cols = pl.ds(al(q * SEQ_LEN, SEQ_LEN), SEQ_LEN)
                o["gin"][:, cols] += b["pr"][k - 1].astype(F32)
        for cp in ox:
            cp.wait()
        o_loc.wait()
        o["out"][...] = b["outr"][...].astype(F32)
        sd.wait()
        o["sv"][...] = b["sv2"][...] + b["svo"][...]
        for cp in fin:
            cp.wait()
        @pl.when(par)
        def _():
            gqf.wait_send()
        @pl.when(jnp.logical_not(par))
        def _():
            gqf.wait_recv()
        for go, cp in w_out:
            @pl.when(go)
            def _():
                cp.wait_send()
        for q in range(R):
            @pl.when((q % 2) == d)
            def _():
                w_fwd[q].wait_send()
        @pl.when(jnp.logical_not(meta_self))
        def _():
            meta_out.wait_send()

    sem = [pltpu.SemaphoreType.DMA((max(n, 1),)) for n in sems.values()]
    res = pl.pallas_call(
        body,
        out_shape=[struct(*s) for s in outs.values()],
        in_specs=[pl.BlockSpec(memory_space=pl.ANY)] * len(names_in),
        out_specs=[pl.BlockSpec(memory_space=pltpu.VMEM)] * len(outs),
        scratch_shapes=[pltpu.VMEM(*s) for s in bufs.values()] + sem + sem + [pltpu.SMEM((8, SEQ_LEN), F32)],
        compiler_params=pltpu.CompilerParams(collective_id=0, has_side_effects=True, vmem_limit_bytes=62 << 20),
        name="encoder_layer",
    )(*[args[n] for n in names_in])
    return dict(zip(outs, res))


def make_shards(R, C):
    def shards(inputs, doc_ids, qkv_weight, qkv_bias, proj_weight, proj_bias, first_gain, first_shift,
               ffn_up, ffn_up_bias, ffn_down, ffn_down_bias, second_gain, second_shift, conv_kernel, cotangent):
        S = inputs.shape[1] // SEQ_LEN
        fb = inputs.shape[0]
        nh = conv_kernel.shape[0]
        qw = qkv_weight.shape[1]
        fc = ffn_up.shape[1]
        pb = proj_weight.shape[0]
        FF = fc * C
        r = lax.axis_index("row")
        c = lax.axis_index("col")
        fbp = -(-fb // 128) * 128

        def line(v, n=SEQ_LEN):
            v = v.astype(F32).reshape(1, -1)
            return jnp.pad(v, ((0, 0), (0, n - v.shape[1])))

        meta = jnp.concatenate([line(doc_ids)] + [line(conv_kernel[j]) for j in range(nh)] + [line(qkv_bias)]
                               + [jnp.zeros((6 - nh, SEQ_LEN), F32)], axis=0)
        rowp = jnp.concatenate([line(v, fbp) for v in (first_gain, first_shift, second_gain, second_shift, proj_bias, ffn_down_bias)]
                               + [jnp.zeros((2, fbp), F32)], axis=0)
        colp = jnp.concatenate([line(ffn_up_bias, fc), jnp.zeros((7, fc), F32)], axis=0)
        res = layer_call(R, C, S, fb, nh, fc, pb, qw, dict(
            x=inputs, cot=cotangent.astype(BF), wq=qkv_weight, wp=proj_weight, wu=ffn_up, wd=ffn_down,
            meta=meta, rowp=rowp, colp=colp))
        sv = res["sv"]

        def feats(k):
            return lax.dynamic_slice(sv, (k, r * fb), (1, fb)).reshape(fb)

        ubias = lax.dynamic_slice_in_dim(sv[8:8 + FF // D].reshape(FF), c * fc, fc, 0)
        heads = lax.dynamic_slice_in_dim(sv, 12 + 2 * c, 2, 0)
        return (res["out"], res["gin"], res["gqw"], heads[0, :qw], res["gpj"], feats(3), feats(0), feats(1),
                res["gup"], ubias, res["gdn"], feats(4), feats(2), feats(5),
                heads[1, :nh * 40].reshape(nh, 40)[:, :CONV])
    return shards


def solution(mesh):
    in_specs = (P("row", ("dp", "col")), P(("dp", "row")), P("row", "col"), P("col"), P("col", "row"), P("row"),
                P("row"), P("row"), P("row", "col"), P("col"), P("row", "col"), P("row"), P("row"), P("row"),
                P("col", None), P("row", ("dp", "col")))
    out_specs = (P("row", ("dp", "col")), P("row", ("dp", "col")), P("row", "col"), P("col"), P("col", "row"), P("row"),
                 P("row"), P("row"), P("row", "col"), P("col"), P("row", "col"), P("row"), P("row"), P("row"),
                 P("col", None))
    fn = make_shards(mesh.shape["row"], mesh.shape["col"])
    return jax.shard_map(fn, mesh=mesh, in_specs=in_specs, out_specs=out_specs, check_vma=False)
```

```python
import functools

import jax
import jax.numpy as jnp
from jax import lax
from jax.experimental import pallas as pl
from jax.experimental.pallas import tpu as pltpu
from jax.sharding import PartitionSpec as P

D = 768
HEAD_DIM = 64
SEQ_LEN = 1024
EPSILON = 1e-05
F32=jnp.float32; BF=jnp.bfloat16
HD=64; SEQ=1024; SEG=16; CONV=33; ITERS=6; L=64
NEG=-1e9

def dg(a,b,ca,cb):
    return lax.dot_general(a,b,(((ca,),(cb,)),((),())),preferred_element_type=F32)
def nn(a,b): return dg(a,b,1,0)
def nt(a,b): return dg(a,b,1,1)
def tn(a,b): return dg(a,b,0,0)
def split(x):
    hi=x.astype(BF); lo=(x-hi.astype(F32)).astype(BF)
    return hi,lo
def cat(hl): return jnp.concatenate(hl,axis=0)
def halves(x):
    n=x.shape[0]//2
    return x[:n]+x[n:]
def nn2(a,b): return halves(nn(cat(split(a)),b))
def nt2(a,b): return halves(nt(cat(split(a)),b))
def nn3(a,b):
    ah,al=split(a); bh,bl=split(b)
    return halves(nn(cat((ah,al)),bh))+nn(ah,bl)
def nt3(a,b):
    ah,al=split(a); bh,bl=split(b)
    return halves(nt(cat((ah,al)),bh))+nt(ah,bl)

def iota(shape,dim): return lax.broadcasted_iota(jnp.int32,shape,dim)
def avg_mat():
    return jnp.where((iota((L,SEQ),1)//SEG)==iota((L,SEQ),0),F32(1.0/SEG),F32(0)).astype(BF)
def pick_mat():
    return jnp.where(iota((L,SEQ),1)==iota((L,SEQ),0)*SEG,F32(1),F32(0)).astype(BF)

def conv_masks(doc_row,mask_ref):
    t=iota((1,SEQ),1)
    for o in range(CONV):
        s=o-CONV//2
        rolled=pltpu.roll(doc_row,(-s)%SEQ,1) if s else doc_row
        ok=(rolled==doc_row)&(t+s>=0)&(t+s<SEQ)
        mask_ref[pl.ds(o,1),:]=jnp.where(ok,F32(1),F32(0))

def head_scores(h,qkv_ref,doc_row,land_row,land_col,k1_ref,k3_ref,k2_ref,ql_ref,kl_ref,sum_ref):
    b=h*3*HD
    q=qkv_ref[b:b+HD,:]; k=qkv_ref[b+HD:b+2*HD,:]; v=qkv_ref[b+2*HD:b+3*HD,:]
    at=avg_mat()
    ql=nt(at,q); kl=nt(at,k)
    ql_ref[h]=ql; kl_ref[h]=kl
    keep=land_col==doc_row
    s1=jnp.where(keep,nn2(kl,q)*0.125,NEG)
    e1=jnp.exp(s1-jnp.max(s1,axis=0,keepdims=True))
    k1_ref[h]=e1/jnp.sum(e1,axis=0,keepdims=True)
    s3=jnp.where(keep,nn2(ql,k)*0.125,NEG)
    e3=jnp.exp(s3-jnp.max(s3,axis=1,keepdims=True))
    k3=e3/jnp.sum(e3,axis=1,keepdims=True)
    k3_ref[h]=k3
    s2=jnp.where(land_col==land_row,nt3(ql,kl)*0.125,NEG)
    e2=jnp.exp(s2-jnp.max(s2,axis=1,keepdims=True))
    k2_ref[h]=e2/jnp.sum(e2,axis=1,keepdims=True)
    sum_ref[h]=nt2(k3,v)

def eye(): return jnp.where(iota((L,L),0)==iota((L,L),1),F32(1),F32(0))

def newton(nh,k2_ref,v_ref,p_ref,n1_ref,n2_ref,n3_ref):
    for h in range(nh):
        v_ref[0,h]=k2_ref[h].T*(1.0/L)
    def step(i,_):
        I=eye()
        P=[nn3(k2_ref[h],v_ref[i,h]) for h in range(nh)]
        N1=[7.0*I-P[h] for h in range(nh)]
        N2=[15.0*I-nn3(P[h],N1[h]) for h in range(nh)]
        N3=[13.0*I-nn3(P[h],N2[h]) for h in range(nh)]
        for h in range(nh):
            p_ref[i,h]=P[h]; n1_ref[i,h]=N1[h]; n2_ref[i,h]=N2[h]; n3_ref[i,h]=N3[h]
            v_ref[i+1,h]=nn3(0.25*v_ref[i,h],N3[h])
        return 0
    lax.fori_loop(0,ITERS,step,0)

def conv_fwd(nh,qkv_ref,mask_ref,w_ref,acc_ref):
    for h in range(nh):
        def group(g,_):
            r=pl.multiple_of(h*3*HD+2*HD+g*16,16)
            v=qkv_ref[pl.ds(r,16),:].astype(F32)
            acc=jnp.zeros((16,SEQ),F32)
            for o in range(CONV):
                s=o-CONV//2
                c=mask_ref[pl.ds(o,1),:]*w_ref[1+h,o]
                acc=acc+(pltpu.roll(v,(-s)%SEQ,1) if s else v)*c
            ro=pl.multiple_of(h*HD+g*16,16)
            acc_ref[pl.ds(ro,16),:]=acc
            return 0
        lax.fori_loop(0,HD//16,group,0)

def head_out(h,k1_ref,inv,sum_ref,mix_ref,acc_ref,att_ref):
    mixed=nn3(inv,sum_ref[h])
    mix_ref[h]=mixed
    mt=mixed.T
    k1=k1_ref[h]
    res=nn3(mt,k1)
    att_ref[h*HD:(h+1)*HD,:]=(res+acc_ref[h*HD:(h+1)*HD,:]).astype(BF)

def newton_bwd(nh,k2_ref,v_ref,p_ref,n1_ref,n2_ref,n3_ref,gv_ref,gk_ref):
    for h in range(nh):
        gk_ref[h]=jnp.zeros((L,L),F32)
    def step(j,_):
        i=ITERS-1-j
        H=range(nh)
        gV=[gv_ref[h] for h in H]; V=[v_ref[i,h] for h in H]
        VT=[V[h].T for h in H]; PT=[p_ref[i,h].T for h in H]
        gN3=[0.25*nn3(VT[h],gV[h]) for h in H]
        gVn=[0.25*nt3(gV[h],n3_ref[i,h]) for h in H]
        gN2=[-nn3(PT[h],gN3[h]) for h in H]
        gN1=[-nn3(PT[h],gN2[h]) for h in H]
        gP=[-nt3(gN3[h],n2_ref[i,h])-nt3(gN2[h],n1_ref[i,h])-gN1[h] for h in H]
        for h in H:
            gk_ref[h]+=nt3(gP[h],V[h])
            gv_ref[h]=gVn[h]+nn3(k2_ref[h].T,gP[h])
        return 0
    lax.fori_loop(0,ITERS,step,0)
    for h in range(nh):
        gk_ref[h]+=gv_ref[h].T*(1.0/L)

def conv_bwd(nh,qkv_ref,g_ref,mask_ref,w_ref,gacc_ref,gw_ref):
    for h in range(nh):
        gw_ref[h]=jnp.zeros((40,8,128),F32)
        def group(g,_):
            r=pl.multiple_of(h*3*HD+2*HD+g*16,16)
            ro=pl.multiple_of(h*HD+g*16,16)
            v=qkv_ref[pl.ds(r,16),:].astype(F32)
            gg=g_ref[pl.ds(ro,16),:].astype(F32)
            acc=jnp.zeros((16,SEQ),F32)
            for o in range(CONV):
                s=o-CONV//2
                m=mask_ref[pl.ds(CONV-1-o,1),:]
                R=(pltpu.roll(gg,s%SEQ,1) if s else gg)*m
                acc=acc+R*w_ref[1+h,o]
                pr=v*R
                x=pr[0:8]+pr[8:16]
                y=x[:,0:128]
                for c in range(1,SEQ//128): y=y+x[:,c*128:(c+1)*128]
                gw_ref[h,o]+=y
            gacc_ref[pl.ds(ro,16),:]=acc
            return 0
        lax.fori_loop(0,HD//16,group,0)

def head_bwd1(h,qkv_ref,g_ref,k1_ref,k3_ref,sum_ref,mix_ref,inv,gv_ref,gs1_ref,gs3_ref,gacc_ref):
    b=h*3*HD
    v=qkv_ref[b+2*HD:b+3*HD,:]
    g=g_ref[h*HD:(h+1)*HD,:]
    k1=k1_ref[h]
    gmix=nt2(k1,g)
    gk1=nn2(mix_ref[h],g)
    gs1_ref[h]=k1*(gk1-jnp.sum(k1*gk1,axis=0,keepdims=True))
    gv_ref[h]=nt3(gmix,sum_ref[h])
    gsum=nn3(inv.T,gmix)
    k3=k3_ref[h]
    gk3=nn2(gsum,v)
    gs3_ref[h]=k3*(gk3-jnp.sum(k3*gk3,axis=1,keepdims=True))
    gacc_ref[h*HD:(h+1)*HD,:]+=nn3(gsum.T,k3)

def head_bwd2(h,qkv_ref,k2_ref,gk_ref,ql_ref,kl_ref,gs1_ref,gs3_ref,gacc_ref,out_ref):
    b=h*3*HD
    q=qkv_ref[b:b+HD,:]; k=qkv_ref[b+HD:b+2*HD,:]
    k2=k2_ref[h]; gk2=gk_ref[h]
    gs2=k2*(gk2-jnp.sum(k2*gk2,axis=1,keepdims=True))
    ql=ql_ref[h]; kl=kl_ref[h]
    gs1=gs1_ref[h]; gs3=gs3_ref[h]
    gkl=nt2(gs1,q)+nn3(gs2.T,ql)
    gql=nt2(gs3,k)+nn3(gs2,kl)
    at=avg_mat()
    gq=(nn3(kl.T,gs1)+nn2(gql.T,at))*0.125
    gk=(nn3(ql.T,gs3)+nn2(gkl.T,at))*0.125
    out_ref[b:b+HD,:]=gq.astype(BF)
    out_ref[b+HD:b+2*HD,:]=gk.astype(BF)
    out_ref[b+2*HD:b+3*HD,:]=gacc_ref[h*HD:(h+1)*HD,:].astype(BF)

MESH = pl.DeviceIdType.MESH


def struct(shape, dtype):
    return jax.ShapeDtypeStruct(shape, dtype)


def remote(src, dst, ss, rs, dev):
    return pltpu.make_async_remote_copy(
        src_ref=src, dst_ref=dst, send_sem=ss, recv_sem=rs, device_id=dev, device_id_type=MESH
    )


def run(*copies):
    for cp in copies:
        cp.start()


def settle(cps, sent=True, got=True):
    for cp in cps:
        if sent:
            cp.wait_send()
        if got:
            cp.wait_recv()


def when(cond, fn):
    if cond is None:
        fn()
    else:
        pl.when(cond)(fn)


def al(x, n):
    return pl.multiple_of(x, n)


def erf(x):
    x = jnp.clip(x, -4.0, 4.0)
    y = x * x
    p = jnp.float32(-2.72614225801306e-10)
    for k in (2.77068142495902e-08, -2.10102402082508e-06, -5.69250639462346e-05,
              -7.34990630326855e-04, -2.95459980854025e-03, -1.60960333262415e-02):
        p = p * y + jnp.float32(k)
    q = jnp.float32(-1.45660718464996e-05)
    for k in (-2.13374055278905e-04, -1.68282697438203e-03, -7.37332916720468e-03, -1.42647390514189e-02):
        q = q * y + jnp.float32(k)
    return x * p / q


def norm_forward(residual, gain, shift):
    average = jnp.mean(residual, axis=1, keepdims=True)
    spread = jnp.mean(residual * residual, axis=1, keepdims=True) - average * average
    scaling = lax.rsqrt(spread + EPSILON)
    normed = (residual - average) * scaling
    return normed * gain + shift, normed, scaling


def norm_backward(upstream, gain, normed, scaling):
    scaled = upstream * gain
    mean_scaled = jnp.mean(scaled, axis=1, keepdims=True)
    crossed = jnp.mean(scaled * normed, axis=1, keepdims=True)
    return scaling * (scaled - mean_scaled - normed * crossed)


def tsum(x):
    return jnp.sum(x, axis=0, keepdims=True)


class RowGather:
    def __init__(self, snd, group, base, ways, place, r, R, cond=None):
        n = len(ways)
        self.cond, self.n, self.relay, self.ways = cond, n, R == 4, ways
        if self.relay:
            X, Y = lax.bitwise_xor(r, 1), lax.bitwise_xor(r, 2)
            self.own = []
            self.fwd = []
            for j in range(n):
                mine = place(j, r)
                self.own.append((snd(group, base + 2 * j, mine, mine, {"row": X}),
                                 snd(group, base + 2 * j + 1, mine, mine, {"row": Y})))
                src = place(j, Y if ways[j] else X)
                self.fwd.append(snd(group, base + 2 * n + j, src, src, {"row": X if ways[j] else Y}))
        else:
            self.own = [tuple(snd(group, base + j * (R - 1) + k - 1, place(j, r), place(j, r), {"row": lax.rem(r + k, R)})
                              for k in range(1, R)) for j in range(n)]

    def start(self):
        def go():
            for j, cps in enumerate(self.own):
                run(*(cps[::-1] if self.ways[j] else cps))
        when(self.cond, go)

    def forward(self):
        if self.relay:
            def go():
                for j in range(self.n):
                    self.own[j][self.ways[j]].wait_recv()
                    self.fwd[j].start()
            when(self.cond, go)

    def finish(self):
        def go():
            for j in range(self.n):
                if self.relay:
                    self.own[j][1 - self.ways[j]].wait_recv()
                    self.fwd[j].wait_recv()
                    self.fwd[j].wait_send()
                else:
                    for cp in self.own[j]:
                        cp.wait_recv()
                for cp in self.own[j]:
                    cp.wait_send()
        when(self.cond, go)


class RowReduce:
    def __init__(self, snd, group, block, recv, lanes, r, R):
        self.block, self.recv, self.lanes, self.r, self.R = block, recv, lanes, r, R
        self.relay = R == 4
        n = len(lanes)
        if self.relay:
            X, Y, Z = lax.bitwise_xor(r, 1), lax.bitwise_xor(r, 2), lax.bitwise_xor(r, 3)
            self.one, self.two, self.mids = [], [], []
            for j, ln in enumerate(lanes):
                P, Q = (X, Y) if j == 0 else (Y, X)
                self.one.append([snd(group, 3 * j, block(Z, ln), recv(1, ln), {"row": P}),
                                 snd(group, 3 * j + 1, block(P, ln), recv(0, ln), {"row": P})])
                self.two.append(snd(group, 3 * j + 2, block(Q, ln), recv(2, ln), {"row": Q}))
                self.mids.append(Q)
        else:
            self.all = [snd(group, k - 1, block(lax.rem(r + k, R), None), recv(k - 1, None), {"row": lax.rem(r + k, R)})
                        for k in range(1, R)]

    def start(self):
        if self.relay:
            for m in range(2):
                for cps in self.one:
                    cps[m].start()
        else:
            run(*self.all)

    def middle(self):
        if self.relay:
            for j, ln in enumerate(self.lanes):
                self.one[j][0].wait_recv()
                ref = self.block(self.mids[j], ln)
                ref[...] = (ref[...].astype(F32) + self.recv(1, ln)[...].astype(F32)).astype(BF)
                self.two[j].start()

    def finish(self):
        if self.relay:
            for cps in self.one:
                settle(cps, got=False)
                cps[1].wait_recv()
            settle(self.two)
            slots = (0, 2)
        else:
            settle(self.all)
            slots = range(self.R - 1)
        ref = self.block(self.r, None)
        t = ref[...].astype(F32)
        for k in slots:
            t = t + self.recv(k, None)[...].astype(F32)
        ref[...] = t.astype(BF)


class LineGather:
    def __init__(self, snd, group, n, place, c, C):
        self.C, self.c, self.n = C, c, n
        m = (C - 1) * n
        self.up = [[snd(group, k * n + j, place(j, c - k), place(j, c - k), {"col": c + 1}) for j in range(n)] for k in range(C - 1)]
        self.dn = [[snd(group, m + k * n + j, place(j, c + k), place(j, c + k), {"col": c - 1}) for j in range(n)] for k in range(C - 1)]

    def up_ok(self, k):
        return (self.c >= k) & (self.c < self.C - 1)

    def dn_ok(self, k):
        return (self.c + k <= self.C - 1) & (self.c > 0)

    def start(self):
        pl.when(self.up_ok(0))(lambda: run(*self.up[0]))
        pl.when(self.dn_ok(0))(lambda: run(*self.dn[0]))

    def step(self, k):
        def got(cps, nxt, ok):
            def go():
                for j in range(self.n):
                    cps[j].wait_recv()
                    if nxt is not None:
                        pl.when(ok)(lambda: nxt[j].start())
            return go
        more = k < self.C - 1
        pl.when(self.c >= k)(got(self.up[k - 1], self.up[k] if more else None, self.up_ok(k) if more else None))
        pl.when(self.c + k <= self.C - 1)(got(self.dn[k - 1], self.dn[k] if more else None, self.dn_ok(k) if more else None))

    def drain(self):
        for k in range(self.C - 1):
            pl.when(self.up_ok(k))(lambda: settle(self.up[k], got=False))
            pl.when(self.dn_ok(k))(lambda: settle(self.dn[k], got=False))


def layer_call(R, C, S, fb, nh, fc, pb, qw, args):
    HB = R // S
    QT = SEQ_LEN // HB
    FF = fc * C
    fh, ph = fc // 2, pb // 2
    fq = fh // 3 // 128 * 128
    fp = fh - fq
    hb = nh * HD
    fbp = -(-fb // 128) * 128
    CH = 256
    relay = R == 4
    NR = 3 if relay else R - 1
    PT = nh + 1
    V = pltpu.VMEM
    small = (nh, L, L)
    any_in = ["x", "cot", "wq", "wp", "wu", "wd"]
    vmem_in = ["doc", "taps", "qb", "g1", "s1", "g2", "s2", "pb", "db", "ub"]
    names_in = any_in + vmem_in
    outs = dict(
        out=((fb, S * SEQ_LEN), BF), gin=((fb, S * SEQ_LEN), F32), gqw=((fb, qw), F32), gup=((fb, fc), F32),
        gdn=((fb, fc), F32), gpj=((pb, fb), F32), sve=((16, D), F32), svl=((PT * HB, D), F32))
    bufs = dict(
        xg=((D, SEQ_LEN), BF), wg=((R, fb, qw), BF), ms=((8, SEQ_LEN), F32), mt=((8, SEQ_LEN), F32),
        rs=((8, fbp), F32), rp=((R, 8, fbp), F32), cs=((8, fc), F32), cp=((C, 8, fc), F32),
        cg=((D, QT), BF), wpf=((R, D, fb), BF), wuf=((D, FF), BF), wdf=((D, FF), BF),
        qkv=((3 * hb, SEQ_LEN), BF), k1=((nh, L, SEQ_LEN), F32), k3=((nh, L, SEQ_LEN), F32), k2=(small, F32),
        ql=(small, F32), kl=(small, F32), sm=(small, F32), mix=(small, F32), nv=((ITERS + 1,) + small, F32),
        np_=((ITERS,) + small, F32), n1=((ITERS,) + small, F32), n2=((ITERS,) + small, F32), n3=((ITERS,) + small, F32),
        mask=((40, SEQ_LEN), F32), acc=((hb, SEQ_LEN), F32), att=((hb, SEQ_LEN), BF), attq=((D, QT), BF),
        resT=((D, QT), F32), prow=((8, D), F32), hidden=((QT, D), F32), hid=((QT, D), BF), nm1=((QT, D), F32),
        sc1=((QT, 1), F32), act=((QT, FF), BF), dact=((QT, FF), F32), res2=((QT, D), F32), gdown=((QT, D), BF),
        gpre=((QT, FF), BF), gattoT=((D, QT), BF), outT=((D, QT), BF), gatt=((hb, SEQ_LEN), BF),
        hid_o=((QT, D), BF), gdown_o=((QT, D), BF), gattoT_o=((D, QT), BF), att_o=((C * ph, QT), BF),
        act_o=((QT, C * fh), BF), gpre_o=((QT, C * fh), BF),
        gu=((D, C * fp), BF), gd=((D, C * fp), BF), gp=((R, C * ph, fb), BF), guq=((D, C * fq), BF), gdq=((D, C * fq), BF),
        ru=((NR, fb, C * fp), BF), rd=((NR, fb, C * fp), BF), rpj=((NR, C * ph, fb), BF),
        zu=((C - 1, fb, fp), BF), zd=((C - 1, fb, fp), BF), zp=((C - 1, ph, fb), BF),
        zuq=((C - 1, D, fq), BF), zdq=((C - 1, D, fq), BF), tuq=((D, fq), BF), tdq=((D, fq), BF),
        ruq=((R - 1, fb, fq), BF), rdq=((R - 1, fb, fq), BF),
        gv=(small, F32), gk=(small, F32), gw=((nh, 40, 8, 128), F32),
        part=((D, SEQ_LEN), BF), pr=((R - 1, fb, SEQ_LEN), BF),
        gq=((R, fb, qw), BF), gqo=((R // 2, fb, qw), BF), gqr=((R, fb, qw), BF), gqz=((C, fb, qw), BF),
        e0=((16, D), F32), er=((R - 1, 16, D), F32), e1=((16, D), F32), ez=((C - 1, 16, D), F32), e2=((16, D), F32), eo=((16, D), F32),
        l0=((PT * HB, D), F32), lr=((R - 1, PT * HB, D), F32), l1=((PT * HB, D), F32), lz=((C - 1, PT * HB, D), F32),
        l2=((PT * HB, D), F32), lo=((PT * HB, D), F32), tmp=((8, D), F32))
    NRP = 1 + 2 * (C - 1)
    sems = dict(
        x=2 * (R - 1), cot=R - 1, rowp=R - 1, colp=C - 1, meta=1, ws=S * C, wr=R, wd2=R,
        zU=4 * (C - 1), zD=2 * (C - 1), rU=NRP * 2 * (R - 1), rD=NRP * (R - 1), rQ=2 * (R - 1), zQ=4 * (C - 1),
        cU=2 * NRP, cD=NRP, cQ=2 * NRP,
        att=HB - 1, gatt=HB - 1, ex=3 + 3 * C, ru=max(6, R - 1), rd=max(6, R - 1), rp=max(3, R - 1), rcol=3 * (C - 1),
        zq=2 * (C - 1), rq=2 * (R - 1), part=R - 1, outx=R - 1,
        gqd=R // 2, gqrow=R, gqcol=C, gqf=1, erow=R - 1, ecol=C - 1, ed=1, lrow=R - 1, lcol=C - 1, ld=1, fin=5, loc=24)

    def body(*refs):
        n = len(names_in)
        i = dict(zip(names_in, refs[:n]))
        o = dict(zip(outs, refs[n:n + len(outs)]))
        k = n + len(outs)
        b = dict(zip(bufs, refs[k:k + len(bufs)]))
        k += len(bufs)
        ss = dict(zip(sems, refs[k:k + len(sems)]))
        k += len(sems)
        rs = dict(zip(sems, refs[k:k + len(sems)]))
        k += len(sems)
        tap_ref = refs[k]
        d = lax.axis_index("dp")
        r = lax.axis_index("row")
        c = lax.axis_index("col")
        a, h = r // HB, lax.rem(r, HB)
        core = {"dp": 1 - d}

        def snd(group, slot, src, dst, dev):
            return remote(src, dst, ss[group].at[slot], rs[group].at[slot], dev)

        def loc(slot, src, dst):
            return pltpu.make_async_copy(src, dst, ss["loc"].at[slot])

        def fr(ref, q):
            return ref.at[pl.ds(al(q * fb, fb), fb), :]

        def peer(k):
            return lax.rem(r + k, R)

        def cpeer(k):
            return lax.rem(c + k, C)

        own = c == h
        bar = pltpu.get_barrier_semaphore()
        for k in range(1, R):
            pl.semaphore_signal(bar, inc=1, device_id={"row": peer(k)}, device_id_type=MESH)
        for k in range(1, C):
            pl.semaphore_signal(bar, inc=1, device_id={"col": cpeer(k)}, device_id_type=MESH)
        pl.semaphore_signal(bar, inc=1, device_id=core, device_id_type=MESH)
        for q in range(R):
            @pl.when(jnp.logical_not(own & (r == q)))
            def _():
                pl.semaphore_signal(bar, inc=1, device_id={"row": q, "col": h}, device_id_type=MESH)
        half = fb // 2

        def xcols(q, part=None):
            rows = slice(None) if part is None else pl.ds(part * half, half)
            return i["x"].at[rows, pl.ds(al(q // HB * SEQ_LEN, SEQ_LEN), SEQ_LEN)]

        x_loc = loc(0, xcols(r), fr(b["xg"], r))
        x_loc.start()

        def cols_of(col, first, width):
            return pl.ds(al(col * fc + d * fh + first, 128), width)

        def wide(ref, row, col, first, width):
            return ref.at[pl.ds(al(row * fb, fb), fb), cols_of(col, first, width)]

        def narrow(ref, row, col):
            return ref.at[row, pl.ds(al(col * pb + d * ph, ph), ph), :]

        bulk_loc = [loc(1, i["wu"].at[:, pl.ds(al(d * fh, fh), fh)], wide(b["wuf"], r, c, 0, fh)),
                    loc(2, i["wd"].at[:, pl.ds(al(d * fh, fh), fh)], wide(b["wdf"], r, c, 0, fh)),
                    loc(3, i["wp"].at[pl.ds(al(d * ph, ph), ph), :], narrow(b["wpf"], r, c))]
        run(*bulk_loc)
        cot_rows = min(fb, 64)
        stage = []
        for s in range(S):
            for f in range(0, fb, cot_rows):
                m = len(stage)
                buf = b["k1"].at[m] if m < nh else b["k3"].at[m - nh]
                stage.append((s, f, m, loc(4 + m, i["cot"].at[f:f + cot_rows, s * SEQ_LEN:(s + 1) * SEQ_LEN], buf.at[0:cot_rows, :])))
        run(*[t[3] for t in stage])
        b["ms"][...] = jnp.zeros((8, SEQ_LEN), F32)
        b["ms"][0:1, :] = i["doc"][...].astype(F32)
        b["ms"][1:1 + nh, 0:CONV] = i["taps"][...]
        b["ms"][1 + nh:2 + nh, 0:qw] = i["qb"][...].astype(F32)
        b["rs"][...] = jnp.zeros((8, fbp), F32)
        for j, name in enumerate(("g1", "s1", "g2", "s2", "pb", "db")):
            b["rs"][j:j + 1, 0:fb] = i[name][...].astype(F32)
        b["cs"][...] = jnp.zeros((8, fc), F32)
        b["cs"][0:1, :] = i["ub"][...].astype(F32)
        for cp in bulk_loc:
            cp.wait()
        x_loc.wait()
        pl.semaphore_wait(bar, R - 1 + C - 1 + 1 + S * C - jnp.where(own, 1, 0))

        if relay:
            xg = RowGather(snd, "x", 0, (0, 1), lambda j, q: b["xg"].at[pl.ds(al(q * fb + j * half, half), half), :], r, R)
            xg.start()
        else:
            xs = [snd("x", k - 1, xcols(peer(k)), fr(b["xg"], r), {"row": peer(k)}) for k in range(1, R)]
            run(*xs)
        par = lax.rem(r, 2) == d
        w_out = []
        for ap in range(S):
            for cq in range(C):
                t = ap * HB + c
                go = par & jnp.logical_not((t == r) & (c == cq))
                cp = remote(i["wq"], b["wg"].at[r], ss["ws"].at[ap * C + cq], rs["wr"].at[r], {"row": t, "col": cq})
                w_out.append((go, cp))
        for go, cp in w_out:
            pl.when(go)(cp.start)
        w_loc = loc(16, i["wq"], b["wg"].at[r])
        pl.when(own & par)(w_loc.start)
        dst_row, dst_col = lax.rem(r, S) * HB + c, r // S
        meta_self = (dst_row == r) & (dst_col == c)
        meta_out = snd("meta", 0, b["ms"], b["mt"], {"row": dst_row, "col": dst_col})
        meta_in = snd("meta", 0, b["ms"], b["mt"], {"row": c * S + a, "col": h})
        meta_loc = loc(17, b["ms"], b["mt"])
        pl.when(jnp.logical_not(meta_self))(meta_out.start)
        pl.when(meta_self)(meta_loc.start)

        def place_u(col):
            return lambda j, row: narrow(b["wpf"], row, col) if j else wide(b["wuf"], row, col, 0, fp)

        def place_d(col):
            return lambda j, row: wide(b["wdf"], row, col, 0, fp)

        def both(j):
            return b["wdf"] if j else b["wuf"]

        zU = LineGather(snd, "zU", 2, lambda j, col: place_u(col)(j, r), c, C)
        zD = LineGather(snd, "zD", 1, lambda j, col: place_d(col)(j, r), c, C)
        at_cols = [(None, c)]
        for k in range(1, C):
            at_cols += [(c >= k, c - k), (c + k <= C - 1, c + k)]
        rU = [RowGather(snd, "rU", m * 2 * (R - 1), (0, 1), place_u(col), r, R, cond) for m, (cond, col) in enumerate(at_cols)]
        rD = [RowGather(snd, "rD", m * (R - 1), (1,), place_d(col), r, R, cond) for m, (cond, col) in enumerate(at_cols)]
        rQ = RowGather(snd, "rQ", 0, (0, 1), lambda j, row: wide(both(j), row, c, fp, fq), r, R)
        zQ = LineGather(snd, "zQ", 2, lambda j, col: both(j).at[:, cols_of(col, fp, fq)], c, C)
        zU.start()
        rQ.start()
        zD.start()

        def cot_at(s, cols):
            return b["gpre"].at[pl.ds(al(s // 3 * fb, fb), fb), cols]

        for s, f, m, cp in stage:
            cp.wait()
            buf = b["k1"].at[m] if m < nh else b["k3"].at[m - nh]
            b["gpre"][s // 3 * fb + f:s // 3 * fb + f + cot_rows, s % 3 * SEQ_LEN:(s % 3 + 1) * SEQ_LEN] = buf[0:cot_rows, :].astype(BF)

        def cot_src(q):
            s = q // HB
            return cot_at(s, pl.ds(al(lax.rem(s, 3) * SEQ_LEN + lax.rem(q, HB) * QT, QT), QT))

        if relay:
            xg.forward()
            rQ.forward()
            xg.finish()
        else:
            settle(xs)
        zU.step(1)
        for m in range(3):
            rU[m].start()
        gs = [snd("cot", k - 1, cot_src(peer(k)), fr(b["cg"], r), {"row": peer(k)}) for k in range(1, R)]
        g_loc = loc(18, cot_src(r), fr(b["cg"], r))
        ps = [snd("rowp", k - 1, b["rs"], b["rp"].at[r], {"row": peer(k)}) for k in range(1, R)]
        p_loc = loc(19, b["rs"], b["rp"].at[r])
        cs = [snd("colp", k - 1, b["cs"], b["cp"].at[c], {"col": cpeer(k)}) for k in range(1, C)]
        c_loc = loc(20, b["cs"], b["cp"].at[c])
        run(*ps, p_loc, *cs, c_loc)
        w_fwd = [snd("wd2", q, b["wg"].at[q], b["wg"].at[q], core) for q in range(R)]
        for q in range(R):
            mine_q = (q % 2) == d
            here_q = own & (r == q)
            w_in = remote(i["wq"], b["wg"].at[q], ss["ws"].at[0], rs["wr"].at[q], {"row": q, "col": h})
            pl.when(mine_q & here_q)(w_loc.wait)
            pl.when(mine_q & jnp.logical_not(here_q))(w_in.wait_recv)
            pl.when(mine_q)(w_fwd[q].start)
        for q in range(R):
            pl.when((q % 2) != d)(w_fwd[q].wait_recv)
        pl.when(jnp.logical_not(meta_self))(meta_in.wait_recv)
        pl.when(meta_self)(meta_loc.wait)
        tap_cp = loc(21, b["mt"], tap_ref)
        tap_cp.start()
        qb = jnp.where(iota((8, qw), 0) == 1 + nh, b["mt"][:, 0:qw], 0.0).astype(BF)
        acc = tn(qb, jnp.ones((8, SEQ_LEN), BF))
        for q in range(R):
            acc = acc + tn(b["wg"][q], b["xg"][q * fb:(q + 1) * fb, :])
        b["qkv"][...] = acc.astype(BF)
        tap_cp.wait()

        doc_row = b["mt"][0:1, :]
        rowb = jnp.broadcast_to(doc_row, (8, SEQ_LEN)).astype(BF)
        pick = pick_mat()
        land_row = nt(rowb, pick)[0:1]
        land_col = nt(pick, rowb)[:, 0:1]
        rQ.finish()
        zQ.start()
        for k in range(2, C):
            zU.step(k)
            rU[2 * k - 1].start()
            rU[2 * k].start()

        def scores(hh):
            head_scores(hh, b["qkv"], doc_row, land_row, land_col, b["k1"], b["k3"], b["k2"], b["ql"], b["kl"], b["sm"])

        scores(0)
        for m in range(3):
            rU[m].forward()
        zD.step(1)
        for m in range(3):
            rD[m].start()
        for hh in range(1, nh):
            scores(hh)
        for k in range(2, C):
            zD.step(k)
            rD[2 * k - 1].start()
            rD[2 * k].start()
        for m in range(3, NRP):
            rU[m].forward()
        zQ.step(1)
        newton(nh, b["k2"], b["nv"], b["np_"], b["n1"], b["n2"], b["n3"])
        zQ.step(2)
        for m in range(3):
            rD[m].forward()
        conv_masks(doc_row, b["mask"])
        conv_fwd(nh, b["qkv"], b["mask"], tap_ref, b["acc"])
        for m in range(3, NRP):
            rD[m].forward()
        for hh in range(nh):
            head_out(hh, b["k1"], b["nv"][ITERS, hh], b["sm"], b["mix"], b["acc"], b["att"])

        def group(k):
            return lax.rem(h + k, HB)

        def hrows(ref, q):
            return ref.at[pl.ds(al(q * hb, hb), hb), :]

        def tcols(ref, q):
            return ref.at[:, pl.ds(al(q * QT, QT), QT)]

        at = [snd("att", k - 1, tcols(b["att"], group(k)), hrows(b["attq"], h), {"row": a * HB + group(k)})
              for k in range(1, HB)]
        run(*at)
        at_loc = loc(0, tcols(b["att"], h), hrows(b["attq"], h))
        at_loc.start()
        for cp in ps + cs:
            cp.wait()
        for cp in (p_loc, c_loc):
            cp.wait()
        prow = jnp.zeros((8, D), F32)
        for q in range(R):
            piece = jnp.concatenate([b["rp"][q], jnp.zeros((8, D - fbp), F32)], axis=1)
            prow = prow + (pltpu.roll(piece, q * fb, 1) if q else piece)
        b["prow"][...] = prow
        def cross(group, slot, cond, *refs):
            cps = [snd(group, slot + j, ref, ref, core) for j, ref in enumerate(refs)]
            when(cond, lambda: run(*cps))
            return cond, cps

        crossed, later = [], []
        for m, (cond, col) in enumerate(at_cols):
            rU[m].finish()
            crossed.append(cross("cU", 2 * m, cond, b["wuf"].at[:, cols_of(col, 0, fp)],
                                 b["wpf"].at[:, pl.ds(al(col * pb + d * ph, ph), ph), :]))
            if m == 0 or m % 2:
                k = (m + 1) // 2
                if k > 2:
                    zQ.step(k)
            both_q = cross("cQ", 2 * m, cond, b["wuf"].at[:, cols_of(col, fp, fq)], b["wdf"].at[:, cols_of(col, fp, fq)])
            crossed.append((cond, both_q[1][:1]))
            later.append((cond, both_q[1][1:]))
        run(*gs, g_loc)
        settle(at)
        at_loc.wait()
        for cond, cps in crossed:
            when(cond, lambda: settle(cps))

        for q in range(R):
            t = tn(b["wpf"][q], b["attq"][...])
            b["resT"][q * fb:(q + 1) * fb, :] = t + b["xg"][q * fb:(q + 1) * fb, pl.ds(al(h * QT, QT), QT)].astype(F32)
        res1 = b["resT"][...].T + b["prow"][4:5, :]
        hidden, nm1, sc1 = norm_forward(res1, b["prow"][0:1, :], b["prow"][1:2, :])
        b["hidden"][...] = hidden
        b["nm1"][...] = nm1
        b["sc1"][...] = sc1
        b["hid"][...] = hidden.astype(BF)
        ex_hid = snd("ex", 0, b["hid"], b["hid_o"], core)
        ex_hid.start()

        def up(j, _):
            cols = pl.ds(al(j * CH, CH), CH)
            per = fc // CH
            bias = b["cp"][j // per, 0:1, pl.ds(al(lax.rem(j, per) * CH, CH), CH)]
            pre = nn(b["hid"][...], b["wuf"][:, cols]) + bias
            cdf = 0.5 + 0.5 * erf(pre * 0.7071067811865476)
            b["act"][:, cols] = (pre * cdf).astype(BF)
            b["dact"][:, cols] = cdf + pre * (jnp.exp(-0.5 * pre * pre) * 0.3989422804014327)
            return 0

        lax.fori_loop(0, FF // CH, up, 0)
        ex_act = [snd("ex", 3 + q, b["act"].at[:, pl.ds(al(q * fc + (1 - d) * fh, fh), fh)],
                      b["act_o"].at[:, q * fh:(q + 1) * fh], core) for q in range(C)]
        run(*ex_act)
        for m, (cond, col) in enumerate(at_cols):
            rD[m].finish()
            later.append(cross("cD", m, cond, b["wdf"].at[:, cols_of(col, 0, fp)]))
        for cond, cps in later:
            when(cond, lambda: settle(cps))

        def down(j, _):
            cols = pl.ds(al(j * CH, CH), CH)
            b["res2"][:, cols] = b["hidden"][:, cols] + nt(b["act"][...], b["wdf"][cols, :]) + b["prow"][5:6, cols]
            return 0

        lax.fori_loop(0, D // CH, down, 0)
        gain2 = b["prow"][2:3, :]
        out, nm2, sc2 = norm_forward(b["res2"][...], gain2, b["prow"][3:4, :])
        settle(gs)
        g_loc.wait()
        ups = b["cg"][...].astype(F32).T
        e0 = b["e0"]
        e0[...] = jnp.zeros((16, D), F32)
        e0[2:3, :] = tsum(ups * nm2)
        e0[5:6, :] = tsum(ups)
        gres2 = norm_backward(ups, gain2, nm2, sc2)
        b["res2"][...] = gres2
        b["gdown"][...] = gres2.astype(BF)
        e0[4:5, :] = tsum(b["gdown"][...].astype(F32))
        ex_gdown = snd("ex", 1, b["gdown"], b["gdown_o"], core)
        ex_gdown.start()
        b["outT"][...] = out.T.astype(BF)
        ox = [snd("outx", k - 1, fr(b["outT"], peer(k)), tcols(o["out"], a * HB + h), {"row": peer(k)}) for k in range(1, R)]
        o_loc = loc(1, fr(b["outT"], r), tcols(o["out"], a * HB + h))
        run(*ox, o_loc)

        def gact(j, _):
            cols = pl.ds(al(j * CH, CH), CH)
            g = nn(b["gdown"][...], b["wdf"][:, cols])
            gp = (g * b["dact"][:, cols]).astype(BF)
            b["gpre"][:, cols] = gp
            per = D // CH
            e0[pl.ds(8 + j // per, 1), pl.ds(al(lax.rem(j, per) * CH, CH), CH)] = tsum(gp.astype(F32))
            return 0

        lax.fori_loop(0, FF // CH, gact, 0)
        ex_gpre = [snd("ex", 3 + C + q, b["gpre"].at[:, pl.ds(al(q * fc + (1 - d) * fh, fh), fh)],
                       b["gpre_o"].at[:, q * fh:(q + 1) * fh], core) for q in range(C)]
        run(*ex_gpre)
        settle(ex_act)
        settle([ex_gdown])

        def grad_block(q, mine, mine_w, other, other_w, dst, dst_q):
            to = slice(q * fh, (q + 1) * fh)
            t = tn(b[mine][...], b[mine_w][:, cols_of(q, 0, fh)]) + tn(b[other][...], b[other_w][:, to])
            b[dst][:, q * fp:(q + 1) * fp] = t[:, :fp].astype(BF)
            b[dst_q][:, q * fq:(q + 1) * fq] = t[:, fp:].astype(BF)

        def scatter_q(base, src, dst):
            cps = [snd("zq", base + k - 1, src.at[:, pl.ds(al(cpeer(k) * fq, fq), fq)], dst.at[k - 1], {"col": cpeer(k)})
                   for k in range(1, C)]
            run(*cps)
            return cps

        def block_of(ref):
            return lambda q, ln: ref.at[pl.ds(al(q * fb, fb), fb), slice(None) if ln is None else ln]

        def recv_of(ref):
            return lambda k, ln: ref.at[k, :, slice(None) if ln is None else ln]

        for q in range(C):
            grad_block(q, "gdown", "act", "gdown_o", "act_o", "gd", "gdq")
        lanes = (slice(0, C * fp // 2), slice(C * fp // 2, C * fp))
        red_d = RowReduce(snd, "rd", block_of(b["gd"]), recv_of(b["rd"]), lanes, r, R)
        red_d.start()
        zqd = scatter_q(0, b["gdq"], b["zdq"])

        def ghid_step(j, _):
            cols = pl.ds(al(j * CH, CH), CH)
            b["hidden"][:, cols] = b["res2"][:, cols] + nt(b["gpre"][...], b["wuf"][cols, :])
            return 0

        lax.fori_loop(0, D // CH, ghid_step, 0)
        ghid = b["hidden"][...]
        nm1 = b["nm1"][...]
        e0[0:1, :] = tsum(ghid * nm1)
        e0[1:2, :] = tsum(ghid)
        gres1 = norm_backward(ghid, b["prow"][0:1, :], nm1, b["sc1"][...])
        e0[3:4, :] = tsum(gres1.astype(BF).astype(F32))
        b["resT"][...] = gres1.T
        b["gattoT"][...] = b["resT"][...].astype(BF)
        ga = jnp.zeros((D, QT), F32)
        for q in range(R):
            ga = ga + nn(b["wpf"][q], b["gattoT"][q * fb:(q + 1) * fb, :])
        b["cg"][...] = ga.astype(BF)
        gt = [snd("gatt", k - 1, hrows(b["cg"], group(k)), tcols(b["gatt"], h), {"row": a * HB + group(k)})
              for k in range(1, HB)]
        run(*gt)
        gt_loc = loc(2, hrows(b["cg"], h), tcols(b["gatt"], h))
        gt_loc.start()
        ex_att = [snd("ex", 2, b["gattoT"], b["gattoT_o"], core)] + [
            snd("ex", 3 + 2 * C + q, b["attq"].at[pl.ds(al(q * pb + (1 - d) * ph, ph), ph), :],
                b["att_o"].at[q * ph:(q + 1) * ph, :], core) for q in range(C)]
        run(*ex_att)
        settle([ex_hid])
        settle(ex_gpre)

        for q in range(C):
            grad_block(q, "hid", "gpre", "hid_o", "gpre_o", "gu", "guq")
        zqu = scatter_q(C - 1, b["guq"], b["zuq"])
        settle(ex_att)
        for q in range(C):
            rows = pl.ds(al(q * pb + d * ph, ph), ph)
            tp = slice(q * ph, (q + 1) * ph)
            for p in range(R):
                f = slice(p * fb, (p + 1) * fb)
                b["gp"][p, tp, :] = (nt(b["attq"][rows, :], b["gattoT"][f, :])
                                     + nt(b["att_o"][tp, :], b["gattoT_o"][f, :])).astype(BF)
        red_d.middle()
        settle(gt)
        gt_loc.wait()
        own_rows = pl.ds(al(r * fb, fb), fb)
        red_u = RowReduce(snd, "ru", block_of(b["gu"]), recv_of(b["ru"]), lanes, r, R)
        red_p = RowReduce(snd, "rp", lambda q, ln: b["gp"].at[q], lambda k, ln: b["rpj"].at[k], (None,), r, R)
        red_u.start()
        red_p.start()
        er = [snd("erow", k - 1, e0, b["er"].at[k - 1], {"row": peer(k)}) for k in range(1, R)]
        run(*er)

        conv_bwd(nh, b["qkv"], b["gatt"], b["mask"], tap_ref, b["acc"], b["gw"])
        for hh in range(nh):
            head_bwd1(hh, b["qkv"], b["gatt"], b["k1"], b["k3"], b["sm"], b["mix"], b["nv"][ITERS, hh], b["gv"], b["k1"], b["k3"], b["acc"])
        red_d.finish()

        def scatter_p(slot, src_of, dst):
            cps = [snd("rcol", slot * (C - 1) + k - 1, src_of(cpeer(k)), dst.at[k - 1], {"col": cpeer(k)}) for k in range(1, C)]
            run(*cps)
            return cps

        def pcol(ref):
            return lambda q: ref.at[own_rows, pl.ds(al(q * fp, fp), fp)]

        rcd = scatter_p(0, pcol(b["gd"]), b["zd"])
        red_u.middle()
        red_p.middle()
        newton_bwd(nh, b["k2"], b["nv"], b["np_"], b["n1"], b["n2"], b["n3"], b["gv"], b["gk"])
        for hh in range(nh):
            head_bwd2(hh, b["qkv"], b["k2"], b["gk"], b["ql"], b["kl"], b["k1"], b["k3"], b["acc"], b["qkv"])

        def total(own_part, buf, m):
            t = own_part.astype(F32)
            for k in range(m):
                t = t + buf[k].astype(F32)
            return t

        for q in range(R):
            b["gq"][q] = nt(b["xg"][q * fb:(q + 1) * fb, :], b["qkv"][...]).astype(BF)
        gqd = [snd("gqd", j, b["gq"].at[2 * j + 1 - d], b["gqo"].at[j], core) for j in range(R // 2)]
        run(*gqd)
        l0 = b["l0"]
        l0[...] = jnp.zeros((PT * HB, D), F32)
        b["tmp"][...] = jnp.zeros((8, D), F32)
        b["tmp"][0:1, 0:qw] = nt(jnp.ones((8, SEQ_LEN), BF), b["qkv"][...])[0:1]
        for hh in range(nh):
            thi, tlo = split(jnp.sum(b["gw"][hh], axis=1))
            one = jnp.ones((8, 128), BF)
            b["tmp"][1 + hh:2 + hh, 0:40] = (nt(one, thi) + nt(one, tlo))[0:1]
        for j in range(PT):
            l0[pl.ds(PT * h + j, 1), :] = b["tmp"][j:j + 1, :]
        lrw = [snd("lrow", k - 1, l0, b["lr"].at[k - 1], {"row": peer(k)}) for k in range(1, R)]
        run(*lrw)
        settle(gqd)
        gq_out = []
        for j in range(R // 2):
            b["gq"][2 * j + d] = (b["gq"][2 * j + d].astype(F32) + b["gqo"][j].astype(F32)).astype(BF)
            q = 2 * j + d
            cp = remote(b["gq"].at[q], b["gqr"].at[r], ss["gqrow"].at[j], rs["gqrow"].at[r], {"row": q})
            lc = loc(3, b["gq"].at[q], b["gqr"].at[r])
            gq_out.append((q, cp, lc))
            pl.when(q != r)(cp.start)
            pl.when(q == r)(lc.start)
        for q in range(R):
            f = slice(q * fb, (q + 1) * fb)
            b["part"][f, :] = nn(b["wg"][q], b["qkv"][...]).astype(BF)
            mine_cols = pl.ds(al(h * QT, QT), QT)
            b["part"][f, mine_cols] = (nn(b["wg"][q], b["qkv"][:, mine_cols]) + b["resT"][f, :]).astype(BF)
        pt = [snd("part", k - 1, fr(b["part"], peer(k)), b["pr"].at[k - 1], {"row": peer(k)}) for k in range(1, R)]
        run(*pt)

        settle(zqd)
        settle(zqu)
        qcols = pl.ds(al(c * fq, fq), fq)
        b["tdq"][...] = total(b["gdq"][:, qcols], b["zdq"], C - 1).astype(BF)
        b["tuq"][...] = total(b["guq"][:, qcols], b["zuq"], C - 1).astype(BF)
        rq = []
        for k in range(1, R):
            rq += [snd("rq", 2 * k - 2, fr(b["tdq"], peer(k)), b["rdq"].at[k - 1], {"row": peer(k)}),
                   snd("rq", 2 * k - 1, fr(b["tuq"], peer(k)), b["ruq"].at[k - 1], {"row": peer(k)})]
        run(*rq)
        red_u.finish()
        red_p.finish()
        rcu = scatter_p(1, pcol(b["gu"]), b["zu"])
        rcp = scatter_p(2, lambda q: b["gp"].at[r, pl.ds(al(q * ph, ph), ph), :], b["zp"])

        def whole(first, buf, m):
            t = first[...]
            for k in range(m):
                t = t + buf[k]
            return t

        for cp in er + lrw:
            cp.wait()
        b["e1"][...] = whole(e0, b["er"], R - 1)
        b["l1"][...] = whole(l0, b["lr"], R - 1)
        ec = [snd("ecol", k - 1, b["e1"], b["ez"].at[k - 1], {"col": cpeer(k)}) for k in range(1, C)]
        lc_ = [snd("lcol", k - 1, b["l1"], b["lz"].at[k - 1], {"col": cpeer(k)}) for k in range(1, C)]
        run(*ec, *lc_)
        gq_col = []
        for hp in range(HB):
            cp = remote(b["gqr"].at[hp], b["gqz"].at[c], ss["gqcol"].at[hp], rs["gqcol"].at[c], {"col": hp})
            lc = loc(4, b["gqr"].at[hp], b["gqz"].at[c])
            gq_col.append((hp, cp, lc))
        @pl.when(par)
        def _():
            for q in range(R):
                cp = remote(b["gq"].at[0], b["gqr"].at[q], ss["gqrow"].at[0], rs["gqrow"].at[q], {"row": q})
                pl.when(q != r)(cp.wait_recv)
        for q, cp, lc in gq_out:
            pl.when(q != r)(cp.wait_send)
            pl.when(q == r)(lc.wait)
        @pl.when(par)
        def _():
            for ap in range(1, S):
                for hp in range(HB):
                    b["gqr"][hp] = (b["gqr"][hp].astype(F32) + b["gqr"][ap * HB + hp].astype(F32)).astype(BF)
            for hp, cp, lc in gq_col:
                pl.when(hp != c)(cp.start)
                pl.when(hp == c)(lc.start)
        half_rows = pl.ds(al(d * ph, ph), ph)
        pcols, qcols2 = pl.ds(al(d * fh, 128), fp), pl.ds(al(d * fh + fp, 128), fq)
        settle(rq)
        o["gdn"][:, qcols2] = total(b["tdq"][own_rows, :], b["rdq"], R - 1)
        o["gup"][:, qcols2] = total(b["tuq"][own_rows, :], b["ruq"], R - 1)
        settle(rcd + rcu + rcp)
        mycols = pl.ds(al(c * fp, fp), fp)
        o["gdn"][:, pcols] = total(b["gd"][own_rows, mycols], b["zd"], C - 1)
        o["gup"][:, pcols] = total(b["gu"][own_rows, mycols], b["zu"], C - 1)
        o["gpj"][half_rows, :] = total(b["gp"][r, pl.ds(al(c * ph, ph), ph), :], b["zp"], C - 1)
        half_cols = pl.ds(al(d * fh, fh), fh)
        fin = [snd("fin", 0, o["gdn"].at[:, half_cols], o["gdn"].at[:, half_cols], core),
               snd("fin", 1, o["gup"].at[:, half_cols], o["gup"].at[:, half_cols], core),
               snd("fin", 2, o["gpj"].at[half_rows, :], o["gpj"].at[half_rows, :], core)]
        run(*fin)
        for cp in ec + lc_:
            cp.wait()
        b["e2"][...] = whole(b["e1"], b["ez"], C - 1)
        b["l2"][...] = whole(b["l1"], b["lz"], C - 1)
        sd = [snd("ed", 0, b["e2"], b["eo"], core), snd("ld", 0, b["l2"], b["lo"], core)]
        run(*sd)
        gqf = snd("gqf", 0, o["gqw"], o["gqw"], core)
        @pl.when(par)
        def _():
            for hp, cp, lc in gq_col:
                pl.when(hp != c)(cp.wait_send)
                pl.when(hp == c)(lc.wait)
                inn = remote(b["gqr"].at[0], b["gqz"].at[hp], ss["gqcol"].at[0], rs["gqcol"].at[hp], {"col": hp})
                pl.when(hp != c)(inn.wait_recv)
            t = b["gqz"][0].astype(F32)
            for q in range(1, C):
                t = t + b["gqz"][q].astype(F32)
            o["gqw"][...] = t
            gqf.start()
        for cp in pt:
            cp.wait()
        if S == 1:
            o["gin"][...] = total(b["part"][own_rows, :], b["pr"], R - 1)
        else:
            o["gin"][...] = jnp.zeros((fb, S * SEQ_LEN), F32)
            o["gin"][:, pl.ds(al(a * SEQ_LEN, SEQ_LEN), SEQ_LEN)] = b["part"][own_rows, :].astype(F32)
            for k in range(1, R):
                q = lax.rem(r + R - k, R) // HB
                cols = pl.ds(al(q * SEQ_LEN, SEQ_LEN), SEQ_LEN)
                o["gin"][:, cols] += b["pr"][k - 1].astype(F32)
        for cp in ox:
            cp.wait()
        o_loc.wait()
        for cp in sd:
            cp.wait()
        o["sve"][...] = b["e2"][...] + b["eo"][...]
        o["svl"][...] = b["l2"][...] + b["lo"][...]
        for cp in fin:
            cp.wait()
        pl.when(par)(gqf.wait_send)
        pl.when(jnp.logical_not(par))(gqf.wait_recv)
        for go, cp in w_out:
            pl.when(go)(cp.wait_send)
        for q in range(R):
            pl.when((q % 2) == d)(w_fwd[q].wait_send)
        pl.when(jnp.logical_not(meta_self))(meta_out.wait_send)
        zU.drain()
        zD.drain()
        zQ.drain()

    sem = [pltpu.SemaphoreType.DMA((max(n, 1),)) for n in sems.values()]
    res = pl.pallas_call(
        body,
        out_shape=[struct(*s) for s in outs.values()],
        in_specs=[pl.BlockSpec(memory_space=pl.ANY)] * len(any_in) + [pl.BlockSpec(memory_space=pltpu.VMEM)] * len(vmem_in),
        out_specs=[pl.BlockSpec(memory_space=pltpu.VMEM)] * len(outs),
        scratch_shapes=[pltpu.VMEM(*s) for s in bufs.values()] + sem + sem + [pltpu.SMEM((8, SEQ_LEN), F32)],
        compiler_params=pltpu.CompilerParams(collective_id=0, has_side_effects=True, vmem_limit_bytes=62 << 20),
        name="encoder_layer",
    )(*[args[n] for n in names_in])
    return dict(zip(outs, res))


def finish_call(R, C, nh, fb, fc, qw, res):
    HB = res["svl"].shape[0] // (nh + 1)
    big = ["gin", "gqw", "gup", "gdn", "gpj"]
    shapes = [struct(res[n].shape, F32) for n in big]
    rows = [fb] * 6 + [fc, qw]

    def body(*refs):
        src = refs[:5]
        out_ref, e_ref, l_ref = refs[5:8]
        dst = refs[8:13]
        o_ref, t_ref = refs[13:15]
        vecs = refs[15:23]
        sem = refs[23]
        cps = [pltpu.make_async_copy(s, t, sem.at[j]) for j, (s, t) in enumerate(zip(src, dst))]
        run(*cps)
        r = lax.axis_index("row")
        c = lax.axis_index("col")
        o_ref[...] = out_ref[...].astype(F32)
        e = e_ref[...]
        mine = pltpu.roll(e, lax.rem(D - r * fb, D), 1)
        for j in range(6):
            vecs[j][...] = mine[j:j + 1, 0:fb]
        vecs[6][...] = e_ref[pl.ds(8 + c, 1), :][:, 0:fc]
        vecs[7][...] = l_ref[pl.ds((nh + 1) * c, 1), :][:, 0:qw]
        for j in range(nh):
            t_ref[j:j + 1, :] = l_ref[pl.ds((nh + 1) * c + 1 + j, 1), :][:, 0:CONV]
        for cp in cps:
            cp.wait()

    A, V = pl.BlockSpec(memory_space=pl.ANY), pl.BlockSpec(memory_space=pltpu.VMEM)
    outs = shapes + [struct(res["out"].shape, F32), struct((nh, CONV), F32)] + [struct((1, n), F32) for n in rows]
    return pl.pallas_call(
        body, out_shape=outs, in_specs=[V] * 8, out_specs=[A] * 5 + [V] * 10,
        scratch_shapes=[pltpu.SemaphoreType.DMA((5,))], name="outputs",
    )(*[res[n] for n in big], res["out"], res["sve"], res["svl"])


def make_shards(R, C):
    def shards(inputs, doc_ids, qkv_weight, qkv_bias, proj_weight, proj_bias, first_gain, first_shift,
               ffn_up, ffn_up_bias, ffn_down, ffn_down_bias, second_gain, second_shift, conv_kernel, cotangent):
        S = inputs.shape[1] // SEQ_LEN
        fb = inputs.shape[0]
        nh = conv_kernel.shape[0]
        qw = qkv_weight.shape[1]
        fc = ffn_up.shape[1]
        res = layer_call(R, C, S, fb, nh, fc, proj_weight.shape[0], qw, dict(
            x=inputs, cot=cotangent, wq=qkv_weight, wp=proj_weight, wu=ffn_up, wd=ffn_down, doc=doc_ids[None],
            taps=conv_kernel, qb=qkv_bias[None], g1=first_gain[None], s1=first_shift[None], g2=second_gain[None],
            s2=second_shift[None], pb=proj_bias[None], db=ffn_down_bias[None], ub=ffn_up_bias[None]))
        gin, gqw, gup, gdn, gpj, out, taps, g1, b1, g2, pbias, dbias, b2, ubias, qbias = finish_call(R, C, nh, fb, fc, qw, res)
        return (out, gin, gqw, qbias.reshape(qw), gpj, pbias.reshape(fb), g1.reshape(fb), b1.reshape(fb), gup,
                ubias.reshape(fc), gdn, dbias.reshape(fb), g2.reshape(fb), b2.reshape(fb), taps)
    return shards


def solution(mesh):
    in_specs = (P("row", ("dp", "col")), P(("dp", "row")), P("row", "col"), P("col"), P("col", "row"), P("row"),
                P("row"), P("row"), P("row", "col"), P("col"), P("row", "col"), P("row"), P("row"), P("row"),
                P("col", None), P("row", ("dp", "col")))
    out_specs = (P("row", ("dp", "col")), P("row", ("dp", "col")), P("row", "col"), P("col"), P("col", "row"), P("row"),
                 P("row"), P("row"), P("row", "col"), P("col"), P("row", "col"), P("row"), P("row"), P("row"),
                 P("col", None))
    fn = make_shards(mesh.shape["row"], mesh.shape["col"])
    return jax.shard_map(fn, mesh=mesh, in_specs=in_specs, out_specs=out_specs, check_vma=False)
```

```python
import functools

import jax
import jax.numpy as jnp
from jax import lax
from jax.experimental import pallas as pl
from jax.experimental.pallas import tpu as pltpu
from jax.sharding import PartitionSpec as P

D = 768
HEAD_DIM = 64
SEQ_LEN = 1024
EPSILON = 1e-05
F32=jnp.float32; BF=jnp.bfloat16
HD=64; SEQ=1024; SEG=16; CONV=33; ITERS=6; L=64
NEG=-1e9

def dg(a,b,ca,cb):
    return lax.dot_general(a,b,(((ca,),(cb,)),((),())),preferred_element_type=F32)
def nn(a,b): return dg(a,b,1,0)
def nt(a,b): return dg(a,b,1,1)
def tn(a,b): return dg(a,b,0,0)
def split(x):
    hi=x.astype(BF); lo=(x-hi.astype(F32)).astype(BF)
    return hi,lo
def cat(hl): return jnp.concatenate(hl,axis=0)
def halves(x):
    n=x.shape[0]//2
    return x[:n]+x[n:]
def nn2(a,b): return halves(nn(cat(split(a)),b))
def nt2(a,b): return halves(nt(cat(split(a)),b))
def nn3(a,b):
    ah,al=split(a); bh,bl=split(b)
    return halves(nn(cat((ah,al)),bh))+nn(ah,bl)
def nt3(a,b):
    ah,al=split(a); bh,bl=split(b)
    return halves(nt(cat((ah,al)),bh))+nt(ah,bl)

def iota(shape,dim): return lax.broadcasted_iota(jnp.int32,shape,dim)
def avg_mat():
    return jnp.where((iota((L,SEQ),1)//SEG)==iota((L,SEQ),0),F32(1.0/SEG),F32(0)).astype(BF)
def pick_mat():
    return jnp.where(iota((L,SEQ),1)==iota((L,SEQ),0)*SEG,F32(1),F32(0)).astype(BF)

def skew(x,left):
    W=x.shape[1]
    j=iota(x.shape,0)
    for bit in range(7):
        m=1<<bit
        x=jnp.where((j&m)!=0,pltpu.roll(x,(W-m) if left else m,1),x)
    return x

def band(w_row):
    return skew(jnp.broadcast_to(pltpu.roll(w_row,128-CONV//2,1),(128,384)),False)

def span(bt):
    return max(bt-1,0),min(bt+2,SEQ//128)

def same_doc(docb_ref,doc_row,bt):
    lo,hi=span(bt)
    col=docb_ref[bt*128:(bt+1)*128,:]
    return jnp.concatenate([col==doc_row[:,n*128:(n+1)*128] for n in range(lo,hi)],axis=1)

def conv_fwd(nh,qkv_ref,docb_ref,doc_row,band_ref,acc_ref):
    for bt in range(SEQ//128):
        lo,hi=span(bt)
        same=same_doc(docb_ref,doc_row,bt)
        off=(lo-bt+1)*128
        for h in range(nh):
            b=h*3*HD+2*HD
            ct=jnp.where(same,band_ref[h,:,off:off+(hi-lo)*128],0.0)
            o=nt(qkv_ref[b:b+HD,lo*128:hi*128],cat(split(ct)))
            acc_ref[h*HD:(h+1)*HD,bt*128:(bt+1)*128]=o[:,:128]+o[:,128:]

def head_scores(h,qkv_ref,doc_row,land_row,land_col,k1_ref,k3_ref,k2_ref,ql_ref,kl_ref,sum_ref):
    b=h*3*HD
    q=qkv_ref[b:b+HD,:]; k=qkv_ref[b+HD:b+2*HD,:]; v=qkv_ref[b+2*HD:b+3*HD,:]
    at=avg_mat()
    ql=nt(at,q); kl=nt(at,k)
    ql_ref[h]=ql; kl_ref[h]=kl
    keep=land_col==doc_row
    s1=jnp.where(keep,nn2(kl,q)*0.125,NEG)
    e1=jnp.exp(s1-jnp.max(s1,axis=0,keepdims=True))
    k1_ref[h]=e1/jnp.sum(e1,axis=0,keepdims=True)
    s3=jnp.where(keep,nn2(ql,k)*0.125,NEG)
    e3=jnp.exp(s3-jnp.max(s3,axis=1,keepdims=True))
    k3=e3/jnp.sum(e3,axis=1,keepdims=True)
    k3_ref[h]=k3
    s2=jnp.where(land_col==land_row,nt3(ql,kl)*0.125,NEG)
    e2=jnp.exp(s2-jnp.max(s2,axis=1,keepdims=True))
    k2_ref[h]=e2/jnp.sum(e2,axis=1,keepdims=True)
    sum_ref[h]=nt2(k3,v)

def eye(): return jnp.where(iota((L,L),0)==iota((L,L),1),F32(1),F32(0))

def newton(nh,k2_ref,v_ref,p_ref,n1_ref,n2_ref,n3_ref):
    for h in range(nh):
        v_ref[0,h]=k2_ref[h].T*(1.0/L)
    def step(i,_):
        I=eye()
        P=[nn3(k2_ref[h],v_ref[i,h]) for h in range(nh)]
        N1=[7.0*I-P[h] for h in range(nh)]
        N2=[15.0*I-nn3(P[h],N1[h]) for h in range(nh)]
        N3=[13.0*I-nn3(P[h],N2[h]) for h in range(nh)]
        for h in range(nh):
            p_ref[i,h]=P[h]; n1_ref[i,h]=N1[h]; n2_ref[i,h]=N2[h]; n3_ref[i,h]=N3[h]
            v_ref[i+1,h]=nn3(0.25*v_ref[i,h],N3[h])
        return 0
    lax.fori_loop(0,ITERS,step,0)

def head_out(h,k1_ref,inv,sum_ref,mix_ref,acc_ref,att_ref):
    mixed=nn3(inv,sum_ref[h])
    mix_ref[h]=mixed
    mt=mixed.T
    k1=k1_ref[h]
    res=nn3(mt,k1)
    att_ref[h*HD:(h+1)*HD,:]=(res+acc_ref[h*HD:(h+1)*HD,:]).astype(BF)

def newton_bwd(nh,k2_ref,v_ref,p_ref,n1_ref,n2_ref,n3_ref,gv_ref,gk_ref):
    for h in range(nh):
        gk_ref[h]=jnp.zeros((L,L),F32)
    def step(j,_):
        i=ITERS-1-j
        H=range(nh)
        gV=[gv_ref[h] for h in H]; V=[v_ref[i,h] for h in H]
        VT=[V[h].T for h in H]; PT=[p_ref[i,h].T for h in H]
        gN3=[0.25*nn3(VT[h],gV[h]) for h in H]
        gVn=[0.25*nt3(gV[h],n3_ref[i,h]) for h in H]
        gN2=[-nn3(PT[h],gN3[h]) for h in H]
        gN1=[-nn3(PT[h],gN2[h]) for h in H]
        gP=[-nt3(gN3[h],n2_ref[i,h])-nt3(gN2[h],n1_ref[i,h])-gN1[h] for h in H]
        for h in H:
            gk_ref[h]+=nt3(gP[h],V[h])
            gv_ref[h]=gVn[h]+nn3(k2_ref[h].T,gP[h])
        return 0
    lax.fori_loop(0,ITERS,step,0)
    for h in range(nh):
        gk_ref[h]+=gv_ref[h].T*(1.0/L)

def conv_bwd(nh,qkv_ref,g_ref,docb_ref,doc_row,band_ref,gacc_ref,gband_ref):
    for bt in range(SEQ//128):
        lo,hi=span(bt)
        same=same_doc(docb_ref,doc_row,bt)
        off=(lo-bt+1)*128
        for h in range(nh):
            b=h*3*HD+2*HD
            lanes=slice(off,off+(hi-lo)*128)
            ct=jnp.where(same,band_ref[h,:,lanes],0.0)
            g=g_ref[h*HD:(h+1)*HD,bt*128:(bt+1)*128]
            gv=nn(jnp.concatenate([g,g],axis=1),cat(split(ct)))
            gb=jnp.where(same,tn(g,qkv_ref[b:b+HD,lo*128:hi*128]),0.0)
            rows=slice(h*HD,(h+1)*HD)
            if bt==0:
                gband_ref[h]=jnp.zeros((128,384),F32)
                gacc_ref[rows,0:256]=gv
            else:
                gacc_ref[rows,lo*128:(bt+1)*128]+=gv[:,:256]
                if hi>bt+1:
                    gacc_ref[rows,(bt+1)*128:hi*128]=gv[:,256:]
            gband_ref[h,:,lanes]+=gb

def tap_row(gband):
    x=skew(gband,True)
    return pltpu.roll(jnp.sum(x,axis=0,keepdims=True),384-(128-CONV//2),1)

def head_bwd1(h,qkv_ref,g_ref,k1_ref,k3_ref,sum_ref,mix_ref,inv,gv_ref,gs1_ref,gs3_ref,gacc_ref):
    b=h*3*HD
    v=qkv_ref[b+2*HD:b+3*HD,:]
    g=g_ref[h*HD:(h+1)*HD,:]
    k1=k1_ref[h]
    gmix=nt2(k1,g)
    gk1=nn2(mix_ref[h],g)
    gs1_ref[h]=k1*(gk1-jnp.sum(k1*gk1,axis=0,keepdims=True))
    gv_ref[h]=nt3(gmix,sum_ref[h])
    gsum=nn3(inv.T,gmix)
    k3=k3_ref[h]
    gk3=nn2(gsum,v)
    gs3_ref[h]=k3*(gk3-jnp.sum(k3*gk3,axis=1,keepdims=True))
    gacc_ref[h*HD:(h+1)*HD,:]+=nn3(gsum.T,k3)

def head_bwd2(h,qkv_ref,k2_ref,gk_ref,ql_ref,kl_ref,gs1_ref,gs3_ref,gacc_ref,out_ref):
    b=h*3*HD
    q=qkv_ref[b:b+HD,:]; k=qkv_ref[b+HD:b+2*HD,:]
    k2=k2_ref[h]; gk2=gk_ref[h]
    gs2=k2*(gk2-jnp.sum(k2*gk2,axis=1,keepdims=True))
    ql=ql_ref[h]; kl=kl_ref[h]
    gs1=gs1_ref[h]; gs3=gs3_ref[h]
    gkl=nt2(gs1,q)+nn3(gs2.T,ql)
    gql=nt2(gs3,k)+nn3(gs2,kl)
    at=avg_mat()
    gq=(nn3(kl.T,gs1)+nn2(gql.T,at))*0.125
    gk=(nn3(ql.T,gs3)+nn2(gkl.T,at))*0.125
    out_ref[b:b+HD,:]=gq.astype(BF)
    out_ref[b+HD:b+2*HD,:]=gk.astype(BF)
    out_ref[b+2*HD:b+3*HD,:]=gacc_ref[h*HD:(h+1)*HD,:].astype(BF)

MESH = pl.DeviceIdType.MESH


def struct(shape, dtype):
    return jax.ShapeDtypeStruct(shape, dtype)


def remote(src, dst, ss, rs, dev):
    return pltpu.make_async_remote_copy(
        src_ref=src, dst_ref=dst, send_sem=ss, recv_sem=rs, device_id=dev, device_id_type=MESH
    )


def run(*copies):
    for cp in copies:
        cp.start()


def settle(cps, sent=True, got=True):
    for cp in cps:
        if sent:
            cp.wait_send()
        if got:
            cp.wait_recv()


def when(cond, fn):
    if cond is None:
        fn()
    else:
        pl.when(cond)(fn)


def al(x, n):
    return pl.multiple_of(x, n)


def gauss(x):
    e = jnp.exp(-0.5 * x * x)
    t = 1.0 / (1.0 + jnp.abs(x) * 0.23164190)
    p = t * 0.5307027145 - 0.7265760135
    p = (p * t + 0.7107068705) * t - 0.1422483680
    q = (p * t + 0.1274147960) * t * e
    return jnp.where(x >= 0, 1.0 - q, q), e * 0.3989422804014327


def norm_forward(residual, gain, shift):
    average = jnp.mean(residual, axis=1, keepdims=True)
    spread = jnp.mean(residual * residual, axis=1, keepdims=True) - average * average
    scaling = lax.rsqrt(spread + EPSILON)
    normed = (residual - average) * scaling
    return normed * gain + shift, normed, scaling


def norm_backward(upstream, gain, normed, scaling):
    scaled = upstream * gain
    mean_scaled = jnp.mean(scaled, axis=1, keepdims=True)
    crossed = jnp.mean(scaled * normed, axis=1, keepdims=True)
    return scaling * (scaled - mean_scaled - normed * crossed)


def tsum(x):
    return jnp.sum(x, axis=0, keepdims=True)


class RowGather:
    def __init__(self, snd, group, base, ways, place, r, R, cond=None):
        n = len(ways)
        self.cond, self.n, self.relay, self.ways = cond, n, R == 4, ways
        if self.relay:
            X, Y = lax.bitwise_xor(r, 1), lax.bitwise_xor(r, 2)
            self.own = []
            self.fwd = []
            for j in range(n):
                mine = place(j, r)
                self.own.append((snd(group, base + 2 * j, mine, mine, {"row": X}),
                                 snd(group, base + 2 * j + 1, mine, mine, {"row": Y})))
                src = place(j, Y if ways[j] else X)
                self.fwd.append(snd(group, base + 2 * n + j, src, src, {"row": X if ways[j] else Y}))
        else:
            self.own = [tuple(snd(group, base + j * (R - 1) + k - 1, place(j, r), place(j, r), {"row": lax.rem(r + k, R)})
                              for k in range(1, R)) for j in range(n)]

    def start(self):
        def go():
            for j, cps in enumerate(self.own):
                run(*(cps[::-1] if self.ways[j] else cps))
        when(self.cond, go)

    def forward(self):
        if self.relay:
            def go():
                for j in range(self.n):
                    self.own[j][self.ways[j]].wait_recv()
                    self.fwd[j].start()
            when(self.cond, go)

    def finish(self):
        def go():
            for j in range(self.n):
                if self.relay:
                    self.own[j][1 - self.ways[j]].wait_recv()
                    self.fwd[j].wait_recv()
                    self.fwd[j].wait_send()
                else:
                    for cp in self.own[j]:
                        cp.wait_recv()
                for cp in self.own[j]:
                    cp.wait_send()
        when(self.cond, go)


class RowReduce:
    def __init__(self, snd, group, block, recv, lanes, r, R):
        self.block, self.recv, self.lanes, self.r, self.R = block, recv, lanes, r, R
        self.relay = R == 4
        n = len(lanes)
        if self.relay:
            X, Y, Z = lax.bitwise_xor(r, 1), lax.bitwise_xor(r, 2), lax.bitwise_xor(r, 3)
            self.one, self.two, self.mids = [], [], []
            for j, ln in enumerate(lanes):
                P, Q = (X, Y) if j == 0 else (Y, X)
                self.one.append([snd(group, 3 * j, block(Z, ln), recv(1, ln), {"row": P}),
                                 snd(group, 3 * j + 1, block(P, ln), recv(0, ln), {"row": P})])
                self.two.append(snd(group, 3 * j + 2, block(Q, ln), recv(2, ln), {"row": Q}))
                self.mids.append(Q)
        else:
            self.all = [snd(group, k - 1, block(lax.rem(r + k, R), None), recv(k - 1, None), {"row": lax.rem(r + k, R)})
                        for k in range(1, R)]

    def start(self):
        if self.relay:
            for cps in self.one:
                cps[0].start()
        else:
            run(*self.all)

    def start_near(self):
        if self.relay:
            for cps in self.one:
                cps[1].start()

    def middle(self):
        if self.relay:
            for j, ln in enumerate(self.lanes):
                self.one[j][0].wait_recv()
                ref = self.block(self.mids[j], ln)
                ref[...] = (ref[...].astype(F32) + self.recv(1, ln)[...].astype(F32)).astype(BF)
                self.two[j].start()

    def total(self):
        if self.relay:
            for cps in self.one:
                settle(cps, got=False)
                cps[1].wait_recv()
            settle(self.two)
            slots = (0, 2)
        else:
            settle(self.all)
            slots = range(self.R - 1)
        t = self.block(self.r, None)[...].astype(F32)
        for k in slots:
            t = t + self.recv(k, None)[...].astype(F32)
        return t

    def finish(self):
        self.block(self.r, None)[...] = self.total().astype(BF)


class LineGather:
    def __init__(self, snd, group, n, place, c, C):
        self.C, self.c, self.n = C, c, n
        m = (C - 1) * n
        self.up = [[snd(group, k * n + j, place(j, c - k), place(j, c - k), {"col": c + 1}) for j in range(n)] for k in range(C - 1)]
        self.dn = [[snd(group, m + k * n + j, place(j, c + k), place(j, c + k), {"col": c - 1}) for j in range(n)] for k in range(C - 1)]

    def up_ok(self, k):
        return (self.c >= k) & (self.c < self.C - 1)

    def dn_ok(self, k):
        return (self.c + k <= self.C - 1) & (self.c > 0)

    def start(self):
        pl.when(self.up_ok(0))(lambda: run(*self.up[0]))
        pl.when(self.dn_ok(0))(lambda: run(*self.dn[0]))

    def step(self, k):
        def got(cps, nxt, ok):
            def go():
                for j in range(self.n):
                    cps[j].wait_recv()
                    if nxt is not None:
                        pl.when(ok)(lambda: nxt[j].start())
            return go
        more = k < self.C - 1
        pl.when(self.c >= k)(got(self.up[k - 1], self.up[k] if more else None, self.up_ok(k) if more else None))
        pl.when(self.c + k <= self.C - 1)(got(self.dn[k - 1], self.dn[k] if more else None, self.dn_ok(k) if more else None))

    def drain(self):
        for k in range(self.C - 1):
            pl.when(self.up_ok(k))(lambda: settle(self.up[k], got=False))
            pl.when(self.dn_ok(k))(lambda: settle(self.dn[k], got=False))


def layer_call(R, C, S, fb, nh, fc, pb, qw, args):
    HB = R // S
    QT = SEQ_LEN // HB
    FF = fc * C
    fh, ph = fc // 2, pb // 2
    fq = fh // 3 // 128 * 128
    fp = fh - fq
    dpw, dqw = fq, fp
    hb = nh * HD
    fbp = -(-fb // 128) * 128
    CH = 256
    relay = R == 4
    NR = 3 if relay else R - 1
    PT = nh + 1
    V = pltpu.VMEM
    small = (nh, L, L)
    any_in = ["x", "cot", "wq", "wp", "wu", "wd"]
    vmem_in = ["doc", "taps", "qb", "g1", "s1", "g2", "s2", "pb", "db", "ub"]
    names_in = any_in + vmem_in
    outs = dict(
        out=((fb, S * SEQ_LEN), BF), gin=((fb, S * SEQ_LEN), F32), gqw=((fb, qw), F32), gup=((fb, fc), F32),
        gdn=((fb, fc), F32), gpj=((pb, fb), F32), sve=((8, fbp), F32), svu=((1, fc), F32), svl=((PT, D), F32))
    bufs = dict(
        xg=((D, SEQ_LEN), BF), wg=((R, fb, qw), BF), ms=((8, SEQ_LEN), F32), mt=((8, SEQ_LEN), F32),
        rs=((8, fbp), F32), rp=((R, 8, fbp), F32), cs=((8, fc), F32), cp=((C, 8, fc), F32),
        cg=((D, QT), BF), wpf=((R, D, fb), BF), wuf=((D, FF), BF), wdf=((D, FF), BF),
        qkv=((3 * hb, SEQ_LEN), BF), k1=((nh, L, SEQ_LEN), F32), k3=((nh, L, SEQ_LEN), F32), k2=(small, F32),
        ql=(small, F32), kl=(small, F32), sm=(small, F32), mix=(small, F32), nv=((ITERS + 1,) + small, F32),
        np_=((ITERS,) + small, F32), n1=((ITERS,) + small, F32), n2=((ITERS,) + small, F32), n3=((ITERS,) + small, F32),
        docb=((SEQ_LEN, 128), F32), band=((nh, 128, 384), F32), gband=((nh, 128, 384), F32), acc=((hb, SEQ_LEN), F32), att=((hb, SEQ_LEN), BF), attq=((D, QT), BF),
        resT=((D, QT), F32), prow=((8, D), F32), hidden=((QT, D), F32), hid=((QT, D), BF), nm1=((QT, D), F32),
        sc1=((QT, 1), F32), act=((QT, FF), BF), dact=((QT, FF), F32), res2=((QT, D), F32), gdown=((QT, D), BF),
        gpre=((QT, FF), BF), gattoT=((D, QT), BF), outT=((D, QT), BF), gatt=((hb, SEQ_LEN), BF),
        hid_o=((QT, D), BF), gdown_o=((QT, D), BF), gattoT_o=((D, QT), BF), att_o=((C * ph, QT), BF),
        act_o=((QT, C * fh), BF), gpre_o=((QT, C * fh), BF),
        gu=((D, C * fh), BF), gd=((D, C * fp), BF), gp=((R, C * ph, fb), BF), gdq=((D, C * fq), BF),
        ru=((NR, fb, C * fh), BF), rd=((NR, fb, C * fp), BF), rpj=((NR, C * ph, fb), BF),
        zu=((C - 1, fb, fh), BF), zd=((C - 1, fb, fp), BF), zp=((C - 1, ph, fb), BF),
        zdq=((C - 1, D, fq), BF), tdq=((D, fq), BF),
        rdq=((R - 1, fb, fq), BF),
        gv=(small, F32), gk=(small, F32),
        part=((D, SEQ_LEN), BF), pr=((R - 1, fb, SEQ_LEN), BF),
        gq=((R, fb, qw), BF), gqo=((R // 2, fb, qw), BF), gqr=((R, fb, qw), BF), gqz=((C, fb, qw), BF),
        e0=((8, D), F32), eb=((R, 8, fbp), F32), er=((R - 1, 8, fbp), F32), e1=((8, fbp), F32), ez=((C - 1, 8, fbp), F32),
        e2=((8, fbp), F32), eo=((8, fbp), F32), u0=((C, 1, fc), F32), uz=((C - 1, 1, fc), F32), u1=((1, fc), F32),
        ur=((R - 1, 1, fc), F32), u2=((1, fc), F32), uo=((1, fc), F32), l0=((PT, D), F32), lz=((C - 1, PT, D), F32),
        l1=((PT, D), F32), lr=((R, PT, D), F32), l2=((PT, D), F32), lo=((PT, D), F32))
    for name, (shape, dtype) in outs.items():
        bufs["o_" + name] = (shape, dtype)
    NRP = 1 + 2 * (C - 1)
    sems = dict(
        x=2 * (R - 1), cot=R - 1, rowp=R - 1, colp=C - 1, meta=1, ws=S * C, wr=R, wd2=R,
        zU=4 * (C - 1), zD=2 * (C - 1), rU=NRP * 2 * (R - 1), rD=NRP * (R - 1), rQ=2 * (R - 1), zQ=2 * (C - 1), zR=2 * (C - 1),
        cU=2 * NRP, cD=NRP, cQ=2 * NRP,
        att=HB - 1, gatt=HB - 1, ex=3 + 3 * C, ru=max(6, R - 1), rd=max(6, R - 1), rp=max(3, R - 1), rcol=3 * (C - 1),
        zq=C - 1, rq=R - 1, part=max(6, R - 1), outx=R - 1,
        gqd=R // 2, gqrow=R, gqcol=C, gqf=1, erow=R - 1, ecol=C - 1, ed=1, ucol=C - 1, urow=R - 1, ud=1, lcol=C - 1, lrow=R, ld=1, fin=5, loc=24, leave=len(outs))

    def body(*refs):
        n = len(names_in)
        i = dict(zip(names_in, refs[:n]))
        final = dict(zip(outs, refs[n:n + len(outs)]))
        k = n + len(outs)
        b = dict(zip(bufs, refs[k:k + len(bufs)]))
        k += len(bufs)
        o = {name: b["o_" + name] for name in outs}
        ss = dict(zip(sems, refs[k:k + len(sems)]))
        k += len(sems)
        rs = dict(zip(sems, refs[k:k + len(sems)]))
        k += len(sems)
        d = lax.axis_index("dp")
        r = lax.axis_index("row")
        c = lax.axis_index("col")
        a, h = r // HB, lax.rem(r, HB)
        core = {"dp": 1 - d}

        def snd(group, slot, src, dst, dev):
            return remote(src, dst, ss[group].at[slot], rs[group].at[slot], dev)

        def loc(slot, src, dst):
            return pltpu.make_async_copy(src, dst, ss["loc"].at[slot])

        def fr(ref, q):
            return ref.at[pl.ds(al(q * fb, fb), fb), :]

        def peer(k):
            return lax.rem(r + k, R)

        def cpeer(k):
            return lax.rem(c + k, C)

        leaving = []

        def leave(*some):
            for name in some:
                cp = pltpu.make_async_copy(o[name], final[name], ss["leave"].at[list(outs).index(name)])
                cp.start()
                leaving.append(cp)

        own = c == h
        bar = pltpu.get_barrier_semaphore()
        for k in range(1, R):
            pl.semaphore_signal(bar, inc=1, device_id={"row": peer(k)}, device_id_type=MESH)
        for k in range(1, C):
            pl.semaphore_signal(bar, inc=1, device_id={"col": cpeer(k)}, device_id_type=MESH)
        pl.semaphore_signal(bar, inc=1, device_id=core, device_id_type=MESH)
        for q in range(R):
            @pl.when(jnp.logical_not(own & (r == q)))
            def _():
                pl.semaphore_signal(bar, inc=1, device_id={"row": q, "col": h}, device_id_type=MESH)
        half = fb // 2

        def xcols(q, part=None):
            rows = slice(None) if part is None else pl.ds(part * half, half)
            return i["x"].at[rows, pl.ds(al(q // HB * SEQ_LEN, SEQ_LEN), SEQ_LEN)]

        x_loc = loc(0, xcols(r), fr(b["xg"], r))
        x_loc.start()

        def cols_of(col, first, width):
            return pl.ds(al(col * fc + d * fh + first, 128), width)

        def wide(ref, row, col, first, width):
            return ref.at[pl.ds(al(row * fb, fb), fb), cols_of(col, first, width)]

        def narrow(ref, row, col):
            return ref.at[row, pl.ds(al(col * pb + d * ph, ph), ph), :]

        bulk_loc = [loc(1, i["wu"].at[:, pl.ds(al(d * fh, fh), fh)], wide(b["wuf"], r, c, 0, fh)),
                    loc(2, i["wd"].at[:, pl.ds(al(d * fh, fh), fh)], wide(b["wdf"], r, c, 0, fh)),
                    loc(3, i["wp"].at[pl.ds(al(d * ph, ph), ph), :], narrow(b["wpf"], r, c))]
        run(*bulk_loc)
        cot_rows = min(fb, 64)
        stage = []
        for s in range(S):
            for f in range(0, fb, cot_rows):
                m = len(stage)
                buf = b["k1"].at[m] if m < nh else b["k3"].at[m - nh]
                stage.append((s, f, m, loc(4 + m, i["cot"].at[f:f + cot_rows, s * SEQ_LEN:(s + 1) * SEQ_LEN], buf.at[0:cot_rows, :])))
        run(*[t[3] for t in stage])
        b["ms"][...] = jnp.zeros((8, SEQ_LEN), F32)
        b["ms"][0:1, :] = i["doc"][...].astype(F32)
        b["ms"][1:1 + nh, 0:CONV] = i["taps"][...]
        b["ms"][1 + nh:2 + nh, 0:qw] = i["qb"][...].astype(F32)
        b["rs"][...] = jnp.zeros((8, fbp), F32)
        for j, name in enumerate(("g1", "s1", "g2", "s2", "pb", "db")):
            b["rs"][j:j + 1, 0:fb] = i[name][...].astype(F32)
        b["cs"][...] = jnp.zeros((8, fc), F32)
        b["cs"][0:1, :] = i["ub"][...].astype(F32)
        for cp in bulk_loc:
            cp.wait()
        x_loc.wait()
        pl.semaphore_wait(bar, R - 1 + C - 1 + 1 + S * C - jnp.where(own, 1, 0))

        def place_u(col):
            return lambda j, row: narrow(b["wpf"], row, col) if j else wide(b["wuf"], row, col, 0, fp)

        def place_d(col):
            return lambda j, row: wide(b["wdf"], row, col, 0, dpw)

        zU = LineGather(snd, "zU", 2, lambda j, col: place_u(col)(j, r), c, C)
        zD = LineGather(snd, "zD", 1, lambda j, col: place_d(col)(j, r), c, C)
        at_cols = [(None, c)]
        for k in range(1, C):
            at_cols += [(c >= k, c - k), (c + k <= C - 1, c + k)]
        rU = [RowGather(snd, "rU", m * 2 * (R - 1), (0, 1), place_u(col), r, R, cond) for m, (cond, col) in enumerate(at_cols)]
        rD = [RowGather(snd, "rD", m * (R - 1), (1,), place_d(col), r, R, cond) for m, (cond, col) in enumerate(at_cols)]
        rQ = RowGather(snd, "rQ", 0, (0, 1), lambda j, row: wide(b["wdf"], row, c, dpw, dqw) if j else wide(b["wuf"], row, c, fp, fq), r, R)
        zQ = LineGather(snd, "zQ", 1, lambda j, col: b["wuf"].at[:, cols_of(col, fp, fq)], c, C)
        zR = LineGather(snd, "zR", 1, lambda j, col: b["wdf"].at[:, cols_of(col, dpw, dqw)], c, C)
        rQ.start()
        zU.start()
        zD.start()
        if relay:
            xg = RowGather(snd, "x", 0, (0, 1), lambda j, q: b["xg"].at[pl.ds(al(q * fb + j * half, half), half), :], r, R)
            xg.start()
        else:
            xs = [snd("x", k - 1, xcols(peer(k)), fr(b["xg"], r), {"row": peer(k)}) for k in range(1, R)]
            run(*xs)
        par = lax.rem(r, 2) == d
        w_out = []
        for ap in range(S):
            for cq in range(C):
                t = ap * HB + c
                go = par & jnp.logical_not((t == r) & (c == cq))
                cp = remote(i["wq"], b["wg"].at[r], ss["ws"].at[ap * C + cq], rs["wr"].at[r], {"row": t, "col": cq})
                w_out.append((go, cp))
        for go, cp in w_out:
            pl.when(go)(cp.start)
        w_loc = loc(16, i["wq"], b["wg"].at[r])
        pl.when(own & par)(w_loc.start)
        dst_row, dst_col = lax.rem(r, S) * HB + c, r // S
        meta_self = (dst_row == r) & (dst_col == c)
        meta_out = snd("meta", 0, b["ms"], b["mt"], {"row": dst_row, "col": dst_col})
        meta_in = snd("meta", 0, b["ms"], b["mt"], {"row": c * S + a, "col": h})
        meta_loc = loc(17, b["ms"], b["mt"])
        pl.when(jnp.logical_not(meta_self))(meta_out.start)
        pl.when(meta_self)(meta_loc.start)

        def cot_at(s, cols):
            return b["gpre"].at[pl.ds(al(s // 3 * fb, fb), fb), cols]

        for s, f, m, cp in stage:
            cp.wait()
            buf = b["k1"].at[m] if m < nh else b["k3"].at[m - nh]
            b["gpre"][s // 3 * fb + f:s // 3 * fb + f + cot_rows, s % 3 * SEQ_LEN:(s % 3 + 1) * SEQ_LEN] = buf[0:cot_rows, :].astype(BF)

        def cot_src(q):
            s = q // HB
            return cot_at(s, pl.ds(al(lax.rem(s, 3) * SEQ_LEN + lax.rem(q, HB) * QT, QT), QT))

        rQ.forward()
        zU.step(1)
        if relay:
            xg.forward()
        zD.step(1)
        for k in range(2, C - 1):
            zU.step(k)
            zD.step(k)
        rQ.finish()
        zQ.start()
        zR.start()
        if relay:
            xg.finish()
        else:
            settle(xs)
        for m in range(2 * C - 3):
            rU[m].start()
        gs = [snd("cot", k - 1, cot_src(peer(k)), fr(b["cg"], r), {"row": peer(k)}) for k in range(1, R)]
        g_loc = loc(18, cot_src(r), fr(b["cg"], r))
        ps = [snd("rowp", k - 1, b["rs"], b["rp"].at[r], {"row": peer(k)}) for k in range(1, R)]
        p_loc = loc(19, b["rs"], b["rp"].at[r])
        cs = [snd("colp", k - 1, b["cs"], b["cp"].at[c], {"col": cpeer(k)}) for k in range(1, C)]
        c_loc = loc(20, b["cs"], b["cp"].at[c])
        run(*ps, p_loc, *cs, c_loc)
        w_fwd = [snd("wd2", q, b["wg"].at[q], b["wg"].at[q], core) for q in range(R)]
        for q in range(R):
            mine_q = (q % 2) == d
            here_q = own & (r == q)
            w_in = remote(i["wq"], b["wg"].at[q], ss["ws"].at[0], rs["wr"].at[q], {"row": q, "col": h})
            pl.when(mine_q & here_q)(w_loc.wait)
            pl.when(mine_q & jnp.logical_not(here_q))(w_in.wait_recv)
            pl.when(mine_q)(w_fwd[q].start)
        for q in range(R):
            pl.when((q % 2) != d)(w_fwd[q].wait_recv)
        pl.when(jnp.logical_not(meta_self))(meta_in.wait_recv)
        pl.when(meta_self)(meta_loc.wait)
        qb = jnp.where(iota((8, qw), 0) == 1 + nh, b["mt"][:, 0:qw], 0.0).astype(BF)
        acc = tn(qb, jnp.ones((8, SEQ_LEN), BF))
        for q in range(R):
            acc = acc + tn(b["wg"][q], b["xg"][q * fb:(q + 1) * fb, :])
        b["qkv"][...] = acc.astype(BF)

        doc_row = b["mt"][0:1, :]
        rowb = jnp.broadcast_to(doc_row, (8, SEQ_LEN)).astype(BF)
        pick = pick_mat()
        land_row = nt(rowb, pick)[0:1]
        land_col = nt(pick, rowb)[:, 0:1]
        def scores(hh):
            head_scores(hh, b["qkv"], doc_row, land_row, land_col, b["k1"], b["k3"], b["k2"], b["ql"], b["kl"], b["sm"])

        for hh in range(nh):
            scores(hh)
        zQ.step(1)
        zU.step(C - 1)
        zD.step(C - 1)
        for m in range(2 * C - 3, NRP):
            rU[m].start()
        for m in range(3):
            rU[m].forward()
        for hh in range(nh):
            b["band"][hh] = band(b["mt"][1 + hh:2 + hh, 0:384])
        one = jnp.where(iota((8, 128), 0) == 0, 1.0, 0.0).astype(BF)
        b["docb"][...] = tn(rowb, one)
        newton(nh, b["k2"], b["nv"], b["np_"], b["n1"], b["n2"], b["n3"])
        zR.step(1)
        for k in range(2, C - 1):
            zQ.step(k)
        conv_fwd(nh, b["qkv"], b["docb"], doc_row, b["band"], b["acc"])
        for hh in range(nh):
            head_out(hh, b["k1"], b["nv"][ITERS, hh], b["sm"], b["mix"], b["acc"], b["att"])

        def group(k):
            return lax.rem(h + k, HB)

        def hrows(ref, q):
            return ref.at[pl.ds(al(q * hb, hb), hb), :]

        def tcols(ref, q):
            return ref.at[:, pl.ds(al(q * QT, QT), QT)]

        at = [snd("att", k - 1, tcols(b["att"], group(k)), hrows(b["attq"], h), {"row": a * HB + group(k)})
              for k in range(1, HB)]
        run(*at)
        at_loc = loc(0, tcols(b["att"], h), hrows(b["attq"], h))
        at_loc.start()
        for m in range(3, NRP):
            rU[m].forward()
        for m in range(NRP):
            rD[m].start()
        for cp in ps + cs:
            cp.wait()
        for cp in (p_loc, c_loc):
            cp.wait()
        prow = jnp.zeros((8, D), F32)
        for q in range(R):
            piece = jnp.concatenate([b["rp"][q], jnp.zeros((8, D - fbp), F32)], axis=1)
            prow = prow + (pltpu.roll(piece, q * fb, 1) if q else piece)
        b["prow"][...] = prow
        def cross(group, slot, cond, *refs):
            cps = [snd(group, slot + j, ref, ref, core) for j, ref in enumerate(refs)]
            when(cond, lambda: run(*cps))
            return cond, cps

        crossed, later = [], []
        for m, (cond, col) in enumerate(at_cols):
            rU[m].finish()
            crossed.append(cross("cU", 2 * m, cond, b["wuf"].at[:, cols_of(col, 0, fp)],
                                 b["wpf"].at[:, pl.ds(al(col * pb + d * ph, ph), ph), :]))
        zQ.step(C - 1)
        for m, (cond, col) in enumerate(at_cols):
            crossed.append(cross("cQ", 2 * m, cond, b["wuf"].at[:, cols_of(col, fp, fq)]))
        settle(at)
        at_loc.wait()
        for cond, cps in crossed:
            when(cond, lambda: settle(cps))

        for q in range(R):
            t = tn(b["wpf"][q], b["attq"][...])
            b["resT"][q * fb:(q + 1) * fb, :] = t + b["xg"][q * fb:(q + 1) * fb, pl.ds(al(h * QT, QT), QT)].astype(F32)
        res1 = b["resT"][...].T + b["prow"][4:5, :]
        hidden, nm1, sc1 = norm_forward(res1, b["prow"][0:1, :], b["prow"][1:2, :])
        b["hidden"][...] = hidden
        b["nm1"][...] = nm1
        b["sc1"][...] = sc1
        b["hid"][...] = hidden.astype(BF)
        ex_hid = snd("ex", 0, b["hid"], b["hid_o"], core)
        ex_hid.start()

        def up(j, _):
            cols = pl.ds(al(j * CH, CH), CH)
            per = fc // CH
            bias = b["cp"][j // per, 0:1, pl.ds(al(lax.rem(j, per) * CH, CH), CH)]
            pre = nn(b["hid"][...], b["wuf"][:, cols]) + bias
            cdf, pdf = gauss(pre)
            b["act"][:, cols] = (pre * cdf).astype(BF)
            b["dact"][:, cols] = cdf + pre * pdf
            return 0

        lax.fori_loop(0, FF // CH // 2, up, 0)
        for m in range(2 * C - 3):
            rD[m].forward()
        for k in range(2, C - 1):
            zR.step(k)
        lax.fori_loop(FF // CH // 2, FF // CH, up, 0)
        for m in range(2 * C - 3, NRP):
            rD[m].forward()
        run(*gs, g_loc)
        zR.step(C - 1)
        for m, (cond, col) in enumerate(at_cols):
            later.append(cross("cQ", 2 * m + 1, cond, b["wdf"].at[:, cols_of(col, dpw, dqw)]))
        ex_act = [snd("ex", 3 + q, b["act"].at[:, pl.ds(al(q * fc + (1 - d) * fh, fh), fh)],
                      b["act_o"].at[:, q * fh:(q + 1) * fh], core) for q in range(C)]
        run(*ex_act)
        for m, (cond, col) in enumerate(at_cols):
            rD[m].finish()
            later.append(cross("cD", m, cond, b["wdf"].at[:, cols_of(col, 0, dpw)]))
        for cond, cps in later:
            when(cond, lambda: settle(cps))

        def down(j, _):
            cols = pl.ds(al(j * CH, CH), CH)
            b["res2"][:, cols] = b["hidden"][:, cols] + nt(b["act"][...], b["wdf"][cols, :]) + b["prow"][5:6, cols]
            return 0

        lax.fori_loop(0, D // CH, down, 0)
        gain2 = b["prow"][2:3, :]
        out, nm2, sc2 = norm_forward(b["res2"][...], gain2, b["prow"][3:4, :])
        settle(gs)
        g_loc.wait()
        ups = b["cg"][...].astype(F32).T
        e0 = b["e0"]
        e0[...] = jnp.zeros((8, D), F32)
        e0[2:3, :] = tsum(ups * nm2)
        e0[5:6, :] = tsum(ups)
        gres2 = norm_backward(ups, gain2, nm2, sc2)
        b["res2"][...] = gres2
        b["gdown"][...] = gres2.astype(BF)
        e0[4:5, :] = tsum(b["gdown"][...].astype(F32))
        ex_gdown = snd("ex", 1, b["gdown"], b["gdown_o"], core)
        ex_gdown.start()
        b["outT"][...] = out.T.astype(BF)
        ox = [snd("outx", k - 1, fr(b["outT"], peer(k)), tcols(o["out"], a * HB + h), {"row": peer(k)}) for k in range(1, R)]
        o_loc = loc(1, fr(b["outT"], r), tcols(o["out"], a * HB + h))
        run(*ox, o_loc)

        def gact(j, _):
            cols = pl.ds(al(j * CH, CH), CH)
            g = nn(b["gdown"][...], b["wdf"][:, cols])
            gp = (g * b["dact"][:, cols]).astype(BF)
            b["gpre"][:, cols] = gp
            per = fc // CH
            b["u0"][j // per, 0:1, pl.ds(al(lax.rem(j, per) * CH, CH), CH)] = tsum(gp.astype(F32))
            return 0

        lax.fori_loop(0, FF // CH, gact, 0)
        ex_gpre = [snd("ex", 3 + C + q, b["gpre"].at[:, pl.ds(al(q * fc + (1 - d) * fh, fh), fh)],
                       b["gpre_o"].at[:, q * fh:(q + 1) * fh], core) for q in range(C)]
        run(*ex_gpre)
        def grad_block(q, mine, mine_w, other, other_w):
            to = slice(q * fh, (q + 1) * fh)
            return tn(b[mine][...], b[mine_w][:, cols_of(q, 0, fh)]) + tn(b[other][...], b[other_w][:, to])

        def block_of(ref):
            return lambda q, ln: ref.at[pl.ds(al(q * fb, fb), fb), slice(None) if ln is None else ln]

        def recv_of(ref):
            return lambda k, ln: ref.at[k, :, slice(None) if ln is None else ln]

        settle(ex_act)
        settle([ex_gdown])
        for q in range(C):
            t = grad_block(q, "gdown", "act", "gdown_o", "act_o")
            b["gd"][:, q * fp:(q + 1) * fp] = t[:, :fp].astype(BF)
            b["gdq"][:, q * fq:(q + 1) * fq] = t[:, fp:].astype(BF)

        def lanes(n):
            return slice(0, n // 2), slice(n // 2, n)

        red_d = RowReduce(snd, "rd", block_of(b["gd"]), recv_of(b["rd"]), lanes(C * fp), r, R)
        red_d.start()
        zqd = [snd("zq", k - 1, b["gdq"].at[:, pl.ds(al(cpeer(k) * fq, fq), fq)], b["zdq"].at[k - 1], {"col": cpeer(k)})
               for k in range(1, C)]
        run(*zqd)

        def ghid_step(j, _):
            cols = pl.ds(al(j * CH, CH), CH)
            b["hidden"][:, cols] = b["res2"][:, cols] + nt(b["gpre"][...], b["wuf"][cols, :])
            return 0

        lax.fori_loop(0, D // CH, ghid_step, 0)
        ghid = b["hidden"][...]
        nm1 = b["nm1"][...]
        e0[0:1, :] = tsum(ghid * nm1)
        e0[1:2, :] = tsum(ghid)
        gres1 = norm_backward(ghid, b["prow"][0:1, :], nm1, b["sc1"][...])
        e0[3:4, :] = tsum(gres1.astype(BF).astype(F32))
        b["resT"][...] = gres1.T
        b["gattoT"][...] = b["resT"][...].astype(BF)
        ga = jnp.zeros((D, QT), F32)
        for q in range(R):
            ga = ga + nn(b["wpf"][q], b["gattoT"][q * fb:(q + 1) * fb, :])
        b["cg"][...] = ga.astype(BF)
        gt = [snd("gatt", k - 1, hrows(b["cg"], group(k)), tcols(b["gatt"], h), {"row": a * HB + group(k)})
              for k in range(1, HB)]
        run(*gt)
        gt_loc = loc(2, hrows(b["cg"], h), tcols(b["gatt"], h))
        gt_loc.start()
        red_d.start_near()
        b["eb"][...] = jnp.zeros((R, 8, fbp), F32)
        for q in range(R):
            b["eb"][q, :, 0:fb] = e0[:, q * fb:(q + 1) * fb]
        er = [snd("erow", k - 1, b["eb"].at[peer(k)], b["er"].at[k - 1], {"row": peer(k)}) for k in range(1, R)]
        uc = [snd("ucol", k - 1, b["u0"].at[cpeer(k)], b["uz"].at[k - 1], {"col": cpeer(k)}) for k in range(1, C)]
        run(*er, *uc)
        ex_att = [snd("ex", 2, b["gattoT"], b["gattoT_o"], core)] + [
            snd("ex", 3 + 2 * C + q, b["attq"].at[pl.ds(al(q * pb + (1 - d) * ph, ph), ph), :],
                b["att_o"].at[q * ph:(q + 1) * ph, :], core) for q in range(C)]
        run(*ex_att)
        settle([ex_hid])
        settle(ex_gpre)
        for q in range(C):
            b["gu"][:, q * fh:(q + 1) * fh] = grad_block(q, "hid", "gpre", "hid_o", "gpre_o").astype(BF)
        own_rows = pl.ds(al(r * fb, fb), fb)
        red_u = RowReduce(snd, "ru", block_of(b["gu"]), recv_of(b["ru"]), lanes(C * fh), r, R)
        settle(ex_att)
        for q in range(C):
            rows = pl.ds(al(q * pb + d * ph, ph), ph)
            tp = slice(q * ph, (q + 1) * ph)
            for p in range(R):
                f = slice(p * fb, (p + 1) * fb)
                b["gp"][p, tp, :] = (nt(b["attq"][rows, :], b["gattoT"][f, :])
                                     + nt(b["att_o"][tp, :], b["gattoT_o"][f, :])).astype(BF)
        red_p = RowReduce(snd, "rp", lambda q, ln: b["gp"].at[q], lambda k, ln: b["rpj"].at[k], (None,), r, R)
        red_p.start()
        red_p.start_near()
        red_u.start()
        def total(own_part, buf, m):
            t = own_part.astype(F32)
            for k in range(m):
                t = t + buf[k].astype(F32)
            return t

        def scatter_p(slot, src_of, dst):
            cps = [snd("rcol", slot * (C - 1) + k - 1, src_of(cpeer(k)), dst.at[k - 1], {"col": cpeer(k)}) for k in range(1, C)]
            run(*cps)
            return cps

        def pcol(ref, n):
            return lambda q: ref.at[own_rows, pl.ds(al(q * n, n), n)]

        qcols = pl.ds(al(c * fq, fq), fq)

        def whole(first, buf, m):
            for k in range(m):
                first = first + buf[k]
            return first

        settle(gt)
        gt_loc.wait()
        conv_bwd(nh, b["qkv"], b["gatt"], b["docb"], doc_row, b["band"], b["acc"], b["gband"])
        for hh in range(nh):
            head_bwd1(hh, b["qkv"], b["gatt"], b["k1"], b["k3"], b["sm"], b["mix"], b["nv"][ITERS, hh], b["gv"], b["k1"], b["k3"], b["acc"])
        red_d.middle()
        newton_bwd(nh, b["k2"], b["nv"], b["np_"], b["n1"], b["n2"], b["n3"], b["gv"], b["gk"])
        red_u.start_near()
        red_p.middle()
        for hh in range(nh):
            head_bwd2(hh, b["qkv"], b["k2"], b["gk"], b["ql"], b["kl"], b["k1"], b["k3"], b["acc"], b["qkv"])

        for q in range(R):
            b["gq"][q] = nt(b["xg"][q * fb:(q + 1) * fb, :], b["qkv"][...]).astype(BF)
        gqd = [snd("gqd", j, b["gq"].at[2 * j + 1 - d], b["gqo"].at[j], core) for j in range(R // 2)]
        run(*gqd)
        l0 = b["l0"]
        l0[...] = jnp.zeros((PT, D), F32)
        l0[0:1, 0:qw] = nt(jnp.ones((8, SEQ_LEN), BF), b["qkv"][...])[0:1]
        for hh in range(nh):
            l0[1 + hh:2 + hh, 0:384] = tap_row(b["gband"][hh])
        lcl = [snd("lcol", k - 1, l0, b["lz"].at[k - 1], {"col": cpeer(k)}) for k in range(1, C)]
        run(*lcl)
        red_u.middle()
        settle(gqd)
        gq_out = []
        for j in range(R // 2):
            b["gq"][2 * j + d] = (b["gq"][2 * j + d].astype(F32) + b["gqo"][j].astype(F32)).astype(BF)
            q = 2 * j + d
            cp = remote(b["gq"].at[q], b["gqr"].at[r], ss["gqrow"].at[j], rs["gqrow"].at[r], {"row": q})
            lc = loc(3, b["gq"].at[q], b["gqr"].at[r])
            gq_out.append((q, cp, lc))
            pl.when(q != r)(cp.start)
            pl.when(q == r)(lc.start)
        for q in range(R):
            f = slice(q * fb, (q + 1) * fb)
            b["part"][f, :] = nn(b["wg"][q], b["qkv"][...]).astype(BF)
            mine_cols = pl.ds(al(h * QT, QT), QT)
            b["part"][f, mine_cols] = (nn(b["wg"][q], b["qkv"][:, mine_cols]) + b["resT"][f, :]).astype(BF)
        red_x = RowReduce(snd, "part", block_of(b["part"]), recv_of(b["pr"]), lanes(SEQ_LEN), r, R)
        if relay:
            red_x.start()
            red_x.start_near()
        else:
            pt = [snd("part", k - 1, fr(b["part"], peer(k)), b["pr"].at[k - 1], {"row": peer(k)}) for k in range(1, R)]
            run(*pt)

        red_d.finish()
        rcd = scatter_p(0, pcol(b["gd"], fp), b["zd"])
        settle(zqd)
        b["tdq"][...] = total(b["gdq"][:, qcols], b["zdq"], C - 1).astype(BF)
        rqd = [snd("rq", k - 1, fr(b["tdq"], peer(k)), b["rdq"].at[k - 1], {"row": peer(k)}) for k in range(1, R)]
        run(*rqd)
        settle(lcl)
        b["l1"][...] = whole(l0[...], b["lz"], C - 1)
        lrw = [remote(b["l1"], b["lr"].at[r], ss["lrow"].at[k - 1], rs["lrow"].at[r], {"row": peer(k)}) for k in range(1, R)]
        run(*lrw)
        b["lr"][r] = b["l1"][...]
        settle(er + uc)
        b["e1"][...] = whole(b["eb"][r], b["er"], R - 1)
        b["u1"][...] = whole(b["u0"][c], b["uz"], C - 1)
        ec = [snd("ecol", k - 1, b["e1"], b["ez"].at[k - 1], {"col": cpeer(k)}) for k in range(1, C)]
        ur = [snd("urow", k - 1, b["u1"], b["ur"].at[k - 1], {"row": peer(k)}) for k in range(1, R)]
        run(*ec, *ur)
        red_u.finish()
        rcu = scatter_p(1, pcol(b["gu"], fh), b["zu"])
        red_p.finish()
        rcp = scatter_p(2, lambda q: b["gp"].at[r, pl.ds(al(q * ph, ph), ph), :], b["zp"])

        gq_col = []
        for hp in range(HB):
            cp = remote(b["gqr"].at[hp], b["gqz"].at[c], ss["gqcol"].at[hp], rs["gqcol"].at[c], {"col": hp})
            lc = loc(4, b["gqr"].at[hp], b["gqz"].at[c])
            gq_col.append((hp, cp, lc))
        @pl.when(par)
        def _():
            for q in range(R):
                cp = remote(b["gq"].at[0], b["gqr"].at[q], ss["gqrow"].at[0], rs["gqrow"].at[q], {"row": q})
                pl.when(q != r)(cp.wait_recv)
        for q, cp, lc in gq_out:
            pl.when(q != r)(cp.wait_send)
            pl.when(q == r)(lc.wait)
        @pl.when(par)
        def _():
            for ap in range(1, S):
                for hp in range(HB):
                    b["gqr"][hp] = (b["gqr"][hp].astype(F32) + b["gqr"][ap * HB + hp].astype(F32)).astype(BF)
            for hp, cp, lc in gq_col:
                pl.when(hp != c)(cp.start)
                pl.when(hp == c)(lc.start)
        red_x.middle()
        half_rows, half_cols = pl.ds(al(d * ph, ph), ph), pl.ds(al(d * fh, fh), fh)
        pcols, qcols2 = pl.ds(al(d * fh, 128), fp), pl.ds(al(d * fh + fp, 128), fq)
        settle(ox)
        o_loc.wait()
        leave("out")
        settle(rqd)
        o["gdn"][:, qcols2] = total(b["tdq"][own_rows, :], b["rdq"], R - 1)
        settle(rcd + rcu + rcp)
        mycols = pl.ds(al(c * fp, fp), fp)
        o["gdn"][:, pcols] = total(b["gd"][own_rows, mycols], b["zd"], C - 1)
        o["gup"][:, half_cols] = total(b["gu"][own_rows, pl.ds(al(c * fh, fh), fh)], b["zu"], C - 1)
        o["gpj"][half_rows, :] = total(b["gp"][r, pl.ds(al(c * ph, ph), ph), :], b["zp"], C - 1)
        fin = [snd("fin", 0, o["gdn"].at[:, half_cols], o["gdn"].at[:, half_cols], core),
               snd("fin", 1, o["gup"].at[:, half_cols], o["gup"].at[:, half_cols], core),
               snd("fin", 2, o["gpj"].at[half_rows, :], o["gpj"].at[half_rows, :], core)]
        run(*fin)
        settle(ec + ur)
        b["e2"][...] = whole(b["e1"][...], b["ez"], C - 1)
        b["u2"][...] = whole(b["u1"][...], b["ur"], R - 1)
        settle(lrw, got=False)
        for k in range(1, R):
            p = peer(k)
            remote(b["l1"], b["lr"].at[p], ss["lrow"].at[0], rs["lrow"].at[p], {"row": p}).wait_recv()
        t = b["lr"][c]
        for q in range(1, S):
            t = t + b["lr"][q * HB + c]
        b["l2"][...] = t
        sd = [snd("ed", 0, b["e2"], b["eo"], core), snd("ud", 0, b["u2"], b["uo"], core), snd("ld", 0, b["l2"], b["lo"], core)]
        run(*sd)
        gqf = snd("gqf", 0, o["gqw"], o["gqw"], core)
        @pl.when(par)
        def _():
            for hp, cp, lc in gq_col:
                pl.when(hp != c)(cp.wait_send)
                pl.when(hp == c)(lc.wait)
                inn = remote(b["gqr"].at[0], b["gqz"].at[hp], ss["gqcol"].at[0], rs["gqcol"].at[hp], {"col": hp})
                pl.when(hp != c)(inn.wait_recv)
            t = b["gqz"][0].astype(F32)
            for q in range(1, C):
                t = t + b["gqz"][q].astype(F32)
            o["gqw"][...] = t
            gqf.start()
        if relay:
            o["gin"][...] = red_x.total()
        elif S == 1:
            settle(pt)
            o["gin"][...] = total(b["part"][own_rows, :], b["pr"], R - 1)
        else:
            settle(pt)
            o["gin"][...] = jnp.zeros((fb, S * SEQ_LEN), F32)
            o["gin"][:, pl.ds(al(a * SEQ_LEN, SEQ_LEN), SEQ_LEN)] = b["part"][own_rows, :].astype(F32)
            for k in range(1, R):
                q = lax.rem(r + R - k, R) // HB
                cols = pl.ds(al(q * SEQ_LEN, SEQ_LEN), SEQ_LEN)
                o["gin"][:, cols] += b["pr"][k - 1].astype(F32)
        leave("gin")
        for cp in sd:
            cp.wait()
        o["sve"][...] = b["e2"][...] + b["eo"][...]
        o["svu"][...] = b["u2"][...] + b["uo"][...]
        o["svl"][...] = b["l2"][...] + b["lo"][...]
        leave("sve", "svu", "svl")
        for cp in fin:
            cp.wait()
        leave("gdn", "gup", "gpj")
        pl.when(par)(gqf.wait_send)
        pl.when(jnp.logical_not(par))(gqf.wait_recv)
        leave("gqw")
        for go, cp in w_out:
            pl.when(go)(cp.wait_send)
        for q in range(R):
            pl.when((q % 2) == d)(w_fwd[q].wait_send)
        pl.when(jnp.logical_not(meta_self))(meta_out.wait_send)
        zU.drain()
        zD.drain()
        zQ.drain()
        zR.drain()
        for cp in leaving:
            cp.wait()

    sem = [pltpu.SemaphoreType.DMA((max(n, 1),)) for n in sems.values()]
    limit = (60 if R == 4 else 62) << 20
    res = pl.pallas_call(
        body,
        out_shape=[struct(*s) for s in outs.values()],
        in_specs=[pl.BlockSpec(memory_space=pl.ANY)] * len(any_in) + [pl.BlockSpec(memory_space=pltpu.VMEM)] * len(vmem_in),
        out_specs=[pl.BlockSpec(memory_space=pl.ANY)] * len(outs),
        scratch_shapes=[pltpu.VMEM(*s) for s in bufs.values()] + sem + sem,
        compiler_params=pltpu.CompilerParams(collective_id=0, has_side_effects=True, vmem_limit_bytes=limit),
        name="encoder_layer",
    )(*[args[n] for n in names_in])
    return dict(zip(outs, res))


def finish_call(nh, fb, fc, qw, res):
    big = ["gin", "gqw", "gup", "gdn", "gpj"]
    shapes = [struct(res[n].shape, F32) for n in big]
    rows = [fb] * 6 + [fc, qw]

    def body(*refs):
        src = refs[:5]
        out_ref, e_ref, u_ref, l_ref = refs[5:9]
        dst = refs[9:14]
        o_ref, t_ref = refs[14:16]
        vecs = refs[16:24]
        sem = refs[24]
        cps = [pltpu.make_async_copy(s, t, sem.at[j]) for j, (s, t) in enumerate(zip(src, dst))]
        run(*cps)
        o_ref[...] = out_ref[...].astype(F32)
        for j in range(6):
            vecs[j][...] = e_ref[j:j + 1, 0:fb]
        vecs[6][...] = u_ref[...]
        vecs[7][...] = l_ref[0:1, 0:qw]
        t_ref[...] = l_ref[1:1 + nh, 0:CONV]
        for cp in cps:
            cp.wait()

    A, V = pl.BlockSpec(memory_space=pl.ANY), pl.BlockSpec(memory_space=pltpu.VMEM)
    outs = shapes + [struct(res["out"].shape, F32), struct((nh, CONV), F32)] + [struct((1, n), F32) for n in rows]
    return pl.pallas_call(
        body, out_shape=outs, in_specs=[V] * 9, out_specs=[A] * 5 + [V] * 10,
        scratch_shapes=[pltpu.SemaphoreType.DMA((5,))], name="outputs",
    )(*[res[n] for n in big], res["out"], res["sve"], res["svu"], res["svl"])


def make_shards(R, C):
    def shards(inputs, doc_ids, qkv_weight, qkv_bias, proj_weight, proj_bias, first_gain, first_shift,
               ffn_up, ffn_up_bias, ffn_down, ffn_down_bias, second_gain, second_shift, conv_kernel, cotangent):
        S = inputs.shape[1] // SEQ_LEN
        fb = inputs.shape[0]
        nh = conv_kernel.shape[0]
        qw = qkv_weight.shape[1]
        fc = ffn_up.shape[1]
        res = layer_call(R, C, S, fb, nh, fc, proj_weight.shape[0], qw, dict(
            x=inputs, cot=cotangent, wq=qkv_weight, wp=proj_weight, wu=ffn_up, wd=ffn_down, doc=doc_ids[None],
            taps=conv_kernel, qb=qkv_bias[None], g1=first_gain[None], s1=first_shift[None], g2=second_gain[None],
            s2=second_shift[None], pb=proj_bias[None], db=ffn_down_bias[None], ub=ffn_up_bias[None]))
        gin, gqw, gup, gdn, gpj, out, taps, g1, b1, g2, pbias, dbias, b2, ubias, qbias = finish_call(nh, fb, fc, qw, res)
        return (out, gin, gqw, qbias.reshape(qw), gpj, pbias.reshape(fb), g1.reshape(fb), b1.reshape(fb), gup,
                ubias.reshape(fc), gdn, dbias.reshape(fb), g2.reshape(fb), b2.reshape(fb), taps)
    return shards


def solution(mesh):
    in_specs = (P("row", ("dp", "col")), P(("dp", "row")), P("row", "col"), P("col"), P("col", "row"), P("row"),
                P("row"), P("row"), P("row", "col"), P("col"), P("row", "col"), P("row"), P("row"), P("row"),
                P("col", None), P("row", ("dp", "col")))
    out_specs = (P("row", ("dp", "col")), P("row", ("dp", "col")), P("row", "col"), P("col"), P("col", "row"), P("row"),
                 P("row"), P("row"), P("row", "col"), P("col"), P("row", "col"), P("row"), P("row"), P("row"),
                 P("col", None))
    fn = make_shards(mesh.shape["row"], mesh.shape["col"])
    return jax.shard_map(fn, mesh=mesh, in_specs=in_specs, out_specs=out_specs, check_vma=False)
```

```python
import functools

import jax
import jax.numpy as jnp
from jax import lax
from jax.experimental import pallas as pl
from jax.experimental.pallas import tpu as pltpu
from jax.sharding import PartitionSpec as P

D = 768
HEAD_DIM = 64
SEQ_LEN = 1024
EPSILON = 1e-05
F32=jnp.float32; BF=jnp.bfloat16
HD=64; SEQ=1024; SEG=16; CONV=33; ITERS=6; L=64
NEG=-1e9

def dg(a,b,ca,cb):
    return lax.dot_general(a,b,(((ca,),(cb,)),((),())),preferred_element_type=F32)
def nn(a,b): return dg(a,b,1,0)
def nt(a,b): return dg(a,b,1,1)
def tn(a,b): return dg(a,b,0,0)
def split(x):
    hi=x.astype(BF); lo=(x-hi.astype(F32)).astype(BF)
    return hi,lo
def cat(hl): return jnp.concatenate(hl,axis=0)
def halves(x):
    n=x.shape[0]//2
    return x[:n]+x[n:]
def nn2(a,b): return halves(nn(cat(split(a)),b))
def nt2(a,b): return halves(nt(cat(split(a)),b))
def nn3(a,b):
    ah,al=split(a); bh,bl=split(b)
    return halves(nn(cat((ah,al)),bh))+nn(ah,bl)
def nt3(a,b):
    ah,al=split(a); bh,bl=split(b)
    return halves(nt(cat((ah,al)),bh))+nt(ah,bl)

def iota(shape,dim): return lax.broadcasted_iota(jnp.int32,shape,dim)
def avg_mat():
    return jnp.where((iota((L,SEQ),1)//SEG)==iota((L,SEQ),0),F32(1.0/SEG),F32(0)).astype(BF)
def pick_mat():
    return jnp.where(iota((L,SEQ),1)==iota((L,SEQ),0)*SEG,F32(1),F32(0)).astype(BF)

def skew(x,left):
    W=x.shape[1]
    j=iota(x.shape,0)
    for bit in range(7):
        m=1<<bit
        x=jnp.where((j&m)!=0,pltpu.roll(x,(W-m) if left else m,1),x)
    return x

def band(w_row):
    return skew(jnp.broadcast_to(pltpu.roll(w_row,128-CONV//2,1),(128,384)),False)

def span(bt):
    return max(bt-1,0),min(bt+2,SEQ//128)

def same_doc(docb_ref,doc_row,bt):
    lo,hi=span(bt)
    col=docb_ref[bt*128:(bt+1)*128,:]
    return jnp.concatenate([col==doc_row[:,n*128:(n+1)*128] for n in range(lo,hi)],axis=1)

def conv_fwd(nh,qkv_ref,docb_ref,doc_row,band_ref,acc_ref):
    for bt in range(SEQ//128):
        lo,hi=span(bt)
        same=same_doc(docb_ref,doc_row,bt)
        off=(lo-bt+1)*128
        for h in range(nh):
            b=h*3*HD+2*HD
            ct=jnp.where(same,band_ref[h,:,off:off+(hi-lo)*128],0.0)
            o=nt(qkv_ref[b:b+HD,lo*128:hi*128],cat(split(ct)))
            acc_ref[h*HD:(h+1)*HD,bt*128:(bt+1)*128]=o[:,:128]+o[:,128:]

def head_scores(h,qkv_ref,doc_row,land_row,land_col,k1_ref,k3_ref,k2_ref,ql_ref,kl_ref,sum_ref):
    b=h*3*HD
    q=qkv_ref[b:b+HD,:]; k=qkv_ref[b+HD:b+2*HD,:]; v=qkv_ref[b+2*HD:b+3*HD,:]
    at=avg_mat()
    ql=nt(at,q); kl=nt(at,k)
    ql_ref[h]=ql; kl_ref[h]=kl
    keep=land_col==doc_row
    s1=jnp.where(keep,nn2(kl,q)*0.125,NEG)
    e1=jnp.exp(s1-jnp.max(s1,axis=0,keepdims=True))
    k1_ref[h]=e1/jnp.sum(e1,axis=0,keepdims=True)
    s3=jnp.where(keep,nn2(ql,k)*0.125,NEG)
    e3=jnp.exp(s3-jnp.max(s3,axis=1,keepdims=True))
    k3=e3/jnp.sum(e3,axis=1,keepdims=True)
    k3_ref[h]=k3
    s2=jnp.where(land_col==land_row,nt3(ql,kl)*0.125,NEG)
    e2=jnp.exp(s2-jnp.max(s2,axis=1,keepdims=True))
    k2_ref[h]=e2/jnp.sum(e2,axis=1,keepdims=True)
    sum_ref[h]=nt2(k3,v)

def eye(): return jnp.where(iota((L,L),0)==iota((L,L),1),F32(1),F32(0))

def newton(nh,k2_ref,v_ref,p_ref,n1_ref,n2_ref,n3_ref):
    for h in range(nh):
        v_ref[0,h]=k2_ref[h].T*(1.0/L)
    def step(i,_):
        I=eye()
        P=[nn3(k2_ref[h],v_ref[i,h]) for h in range(nh)]
        N1=[7.0*I-P[h] for h in range(nh)]
        N2=[15.0*I-nn3(P[h],N1[h]) for h in range(nh)]
        N3=[13.0*I-nn3(P[h],N2[h]) for h in range(nh)]
        for h in range(nh):
            p_ref[i,h]=P[h]; n1_ref[i,h]=N1[h]; n2_ref[i,h]=N2[h]; n3_ref[i,h]=N3[h]
            v_ref[i+1,h]=nn3(0.25*v_ref[i,h],N3[h])
        return 0
    lax.fori_loop(0,ITERS,step,0)

def head_out(h,k1_ref,inv,sum_ref,mix_ref,acc_ref,att_ref):
    mixed=nn3(inv,sum_ref[h])
    mix_ref[h]=mixed
    mt=mixed.T
    k1=k1_ref[h]
    res=nn3(mt,k1)
    att_ref[h*HD:(h+1)*HD,:]=(res+acc_ref[h*HD:(h+1)*HD,:]).astype(BF)

def newton_bwd(nh,k2_ref,v_ref,p_ref,n1_ref,n2_ref,n3_ref,gv_ref,gk_ref):
    for h in range(nh):
        gk_ref[h]=jnp.zeros((L,L),F32)
    def step(j,_):
        i=ITERS-1-j
        H=range(nh)
        gV=[gv_ref[h] for h in H]; V=[v_ref[i,h] for h in H]
        VT=[V[h].T for h in H]; PT=[p_ref[i,h].T for h in H]
        gN3=[0.25*nn3(VT[h],gV[h]) for h in H]
        gVn=[0.25*nt3(gV[h],n3_ref[i,h]) for h in H]
        gN2=[-nn3(PT[h],gN3[h]) for h in H]
        gN1=[-nn3(PT[h],gN2[h]) for h in H]
        gP=[-nt3(gN3[h],n2_ref[i,h])-nt3(gN2[h],n1_ref[i,h])-gN1[h] for h in H]
        for h in H:
            gk_ref[h]+=nt3(gP[h],V[h])
            gv_ref[h]=gVn[h]+nn3(k2_ref[h].T,gP[h])
        return 0
    lax.fori_loop(0,ITERS,step,0)
    for h in range(nh):
        gk_ref[h]+=gv_ref[h].T*(1.0/L)

def conv_bwd(nh,qkv_ref,g_ref,docb_ref,doc_row,band_ref,gacc_ref,gband_ref):
    for bt in range(SEQ//128):
        lo,hi=span(bt)
        same=same_doc(docb_ref,doc_row,bt)
        off=(lo-bt+1)*128
        for h in range(nh):
            b=h*3*HD+2*HD
            lanes=slice(off,off+(hi-lo)*128)
            ct=jnp.where(same,band_ref[h,:,lanes],0.0)
            g=g_ref[h*HD:(h+1)*HD,bt*128:(bt+1)*128]
            gv=nn(jnp.concatenate([g,g],axis=1),cat(split(ct)))
            gb=jnp.where(same,tn(g,qkv_ref[b:b+HD,lo*128:hi*128]),0.0)
            rows=slice(h*HD,(h+1)*HD)
            if bt==0:
                gband_ref[h]=jnp.zeros((128,384),F32)
                gacc_ref[rows,0:256]=gv
            else:
                gacc_ref[rows,lo*128:(bt+1)*128]+=gv[:,:256]
                if hi>bt+1:
                    gacc_ref[rows,(bt+1)*128:hi*128]=gv[:,256:]
            gband_ref[h,:,lanes]+=gb

def tap_row(gband):
    x=skew(gband,True)
    return pltpu.roll(jnp.sum(x,axis=0,keepdims=True),384-(128-CONV//2),1)

def head_bwd1(h,qkv_ref,g_ref,k1_ref,k3_ref,sum_ref,mix_ref,inv,gv_ref,gs1_ref,gs3_ref,gacc_ref):
    b=h*3*HD
    v=qkv_ref[b+2*HD:b+3*HD,:]
    g=g_ref[h*HD:(h+1)*HD,:]
    k1=k1_ref[h]
    gmix=nt2(k1,g)
    gk1=nn2(mix_ref[h],g)
    gs1_ref[h]=k1*(gk1-jnp.sum(k1*gk1,axis=0,keepdims=True))
    gv_ref[h]=nt3(gmix,sum_ref[h])
    gsum=nn3(inv.T,gmix)
    k3=k3_ref[h]
    gk3=nn2(gsum,v)
    gs3_ref[h]=k3*(gk3-jnp.sum(k3*gk3,axis=1,keepdims=True))
    gacc_ref[h*HD:(h+1)*HD,:]+=nn3(gsum.T,k3)

def head_bwd2(h,qkv_ref,k2_ref,gk_ref,ql_ref,kl_ref,gs1_ref,gs3_ref,gacc_ref,out_ref):
    b=h*3*HD
    q=qkv_ref[b:b+HD,:]; k=qkv_ref[b+HD:b+2*HD,:]
    k2=k2_ref[h]; gk2=gk_ref[h]
    gs2=k2*(gk2-jnp.sum(k2*gk2,axis=1,keepdims=True))
    ql=ql_ref[h]; kl=kl_ref[h]
    gs1=gs1_ref[h]; gs3=gs3_ref[h]
    gkl=nt2(gs1,q)+nn3(gs2.T,ql)
    gql=nt2(gs3,k)+nn3(gs2,kl)
    at=avg_mat()
    gq=(nn3(kl.T,gs1)+nn2(gql.T,at))*0.125
    gk=(nn3(ql.T,gs3)+nn2(gkl.T,at))*0.125
    out_ref[b:b+HD,:]=gq.astype(BF)
    out_ref[b+HD:b+2*HD,:]=gk.astype(BF)
    out_ref[b+2*HD:b+3*HD,:]=gacc_ref[h*HD:(h+1)*HD,:].astype(BF)

MESH = pl.DeviceIdType.MESH


def struct(shape, dtype):
    return jax.ShapeDtypeStruct(shape, dtype)


def remote(src, dst, ss, rs, dev):
    return pltpu.make_async_remote_copy(
        src_ref=src, dst_ref=dst, send_sem=ss, recv_sem=rs, device_id=dev, device_id_type=MESH
    )


def run(*copies):
    for cp in copies:
        cp.start()


def settle(cps, sent=True, got=True):
    for cp in cps:
        if sent:
            cp.wait_send()
        if got:
            cp.wait_recv()


def when(cond, fn):
    if cond is None:
        fn()
    else:
        pl.when(cond)(fn)


def al(x, n):
    return pl.multiple_of(x, n)


def gauss(x):
    e = jnp.exp(-0.5 * x * x)
    t = 1.0 / (1.0 + jnp.abs(x) * 0.23164190)
    p = t * 0.5307027145 - 0.7265760135
    p = (p * t + 0.7107068705) * t - 0.1422483680
    q = (p * t + 0.1274147960) * t * e
    return jnp.where(x >= 0, 1.0 - q, q), e * 0.3989422804014327


def norm_forward(residual, gain, shift):
    average = jnp.mean(residual, axis=1, keepdims=True)
    spread = jnp.mean(residual * residual, axis=1, keepdims=True) - average * average
    scaling = lax.rsqrt(spread + EPSILON)
    normed = (residual - average) * scaling
    return normed * gain + shift, normed, scaling


def norm_backward(upstream, gain, normed, scaling):
    scaled = upstream * gain
    mean_scaled = jnp.mean(scaled, axis=1, keepdims=True)
    crossed = jnp.mean(scaled * normed, axis=1, keepdims=True)
    return scaling * (scaled - mean_scaled - normed * crossed)


def tsum(x):
    return jnp.sum(x, axis=0, keepdims=True)


class Pool:
    def __init__(self, entries):
        self.at = entries


class RowGather:
    def __init__(self, snd, group, base, ways, place, r, R, cond=None):
        n = len(ways)
        self.cond, self.n, self.relay, self.ways = cond, n, R == 4, ways
        if self.relay:
            X, Y = lax.bitwise_xor(r, 1), lax.bitwise_xor(r, 2)
            self.own = []
            self.fwd = []
            for j in range(n):
                mine = place(j, r)
                self.own.append((snd(group, base + 2 * j, mine, mine, {"row": X}),
                                 snd(group, base + 2 * j + 1, mine, mine, {"row": Y})))
                src = place(j, Y if ways[j] else X)
                self.fwd.append(snd(group, base + 2 * n + j, src, src, {"row": X if ways[j] else Y}))
        else:
            self.own = [tuple(snd(group, base + j * (R - 1) + k - 1, place(j, r), place(j, r), {"row": lax.rem(r + k, R)})
                              for k in range(1, R)) for j in range(n)]

    def start(self):
        def go():
            if self.relay:
                for j, cps in enumerate(self.own):
                    cps[self.ways[j]].start()
                for j, cps in enumerate(self.own):
                    cps[1 - self.ways[j]].start()
            else:
                for cps in self.own:
                    run(*cps)
        when(self.cond, go)

    def forward(self):
        if self.relay:
            def go():
                for j in range(self.n):
                    self.own[j][self.ways[j]].wait_recv()
                    self.fwd[j].start()
            when(self.cond, go)

    def finish(self):
        def go():
            for j in range(self.n):
                if self.relay:
                    self.own[j][1 - self.ways[j]].wait_recv()
                    self.fwd[j].wait_recv()
                    self.fwd[j].wait_send()
                else:
                    for cp in self.own[j]:
                        cp.wait_recv()
                for cp in self.own[j]:
                    cp.wait_send()
        when(self.cond, go)


class RowReduce:
    def __init__(self, snd, group, block, recv, lanes, r, R):
        self.block, self.recv, self.lanes, self.r, self.R = block, recv, lanes, r, R
        self.relay = R == 4
        n = len(lanes)
        if self.relay:
            X, Y, Z = lax.bitwise_xor(r, 1), lax.bitwise_xor(r, 2), lax.bitwise_xor(r, 3)
            self.one, self.two, self.mids = [], [], []
            for j, ln in enumerate(lanes):
                P, Q = (X, Y) if j == 0 else (Y, X)
                self.one.append([snd(group, 3 * j, block(Z, ln), recv(1, ln), {"row": P}),
                                 snd(group, 3 * j + 1, block(P, ln), recv(0, ln), {"row": P})])
                self.two.append(snd(group, 3 * j + 2, block(Q, ln), recv(2, ln), {"row": Q}))
                self.mids.append(Q)
        else:
            self.all = [snd(group, k - 1, block(lax.rem(r + k, R), None), recv(k - 1, None), {"row": lax.rem(r + k, R)})
                        for k in range(1, R)]

    def start(self):
        if self.relay:
            for cps in self.one:
                cps[0].start()
        else:
            run(*self.all)

    def start_near(self):
        if self.relay:
            for cps in self.one:
                cps[1].start()

    def middle(self):
        if self.relay:
            for j, ln in enumerate(self.lanes):
                self.one[j][0].wait_recv()
                ref = self.block(self.mids[j], ln)
                ref[...] = (ref[...].astype(F32) + self.recv(1, ln)[...].astype(F32)).astype(BF)
                self.two[j].start()

    def total(self):
        if self.relay:
            for cps in self.one:
                settle(cps, got=False)
                cps[1].wait_recv()
            settle(self.two)
            slots = (0, 2)
        else:
            settle(self.all)
            slots = range(self.R - 1)
        t = self.block(self.r, None)[...].astype(F32)
        for k in slots:
            t = t + self.recv(k, None)[...].astype(F32)
        return t

    def finish(self):
        self.block(self.r, None)[...] = self.total().astype(BF)


class LineGather:
    def __init__(self, snd, group, n, place, c, C):
        self.C, self.c, self.n = C, c, n
        m = (C - 1) * n
        self.up = [[snd(group, k * n + j, place(j, c - k), place(j, c - k), {"col": c + 1}) for j in range(n)] for k in range(C - 1)]
        self.dn = [[snd(group, m + k * n + j, place(j, c + k), place(j, c + k), {"col": c - 1}) for j in range(n)] for k in range(C - 1)]

    def up_ok(self, k):
        return (self.c >= k) & (self.c < self.C - 1)

    def dn_ok(self, k):
        return (self.c + k <= self.C - 1) & (self.c > 0)

    def start(self):
        pl.when(self.up_ok(0))(lambda: run(*self.up[0]))
        pl.when(self.dn_ok(0))(lambda: run(*self.dn[0]))

    def step(self, k):
        def got(cps, nxt, ok):
            def go():
                for j in range(self.n):
                    cps[j].wait_recv()
                    if nxt is not None:
                        pl.when(ok)(lambda: nxt[j].start())
            return go
        more = k < self.C - 1
        pl.when(self.c >= k)(got(self.up[k - 1], self.up[k] if more else None, self.up_ok(k) if more else None))
        pl.when(self.c + k <= self.C - 1)(got(self.dn[k - 1], self.dn[k] if more else None, self.dn_ok(k) if more else None))

    def forward(self, k):
        def on(cps, nxt):
            def go():
                for j in range(self.n):
                    cps[j].wait_recv()
                    nxt[j].start()
            return go
        pl.when(self.up_ok(k))(on(self.up[k - 1], self.up[k]))
        pl.when(self.dn_ok(k))(on(self.dn[k - 1], self.dn[k]))

    def land(self):
        for k in range(1, self.C):
            pl.when(self.c == self.C - 1)(lambda: settle(self.up[k - 1], sent=False))
            pl.when(self.c == 0)(lambda: settle(self.dn[k - 1], sent=False))

    def drain(self):
        for k in range(self.C - 1):
            pl.when(self.up_ok(k))(lambda: settle(self.up[k], got=False))
            pl.when(self.dn_ok(k))(lambda: settle(self.dn[k], got=False))


def layer_call(R, C, S, fb, nh, fc, pb, qw, args):
    HB = R // S
    QT = SEQ_LEN // HB
    FF = fc * C
    fh, ph = fc // 2, pb // 2
    fq = fh // 3 // 128 * 128
    fp = fh - fq
    dpw, dqw = fq, fp
    hb = nh * HD
    fbp = -(-fb // 128) * 128
    CH = 256
    FH = FF // 2
    relay = R == 4
    NR = 3 if relay else R - 1
    PT = nh + 1
    V = pltpu.VMEM
    small = (nh, L, L)
    any_in = ["x", "cot", "wq", "wp", "wu", "wd"]
    vmem_in = ["doc", "taps", "g1", "s1", "g2", "s2", "qb", "ub", "pb", "db"]
    names_in = any_in + vmem_in
    outs = dict(
        out=((fb, S * SEQ_LEN), BF), gin=((fb, S * SEQ_LEN), F32), gqw=((fb, qw), F32), gup=((fb, fc), F32),
        gdn=((fb, fc), F32), gpj=((pb, fb), F32), sve=((8, fbp), F32), svu=((1, fc), F32), svl=((PT, D), F32))
    bufs = dict(
        xg=((D, SEQ_LEN), BF), wg=((R, fb, qw), BF), ms=((8, SEQ_LEN), F32), mt=((8, SEQ_LEN), F32),
        rs=((8, fbp), F32), rp=((R, 8, fbp), F32), cs=((8, fc), F32), cp=((C, 8, fc), F32),
        cg=((D, QT), BF), wpf=((R, D, fb), BF), wuf=((D, FF), BF), wdf=((D, FF), BF),
        qkv=((3 * hb, SEQ_LEN), BF), k1=((nh, L, SEQ_LEN), F32), k3=((nh, L, SEQ_LEN), F32), k2=(small, F32),
        ql=(small, F32), kl=(small, F32), sm=(small, F32), mix=(small, F32), nv=((ITERS + 1,) + small, F32),
        np_=((ITERS,) + small, F32), n1=((ITERS,) + small, F32), n2=((ITERS,) + small, F32), n3=((ITERS,) + small, F32),
        docb=((SEQ_LEN, 128), F32), band=((nh, 128, 384), F32), gband=((nh, 128, 384), F32), acc=((hb, SEQ_LEN), F32), att=((hb, SEQ_LEN), BF), attq=((D, QT), BF),
        resT=((D, QT), F32), prow=((8, D), F32), hidden=((QT, D), F32), hid=((QT, D), BF), nm1=((QT, D), F32),
        sc1=((QT, 1), F32), act=((QT, FF), BF), dact=((QT, FF), F32), res2=((QT, D), F32), gdown=((QT, D), BF),
        gpre=((QT, FF), BF), gattoT=((D, QT), BF), outT=((D, QT), BF), gatt=((hb, SEQ_LEN), BF),
        hid_o=((QT, D), BF), gdown_o=((QT, D), BF), gattoT_o=((D, QT), BF), att_o=((C * ph, QT), BF),
        act_o=((QT, C * fh), BF), gpre_o=((QT, C * fh), BF),
        gu=((D, C * fp), BF), guq=((D, C * fq), BF), gd=((D, C * fp), BF), gp=((R, C * ph, fb), BF), gdq=((D, C * fq), BF),
        ru=((NR, fb, C * fp), BF), rd=((NR, fb, C * fp), BF), rpj=((NR, C * ph, fb), BF),
        zu=((C - 1, fb, fp), BF), zd=((C - 1, fb, fp), BF), zp=((C - 1, ph, fb), BF),
        zdq=((C - 1, D, fq), BF), zuq=((C - 1, D, fq), BF), tuq=((D, fq), BF), tdq=((D, fq), BF),
        rdq=((R - 1, fb, fq), BF), ruq=((R - 1, fb, fq), BF),
        gv=(small, F32), gk=(small, F32),
        part=((D, SEQ_LEN), BF), pr=((R - 1, fb, SEQ_LEN), BF),
        gq=((R, fb, qw), BF), gqo=((R // 2, fb, qw), BF), gqr=((R, fb, qw), BF), gqz=((C, fb, qw), BF),
        e0=((8, D), F32), eb=((R, 8, fbp), F32), er=((R - 1, 8, fbp), F32), e1=((8, fbp), F32), ez=((C - 1, 8, fbp), F32),
        e2=((8, fbp), F32), eo=((8, fbp), F32), u0=((C, 1, fc), F32), uz=((C - 1, 1, fc), F32), u1=((1, fc), F32),
        ur=((R - 1, 1, fc), F32), u2=((1, fc), F32), uo=((1, fc), F32), l0=((PT, D), F32), lz=((C - 1, PT, D), F32),
        l1=((PT, D), F32), lr=((R, PT, D), F32), l2=((PT, D), F32), lo=((PT, D), F32))
    NRP = 1 + 2 * (C - 1)
    sems = dict(
        x=2 * (R - 1), cot=R - 1, rowp=R - 1, colp=C - 1, meta=1, ws=S * C, wr=R, wd2=R,
        zU=4 * (C - 1), zD=2 * (C - 1), rU=C * 2 * (R - 1), rD=C * (R - 1), rQ=2 * (R - 1), zQ=2 * (C - 1), zR=2 * (C - 1),
        cU=2 * C, cD=C, cQ=2 * C,
        att=HB - 1, gatt=HB - 1, ex=5 + C, ru=max(6, R - 1), rd=max(6, R - 1), rp=max(3, R - 1), rcol=3 * (C - 1),
        zq=2 * (C - 1), rq=2 * (R - 1), part=max(6, R - 1), outx=R - 1,
        gqd=R // 2, gqrow=R, gqcol=C, gqf=1, erow=R - 1, ecol=C - 1, ed=1, ucol=C - 1, urow=R - 1, ud=1, lcol=C - 1, lrow=R, ld=1, fin=3)
    local = dict(loc=21)

    late_sems = ["ru", "rd", "rp", "rcol", "zq", "rq", "part", "gqd", "gqrow", "gqcol", "gqf", "erow", "ecol", "ed", "ucol",
                 "urow", "ud", "lcol", "lrow", "ld", "fin"]
    first_sems = [g for g in sems if g not in late_sems]

    def body(*refs):
        n = len(names_in)
        i = dict(zip(names_in, refs[:n]))
        o = dict(zip(outs, refs[n:n + len(outs)]))
        k = n + len(outs)
        b = dict(zip(bufs, refs[k:k + len(bufs)]))
        k += len(bufs)
        ss = dict(zip(first_sems + list(local), refs[k:]))
        k += len(first_sems) + len(local)
        rs = dict(zip(sems, refs[k:]))
        free = [ss[g].at[j] for g in ("rU", "rD", "zU", "zD", "zQ", "zR", "cU", "cD", "cQ", "rQ", "x") for j in range(sems[g])]
        for g in late_sems:
            ss[g] = Pool(free[:sems[g]])
            free = free[sems[g]:]
        d = lax.axis_index("dp")
        r = lax.axis_index("row")
        c = lax.axis_index("col")
        a, h = r // HB, lax.rem(r, HB)
        core = {"dp": 1 - d}

        def snd(group, slot, src, dst, dev):
            return remote(src, dst, ss[group].at[slot], rs[group].at[slot], dev)

        def loc(slot, src, dst):
            return pltpu.make_async_copy(src, dst, ss["loc"].at[slot])

        def fr(ref, q):
            return ref.at[pl.ds(al(q * fb, fb), fb), :]

        def peer(k):
            return lax.rem(r + k, R)

        def cpeer(k):
            return lax.rem(c + k, C)

        own = c == h
        bar = pltpu.get_barrier_semaphore()
        for k in range(1, R):
            pl.semaphore_signal(bar, inc=1, device_id={"row": peer(k)}, device_id_type=MESH)
        for k in range(1, C):
            pl.semaphore_signal(bar, inc=1, device_id={"col": cpeer(k)}, device_id_type=MESH)
        pl.semaphore_signal(bar, inc=1, device_id=core, device_id_type=MESH)
        for q in range(R):
            @pl.when(jnp.logical_not(own & (r == q)))
            def _():
                pl.semaphore_signal(bar, inc=1, device_id={"row": q, "col": h}, device_id_type=MESH)
        half = fb // 2

        def xcols(q, part=None):
            rows = slice(None) if part is None else pl.ds(part * half, half)
            return i["x"].at[rows, pl.ds(al(q // HB * SEQ_LEN, SEQ_LEN), SEQ_LEN)]

        x_loc = loc(0, xcols(r), fr(b["xg"], r))
        x_loc.start()

        def cols_of(col, first, width):
            return pl.ds(al(d * (FF // 2) + col * fh + first, 128), width)

        def wide(ref, row, col, first, width):
            return ref.at[pl.ds(al(row * fb, fb), fb), cols_of(col, first, width)]

        def narrow(ref, row, col):
            return ref.at[row, pl.ds(al(col * pb + d * ph, ph), ph), :]

        bulk_loc = [loc(1, i["wu"].at[:, pl.ds(al(d * fh, fh), fh)], wide(b["wuf"], r, c, 0, fh)),
                    loc(2, i["wd"].at[:, pl.ds(al(d * fh, fh), fh)], wide(b["wdf"], r, c, 0, fh)),
                    loc(3, i["wp"].at[pl.ds(al(d * ph, ph), ph), :], narrow(b["wpf"], r, c))]
        run(*bulk_loc)
        cot_rows = min(fb, 64)
        stage = []
        for s in range(S):
            for f in range(0, fb, cot_rows):
                m = len(stage)
                buf = b["k1"].at[m] if m < nh else b["k3"].at[m - nh]
                stage.append((s, f, m, loc(4 + m, i["cot"].at[f:f + cot_rows, s * SEQ_LEN:(s + 1) * SEQ_LEN], buf.at[0:cot_rows, :])))
        run(*[t[3] for t in stage])
        b["ms"][...] = jnp.zeros((8, SEQ_LEN), F32)
        b["ms"][0:1, :] = i["doc"][...].astype(F32)
        b["ms"][1:1 + nh, 0:CONV] = i["taps"][...]
        b["ms"][1 + nh:2 + nh, 0:qw] = i["qb"][...].astype(F32).reshape(1, qw)
        b["rs"][...] = jnp.zeros((8, fbp), F32)
        for j, name in enumerate(("g1", "s1", "g2", "s2")):
            b["rs"][j:j + 1, 0:fb] = i[name][...]
        b["rs"][4:5, 0:fb] = i["pb"][...].astype(F32).reshape(1, fb)
        b["rs"][5:6, 0:fb] = i["db"][...].astype(F32).reshape(1, fb)
        b["cs"][...] = jnp.zeros((8, fc), F32)
        b["cs"][0:1, :] = i["ub"][...].astype(F32).reshape(1, fc)
        for cp in bulk_loc:
            cp.wait()
        x_loc.wait()
        pl.semaphore_wait(bar, R - 1 + C - 1 + 1 + S * C - jnp.where(own, 1, 0))

        dst_row, dst_col = lax.rem(r, S) * HB + c, r // S
        meta_self = (dst_row == r) & (dst_col == c)
        meta_out = snd("meta", 0, b["ms"], b["mt"], {"row": dst_row, "col": dst_col})
        meta_in = snd("meta", 0, b["ms"], b["mt"], {"row": c * S + a, "col": h})
        meta_loc = loc(17, b["ms"], b["mt"])
        pl.when(jnp.logical_not(meta_self))(meta_out.start)
        pl.when(meta_self)(meta_loc.start)

        def place_u(col):
            return lambda j, row: narrow(b["wpf"], row, col) if j else wide(b["wuf"], row, col, 0, fp)

        def place_d(col):
            return lambda j, row: wide(b["wdf"], row, col, 0, dpw)

        zU = LineGather(snd, "zU", 2, lambda j, col: place_u(col)(j, r), c, C)
        zD = LineGather(snd, "zD", 1, lambda j, col: place_d(col)(j, r), c, C)
        at_cols = [(None, c)]
        for k in range(1, C):
            at_cols += [(c >= k, c - k), (c + k <= C - 1, c + k)]
        rU = [RowGather(snd, "rU", col * 2 * (R - 1), (0, 1), place_u(col), r, R, cond) for cond, col in at_cols]
        rD = [RowGather(snd, "rD", col * (R - 1), (1,), place_d(col), r, R, cond) for cond, col in at_cols]
        rQ = RowGather(snd, "rQ", 0, (0, 1), lambda j, row: wide(b["wdf"], row, c, dpw, dqw) if j else wide(b["wuf"], row, c, fp, fq), r, R)
        zQ = LineGather(snd, "zQ", 1, lambda j, col: b["wuf"].at[:, cols_of(col, fp, fq)], c, C)
        zR = LineGather(snd, "zR", 1, lambda j, col: b["wdf"].at[:, cols_of(col, dpw, dqw)], c, C)
        zU.start()
        zD.start()
        if relay:
            xg = RowGather(snd, "x", 0, (0, 1), lambda j, q: b["xg"].at[pl.ds(al(q * fb + j * half, half), half), :], r, R)
            xg.start()
        else:
            xs = [snd("x", k - 1, xcols(peer(k)), fr(b["xg"], r), {"row": peer(k)}) for k in range(1, R)]
            run(*xs)
        par = lax.rem(r, 2) == d
        w_out = []
        for ap in range(S):
            for cq in range(C):
                t = ap * HB + c
                go = par & jnp.logical_not((t == r) & (c == cq))
                cp = remote(i["wq"], b["wg"].at[r], ss["ws"].at[ap * C + cq], rs["wr"].at[r], {"row": t, "col": cq})
                w_out.append((go, cp))
        for go, cp in w_out:
            pl.when(go)(cp.start)
        w_loc = loc(16, i["wq"], b["wg"].at[r])
        pl.when(own & par)(w_loc.start)
        def cot_at(s, cols):
            return b["gpre"].at[pl.ds(al(s // 3 * fb, fb), fb), cols]

        for s, f, m, cp in stage:
            cp.wait()
            buf = b["k1"].at[m] if m < nh else b["k3"].at[m - nh]
            b["gpre"][s // 3 * fb + f:s // 3 * fb + f + cot_rows, s % 3 * SEQ_LEN:(s % 3 + 1) * SEQ_LEN] = buf[0:cot_rows, :].astype(BF)

        def cot_src(q):
            s = q // HB
            return cot_at(s, pl.ds(al(lax.rem(s, 3) * SEQ_LEN + lax.rem(q, HB) * QT, QT), QT))

        zU.step(1)
        if relay:
            xg.forward()
        rQ.start()
        zD.forward(1)
        pl.when(jnp.logical_not(meta_self))(meta_in.wait_recv)
        pl.when(meta_self)(meta_loc.wait)
        doc_row = b["mt"][0:1, :]
        rowb = jnp.broadcast_to(doc_row, (8, SEQ_LEN)).astype(BF)
        pick = pick_mat()
        land_row = nt(rowb, pick)[0:1]
        land_col = nt(pick, rowb)[:, 0:1]
        for hh in range(nh):
            b["band"][hh] = band(b["mt"][1 + hh:2 + hh, 0:384])
        one = jnp.where(iota((8, 128), 0) == 0, 1.0, 0.0).astype(BF)
        b["docb"][...] = tn(rowb, one)
        rQ.forward()
        for k in range(2, C - 1):
            zU.step(k)
            zD.forward(k)
        rQ.finish()
        zQ.start()
        if relay:
            xg.finish()
        else:
            settle(xs)
        for m in range(2 * C - 3):
            rU[m].start()
        gs = [snd("cot", k - 1, cot_src(peer(k)), fr(b["cg"], r), {"row": peer(k)}) for k in range(1, R)]
        g_loc = loc(18, cot_src(r), fr(b["cg"], r))
        ps = [snd("rowp", k - 1, b["rs"], b["rp"].at[r], {"row": peer(k)}) for k in range(1, R)]
        p_loc = loc(19, b["rs"], b["rp"].at[r])
        cs = [snd("colp", k - 1, b["cs"], b["cp"].at[c], {"col": cpeer(k)}) for k in range(1, C)]
        c_loc = loc(20, b["cs"], b["cp"].at[c])
        run(*ps, p_loc, *cs, c_loc)
        w_fwd = [snd("wd2", q, b["wg"].at[q], b["wg"].at[q], core) for q in range(R)]
        for q in range(R):
            mine_q = (q % 2) == d
            here_q = own & (r == q)
            w_in = remote(i["wq"], b["wg"].at[q], ss["ws"].at[0], rs["wr"].at[q], {"row": q, "col": h})
            pl.when(mine_q & here_q)(w_loc.wait)
            pl.when(mine_q & jnp.logical_not(here_q))(w_in.wait_recv)
            pl.when(mine_q)(w_fwd[q].start)
        for q in range(R):
            pl.when((q % 2) != d)(w_fwd[q].wait_recv)
        qb = jnp.where(iota((8, qw), 0) == 1 + nh, b["mt"][:, 0:qw], 0.0).astype(BF)
        acc = tn(qb, jnp.ones((8, SEQ_LEN), BF))
        for q in range(R):
            acc = acc + tn(b["wg"][q], b["xg"][q * fb:(q + 1) * fb, :])
        b["qkv"][...] = acc.astype(BF)

        def scores(hh):
            head_scores(hh, b["qkv"], doc_row, land_row, land_col, b["k1"], b["k3"], b["k2"], b["ql"], b["kl"], b["sm"])

        for hh in range(nh):
            scores(hh)
        zQ.forward(1)
        zR.start()
        zU.step(C - 1)
        for m in range(2 * C - 3, NRP):
            rU[m].start()
        newton(nh, b["k2"], b["nv"], b["np_"], b["n1"], b["n2"], b["n3"])
        for k in range(2, C - 1):
            zQ.forward(k)
        for m in range(3):
            rU[m].forward()
        conv_fwd(nh, b["qkv"], b["docb"], doc_row, b["band"], b["acc"])
        for hh in range(nh):
            head_out(hh, b["k1"], b["nv"][ITERS, hh], b["sm"], b["mix"], b["acc"], b["att"])

        def group(k):
            return lax.rem(h + k, HB)

        def hrows(ref, q):
            return ref.at[pl.ds(al(q * hb, hb), hb), :]

        def tcols(ref, q):
            return ref.at[:, pl.ds(al(q * QT, QT), QT)]

        at = [snd("att", k - 1, tcols(b["att"], group(k)), hrows(b["attq"], h), {"row": a * HB + group(k)})
              for k in range(1, HB)]
        run(*at)
        at_loc = loc(0, tcols(b["att"], h), hrows(b["attq"], h))
        at_loc.start()
        for m in range(3, NRP):
            rU[m].forward()
        zD.land()
        for m in range(NRP):
            rD[m].start()
        zR.forward(1)
        for cp in ps + cs:
            cp.wait()
        for cp in (p_loc, c_loc):
            cp.wait()
        prow = jnp.zeros((8, D), F32)
        for q in range(R):
            piece = jnp.concatenate([b["rp"][q], jnp.zeros((8, D - fbp), F32)], axis=1)
            prow = prow + (pltpu.roll(piece, q * fb, 1) if q else piece)
        b["prow"][...] = prow
        def cross(group, slot, cond, *refs):
            cps = [snd(group, slot + j, ref, ref, core) for j, ref in enumerate(refs)]
            when(cond, lambda: run(*cps))
            return cond, cps

        crossed, later = [], []
        for m, (cond, col) in enumerate(at_cols):
            rU[m].finish()
            crossed.append(cross("cU", 2 * col, cond, b["wuf"].at[:, cols_of(col, 0, fp)],
                                 b["wpf"].at[:, pl.ds(al(col * pb + d * ph, ph), ph), :]))
        zQ.land()
        for m, (cond, col) in enumerate(at_cols):
            crossed.append(cross("cQ", 2 * col, cond, b["wuf"].at[:, cols_of(col, fp, fq)]))
        settle(at)
        at_loc.wait()
        for cond, cps in crossed:
            when(cond, lambda: settle(cps))

        for q in range(R):
            t = tn(b["wpf"][q], b["attq"][...])
            b["resT"][q * fb:(q + 1) * fb, :] = t + b["xg"][q * fb:(q + 1) * fb, pl.ds(al(h * QT, QT), QT)].astype(F32)
        res1 = b["resT"][...].T + b["prow"][4:5, :]
        hidden, nm1, sc1 = norm_forward(res1, b["prow"][0:1, :], b["prow"][1:2, :])
        b["hidden"][...] = hidden
        b["nm1"][...] = nm1
        b["sc1"][...] = sc1
        b["hid"][...] = hidden.astype(BF)
        ex_hid = snd("ex", 0, b["hid"], b["hid_o"], core)
        ex_hid.start()

        def up(j, _):
            cols = pl.ds(al(j * fh, 128), fh)
            bias = b["cp"][lax.rem(j, C), 0:1, pl.ds(al(j // C * fh, 128), fh)]
            pre = nn(b["hid"][...], b["wuf"][:, cols]) + bias
            cdf, pdf = gauss(pre)
            b["act"][:, cols] = (pre * cdf).astype(BF)
            b["dact"][:, cols] = cdf + pre * pdf
            return 0

        lax.fori_loop(0, C, up, 0)
        for m in range(2 * C - 3):
            rD[m].forward()
        for k in range(2, C - 1):
            zR.forward(k)
        lax.fori_loop(C, 2 * C, up, 0)
        for m in range(2 * C - 3, NRP):
            rD[m].forward()
        run(*gs, g_loc)
        zR.land()
        for m, (cond, col) in enumerate(at_cols):
            later.append(cross("cQ", 2 * col + 1, cond, b["wdf"].at[:, cols_of(col, dpw, dqw)]))
        other_half = pl.ds(al((1 - d) * FH, 128), FH)
        ex_act = [snd("ex", 3, b["act"].at[:, other_half], b["act_o"], core)]
        run(*ex_act)
        for m, (cond, col) in enumerate(at_cols):
            rD[m].finish()
            later.append(cross("cD", col, cond, b["wdf"].at[:, cols_of(col, 0, dpw)]))
        for cond, cps in later:
            when(cond, lambda: settle(cps))
        for line in (zU, zD, zQ, zR):
            line.drain()

        def down(j, _):
            cols = pl.ds(al(j * CH, CH), CH)
            b["res2"][:, cols] = b["hidden"][:, cols] + nt(b["act"][...], b["wdf"][cols, :]) + b["prow"][5:6, cols]
            return 0

        lax.fori_loop(0, D // CH, down, 0)
        gain2 = b["prow"][2:3, :]
        out, nm2, sc2 = norm_forward(b["res2"][...], gain2, b["prow"][3:4, :])
        settle(gs)
        g_loc.wait()
        ups = b["cg"][...].astype(F32).T
        e0 = b["e0"]
        e0[...] = jnp.zeros((8, D), F32)
        e0[2:3, :] = tsum(ups * nm2)
        e0[5:6, :] = tsum(ups)
        gres2 = norm_backward(ups, gain2, nm2, sc2)
        b["res2"][...] = gres2
        b["gdown"][...] = gres2.astype(BF)
        e0[4:5, :] = tsum(b["gdown"][...].astype(F32))
        ex_gdown = snd("ex", 1, b["gdown"], b["gdown_o"], core)
        ex_gdown.start()
        b["outT"][...] = out.T.astype(BF)
        ox = [snd("outx", k - 1, fr(b["outT"], peer(k)), tcols(o["out"], a * HB + h), {"row": peer(k)}) for k in range(1, R)]
        o_loc = loc(1, fr(b["outT"], r), tcols(o["out"], a * HB + h))
        run(*ox, o_loc)

        def gact(j, _):
            cols = pl.ds(al(j * fh, 128), fh)
            g = nn(b["gdown"][...], b["wdf"][:, cols])
            gp = (g * b["dact"][:, cols]).astype(BF)
            b["gpre"][:, cols] = gp
            b["u0"][lax.rem(j, C), 0:1, pl.ds(al(j // C * fh, 128), fh)] = tsum(gp.astype(F32))
            return 0

        lax.fori_loop(0, 2 * C, gact, 0)
        ex_gpre = [snd("ex", 4, b["gpre"].at[:, other_half], b["gpre_o"], core)]
        run(*ex_gpre)
        def grad_block(q, mine, mine_w, other, other_w, dst, dst_q):
            to = slice(q * fh, (q + 1) * fh)
            t = tn(b[mine][...], b[mine_w][:, cols_of(q, 0, fh)]) + tn(b[other][...], b[other_w][:, to])
            b[dst][:, q * fp:(q + 1) * fp] = t[:, :fp].astype(BF)
            b[dst_q][:, q * fq:(q + 1) * fq] = t[:, fp:].astype(BF)

        def scatter_q(base, src, dst):
            cps = [snd("zq", base + k - 1, src.at[:, pl.ds(al(cpeer(k) * fq, fq), fq)], dst.at[k - 1], {"col": cpeer(k)})
                   for k in range(1, C)]
            run(*cps)
            return cps

        def block_of(ref):
            return lambda q, ln: ref.at[pl.ds(al(q * fb, fb), fb), slice(None) if ln is None else ln]

        def recv_of(ref):
            return lambda k, ln: ref.at[k, :, slice(None) if ln is None else ln]

        settle(ex_act)
        settle([ex_gdown])
        for q in range(C):
            grad_block(q, "gdown", "act", "gdown_o", "act_o", "gd", "gdq")

        def lanes(n):
            return slice(0, n // 2), slice(n // 2, n)

        red_d = RowReduce(snd, "rd", block_of(b["gd"]), recv_of(b["rd"]), lanes(C * fp), r, R)
        red_d.start()
        zqd = scatter_q(0, b["gdq"], b["zdq"])

        def ghid_step(j, _):
            cols = pl.ds(al(j * CH, CH), CH)
            b["hidden"][:, cols] = b["res2"][:, cols] + nt(b["gpre"][...], b["wuf"][cols, :])
            return 0

        lax.fori_loop(0, D // CH, ghid_step, 0)
        ghid = b["hidden"][...]
        nm1 = b["nm1"][...]
        e0[0:1, :] = tsum(ghid * nm1)
        e0[1:2, :] = tsum(ghid)
        gres1 = norm_backward(ghid, b["prow"][0:1, :], nm1, b["sc1"][...])
        e0[3:4, :] = tsum(gres1.astype(BF).astype(F32))
        b["resT"][...] = gres1.T
        b["gattoT"][...] = b["resT"][...].astype(BF)
        ga = jnp.zeros((D, QT), F32)
        for q in range(R):
            ga = ga + nn(b["wpf"][q], b["gattoT"][q * fb:(q + 1) * fb, :])
        b["cg"][...] = ga.astype(BF)
        gt = [snd("gatt", k - 1, hrows(b["cg"], group(k)), tcols(b["gatt"], h), {"row": a * HB + group(k)})
              for k in range(1, HB)]
        run(*gt)
        gt_loc = loc(2, hrows(b["cg"], h), tcols(b["gatt"], h))
        gt_loc.start()
        red_d.start_near()
        b["eb"][...] = jnp.zeros((R, 8, fbp), F32)
        for q in range(R):
            b["eb"][q, :, 0:fb] = e0[:, q * fb:(q + 1) * fb]
        er = [snd("erow", k - 1, b["eb"].at[peer(k)], b["er"].at[k - 1], {"row": peer(k)}) for k in range(1, R)]
        uc = [snd("ucol", k - 1, b["u0"].at[cpeer(k)], b["uz"].at[k - 1], {"col": cpeer(k)}) for k in range(1, C)]
        run(*er, *uc)
        ex_att = [snd("ex", 2, b["gattoT"], b["gattoT_o"], core)] + [
            snd("ex", 5 + q, b["attq"].at[pl.ds(al(q * pb + (1 - d) * ph, ph), ph), :],
                b["att_o"].at[q * ph:(q + 1) * ph, :], core) for q in range(C)]
        run(*ex_att)
        settle([ex_hid])
        settle(ex_gpre)
        for q in range(C):
            grad_block(q, "hid", "gpre", "hid_o", "gpre_o", "gu", "guq")
        zqu = scatter_q(C - 1, b["guq"], b["zuq"])
        own_rows = pl.ds(al(r * fb, fb), fb)
        red_u = RowReduce(snd, "ru", block_of(b["gu"]), recv_of(b["ru"]), lanes(C * fp), r, R)
        settle(ex_att)
        for q in range(C):
            rows = pl.ds(al(q * pb + d * ph, ph), ph)
            tp = slice(q * ph, (q + 1) * ph)
            for p in range(R):
                f = slice(p * fb, (p + 1) * fb)
                b["gp"][p, tp, :] = (nt(b["attq"][rows, :], b["gattoT"][f, :])
                                     + nt(b["att_o"][tp, :], b["gattoT_o"][f, :])).astype(BF)
        red_p = RowReduce(snd, "rp", lambda q, ln: b["gp"].at[q], lambda k, ln: b["rpj"].at[k], (None,), r, R)
        red_p.start()
        red_p.start_near()
        red_u.start()
        def total(own_part, buf, m):
            t = own_part.astype(F32)
            for k in range(m):
                t = t + buf[k].astype(F32)
            return t

        def scatter_p(slot, src_of, dst):
            cps = [snd("rcol", slot * (C - 1) + k - 1, src_of(cpeer(k)), dst.at[k - 1], {"col": cpeer(k)}) for k in range(1, C)]
            run(*cps)
            return cps

        def pcol(ref, n):
            return lambda q: ref.at[own_rows, pl.ds(al(q * n, n), n)]

        qcols = pl.ds(al(c * fq, fq), fq)

        def whole(first, buf, m):
            for k in range(m):
                first = first + buf[k]
            return first

        settle(gt)
        gt_loc.wait()
        conv_bwd(nh, b["qkv"], b["gatt"], b["docb"], doc_row, b["band"], b["acc"], b["gband"])
        for hh in range(nh):
            head_bwd1(hh, b["qkv"], b["gatt"], b["k1"], b["k3"], b["sm"], b["mix"], b["nv"][ITERS, hh], b["gv"], b["k1"], b["k3"], b["acc"])
        red_d.middle()
        newton_bwd(nh, b["k2"], b["nv"], b["np_"], b["n1"], b["n2"], b["n3"], b["gv"], b["gk"])
        red_u.start_near()
        red_p.middle()
        for hh in range(nh):
            head_bwd2(hh, b["qkv"], b["k2"], b["gk"], b["ql"], b["kl"], b["k1"], b["k3"], b["acc"], b["qkv"])

        for q in range(R):
            b["gq"][q] = nt(b["xg"][q * fb:(q + 1) * fb, :], b["qkv"][...]).astype(BF)
        gqd = [snd("gqd", j, b["gq"].at[2 * j + 1 - d], b["gqo"].at[j], core) for j in range(R // 2)]
        run(*gqd)
        settle(gqd)
        gq_out = []
        for j in range(R // 2):
            b["gq"][2 * j + d] = (b["gq"][2 * j + d].astype(F32) + b["gqo"][j].astype(F32)).astype(BF)
            q = 2 * j + d
            cp = remote(b["gq"].at[q], b["gqr"].at[r], ss["gqrow"].at[j], rs["gqrow"].at[r], {"row": q})
            lc = loc(3, b["gq"].at[q], b["gqr"].at[r])
            gq_out.append((q, cp, lc))
            pl.when(q != r)(cp.start)
            pl.when(q == r)(lc.start)
        l0 = b["l0"]
        l0[...] = jnp.zeros((PT, D), F32)
        l0[0:1, 0:qw] = nt(jnp.ones((8, SEQ_LEN), BF), b["qkv"][...])[0:1]
        for hh in range(nh):
            l0[1 + hh:2 + hh, 0:384] = tap_row(b["gband"][hh])
        lcl = [snd("lcol", k - 1, l0, b["lz"].at[k - 1], {"col": cpeer(k)}) for k in range(1, C)]
        run(*lcl)
        red_u.middle()
        for q in range(R):
            f = slice(q * fb, (q + 1) * fb)
            b["part"][f, :] = nn(b["wg"][q], b["qkv"][...]).astype(BF)
            mine_cols = pl.ds(al(h * QT, QT), QT)
            b["part"][f, mine_cols] = (nn(b["wg"][q], b["qkv"][:, mine_cols]) + b["resT"][f, :]).astype(BF)
        red_x = RowReduce(snd, "part", block_of(b["part"]), recv_of(b["pr"]), lanes(SEQ_LEN), r, R)
        if relay:
            red_x.start()
            red_x.start_near()
        else:
            pt = [snd("part", k - 1, fr(b["part"], peer(k)), b["pr"].at[k - 1], {"row": peer(k)}) for k in range(1, R)]
            run(*pt)

        red_d.finish()
        rcd = scatter_p(0, pcol(b["gd"], fp), b["zd"])

        def second_q(base, cps, src, buf, mid, dst):
            settle(cps)
            b[mid][...] = total(b[src][:, qcols], b[buf], C - 1).astype(BF)
            out = [snd("rq", base + k - 1, fr(b[mid], peer(k)), b[dst].at[k - 1], {"row": peer(k)}) for k in range(1, R)]
            run(*out)
            return out

        rqd = second_q(0, zqd, "gdq", "zdq", "tdq", "rdq")
        rqu = second_q(R - 1, zqu, "guq", "zuq", "tuq", "ruq")
        gq_col = []
        for hp in range(HB):
            cp = remote(b["gqr"].at[hp], b["gqz"].at[c], ss["gqcol"].at[hp], rs["gqcol"].at[c], {"col": hp})
            lc = loc(4, b["gqr"].at[hp], b["gqz"].at[c])
            gq_col.append((hp, cp, lc))
        @pl.when(par)
        def _():
            for q in range(R):
                cp = remote(b["gq"].at[0], b["gqr"].at[q], ss["gqrow"].at[0], rs["gqrow"].at[q], {"row": q})
                pl.when(q != r)(cp.wait_recv)
        for q, cp, lc in gq_out:
            pl.when(q != r)(cp.wait_send)
            pl.when(q == r)(lc.wait)
        @pl.when(par)
        def _():
            for ap in range(1, S):
                for hp in range(HB):
                    b["gqr"][hp] = (b["gqr"][hp].astype(F32) + b["gqr"][ap * HB + hp].astype(F32)).astype(BF)
            for hp, cp, lc in gq_col:
                pl.when(hp != c)(cp.start)
                pl.when(hp == c)(lc.start)
        settle(lcl)
        b["l1"][...] = whole(l0[...], b["lz"], C - 1)
        lrw = [remote(b["l1"], b["lr"].at[r], ss["lrow"].at[k - 1], rs["lrow"].at[r], {"row": peer(k)}) for k in range(1, R)]
        run(*lrw)
        b["lr"][r] = b["l1"][...]
        settle(er + uc)
        b["e1"][...] = whole(b["eb"][r], b["er"], R - 1)
        b["u1"][...] = whole(b["u0"][c], b["uz"], C - 1)
        ec = [snd("ecol", k - 1, b["e1"], b["ez"].at[k - 1], {"col": cpeer(k)}) for k in range(1, C)]
        ur = [snd("urow", k - 1, b["u1"], b["ur"].at[k - 1], {"row": peer(k)}) for k in range(1, R)]
        run(*ec, *ur)
        red_u.finish()
        rcu = scatter_p(1, pcol(b["gu"], fp), b["zu"])
        red_p.finish()
        rcp = scatter_p(2, lambda q: b["gp"].at[r, pl.ds(al(q * ph, ph), ph), :], b["zp"])

        red_x.middle()
        half_rows, half_cols = pl.ds(al(d * ph, ph), ph), pl.ds(al(d * fh, fh), fh)
        pcols, qcols2 = pl.ds(al(d * fh, 128), fp), pl.ds(al(d * fh + fp, 128), fq)
        settle(ox)
        o_loc.wait()
        settle(rqd + rqu)
        o["gdn"][:, qcols2] = total(b["tdq"][own_rows, :], b["rdq"], R - 1)
        o["gup"][:, qcols2] = total(b["tuq"][own_rows, :], b["ruq"], R - 1)
        settle(rcd + rcu + rcp)
        mycols = pl.ds(al(c * fp, fp), fp)
        o["gdn"][:, pcols] = total(b["gd"][own_rows, mycols], b["zd"], C - 1)
        o["gup"][:, pcols] = total(b["gu"][own_rows, mycols], b["zu"], C - 1)
        o["gpj"][half_rows, :] = total(b["gp"][r, pl.ds(al(c * ph, ph), ph), :], b["zp"], C - 1)
        fin = [snd("fin", 0, o["gdn"].at[:, half_cols], o["gdn"].at[:, half_cols], core),
               snd("fin", 1, o["gup"].at[:, half_cols], o["gup"].at[:, half_cols], core),
               snd("fin", 2, o["gpj"].at[half_rows, :], o["gpj"].at[half_rows, :], core)]
        run(*fin)
        settle(ec + ur)
        b["e2"][...] = whole(b["e1"][...], b["ez"], C - 1)
        b["u2"][...] = whole(b["u1"][...], b["ur"], R - 1)
        settle(lrw, got=False)
        for k in range(1, R):
            p = peer(k)
            remote(b["l1"], b["lr"].at[p], ss["lrow"].at[0], rs["lrow"].at[p], {"row": p}).wait_recv()
        t = b["lr"][c]
        for q in range(1, S):
            t = t + b["lr"][q * HB + c]
        b["l2"][...] = t
        sd = [snd("ed", 0, b["e2"], b["eo"], core), snd("ud", 0, b["u2"], b["uo"], core), snd("ld", 0, b["l2"], b["lo"], core)]
        run(*sd)
        gqf = snd("gqf", 0, o["gqw"], o["gqw"], core)
        @pl.when(par)
        def _():
            for hp, cp, lc in gq_col:
                pl.when(hp != c)(cp.wait_send)
                pl.when(hp == c)(lc.wait)
                inn = remote(b["gqr"].at[0], b["gqz"].at[hp], ss["gqcol"].at[0], rs["gqcol"].at[hp], {"col": hp})
                pl.when(hp != c)(inn.wait_recv)
            t = b["gqz"][0].astype(F32)
            for q in range(1, C):
                t = t + b["gqz"][q].astype(F32)
            o["gqw"][...] = t
            gqf.start()
        if relay:
            o["gin"][...] = red_x.total()
        elif S == 1:
            settle(pt)
            o["gin"][...] = total(b["part"][own_rows, :], b["pr"], R - 1)
        else:
            settle(pt)
            o["gin"][...] = jnp.zeros((fb, S * SEQ_LEN), F32)
            o["gin"][:, pl.ds(al(a * SEQ_LEN, SEQ_LEN), SEQ_LEN)] = b["part"][own_rows, :].astype(F32)
            for k in range(1, R):
                q = lax.rem(r + R - k, R) // HB
                cols = pl.ds(al(q * SEQ_LEN, SEQ_LEN), SEQ_LEN)
                o["gin"][:, cols] += b["pr"][k - 1].astype(F32)
        for cp in sd:
            cp.wait()
        o["sve"][...] = b["e2"][...] + b["eo"][...]
        o["svu"][...] = b["u2"][...] + b["uo"][...]
        o["svl"][...] = b["l2"][...] + b["lo"][...]
        for cp in fin:
            cp.wait()
        pl.when(par)(gqf.wait_send)
        pl.when(jnp.logical_not(par))(gqf.wait_recv)
        for go, cp in w_out:
            pl.when(go)(cp.wait_send)
        for q in range(R):
            pl.when((q % 2) == d)(w_fwd[q].wait_send)
        pl.when(jnp.logical_not(meta_self))(meta_out.wait_send)

    def dma(n):
        return pltpu.SemaphoreType.DMA((n,))

    sem = [dma(sems[g]) for g in first_sems] + [dma(n) for n in local.values()] + [dma(n) for n in sems.values()]
    limit = (58 if R == 4 else 60) << 20
    res = pl.pallas_call(
        body,
        out_shape=[pltpu.VMEM(*s) for s in outs.values()],
        in_specs=[pl.BlockSpec(memory_space=pl.ANY)] * len(any_in) + [pl.BlockSpec(memory_space=pltpu.VMEM)] * len(vmem_in),
        out_specs=[pl.BlockSpec(memory_space=pltpu.VMEM)] * len(outs),
        scratch_shapes=[pltpu.VMEM(*s) for s in bufs.values()] + sem,
        compiler_params=pltpu.CompilerParams(collective_id=0, has_side_effects=True, vmem_limit_bytes=limit),
        name="encoder_layer",
    )(*[args[n] for n in names_in])
    return dict(zip(outs, res))


def finish_call(nh, fb, fc, qw, res):
    big = ["gin", "gqw", "gup", "gdn", "gpj"]
    shapes = [struct(res[n].shape, F32) for n in big]
    rows = [fb] * 6 + [fc, qw]

    def body(*refs):
        src = refs[:5]
        out_ref, e_ref, u_ref, l_ref = refs[5:9]
        dst = refs[9:14]
        o_ref, t_ref = refs[14:16]
        vecs = refs[16:24]
        sem = refs[24]
        cps = [pltpu.make_async_copy(s, t, sem.at[j]) for j, (s, t) in enumerate(zip(src, dst))]
        run(*cps)
        o_ref[...] = out_ref[...].astype(F32)
        for j in range(6):
            vecs[j][...] = e_ref[j:j + 1, 0:fb]
        vecs[6][...] = u_ref[0, :]
        vecs[7][...] = l_ref[0, 0:qw]
        t_ref[...] = l_ref[1:1 + nh, 0:CONV]
        for cp in cps:
            cp.wait()

    A, V = pl.BlockSpec(memory_space=pl.ANY), pl.BlockSpec(memory_space=pltpu.VMEM)
    outs = shapes + [struct(res["out"].shape, F32), struct((nh, CONV), F32)] + [struct((1, n), F32) for n in rows[:6]] + [struct((n,), F32) for n in rows[6:]]
    return pl.pallas_call(
        body, out_shape=outs, in_specs=[V] * 9, out_specs=[A] * 5 + [V] * 10,
        scratch_shapes=[pltpu.SemaphoreType.DMA((5,))], name="outputs",
    )(*[pltpu.with_memory_space_constraint(res[n], pltpu.VMEM) for n in big + ["out", "sve", "svu", "svl"]])


def make_shards(R, C):
    def shards(inputs, doc_ids, qkv_weight, qkv_bias, proj_weight, proj_bias, first_gain, first_shift,
               ffn_up, ffn_up_bias, ffn_down, ffn_down_bias, second_gain, second_shift, conv_kernel, cotangent):
        S = inputs.shape[1] // SEQ_LEN
        fb = inputs.shape[0]
        nh = conv_kernel.shape[0]
        qw = qkv_weight.shape[1]
        fc = ffn_up.shape[1]
        res = layer_call(R, C, S, fb, nh, fc, proj_weight.shape[0], qw, dict(
            x=inputs, cot=cotangent, wq=qkv_weight, wp=proj_weight, wu=ffn_up, wd=ffn_down, doc=doc_ids[None],
            taps=conv_kernel, g1=first_gain[None], s1=first_shift[None], g2=second_gain[None], s2=second_shift[None],
            qb=qkv_bias, ub=ffn_up_bias, pb=proj_bias, db=ffn_down_bias))
        gin, gqw, gup, gdn, gpj, out, taps, g1, b1, g2, pbias, dbias, b2, ubias, qbias = finish_call(nh, fb, fc, qw, res)
        return (out, gin, gqw, qbias, gpj, pbias.reshape(fb), g1.reshape(fb), b1.reshape(fb), gup,
                ubias, gdn, dbias.reshape(fb), g2.reshape(fb), b2.reshape(fb), taps)
    return shards


def solution(mesh):
    in_specs = (P("row", ("dp", "col")), P(("dp", "row")), P("row", "col"), P("col"), P("col", "row"), P("row"),
                P("row"), P("row"), P("row", "col"), P("col"), P("row", "col"), P("row"), P("row"), P("row"),
                P("col", None), P("row", ("dp", "col")))
    out_specs = (P("row", ("dp", "col")), P("row", ("dp", "col")), P("row", "col"), P("col"), P("col", "row"), P("row"),
                 P("row"), P("row"), P("row", "col"), P("col"), P("row", "col"), P("row"), P("row"), P("row"),
                 P("col", None))
    fn = make_shards(mesh.shape["row"], mesh.shape["col"])
    return jax.shard_map(fn, mesh=mesh, in_specs=in_specs, out_specs=out_specs, check_vma=False)
```

```python
import functools

import jax
import jax.numpy as jnp
from jax import lax
from jax.experimental import pallas as pl
from jax.experimental.pallas import tpu as pltpu
from jax.sharding import PartitionSpec as P

D = 768
HEAD_DIM = 64
SEQ_LEN = 1024
EPSILON = 1e-05
F32=jnp.float32; BF=jnp.bfloat16
HD=64; SEQ=1024; SEG=16; CONV=33; ITERS=6; L=64
NEG=-1e9

def dg(a,b,ca,cb):
    return lax.dot_general(a,b,(((ca,),(cb,)),((),())),preferred_element_type=F32)
def nn(a,b): return dg(a,b,1,0)
def nt(a,b): return dg(a,b,1,1)
def tn(a,b): return dg(a,b,0,0)
def split(x):
    hi=x.astype(BF); lo=(x-hi.astype(F32)).astype(BF)
    return hi,lo
def cat(hl): return jnp.concatenate(hl,axis=0)
def halves(x):
    n=x.shape[0]//2
    return x[:n]+x[n:]
def nn2(a,b): return halves(nn(cat(split(a)),b))
def nt2(a,b): return halves(nt(cat(split(a)),b))
def nn3(a,b):
    ah,al=split(a); bh,bl=split(b)
    return halves(nn(cat((ah,al)),bh))+nn(ah,bl)
def nt3(a,b):
    ah,al=split(a); bh,bl=split(b)
    return halves(nt(cat((ah,al)),bh))+nt(ah,bl)

def iota(shape,dim): return lax.broadcasted_iota(jnp.int32,shape,dim)
def avg_mat():
    return jnp.where((iota((L,SEQ),1)//SEG)==iota((L,SEQ),0),F32(1.0/SEG),F32(0)).astype(BF)
def pick_mat():
    return jnp.where(iota((L,SEQ),1)==iota((L,SEQ),0)*SEG,F32(1),F32(0)).astype(BF)

def skew(x,left):
    W=x.shape[1]
    j=iota(x.shape,0)
    for bit in range(7):
        m=1<<bit
        x=jnp.where((j&m)!=0,pltpu.roll(x,(W-m) if left else m,1),x)
    return x

def band(w_row):
    return skew(jnp.broadcast_to(pltpu.roll(w_row,128-CONV//2,1),(128,384)),False)

def span(bt):
    return max(bt-1,0),min(bt+2,SEQ//128)

def same_doc(docb_ref,doc_row,bt):
    lo,hi=span(bt)
    col=docb_ref[bt*128:(bt+1)*128,:]
    return jnp.concatenate([col==doc_row[:,n*128:(n+1)*128] for n in range(lo,hi)],axis=1)

def conv_fwd(nh,qkv_ref,docb_ref,doc_row,band_ref,acc_ref):
    for bt in range(SEQ//128):
        lo,hi=span(bt)
        same=same_doc(docb_ref,doc_row,bt)
        off=(lo-bt+1)*128
        for h in range(nh):
            b=h*3*HD+2*HD
            ct=jnp.where(same,band_ref[h,:,off:off+(hi-lo)*128],0.0)
            o=nt(qkv_ref[b:b+HD,lo*128:hi*128],cat(split(ct)))
            acc_ref[h*HD:(h+1)*HD,bt*128:(bt+1)*128]=o[:,:128]+o[:,128:]

def head_scores(h,qkv_ref,doc_row,land_row,land_col,k1_ref,k3_ref,k2_ref,ql_ref,kl_ref,sum_ref):
    b=h*3*HD
    q=qkv_ref[b:b+HD,:]; k=qkv_ref[b+HD:b+2*HD,:]; v=qkv_ref[b+2*HD:b+3*HD,:]
    at=avg_mat()
    ql=nt(at,q); kl=nt(at,k)
    ql_ref[h]=ql; kl_ref[h]=kl
    keep=land_col==doc_row
    s1=jnp.where(keep,nn2(kl,q)*0.125,NEG)
    e1=jnp.exp(s1-jnp.max(s1,axis=0,keepdims=True))
    k1_ref[h]=e1/jnp.sum(e1,axis=0,keepdims=True)
    s3=jnp.where(keep,nn2(ql,k)*0.125,NEG)
    e3=jnp.exp(s3-jnp.max(s3,axis=1,keepdims=True))
    k3=e3/jnp.sum(e3,axis=1,keepdims=True)
    k3_ref[h]=k3
    s2=jnp.where(land_col==land_row,nt3(ql,kl)*0.125,NEG)
    e2=jnp.exp(s2-jnp.max(s2,axis=1,keepdims=True))
    k2_ref[h]=e2/jnp.sum(e2,axis=1,keepdims=True)
    sum_ref[h]=nt2(k3,v)

def eye(): return jnp.where(iota((L,L),0)==iota((L,L),1),F32(1),F32(0))

def newton(nh,k2_ref,v_ref,p_ref,n1_ref,n2_ref,n3_ref):
    for h in range(nh):
        v_ref[0,h]=k2_ref[h].T*(1.0/L)
    def step(i,_):
        I=eye()
        P=[nn3(k2_ref[h],v_ref[i,h]) for h in range(nh)]
        N1=[7.0*I-P[h] for h in range(nh)]
        N2=[15.0*I-nn3(P[h],N1[h]) for h in range(nh)]
        N3=[13.0*I-nn3(P[h],N2[h]) for h in range(nh)]
        for h in range(nh):
            p_ref[i,h]=P[h]; n1_ref[i,h]=N1[h]; n2_ref[i,h]=N2[h]; n3_ref[i,h]=N3[h]
            v_ref[i+1,h]=nn3(0.25*v_ref[i,h],N3[h])
        return 0
    lax.fori_loop(0,ITERS,step,0)

def head_out(h,k1_ref,inv,sum_ref,mix_ref,acc_ref,att_ref):
    mixed=nn3(inv,sum_ref[h])
    mix_ref[h]=mixed
    mt=mixed.T
    k1=k1_ref[h]
    res=nn3(mt,k1)
    att_ref[h*HD:(h+1)*HD,:]=(res+acc_ref[h*HD:(h+1)*HD,:]).astype(BF)

def newton_bwd(nh,k2_ref,v_ref,p_ref,n1_ref,n2_ref,n3_ref,gv_ref,gk_ref):
    for h in range(nh):
        gk_ref[h]=jnp.zeros((L,L),F32)
    def step(j,_):
        i=ITERS-1-j
        H=range(nh)
        gV=[gv_ref[h] for h in H]; V=[v_ref[i,h] for h in H]
        VT=[V[h].T for h in H]; PT=[p_ref[i,h].T for h in H]
        gN3=[0.25*nn3(VT[h],gV[h]) for h in H]
        gVn=[0.25*nt3(gV[h],n3_ref[i,h]) for h in H]
        gN2=[-nn3(PT[h],gN3[h]) for h in H]
        gN1=[-nn3(PT[h],gN2[h]) for h in H]
        gP=[-nt3(gN3[h],n2_ref[i,h])-nt3(gN2[h],n1_ref[i,h])-gN1[h] for h in H]
        for h in H:
            gk_ref[h]+=nt3(gP[h],V[h])
            gv_ref[h]=gVn[h]+nn3(k2_ref[h].T,gP[h])
        return 0
    lax.fori_loop(0,ITERS,step,0)
    for h in range(nh):
        gk_ref[h]+=gv_ref[h].T*(1.0/L)

def conv_bwd(nh,qkv_ref,g_ref,docb_ref,doc_row,band_ref,gacc_ref,gband_ref):
    for bt in range(SEQ//128):
        lo,hi=span(bt)
        same=same_doc(docb_ref,doc_row,bt)
        off=(lo-bt+1)*128
        for h in range(nh):
            b=h*3*HD+2*HD
            lanes=slice(off,off+(hi-lo)*128)
            ct=jnp.where(same,band_ref[h,:,lanes],0.0)
            g=g_ref[h*HD:(h+1)*HD,bt*128:(bt+1)*128]
            gv=nn(jnp.concatenate([g,g],axis=1),cat(split(ct)))
            gb=jnp.where(same,tn(g,qkv_ref[b:b+HD,lo*128:hi*128]),0.0)
            rows=slice(h*HD,(h+1)*HD)
            if bt==0:
                gband_ref[h]=jnp.zeros((128,384),F32)
                gacc_ref[rows,0:256]=gv
            else:
                gacc_ref[rows,lo*128:(bt+1)*128]+=gv[:,:256]
                if hi>bt+1:
                    gacc_ref[rows,(bt+1)*128:hi*128]=gv[:,256:]
            gband_ref[h,:,lanes]+=gb

def tap_row(gband):
    x=skew(gband,True)
    return pltpu.roll(jnp.sum(x,axis=0,keepdims=True),384-(128-CONV//2),1)

def head_bwd1(h,qkv_ref,g_ref,k1_ref,k3_ref,sum_ref,mix_ref,inv,gv_ref,gs1_ref,gs3_ref,gacc_ref):
    b=h*3*HD
    v=qkv_ref[b+2*HD:b+3*HD,:]
    g=g_ref[h*HD:(h+1)*HD,:]
    k1=k1_ref[h]
    gmix=nt2(k1,g)
    gk1=nn2(mix_ref[h],g)
    gs1_ref[h]=k1*(gk1-jnp.sum(k1*gk1,axis=0,keepdims=True))
    gv_ref[h]=nt3(gmix,sum_ref[h])
    gsum=nn3(inv.T,gmix)
    k3=k3_ref[h]
    gk3=nn2(gsum,v)
    gs3_ref[h]=k3*(gk3-jnp.sum(k3*gk3,axis=1,keepdims=True))
    gacc_ref[h*HD:(h+1)*HD,:]+=nn3(gsum.T,k3)

def head_bwd2(h,qkv_ref,k2_ref,gk_ref,ql_ref,kl_ref,gs1_ref,gs3_ref,gacc_ref,out_ref):
    b=h*3*HD
    q=qkv_ref[b:b+HD,:]; k=qkv_ref[b+HD:b+2*HD,:]
    k2=k2_ref[h]; gk2=gk_ref[h]
    gs2=k2*(gk2-jnp.sum(k2*gk2,axis=1,keepdims=True))
    ql=ql_ref[h]; kl=kl_ref[h]
    gs1=gs1_ref[h]; gs3=gs3_ref[h]
    gkl=nt2(gs1,q)+nn3(gs2.T,ql)
    gql=nt2(gs3,k)+nn3(gs2,kl)
    at=avg_mat()
    gq=(nn3(kl.T,gs1)+nn2(gql.T,at))*0.125
    gk=(nn3(ql.T,gs3)+nn2(gkl.T,at))*0.125
    out_ref[b:b+HD,:]=gq.astype(BF)
    out_ref[b+HD:b+2*HD,:]=gk.astype(BF)
    out_ref[b+2*HD:b+3*HD,:]=gacc_ref[h*HD:(h+1)*HD,:].astype(BF)

MESH = pl.DeviceIdType.MESH


def struct(shape, dtype):
    return jax.ShapeDtypeStruct(shape, dtype)


def remote(src, dst, ss, rs, dev):
    return pltpu.make_async_remote_copy(
        src_ref=src, dst_ref=dst, send_sem=ss, recv_sem=rs, device_id=dev, device_id_type=MESH
    )


def run(*copies):
    for cp in copies:
        cp.start()


def settle(cps, sent=True, got=True):
    for cp in cps:
        if sent:
            cp.wait_send()
        if got:
            cp.wait_recv()


def when(cond, fn):
    if cond is None:
        fn()
    else:
        pl.when(cond)(fn)


def al(x, n):
    return pl.multiple_of(x, n)


def gauss(x):
    e = jnp.exp(-0.5 * x * x)
    t = 1.0 / (1.0 + jnp.abs(x) * 0.23164190)
    p = t * 0.5307027145 - 0.7265760135
    p = (p * t + 0.7107068705) * t - 0.1422483680
    q = (p * t + 0.1274147960) * t * e
    return jnp.where(x >= 0, 1.0 - q, q), e * 0.3989422804014327


def norm_forward(residual, gain, shift):
    average = jnp.mean(residual, axis=1, keepdims=True)
    spread = jnp.mean(residual * residual, axis=1, keepdims=True) - average * average
    scaling = lax.rsqrt(spread + EPSILON)
    normed = (residual - average) * scaling
    return normed * gain + shift, normed, scaling


def norm_backward(upstream, gain, normed, scaling):
    scaled = upstream * gain
    mean_scaled = jnp.mean(scaled, axis=1, keepdims=True)
    crossed = jnp.mean(scaled * normed, axis=1, keepdims=True)
    return scaling * (scaled - mean_scaled - normed * crossed)


def tsum(x):
    return jnp.sum(x, axis=0, keepdims=True)


class Pool:
    def __init__(self, entries):
        self.at = entries


class RowGather:
    def __init__(self, snd, group, base, ways, place, r, R, cond=None):
        n = len(ways)
        self.cond, self.n, self.relay, self.ways = cond, n, R == 4, ways
        if self.relay:
            X, Y = lax.bitwise_xor(r, 1), lax.bitwise_xor(r, 2)
            self.own = []
            self.fwd = []
            for j in range(n):
                mine = place(j, r)
                self.own.append((snd(group, base + 2 * j, mine, mine, {"row": X}),
                                 snd(group, base + 2 * j + 1, mine, mine, {"row": Y})))
                src = place(j, Y if ways[j] else X)
                self.fwd.append(snd(group, base + 2 * n + j, src, src, {"row": X if ways[j] else Y}))
        else:
            self.own = [tuple(snd(group, base + j * (R - 1) + k - 1, place(j, r), place(j, r), {"row": lax.rem(r + k, R)})
                              for k in range(1, R)) for j in range(n)]

    def start(self):
        def go():
            if self.relay:
                for j, cps in enumerate(self.own):
                    cps[self.ways[j]].start()
                for j, cps in enumerate(self.own):
                    cps[1 - self.ways[j]].start()
            else:
                for cps in self.own:
                    run(*cps)
        when(self.cond, go)

    def forward(self):
        if self.relay:
            def go():
                for j in range(self.n):
                    self.own[j][self.ways[j]].wait_recv()
                    self.fwd[j].start()
            when(self.cond, go)

    def finish(self):
        def go():
            for j in range(self.n):
                if self.relay:
                    self.own[j][1 - self.ways[j]].wait_recv()
                    self.fwd[j].wait_recv()
                    self.fwd[j].wait_send()
                else:
                    for cp in self.own[j]:
                        cp.wait_recv()
                for cp in self.own[j]:
                    cp.wait_send()
        when(self.cond, go)


class RowReduce:
    def __init__(self, snd, group, block, recv, lanes, r, R):
        self.block, self.recv, self.lanes, self.r, self.R = block, recv, lanes, r, R
        self.relay = R == 4
        n = len(lanes)
        if self.relay:
            X, Y, Z = lax.bitwise_xor(r, 1), lax.bitwise_xor(r, 2), lax.bitwise_xor(r, 3)
            self.one, self.two, self.mids = [], [], []
            for j, ln in enumerate(lanes):
                P, Q = (X, Y) if j == 0 else (Y, X)
                self.one.append([snd(group, 3 * j, block(Z, ln), recv(1, ln), {"row": P}),
                                 snd(group, 3 * j + 1, block(P, ln), recv(0, ln), {"row": P})])
                self.two.append(snd(group, 3 * j + 2, block(Q, ln), recv(2, ln), {"row": Q}))
                self.mids.append(Q)
        else:
            self.all = [snd(group, k - 1, block(lax.rem(r + k, R), None), recv(k - 1, None), {"row": lax.rem(r + k, R)})
                        for k in range(1, R)]

    def start(self):
        if self.relay:
            for cps in self.one:
                cps[0].start()
        else:
            run(*self.all)

    def start_near(self):
        if self.relay:
            for cps in self.one:
                cps[1].start()

    def middle(self):
        if self.relay:
            for j, ln in enumerate(self.lanes):
                self.one[j][0].wait_recv()
                ref = self.block(self.mids[j], ln)
                ref[...] = (ref[...].astype(F32) + self.recv(1, ln)[...].astype(F32)).astype(BF)
                self.two[j].start()

    def total(self):
        if self.relay:
            for cps in self.one:
                settle(cps, got=False)
                cps[1].wait_recv()
            settle(self.two)
            slots = (0, 2)
        else:
            settle(self.all)
            slots = range(self.R - 1)
        t = self.block(self.r, None)[...].astype(F32)
        for k in slots:
            t = t + self.recv(k, None)[...].astype(F32)
        return t

    def finish(self):
        self.block(self.r, None)[...] = self.total().astype(BF)


class LineReduce:
    def __init__(self, snd, group, base, piece, up, dn, c, C):
        self.piece, self.ups, self.dns, self.c, self.C = piece, up, dn, c, C
        m = C - 1
        self.up = {q: snd(group, base + q - 1, up.at[q - 1], up.at[q - 1], {"col": c + 1}) for q in range(1, C)}
        self.dn = {q: snd(group, base + m + q, dn.at[q], dn.at[q], {"col": c - 1}) for q in range(C - 1)}
        self.up0 = {q: snd(group, base + q - 1, piece(q), up.at[q - 1], {"col": c + 1}) for q in range(1, C)}
        self.dn0 = {q: snd(group, base + m + q, piece(q), dn.at[q], {"col": c - 1}) for q in range(C - 1)}

    def start(self):
        pl.when(self.c == 0)(lambda: run(*[self.up0[q] for q in range(self.C - 1, 0, -1)]))
        pl.when(self.c == self.C - 1)(lambda: run(*[self.dn0[q] for q in range(self.C - 1)]))

    def pump(self, k):
        C = self.C

        def go(cps, buf, off, mine, rest):
            def f():
                for q in rest:
                    cps[q].wait_recv()
                    buf[q - off] = (buf[q - off].astype(F32) + self.piece(q)[...].astype(F32)).astype(BF)
                    cps[q].start()
            return f
        pl.when(self.c == k)(go(self.up, self.ups, 1, k, range(C - 1, k, -1)))
        pl.when(self.c == C - 1 - k)(go(self.dn, self.dns, 0, C - 1 - k, range(C - 1 - k)))

    def total(self, own, out):
        C = self.C
        for k in range(C):
            @pl.when(self.c == k)
            def _():
                t = own.astype(F32)
                if k > 0:
                    self.up[k].wait_recv()
                    t = t + self.ups[k - 1].astype(F32)
                if k < C - 1:
                    self.dn[k].wait_recv()
                    t = t + self.dns[k].astype(F32)
                out[...] = t.astype(BF)
                if k < C - 1:
                    settle([(self.up0 if k == 0 else self.up)[q] for q in range(k + 1, C)], got=False)
                if k > 0:
                    settle([(self.dn0 if k == C - 1 else self.dn)[q] for q in range(k)], got=False)


class LineGather:
    def __init__(self, snd, group, n, place, c, C):
        self.C, self.c, self.n = C, c, n
        m = (C - 1) * n
        self.up = [[snd(group, k * n + j, place(j, c - k), place(j, c - k), {"col": c + 1}) for j in range(n)] for k in range(C - 1)]
        self.dn = [[snd(group, m + k * n + j, place(j, c + k), place(j, c + k), {"col": c - 1}) for j in range(n)] for k in range(C - 1)]

    def up_ok(self, k):
        return (self.c >= k) & (self.c < self.C - 1)

    def dn_ok(self, k):
        return (self.c + k <= self.C - 1) & (self.c > 0)

    def start(self):
        pl.when(self.up_ok(0))(lambda: run(*self.up[0]))
        pl.when(self.dn_ok(0))(lambda: run(*self.dn[0]))

    def step(self, k):
        def got(cps, nxt, ok):
            def go():
                for j in range(self.n):
                    cps[j].wait_recv()
                    if nxt is not None:
                        pl.when(ok)(lambda: nxt[j].start())
            return go
        more = k < self.C - 1
        pl.when(self.c >= k)(got(self.up[k - 1], self.up[k] if more else None, self.up_ok(k) if more else None))
        pl.when(self.c + k <= self.C - 1)(got(self.dn[k - 1], self.dn[k] if more else None, self.dn_ok(k) if more else None))

    def forward(self, k):
        def on(cps, nxt):
            def go():
                for j in range(self.n):
                    cps[j].wait_recv()
                    nxt[j].start()
            return go
        pl.when(self.up_ok(k))(on(self.up[k - 1], self.up[k]))
        pl.when(self.dn_ok(k))(on(self.dn[k - 1], self.dn[k]))

    def land(self):
        for k in range(1, self.C):
            pl.when(self.c == self.C - 1)(lambda: settle(self.up[k - 1], sent=False))
            pl.when(self.c == 0)(lambda: settle(self.dn[k - 1], sent=False))

    def drain(self):
        for k in range(self.C - 1):
            pl.when(self.up_ok(k))(lambda: settle(self.up[k], got=False))
            pl.when(self.dn_ok(k))(lambda: settle(self.dn[k], got=False))


def layer_call(R, C, S, fb, nh, fc, pb, qw, args):
    HB = R // S
    QT = SEQ_LEN // HB
    FF = fc * C
    fh, ph = fc // 2, pb // 2
    fq = fh // 3 // 128 * 128
    fp = fh - fq
    dpw, dqw = fq, fp
    hb = nh * HD
    fbp = -(-fb // 128) * 128
    CH = 256
    FH = FF // 2
    relay = R == 4
    NR = 3 if relay else R - 1
    PT = nh + 1
    V = pltpu.VMEM
    small = (nh, L, L)
    any_in = ["x", "cot", "wq", "wp", "wu", "wd"]
    vmem_in = ["doc", "taps", "g1", "s1", "g2", "s2", "qb", "ub", "pb", "db"]
    names_in = any_in + vmem_in
    outs = dict(
        out=((fb, S * SEQ_LEN), BF), gin=((fb, S * SEQ_LEN), F32), gqw=((fb, qw), F32), gup=((fb, fc), F32),
        gdn=((fb, fc), F32), gpj=((pb, fb), F32), sve=((8, fbp), F32), svu=((1, fc), F32), svl=((PT, D), F32))
    bufs = dict(
        xg=((D, SEQ_LEN), BF), wg=((R, fb, qw), BF), ms=((8, SEQ_LEN), F32), mt=((8, SEQ_LEN), F32),
        rs=((8, fbp), F32), rp=((R, 8, fbp), F32), cs=((8, fc), F32), cp=((C, 8, fc), F32),
        cg=((D, QT), BF), wpf=((R, D, fb), BF), wuf=((D, FF), BF), wdf=((D, FF), BF),
        qkv=((3 * hb, SEQ_LEN), BF), k1=((nh, L, SEQ_LEN), F32), k3=((nh, L, SEQ_LEN), F32), k2=(small, F32),
        ql=(small, F32), kl=(small, F32), sm=(small, F32), mix=(small, F32), nv=((ITERS + 1,) + small, F32),
        np_=((ITERS,) + small, F32), n1=((ITERS,) + small, F32), n2=((ITERS,) + small, F32), n3=((ITERS,) + small, F32),
        docb=((SEQ_LEN, 128), F32), band=((nh, 128, 384), F32), gband=((nh, 128, 384), F32), acc=((hb, SEQ_LEN), F32), att=((hb, SEQ_LEN), BF), attq=((D, QT), BF),
        resT=((D, QT), F32), prow=((8, D), F32), hidden=((QT, D), F32), hid=((QT, D), BF), nm1=((QT, D), F32),
        sc1=((QT, 1), F32), act=((QT, FF), BF), dact=((QT, FF), F32), res2=((QT, D), F32), gdown=((QT, D), BF),
        gpre=((QT, FF), BF), gattoT=((D, QT), BF), outT=((D, QT), BF), gatt=((hb, SEQ_LEN), BF),
        hid_o=((QT, D), BF), gdown_o=((QT, D), BF), gattoT_o=((D, QT), BF), att_o=((C * ph, QT), BF),
        act_o=((QT, C * fh), BF), gpre_o=((QT, C * fh), BF),
        gu=((D, C * fp), BF), guq=((D, C * fq), BF), gd=((D, C * fp), BF), gp=((R, C * ph, fb), BF), gdq=((D, C * fq), BF),
        ru=((NR, fb, C * fp), BF), rd=((NR, fb, C * fp), BF), rpj=((NR, C * ph, fb), BF),
        zu=((C - 1, fb, fp), BF), zd=((C - 1, fb, fp), BF), zp=((C - 1, ph, fb), BF),
        zdq=((C - 1, D, fq), BF), zuq=((C - 1, D, fq), BF), zdr=((C - 1, D, fq), BF), zur=((C - 1, D, fq), BF), tuq=((D, fq), BF), tdq=((D, fq), BF),
        rdq=((R - 1, fb, fq), BF), ruq=((R - 1, fb, fq), BF),
        gv=(small, F32), gk=(small, F32),
        part=((D, SEQ_LEN), BF), pr=((R - 1, fb, SEQ_LEN), BF),
        gq=((R, fb, qw), BF), gqo=((R // 2, fb, qw), BF), gqr=((R, fb, qw), BF), gqz=((C, fb, qw), BF),
        e0=((8, D), F32), eb=((R, 8, fbp), F32), er=((R - 1, 8, fbp), F32), e1=((8, fbp), F32), ez=((C - 1, 8, fbp), F32),
        e2=((8, fbp), F32), eo=((8, fbp), F32), u0=((C, 1, fc), F32), uz=((C - 1, 1, fc), F32), u1=((1, fc), F32),
        ur=((R - 1, 1, fc), F32), u2=((1, fc), F32), uo=((1, fc), F32), l0=((PT, D), F32), lz=((C - 1, PT, D), F32),
        l1=((PT, D), F32), lr=((R, PT, D), F32), l2=((PT, D), F32), lo=((PT, D), F32))
    NRP = 1 + 2 * (C - 1)
    sems = dict(
        x=2 * (R - 1), cot=R - 1, rowp=R - 1, colp=C - 1, meta=1, ws=S * C, wr=R, wd2=R,
        zU=4 * (C - 1), zD=2 * (C - 1), rU=C * 2 * (R - 1), rD=C * (R - 1), rQ=R - 1, rS=R - 1, zQ=2 * (C - 1), zR=2 * (C - 1),
        cU=2 * C, cD=C, cQ=2 * C,
        att=HB - 1, gatt=HB - 1, ex=5 + C, ru=max(6, R - 1), rd=max(6, R - 1), rp=max(3, R - 1), rcol=3 * (C - 1),
        zq=4 * (C - 1), rq=2 * (R - 1), part=max(6, R - 1), outx=R - 1,
        gqd=R // 2, gqrow=R, gqcol=C, gqf=1, erow=R - 1, ecol=C - 1, ed=1, ucol=C - 1, urow=R - 1, ud=1, lcol=C - 1, lrow=R, ld=1, fin=3)
    local = dict(loc=21)

    late_sems = ["ru", "rd", "rp", "rcol", "zq", "rq", "part", "gqd", "gqrow", "gqcol", "gqf", "erow", "ecol", "ed", "ucol",
                 "urow", "ud", "lcol", "lrow", "ld", "fin"]
    first_sems = [g for g in sems if g not in late_sems]

    def body(*refs):
        n = len(names_in)
        i = dict(zip(names_in, refs[:n]))
        o = dict(zip(outs, refs[n:n + len(outs)]))
        k = n + len(outs)
        b = dict(zip(bufs, refs[k:k + len(bufs)]))
        k += len(bufs)
        ss = dict(zip(first_sems + list(local), refs[k:]))
        k += len(first_sems) + len(local)
        rs = dict(zip(sems, refs[k:]))
        free = [ss[g].at[j] for g in ("rU", "rD", "zU", "zD", "zQ", "zR", "cU", "cD", "cQ", "rQ", "rS", "x") for j in range(sems[g])]
        for g in late_sems:
            ss[g] = Pool(free[:sems[g]])
            free = free[sems[g]:]
        d = lax.axis_index("dp")
        r = lax.axis_index("row")
        c = lax.axis_index("col")
        a, h = r // HB, lax.rem(r, HB)
        core = {"dp": 1 - d}

        def snd(group, slot, src, dst, dev):
            return remote(src, dst, ss[group].at[slot], rs[group].at[slot], dev)

        def loc(slot, src, dst):
            return pltpu.make_async_copy(src, dst, ss["loc"].at[slot])

        def fr(ref, q):
            return ref.at[pl.ds(al(q * fb, fb), fb), :]

        def peer(k):
            return lax.rem(r + k, R)

        def cpeer(k):
            return lax.rem(c + k, C)

        own = c == h
        bar = pltpu.get_barrier_semaphore()
        for k in range(1, R):
            pl.semaphore_signal(bar, inc=1, device_id={"row": peer(k)}, device_id_type=MESH)
        for k in range(1, C):
            pl.semaphore_signal(bar, inc=1, device_id={"col": cpeer(k)}, device_id_type=MESH)
        pl.semaphore_signal(bar, inc=1, device_id=core, device_id_type=MESH)
        for q in range(R):
            @pl.when(jnp.logical_not(own & (r == q)))
            def _():
                pl.semaphore_signal(bar, inc=1, device_id={"row": q, "col": h}, device_id_type=MESH)
        half = fb // 2

        def xcols(q, part=None):
            rows = slice(None) if part is None else pl.ds(part * half, half)
            return i["x"].at[rows, pl.ds(al(q // HB * SEQ_LEN, SEQ_LEN), SEQ_LEN)]

        x_loc = loc(0, xcols(r), fr(b["xg"], r))
        x_loc.start()

        def cols_of(col, first, width):
            return pl.ds(al(d * (FF // 2) + col * fh + first, 128), width)

        def wide(ref, row, col, first, width):
            return ref.at[pl.ds(al(row * fb, fb), fb), cols_of(col, first, width)]

        def narrow(ref, row, col):
            return ref.at[row, pl.ds(al(col * pb + d * ph, ph), ph), :]

        bulk_loc = [loc(1, i["wu"].at[:, pl.ds(al(d * fh, fh), fh)], wide(b["wuf"], r, c, 0, fh)),
                    loc(2, i["wd"].at[:, pl.ds(al(d * fh, fh), fh)], wide(b["wdf"], r, c, 0, fh)),
                    loc(3, i["wp"].at[pl.ds(al(d * ph, ph), ph), :], narrow(b["wpf"], r, c))]
        run(*bulk_loc)
        cot_rows = min(fb, 64)
        stage = []
        for s in range(S):
            for f in range(0, fb, cot_rows):
                m = len(stage)
                buf = b["k1"].at[m] if m < nh else b["k3"].at[m - nh]
                stage.append((s, f, m, loc(4 + m, i["cot"].at[f:f + cot_rows, s * SEQ_LEN:(s + 1) * SEQ_LEN], buf.at[0:cot_rows, :])))
        run(*[t[3] for t in stage])
        b["ms"][...] = jnp.zeros((8, SEQ_LEN), F32)
        b["ms"][0:1, :] = i["doc"][...].astype(F32)
        b["ms"][1:1 + nh, 0:CONV] = i["taps"][...]
        b["ms"][1 + nh:2 + nh, 0:qw] = i["qb"][...].astype(F32).reshape(1, qw)
        b["rs"][...] = jnp.zeros((8, fbp), F32)
        for j, name in enumerate(("g1", "s1", "g2", "s2")):
            b["rs"][j:j + 1, 0:fb] = i[name][...]
        b["rs"][4:5, 0:fb] = i["pb"][...].astype(F32).reshape(1, fb)
        b["rs"][5:6, 0:fb] = i["db"][...].astype(F32).reshape(1, fb)
        b["cs"][...] = jnp.zeros((8, fc), F32)
        b["cs"][0:1, :] = i["ub"][...].astype(F32).reshape(1, fc)
        for cp in bulk_loc:
            cp.wait()
        x_loc.wait()
        pl.semaphore_wait(bar, R - 1 + C - 1 + 1 + S * C - jnp.where(own, 1, 0))

        dst_row, dst_col = lax.rem(r, S) * HB + c, r // S
        meta_self = (dst_row == r) & (dst_col == c)
        meta_out = snd("meta", 0, b["ms"], b["mt"], {"row": dst_row, "col": dst_col})
        meta_in = snd("meta", 0, b["ms"], b["mt"], {"row": c * S + a, "col": h})
        meta_loc = loc(17, b["ms"], b["mt"])
        pl.when(jnp.logical_not(meta_self))(meta_out.start)
        pl.when(meta_self)(meta_loc.start)

        def place_u(col):
            return lambda j, row: narrow(b["wpf"], row, col) if j else wide(b["wuf"], row, col, 0, fp)

        def place_d(col):
            return lambda j, row: wide(b["wdf"], row, col, 0, dpw)

        zU = LineGather(snd, "zU", 2, lambda j, col: place_u(col)(j, r), c, C)
        zD = LineGather(snd, "zD", 1, lambda j, col: place_d(col)(j, r), c, C)
        at_cols = [(None, c)]
        for k in range(1, C):
            at_cols += [(c >= k, c - k), (c + k <= C - 1, c + k)]
        rU = [RowGather(snd, "rU", col * 2 * (R - 1), (0, 1), place_u(col), r, R, cond) for cond, col in at_cols]
        rD = [RowGather(snd, "rD", col * (R - 1), (1,), place_d(col), r, R, cond) for cond, col in at_cols]
        rQ = RowGather(snd, "rQ", 0, (0,), lambda j, row: wide(b["wuf"], row, c, fp, fq), r, R)
        rS = RowGather(snd, "rS", 0, (1,), lambda j, row: wide(b["wdf"], row, c, dpw, dqw), r, R)
        rQ.start()
        zQ = LineGather(snd, "zQ", 1, lambda j, col: b["wuf"].at[:, cols_of(col, fp, fq)], c, C)
        zR = LineGather(snd, "zR", 1, lambda j, col: b["wdf"].at[:, cols_of(col, dpw, dqw)], c, C)
        zU.start()
        zD.start()
        if relay:
            xg = RowGather(snd, "x", 0, (0, 1), lambda j, q: b["xg"].at[pl.ds(al(q * fb + j * half, half), half), :], r, R)
            xg.start()
        else:
            xs = [snd("x", k - 1, xcols(peer(k)), fr(b["xg"], r), {"row": peer(k)}) for k in range(1, R)]
            run(*xs)
        par = lax.rem(r, 2) == d
        w_out = []
        for ap in range(S):
            for cq in range(C):
                t = ap * HB + c
                go = par & jnp.logical_not((t == r) & (c == cq))
                cp = remote(i["wq"], b["wg"].at[r], ss["ws"].at[ap * C + cq], rs["wr"].at[r], {"row": t, "col": cq})
                w_out.append((go, cp))
        for go, cp in w_out:
            pl.when(go)(cp.start)
        w_loc = loc(16, i["wq"], b["wg"].at[r])
        pl.when(own & par)(w_loc.start)
        def cot_at(s, cols):
            return b["gpre"].at[pl.ds(al(s // 3 * fb, fb), fb), cols]

        for s, f, m, cp in stage:
            cp.wait()
            buf = b["k1"].at[m] if m < nh else b["k3"].at[m - nh]
            b["gpre"][s // 3 * fb + f:s // 3 * fb + f + cot_rows, s % 3 * SEQ_LEN:(s % 3 + 1) * SEQ_LEN] = buf[0:cot_rows, :].astype(BF)

        def cot_src(q):
            s = q // HB
            return cot_at(s, pl.ds(al(lax.rem(s, 3) * SEQ_LEN + lax.rem(q, HB) * QT, QT), QT))

        zU.step(1)
        if relay:
            xg.forward()
        rQ.forward()
        rS.start()
        zD.forward(1)
        pl.when(jnp.logical_not(meta_self))(meta_in.wait_recv)
        pl.when(meta_self)(meta_loc.wait)
        doc_row = b["mt"][0:1, :]
        rowb = jnp.broadcast_to(doc_row, (8, SEQ_LEN)).astype(BF)
        pick = pick_mat()
        land_row = nt(rowb, pick)[0:1]
        land_col = nt(pick, rowb)[:, 0:1]
        for hh in range(nh):
            b["band"][hh] = band(b["mt"][1 + hh:2 + hh, 0:384])
        one = jnp.where(iota((8, 128), 0) == 0, 1.0, 0.0).astype(BF)
        b["docb"][...] = tn(rowb, one)
        for k in range(2, C - 1):
            zU.step(k)
            zD.forward(k)
        rQ.finish()
        zQ.start()
        rS.forward()
        if relay:
            xg.finish()
        else:
            settle(xs)
        for m in range(2 * C - 3):
            rU[m].start()
        gs = [snd("cot", k - 1, cot_src(peer(k)), fr(b["cg"], r), {"row": peer(k)}) for k in range(1, R)]
        g_loc = loc(18, cot_src(r), fr(b["cg"], r))
        ps = [snd("rowp", k - 1, b["rs"], b["rp"].at[r], {"row": peer(k)}) for k in range(1, R)]
        p_loc = loc(19, b["rs"], b["rp"].at[r])
        cs = [snd("colp", k - 1, b["cs"], b["cp"].at[c], {"col": cpeer(k)}) for k in range(1, C)]
        c_loc = loc(20, b["cs"], b["cp"].at[c])
        run(*ps, p_loc, *cs, c_loc)
        w_fwd = [snd("wd2", q, b["wg"].at[q], b["wg"].at[q], core) for q in range(R)]
        for q in range(R):
            mine_q = (q % 2) == d
            here_q = own & (r == q)
            w_in = remote(i["wq"], b["wg"].at[q], ss["ws"].at[0], rs["wr"].at[q], {"row": q, "col": h})
            pl.when(mine_q & here_q)(w_loc.wait)
            pl.when(mine_q & jnp.logical_not(here_q))(w_in.wait_recv)
            pl.when(mine_q)(w_fwd[q].start)
        for q in range(R):
            pl.when((q % 2) != d)(w_fwd[q].wait_recv)
        qb = jnp.where(iota((8, qw), 0) == 1 + nh, b["mt"][:, 0:qw], 0.0).astype(BF)
        acc = tn(qb, jnp.ones((8, SEQ_LEN), BF))
        for q in range(R):
            acc = acc + tn(b["wg"][q], b["xg"][q * fb:(q + 1) * fb, :])
        b["qkv"][...] = acc.astype(BF)

        def scores(hh):
            head_scores(hh, b["qkv"], doc_row, land_row, land_col, b["k1"], b["k3"], b["k2"], b["ql"], b["kl"], b["sm"])

        for hh in range(nh):
            scores(hh)
        zQ.forward(1)
        rS.finish()
        zR.start()
        zU.step(C - 1)
        for m in range(2 * C - 3, NRP):
            rU[m].start()
        newton(nh, b["k2"], b["nv"], b["np_"], b["n1"], b["n2"], b["n3"])
        for k in range(2, C - 1):
            zQ.forward(k)
        for m in range(3):
            rU[m].forward()
        conv_fwd(nh, b["qkv"], b["docb"], doc_row, b["band"], b["acc"])
        for hh in range(nh):
            head_out(hh, b["k1"], b["nv"][ITERS, hh], b["sm"], b["mix"], b["acc"], b["att"])

        def group(k):
            return lax.rem(h + k, HB)

        def hrows(ref, q):
            return ref.at[pl.ds(al(q * hb, hb), hb), :]

        def tcols(ref, q):
            return ref.at[:, pl.ds(al(q * QT, QT), QT)]

        at = [snd("att", k - 1, tcols(b["att"], group(k)), hrows(b["attq"], h), {"row": a * HB + group(k)})
              for k in range(1, HB)]
        run(*at)
        at_loc = loc(0, tcols(b["att"], h), hrows(b["attq"], h))
        at_loc.start()
        for m in range(3, NRP):
            rU[m].forward()
        zD.land()
        for m in range(NRP):
            rD[m].start()
        zR.forward(1)
        for cp in ps + cs:
            cp.wait()
        for cp in (p_loc, c_loc):
            cp.wait()
        prow = jnp.zeros((8, D), F32)
        for q in range(R):
            piece = jnp.concatenate([b["rp"][q], jnp.zeros((8, D - fbp), F32)], axis=1)
            prow = prow + (pltpu.roll(piece, q * fb, 1) if q else piece)
        b["prow"][...] = prow
        def cross(group, slot, cond, *refs):
            cps = [snd(group, slot + j, ref, ref, core) for j, ref in enumerate(refs)]
            when(cond, lambda: run(*cps))
            return cond, cps

        crossed, later = [], []
        for m, (cond, col) in enumerate(at_cols):
            rU[m].finish()
            crossed.append(cross("cU", 2 * col, cond, b["wuf"].at[:, cols_of(col, 0, fp)],
                                 b["wpf"].at[:, pl.ds(al(col * pb + d * ph, ph), ph), :]))
        zQ.land()
        for k in range(2, C - 1):
            zR.forward(k)
        for m, (cond, col) in enumerate(at_cols):
            crossed.append(cross("cQ", 2 * col, cond, b["wuf"].at[:, cols_of(col, fp, fq)]))
        settle(at)
        at_loc.wait()
        for cond, cps in crossed:
            when(cond, lambda: settle(cps))

        for q in range(R):
            t = tn(b["wpf"][q], b["attq"][...])
            b["resT"][q * fb:(q + 1) * fb, :] = t + b["xg"][q * fb:(q + 1) * fb, pl.ds(al(h * QT, QT), QT)].astype(F32)
        res1 = b["resT"][...].T + b["prow"][4:5, :]
        hidden, nm1, sc1 = norm_forward(res1, b["prow"][0:1, :], b["prow"][1:2, :])
        b["hidden"][...] = hidden
        b["nm1"][...] = nm1
        b["sc1"][...] = sc1
        b["hid"][...] = hidden.astype(BF)
        ex_hid = snd("ex", 0, b["hid"], b["hid_o"], core)
        ex_hid.start()

        def up(j, _):
            cols = pl.ds(al(j * fh, 128), fh)
            bias = b["cp"][lax.rem(j, C), 0:1, pl.ds(al(j // C * fh, 128), fh)]
            pre = nn(b["hid"][...], b["wuf"][:, cols]) + bias
            cdf, pdf = gauss(pre)
            b["act"][:, cols] = (pre * cdf).astype(BF)
            b["dact"][:, cols] = cdf + pre * pdf
            return 0

        lax.fori_loop(0, C, up, 0)
        for m in range(2 * C - 3):
            rD[m].forward()
        lax.fori_loop(C, 2 * C, up, 0)
        for m in range(2 * C - 3, NRP):
            rD[m].forward()
        run(*gs, g_loc)
        zR.land()
        for m, (cond, col) in enumerate(at_cols):
            later.append(cross("cQ", 2 * col + 1, cond, b["wdf"].at[:, cols_of(col, dpw, dqw)]))
        other_half = pl.ds(al((1 - d) * FH, 128), FH)
        ex_act = [snd("ex", 3, b["act"].at[:, other_half], b["act_o"], core)]
        run(*ex_act)
        for m, (cond, col) in enumerate(at_cols):
            rD[m].finish()
            later.append(cross("cD", col, cond, b["wdf"].at[:, cols_of(col, 0, dpw)]))
        for cond, cps in later:
            when(cond, lambda: settle(cps))
        for line in (zU, zD, zQ, zR):
            line.drain()

        def down(j, _):
            cols = pl.ds(al(j * CH, CH), CH)
            b["res2"][:, cols] = b["hidden"][:, cols] + nt(b["act"][...], b["wdf"][cols, :]) + b["prow"][5:6, cols]
            return 0

        lax.fori_loop(0, D // CH, down, 0)
        gain2 = b["prow"][2:3, :]
        out, nm2, sc2 = norm_forward(b["res2"][...], gain2, b["prow"][3:4, :])
        settle(gs)
        g_loc.wait()
        ups = b["cg"][...].astype(F32).T
        e0 = b["e0"]
        e0[...] = jnp.zeros((8, D), F32)
        e0[2:3, :] = tsum(ups * nm2)
        e0[5:6, :] = tsum(ups)
        gres2 = norm_backward(ups, gain2, nm2, sc2)
        b["res2"][...] = gres2
        b["gdown"][...] = gres2.astype(BF)
        e0[4:5, :] = tsum(b["gdown"][...].astype(F32))
        ex_gdown = snd("ex", 1, b["gdown"], b["gdown_o"], core)
        ex_gdown.start()
        b["outT"][...] = out.T.astype(BF)
        ox = [snd("outx", k - 1, fr(b["outT"], peer(k)), tcols(o["out"], a * HB + h), {"row": peer(k)}) for k in range(1, R)]
        o_loc = loc(1, fr(b["outT"], r), tcols(o["out"], a * HB + h))
        run(*ox, o_loc)

        def gact(j, _):
            cols = pl.ds(al(j * fh, 128), fh)
            g = nn(b["gdown"][...], b["wdf"][:, cols])
            gp = (g * b["dact"][:, cols]).astype(BF)
            b["gpre"][:, cols] = gp
            b["u0"][lax.rem(j, C), 0:1, pl.ds(al(j // C * fh, 128), fh)] = tsum(gp.astype(F32))
            return 0

        lax.fori_loop(0, 2 * C, gact, 0)
        ex_gpre = [snd("ex", 4, b["gpre"].at[:, other_half], b["gpre_o"], core)]
        run(*ex_gpre)
        def grad_block(q, mine, mine_w, other, other_w, dst, dst_q):
            to = slice(q * fh, (q + 1) * fh)
            t = tn(b[mine][...], b[mine_w][:, cols_of(q, 0, fh)]) + tn(b[other][...], b[other_w][:, to])
            b[dst][:, q * fp:(q + 1) * fp] = t[:, :fp].astype(BF)
            b[dst_q][:, q * fq:(q + 1) * fq] = t[:, fp:].astype(BF)

        def scatter_q(base, src, up_buf, dn_buf):
            line = LineReduce(snd, "zq", base, lambda q: src.at[:, q * fq:(q + 1) * fq], up_buf, dn_buf, c, C)
            line.start()
            return line

        def block_of(ref):
            return lambda q, ln: ref.at[pl.ds(al(q * fb, fb), fb), slice(None) if ln is None else ln]

        def recv_of(ref):
            return lambda k, ln: ref.at[k, :, slice(None) if ln is None else ln]

        settle(ex_act)
        settle([ex_gdown])
        for q in range(C):
            grad_block(q, "gdown", "act", "gdown_o", "act_o", "gd", "gdq")

        def lanes(n):
            return slice(0, n // 2), slice(n // 2, n)

        red_d = RowReduce(snd, "rd", block_of(b["gd"]), recv_of(b["rd"]), lanes(C * fp), r, R)
        red_d.start()
        zqd = scatter_q(0, b["gdq"], b["zdq"], b["zdr"])

        def ghid_step(j, _):
            cols = pl.ds(al(j * CH, CH), CH)
            b["hidden"][:, cols] = b["res2"][:, cols] + nt(b["gpre"][...], b["wuf"][cols, :])
            return 0

        lax.fori_loop(0, D // CH, ghid_step, 0)
        ghid = b["hidden"][...]
        nm1 = b["nm1"][...]
        e0[0:1, :] = tsum(ghid * nm1)
        e0[1:2, :] = tsum(ghid)
        gres1 = norm_backward(ghid, b["prow"][0:1, :], nm1, b["sc1"][...])
        e0[3:4, :] = tsum(gres1.astype(BF).astype(F32))
        b["resT"][...] = gres1.T
        b["gattoT"][...] = b["resT"][...].astype(BF)
        ga = jnp.zeros((D, QT), F32)
        for q in range(R):
            ga = ga + nn(b["wpf"][q], b["gattoT"][q * fb:(q + 1) * fb, :])
        b["cg"][...] = ga.astype(BF)
        gt = [snd("gatt", k - 1, hrows(b["cg"], group(k)), tcols(b["gatt"], h), {"row": a * HB + group(k)})
              for k in range(1, HB)]
        run(*gt)
        gt_loc = loc(2, hrows(b["cg"], h), tcols(b["gatt"], h))
        gt_loc.start()
        red_d.start_near()
        b["eb"][...] = jnp.zeros((R, 8, fbp), F32)
        for q in range(R):
            b["eb"][q, :, 0:fb] = e0[:, q * fb:(q + 1) * fb]
        er = [snd("erow", k - 1, b["eb"].at[peer(k)], b["er"].at[k - 1], {"row": peer(k)}) for k in range(1, R)]
        uc = [snd("ucol", k - 1, b["u0"].at[cpeer(k)], b["uz"].at[k - 1], {"col": cpeer(k)}) for k in range(1, C)]
        run(*er, *uc)
        ex_att = [snd("ex", 2, b["gattoT"], b["gattoT_o"], core)] + [
            snd("ex", 5 + q, b["attq"].at[pl.ds(al(q * pb + (1 - d) * ph, ph), ph), :],
                b["att_o"].at[q * ph:(q + 1) * ph, :], core) for q in range(C)]
        run(*ex_att)
        settle([ex_hid])
        settle(ex_gpre)
        for q in range(C):
            grad_block(q, "hid", "gpre", "hid_o", "gpre_o", "gu", "guq")
        zqu = scatter_q(2 * (C - 1), b["guq"], b["zuq"], b["zur"])
        own_rows = pl.ds(al(r * fb, fb), fb)
        red_u = RowReduce(snd, "ru", block_of(b["gu"]), recv_of(b["ru"]), lanes(C * fp), r, R)
        settle(ex_att)
        for q in range(C):
            rows = pl.ds(al(q * pb + d * ph, ph), ph)
            tp = slice(q * ph, (q + 1) * ph)
            for p in range(R):
                f = slice(p * fb, (p + 1) * fb)
                b["gp"][p, tp, :] = (nt(b["attq"][rows, :], b["gattoT"][f, :])
                                     + nt(b["att_o"][tp, :], b["gattoT_o"][f, :])).astype(BF)
        red_p = RowReduce(snd, "rp", lambda q, ln: b["gp"].at[q], lambda k, ln: b["rpj"].at[k], (None,), r, R)
        red_p.start()
        red_p.start_near()
        red_u.start()
        def total(own_part, buf, m):
            t = own_part.astype(F32)
            for k in range(m):
                t = t + buf[k].astype(F32)
            return t

        def scatter_p(slot, src_of, dst):
            cps = [snd("rcol", slot * (C - 1) + k - 1, src_of(cpeer(k)), dst.at[k - 1], {"col": cpeer(k)}) for k in range(1, C)]
            run(*cps)
            return cps

        def pcol(ref, n):
            return lambda q: ref.at[own_rows, pl.ds(al(q * n, n), n)]

        qcols = pl.ds(al(c * fq, fq), fq)

        def whole(first, buf, m):
            for k in range(m):
                first = first + buf[k]
            return first

        settle(gt)
        gt_loc.wait()
        conv_bwd(nh, b["qkv"], b["gatt"], b["docb"], doc_row, b["band"], b["acc"], b["gband"])
        for hh in range(nh):
            head_bwd1(hh, b["qkv"], b["gatt"], b["k1"], b["k3"], b["sm"], b["mix"], b["nv"][ITERS, hh], b["gv"], b["k1"], b["k3"], b["acc"])
        zqd.pump(1)
        red_d.middle()
        newton_bwd(nh, b["k2"], b["nv"], b["np_"], b["n1"], b["n2"], b["n3"], b["gv"], b["gk"])
        red_u.start_near()
        red_p.middle()
        for hh in range(nh):
            head_bwd2(hh, b["qkv"], b["k2"], b["gk"], b["ql"], b["kl"], b["k1"], b["k3"], b["acc"], b["qkv"])

        for q in range(R):
            b["gq"][q] = nt(b["xg"][q * fb:(q + 1) * fb, :], b["qkv"][...]).astype(BF)
        gqd = [snd("gqd", j, b["gq"].at[2 * j + 1 - d], b["gqo"].at[j], core) for j in range(R // 2)]
        run(*gqd)
        settle(gqd)
        gq_out = []
        for j in range(R // 2):
            b["gq"][2 * j + d] = (b["gq"][2 * j + d].astype(F32) + b["gqo"][j].astype(F32)).astype(BF)
            q = 2 * j + d
            cp = remote(b["gq"].at[q], b["gqr"].at[r], ss["gqrow"].at[j], rs["gqrow"].at[r], {"row": q})
            lc = loc(3, b["gq"].at[q], b["gqr"].at[r])
            gq_out.append((q, cp, lc))
            pl.when(q != r)(cp.start)
            pl.when(q == r)(lc.start)
        l0 = b["l0"]
        l0[...] = jnp.zeros((PT, D), F32)
        l0[0:1, 0:qw] = nt(jnp.ones((8, SEQ_LEN), BF), b["qkv"][...])[0:1]
        for hh in range(nh):
            l0[1 + hh:2 + hh, 0:384] = tap_row(b["gband"][hh])
        lcl = [snd("lcol", k - 1, l0, b["lz"].at[k - 1], {"col": cpeer(k)}) for k in range(1, C)]
        run(*lcl)
        red_u.middle()
        for k in range(2, C - 1):
            zqd.pump(k)
        zqu.pump(1)
        for q in range(R):
            f = slice(q * fb, (q + 1) * fb)
            b["part"][f, :] = nn(b["wg"][q], b["qkv"][...]).astype(BF)
            mine_cols = pl.ds(al(h * QT, QT), QT)
            b["part"][f, mine_cols] = (nn(b["wg"][q], b["qkv"][:, mine_cols]) + b["resT"][f, :]).astype(BF)
        red_x = RowReduce(snd, "part", block_of(b["part"]), recv_of(b["pr"]), lanes(SEQ_LEN), r, R)
        if relay:
            red_x.start()
            red_x.start_near()
        else:
            pt = [snd("part", k - 1, fr(b["part"], peer(k)), b["pr"].at[k - 1], {"row": peer(k)}) for k in range(1, R)]
            run(*pt)

        red_d.finish()
        rcd = scatter_p(0, pcol(b["gd"], fp), b["zd"])

        def second_q(base, line, src, mid, dst):
            line.total(b[src][:, qcols], b[mid])
            out = [snd("rq", base + k - 1, fr(b[mid], peer(k)), b[dst].at[k - 1], {"row": peer(k)}) for k in range(1, R)]
            run(*out)
            return out

        rqd = second_q(0, zqd, "gdq", "tdq", "rdq")
        for k in range(2, C - 1):
            zqu.pump(k)
        gq_col = []
        for hp in range(HB):
            cp = remote(b["gqr"].at[hp], b["gqz"].at[c], ss["gqcol"].at[hp], rs["gqcol"].at[c], {"col": hp})
            lc = loc(4, b["gqr"].at[hp], b["gqz"].at[c])
            gq_col.append((hp, cp, lc))
        @pl.when(par)
        def _():
            for q in range(R):
                cp = remote(b["gq"].at[0], b["gqr"].at[q], ss["gqrow"].at[0], rs["gqrow"].at[q], {"row": q})
                pl.when(q != r)(cp.wait_recv)
        for q, cp, lc in gq_out:
            pl.when(q != r)(cp.wait_send)
            pl.when(q == r)(lc.wait)
        @pl.when(par)
        def _():
            for ap in range(1, S):
                for hp in range(HB):
                    b["gqr"][hp] = (b["gqr"][hp].astype(F32) + b["gqr"][ap * HB + hp].astype(F32)).astype(BF)
            for hp, cp, lc in gq_col:
                pl.when(hp != c)(cp.start)
                pl.when(hp == c)(lc.start)
        rqu = second_q(R - 1, zqu, "guq", "tuq", "ruq")
        settle(lcl)
        b["l1"][...] = whole(l0[...], b["lz"], C - 1)
        lrw = [remote(b["l1"], b["lr"].at[r], ss["lrow"].at[k - 1], rs["lrow"].at[r], {"row": peer(k)}) for k in range(1, R)]
        run(*lrw)
        b["lr"][r] = b["l1"][...]
        settle(er + uc)
        b["e1"][...] = whole(b["eb"][r], b["er"], R - 1)
        b["u1"][...] = whole(b["u0"][c], b["uz"], C - 1)
        ec = [snd("ecol", k - 1, b["e1"], b["ez"].at[k - 1], {"col": cpeer(k)}) for k in range(1, C)]
        ur = [snd("urow", k - 1, b["u1"], b["ur"].at[k - 1], {"row": peer(k)}) for k in range(1, R)]
        run(*ec, *ur)
        red_u.finish()
        rcu = scatter_p(1, pcol(b["gu"], fp), b["zu"])
        red_p.finish()
        rcp = scatter_p(2, lambda q: b["gp"].at[r, pl.ds(al(q * ph, ph), ph), :], b["zp"])

        red_x.middle()
        half_rows, half_cols = pl.ds(al(d * ph, ph), ph), pl.ds(al(d * fh, fh), fh)
        pcols, qcols2 = pl.ds(al(d * fh, 128), fp), pl.ds(al(d * fh + fp, 128), fq)
        settle(ox)
        o_loc.wait()
        settle(rqd + rqu)
        o["gdn"][:, qcols2] = total(b["tdq"][own_rows, :], b["rdq"], R - 1)
        o["gup"][:, qcols2] = total(b["tuq"][own_rows, :], b["ruq"], R - 1)
        settle(rcd + rcu + rcp)
        mycols = pl.ds(al(c * fp, fp), fp)
        o["gdn"][:, pcols] = total(b["gd"][own_rows, mycols], b["zd"], C - 1)
        o["gup"][:, pcols] = total(b["gu"][own_rows, mycols], b["zu"], C - 1)
        o["gpj"][half_rows, :] = total(b["gp"][r, pl.ds(al(c * ph, ph), ph), :], b["zp"], C - 1)
        fin = [snd("fin", 0, o["gdn"].at[:, half_cols], o["gdn"].at[:, half_cols], core),
               snd("fin", 1, o["gup"].at[:, half_cols], o["gup"].at[:, half_cols], core),
               snd("fin", 2, o["gpj"].at[half_rows, :], o["gpj"].at[half_rows, :], core)]
        run(*fin)
        settle(ec + ur)
        b["e2"][...] = whole(b["e1"][...], b["ez"], C - 1)
        b["u2"][...] = whole(b["u1"][...], b["ur"], R - 1)
        settle(lrw, got=False)
        for k in range(1, R):
            p = peer(k)
            remote(b["l1"], b["lr"].at[p], ss["lrow"].at[0], rs["lrow"].at[p], {"row": p}).wait_recv()
        t = b["lr"][c]
        for q in range(1, S):
            t = t + b["lr"][q * HB + c]
        b["l2"][...] = t
        sd = [snd("ed", 0, b["e2"], b["eo"], core), snd("ud", 0, b["u2"], b["uo"], core), snd("ld", 0, b["l2"], b["lo"], core)]
        run(*sd)
        gqf = snd("gqf", 0, o["gqw"], o["gqw"], core)
        @pl.when(par)
        def _():
            for hp, cp, lc in gq_col:
                pl.when(hp != c)(cp.wait_send)
                pl.when(hp == c)(lc.wait)
                inn = remote(b["gqr"].at[0], b["gqz"].at[hp], ss["gqcol"].at[0], rs["gqcol"].at[hp], {"col": hp})
                pl.when(hp != c)(inn.wait_recv)
            t = b["gqz"][0].astype(F32)
            for q in range(1, C):
                t = t + b["gqz"][q].astype(F32)
            o["gqw"][...] = t
            gqf.start()
        if relay:
            o["gin"][...] = red_x.total()
        elif S == 1:
            settle(pt)
            o["gin"][...] = total(b["part"][own_rows, :], b["pr"], R - 1)
        else:
            settle(pt)
            o["gin"][...] = jnp.zeros((fb, S * SEQ_LEN), F32)
            o["gin"][:, pl.ds(al(a * SEQ_LEN, SEQ_LEN), SEQ_LEN)] = b["part"][own_rows, :].astype(F32)
            for k in range(1, R):
                q = lax.rem(r + R - k, R) // HB
                cols = pl.ds(al(q * SEQ_LEN, SEQ_LEN), SEQ_LEN)
                o["gin"][:, cols] += b["pr"][k - 1].astype(F32)
        for cp in sd:
            cp.wait()
        o["sve"][...] = b["e2"][...] + b["eo"][...]
        o["svu"][...] = b["u2"][...] + b["uo"][...]
        o["svl"][...] = b["l2"][...] + b["lo"][...]
        for cp in fin:
            cp.wait()
        pl.when(par)(gqf.wait_send)
        pl.when(jnp.logical_not(par))(gqf.wait_recv)
        for go, cp in w_out:
            pl.when(go)(cp.wait_send)
        for q in range(R):
            pl.when((q % 2) == d)(w_fwd[q].wait_send)
        pl.when(jnp.logical_not(meta_self))(meta_out.wait_send)

    def dma(n):
        return pltpu.SemaphoreType.DMA((n,))

    sem = [dma(sems[g]) for g in first_sems] + [dma(n) for n in local.values()] + [dma(n) for n in sems.values()]
    limit = (59 if R == 4 else 61) << 20
    res = pl.pallas_call(
        body,
        out_shape=[pltpu.VMEM(*s) for s in outs.values()],
        in_specs=[pl.BlockSpec(memory_space=pl.ANY)] * len(any_in) + [pl.BlockSpec(memory_space=pltpu.VMEM)] * len(vmem_in),
        out_specs=[pl.BlockSpec(memory_space=pltpu.VMEM)] * len(outs),
        scratch_shapes=[pltpu.VMEM(*s) for s in bufs.values()] + sem,
        compiler_params=pltpu.CompilerParams(collective_id=0, has_side_effects=True, vmem_limit_bytes=limit),
        name="encoder_layer",
    )(*[args[n] for n in names_in])
    return dict(zip(outs, res))


def finish_call(nh, fb, fc, qw, res):
    big = ["gin", "gqw", "gup", "gdn", "gpj"]
    shapes = [struct(res[n].shape, F32) for n in big]
    rows = [fb] * 6 + [fc, qw]

    def body(*refs):
        src = refs[:5]
        out_ref, e_ref, u_ref, l_ref = refs[5:9]
        dst = refs[9:14]
        o_ref, t_ref = refs[14:16]
        vecs = refs[16:24]
        sem = refs[24]
        cps = [pltpu.make_async_copy(s, t, sem.at[j]) for j, (s, t) in enumerate(zip(src, dst))]
        run(*cps)
        o_ref[...] = out_ref[...].astype(F32)
        for j in range(6):
            vecs[j][...] = e_ref[j:j + 1, 0:fb]
        vecs[6][...] = u_ref[0, :]
        vecs[7][...] = l_ref[0, 0:qw]
        t_ref[...] = l_ref[1:1 + nh, 0:CONV]
        for cp in cps:
            cp.wait()

    A, V = pl.BlockSpec(memory_space=pl.ANY), pl.BlockSpec(memory_space=pltpu.VMEM)
    outs = shapes + [struct(res["out"].shape, F32), struct((nh, CONV), F32)] + [struct((1, n), F32) for n in rows[:6]] + [struct((n,), F32) for n in rows[6:]]
    return pl.pallas_call(
        body, out_shape=outs, in_specs=[V] * 9, out_specs=[A] * 5 + [V] * 10,
        scratch_shapes=[pltpu.SemaphoreType.DMA((5,))], name="outputs",
        compiler_params=pltpu.CompilerParams(vmem_limit_bytes=8 << 20),
    )(*[pltpu.with_memory_space_constraint(res[n], pltpu.VMEM) for n in big + ["out", "sve", "svu", "svl"]])


def make_shards(R, C):
    def shards(inputs, doc_ids, qkv_weight, qkv_bias, proj_weight, proj_bias, first_gain, first_shift,
               ffn_up, ffn_up_bias, ffn_down, ffn_down_bias, second_gain, second_shift, conv_kernel, cotangent):
        S = inputs.shape[1] // SEQ_LEN
        fb = inputs.shape[0]
        nh = conv_kernel.shape[0]
        qw = qkv_weight.shape[1]
        fc = ffn_up.shape[1]
        res = layer_call(R, C, S, fb, nh, fc, proj_weight.shape[0], qw, dict(
            x=inputs, cot=cotangent, wq=qkv_weight, wp=proj_weight, wu=ffn_up, wd=ffn_down, doc=doc_ids[None],
            taps=conv_kernel, g1=first_gain[None], s1=first_shift[None], g2=second_gain[None], s2=second_shift[None],
            qb=qkv_bias, ub=ffn_up_bias, pb=proj_bias, db=ffn_down_bias))
        gin, gqw, gup, gdn, gpj, out, taps, g1, b1, g2, pbias, dbias, b2, ubias, qbias = finish_call(nh, fb, fc, qw, res)
        return (out, gin, gqw, qbias, gpj, pbias.reshape(fb), g1.reshape(fb), b1.reshape(fb), gup,
                ubias, gdn, dbias.reshape(fb), g2.reshape(fb), b2.reshape(fb), taps)
    return shards


def solution(mesh):
    in_specs = (P("row", ("dp", "col")), P(("dp", "row")), P("row", "col"), P("col"), P("col", "row"), P("row"),
                P("row"), P("row"), P("row", "col"), P("col"), P("row", "col"), P("row"), P("row"), P("row"),
                P("col", None), P("row", ("dp", "col")))
    out_specs = (P("row", ("dp", "col")), P("row", ("dp", "col")), P("row", "col"), P("col"), P("col", "row"), P("row"),
                 P("row"), P("row"), P("row", "col"), P("col"), P("row", "col"), P("row"), P("row"), P("row"),
                 P("col", None))
    fn = make_shards(mesh.shape["row"], mesh.shape["col"])
    return jax.shard_map(fn, mesh=mesh, in_specs=in_specs, out_specs=out_specs, check_vma=False)
```

```python
import functools

import jax
import jax.numpy as jnp
from jax import lax
from jax.experimental import pallas as pl
from jax.experimental.pallas import tpu as pltpu
from jax.sharding import PartitionSpec as P

D = 768
HEAD_DIM = 64
SEQ_LEN = 1024
EPSILON = 1e-05
F32=jnp.float32; BF=jnp.bfloat16
HD=64; SEQ=1024; SEG=16; CONV=33; ITERS=6; L=64
NEG=-1e9

def dg(a,b,ca,cb):
    return lax.dot_general(a,b,(((ca,),(cb,)),((),())),preferred_element_type=F32)
def nn(a,b): return dg(a,b,1,0)
def nt(a,b): return dg(a,b,1,1)
def tn(a,b): return dg(a,b,0,0)
def split(x):
    hi=x.astype(BF); lo=(x-hi.astype(F32)).astype(BF)
    return hi,lo
def cat(hl): return jnp.concatenate(hl,axis=0)
def halves(x):
    n=x.shape[0]//2
    return x[:n]+x[n:]
def nn2(a,b): return halves(nn(cat(split(a)),b))
def nt2(a,b): return halves(nt(cat(split(a)),b))
def nn3(a,b):
    ah,al=split(a); bh,bl=split(b)
    return halves(nn(cat((ah,al)),bh))+nn(ah,bl)
def nt3(a,b):
    ah,al=split(a); bh,bl=split(b)
    return halves(nt(cat((ah,al)),bh))+nt(ah,bl)

def iota(shape,dim): return lax.broadcasted_iota(jnp.int32,shape,dim)
def avg_mat():
    return jnp.where((iota((L,SEQ),1)//SEG)==iota((L,SEQ),0),F32(1.0/SEG),F32(0)).astype(BF)
def pick_mat():
    return jnp.where(iota((L,SEQ),1)==iota((L,SEQ),0)*SEG,F32(1),F32(0)).astype(BF)

def skew(x,left):
    W=x.shape[1]
    j=iota(x.shape,0)
    for bit in range(7):
        m=1<<bit
        x=jnp.where((j&m)!=0,pltpu.roll(x,(W-m) if left else m,1),x)
    return x

def band(w_row):
    return skew(jnp.broadcast_to(pltpu.roll(w_row,128-CONV//2,1),(128,384)),False)

def span(bt):
    return max(bt-1,0),min(bt+2,SEQ//128)

def same_doc(docb_ref,doc_row,bt):
    lo,hi=span(bt)
    col=docb_ref[bt*128:(bt+1)*128,:]
    return jnp.concatenate([col==doc_row[:,n*128:(n+1)*128] for n in range(lo,hi)],axis=1)

def conv_fwd(nh,qkv_ref,docb_ref,doc_row,band_ref,acc_ref):
    for bt in range(SEQ//128):
        lo,hi=span(bt)
        same=same_doc(docb_ref,doc_row,bt)
        off=(lo-bt+1)*128
        for h in range(nh):
            b=h*3*HD+2*HD
            ct=jnp.where(same,band_ref[h,:,off:off+(hi-lo)*128],0.0)
            o=nt(qkv_ref[b:b+HD,lo*128:hi*128],cat(split(ct)))
            acc_ref[h*HD:(h+1)*HD,bt*128:(bt+1)*128]=o[:,:128]+o[:,128:]

def head_scores(h,qkv_ref,doc_row,land_row,land_col,k1_ref,k3_ref,k2_ref,ql_ref,kl_ref,sum_ref):
    b=h*3*HD
    q=qkv_ref[b:b+HD,:]; k=qkv_ref[b+HD:b+2*HD,:]; v=qkv_ref[b+2*HD:b+3*HD,:]
    at=avg_mat()
    ql=nt(at,q); kl=nt(at,k)
    ql_ref[h]=ql; kl_ref[h]=kl
    keep=land_col==doc_row
    s1=jnp.where(keep,nn2(kl,q)*0.125,NEG)
    e1=jnp.exp(s1-jnp.max(s1,axis=0,keepdims=True))
    k1_ref[h]=e1/jnp.sum(e1,axis=0,keepdims=True)
    s3=jnp.where(keep,nn2(ql,k)*0.125,NEG)
    e3=jnp.exp(s3-jnp.max(s3,axis=1,keepdims=True))
    k3=e3/jnp.sum(e3,axis=1,keepdims=True)
    k3_ref[h]=k3
    s2=jnp.where(land_col==land_row,nt3(ql,kl)*0.125,NEG)
    e2=jnp.exp(s2-jnp.max(s2,axis=1,keepdims=True))
    k2_ref[h]=e2/jnp.sum(e2,axis=1,keepdims=True)
    sum_ref[h]=nt2(k3,v)

def eye(): return jnp.where(iota((L,L),0)==iota((L,L),1),F32(1),F32(0))

def newton(nh,k2_ref,v_ref,p_ref,n1_ref,n2_ref,n3_ref):
    for h in range(nh):
        v_ref[0,h]=k2_ref[h].T*(1.0/L)
    def step(i,_):
        I=eye()
        P=[nn3(k2_ref[h],v_ref[i,h]) for h in range(nh)]
        N1=[7.0*I-P[h] for h in range(nh)]
        N2=[15.0*I-nn3(P[h],N1[h]) for h in range(nh)]
        N3=[13.0*I-nn3(P[h],N2[h]) for h in range(nh)]
        for h in range(nh):
            p_ref[i,h]=P[h]; n1_ref[i,h]=N1[h]; n2_ref[i,h]=N2[h]; n3_ref[i,h]=N3[h]
            v_ref[i+1,h]=nn3(0.25*v_ref[i,h],N3[h])
        return 0
    lax.fori_loop(0,ITERS,step,0)

def head_out(h,k1_ref,inv,sum_ref,mix_ref,acc_ref,att_ref):
    mixed=nn3(inv,sum_ref[h])
    mix_ref[h]=mixed
    mt=mixed.T
    k1=k1_ref[h]
    res=nn3(mt,k1)
    att_ref[h*HD:(h+1)*HD,:]=(res+acc_ref[h*HD:(h+1)*HD,:]).astype(BF)

def newton_bwd(nh,k2_ref,v_ref,p_ref,n1_ref,n2_ref,n3_ref,gv_ref,gk_ref):
    for h in range(nh):
        gk_ref[h]=jnp.zeros((L,L),F32)
    def step(j,_):
        i=ITERS-1-j
        H=range(nh)
        gV=[gv_ref[h] for h in H]; V=[v_ref[i,h] for h in H]
        VT=[V[h].T for h in H]; PT=[p_ref[i,h].T for h in H]
        gN3=[0.25*nn3(VT[h],gV[h]) for h in H]
        gVn=[0.25*nt3(gV[h],n3_ref[i,h]) for h in H]
        gN2=[-nn3(PT[h],gN3[h]) for h in H]
        gN1=[-nn3(PT[h],gN2[h]) for h in H]
        gP=[-nt3(gN3[h],n2_ref[i,h])-nt3(gN2[h],n1_ref[i,h])-gN1[h] for h in H]
        for h in H:
            gk_ref[h]+=nt3(gP[h],V[h])
            gv_ref[h]=gVn[h]+nn3(k2_ref[h].T,gP[h])
        return 0
    lax.fori_loop(0,ITERS,step,0)
    for h in range(nh):
        gk_ref[h]+=gv_ref[h].T*(1.0/L)

def conv_bwd(nh,qkv_ref,g_ref,docb_ref,doc_row,band_ref,gacc_ref,gband_ref):
    for bt in range(SEQ//128):
        lo,hi=span(bt)
        same=same_doc(docb_ref,doc_row,bt)
        off=(lo-bt+1)*128
        for h in range(nh):
            b=h*3*HD+2*HD
            lanes=slice(off,off+(hi-lo)*128)
            ct=jnp.where(same,band_ref[h,:,lanes],0.0)
            g=g_ref[h*HD:(h+1)*HD,bt*128:(bt+1)*128]
            gv=nn(jnp.concatenate([g,g],axis=1),cat(split(ct)))
            gb=jnp.where(same,tn(g,qkv_ref[b:b+HD,lo*128:hi*128]),0.0)
            rows=slice(h*HD,(h+1)*HD)
            if bt==0:
                gband_ref[h]=jnp.zeros((128,384),F32)
                gacc_ref[rows,0:256]=gv
            else:
                gacc_ref[rows,lo*128:(bt+1)*128]+=gv[:,:256]
                if hi>bt+1:
                    gacc_ref[rows,(bt+1)*128:hi*128]=gv[:,256:]
            gband_ref[h,:,lanes]+=gb

def tap_row(gband):
    x=skew(gband,True)
    return pltpu.roll(jnp.sum(x,axis=0,keepdims=True),384-(128-CONV//2),1)

def head_bwd1(h,qkv_ref,g_ref,k1_ref,k3_ref,sum_ref,mix_ref,inv,gv_ref,gs1_ref,gs3_ref,gacc_ref):
    b=h*3*HD
    v=qkv_ref[b+2*HD:b+3*HD,:]
    g=g_ref[h*HD:(h+1)*HD,:]
    k1=k1_ref[h]
    gmix=nt2(k1,g)
    gk1=nn2(mix_ref[h],g)
    gs1_ref[h]=k1*(gk1-jnp.sum(k1*gk1,axis=0,keepdims=True))
    gv_ref[h]=nt3(gmix,sum_ref[h])
    gsum=nn3(inv.T,gmix)
    k3=k3_ref[h]
    gk3=nn2(gsum,v)
    gs3_ref[h]=k3*(gk3-jnp.sum(k3*gk3,axis=1,keepdims=True))
    gacc_ref[h*HD:(h+1)*HD,:]+=nn3(gsum.T,k3)

def head_bwd2(h,qkv_ref,k2_ref,gk_ref,ql_ref,kl_ref,gs1_ref,gs3_ref,gacc_ref,out_ref):
    b=h*3*HD
    q=qkv_ref[b:b+HD,:]; k=qkv_ref[b+HD:b+2*HD,:]
    k2=k2_ref[h]; gk2=gk_ref[h]
    gs2=k2*(gk2-jnp.sum(k2*gk2,axis=1,keepdims=True))
    ql=ql_ref[h]; kl=kl_ref[h]
    gs1=gs1_ref[h]; gs3=gs3_ref[h]
    gkl=nt2(gs1,q)+nn3(gs2.T,ql)
    gql=nt2(gs3,k)+nn3(gs2,kl)
    at=avg_mat()
    gq=(nn3(kl.T,gs1)+nn2(gql.T,at))*0.125
    gk=(nn3(ql.T,gs3)+nn2(gkl.T,at))*0.125
    out_ref[b:b+HD,:]=gq.astype(BF)
    out_ref[b+HD:b+2*HD,:]=gk.astype(BF)
    out_ref[b+2*HD:b+3*HD,:]=gacc_ref[h*HD:(h+1)*HD,:].astype(BF)

MESH = pl.DeviceIdType.MESH


def struct(shape, dtype):
    return jax.ShapeDtypeStruct(shape, dtype)


def remote(src, dst, ss, rs, dev):
    return pltpu.make_async_remote_copy(
        src_ref=src, dst_ref=dst, send_sem=ss, recv_sem=rs, device_id=dev, device_id_type=MESH
    )


def run(*copies):
    for cp in copies:
        cp.start()


def settle(cps, sent=True, got=True):
    for cp in cps:
        if sent:
            cp.wait_send()
        if got:
            cp.wait_recv()


def when(cond, fn):
    if cond is None:
        fn()
    else:
        pl.when(cond)(fn)


def al(x, n):
    return pl.multiple_of(x, n)


def gauss(x):
    e = jnp.exp(-0.5 * x * x)
    t = 1.0 / (1.0 + jnp.abs(x) * 0.23164190)
    p = t * 0.5307027145 - 0.7265760135
    p = (p * t + 0.7107068705) * t - 0.1422483680
    q = (p * t + 0.1274147960) * t * e
    return jnp.where(x >= 0, 1.0 - q, q), e * 0.3989422804014327


def norm_forward(residual, gain, shift):
    average = jnp.mean(residual, axis=1, keepdims=True)
    spread = jnp.mean(residual * residual, axis=1, keepdims=True) - average * average
    scaling = lax.rsqrt(spread + EPSILON)
    normed = (residual - average) * scaling
    return normed * gain + shift, normed, scaling


def norm_backward(upstream, gain, normed, scaling):
    scaled = upstream * gain
    mean_scaled = jnp.mean(scaled, axis=1, keepdims=True)
    crossed = jnp.mean(scaled * normed, axis=1, keepdims=True)
    return scaling * (scaled - mean_scaled - normed * crossed)


def tsum(x):
    return jnp.sum(x, axis=0, keepdims=True)


class Pool:
    def __init__(self, entries):
        self.at = entries


class RowGather:
    def __init__(self, snd, group, base, ways, place, r, R, cond=None):
        n = len(ways)
        self.cond, self.n, self.relay, self.ways = cond, n, R == 4, ways
        if self.relay:
            X, Y = lax.bitwise_xor(r, 1), lax.bitwise_xor(r, 2)
            self.own = []
            self.fwd = []
            for j in range(n):
                mine = place(j, r)
                self.own.append((snd(group, base + 2 * j, mine, mine, {"row": X}),
                                 snd(group, base + 2 * j + 1, mine, mine, {"row": Y})))
                src = place(j, Y if ways[j] else X)
                self.fwd.append(snd(group, base + 2 * n + j, src, src, {"row": X if ways[j] else Y}))
        else:
            self.own = [tuple(snd(group, base + j * (R - 1) + k - 1, place(j, r), place(j, r), {"row": lax.rem(r + k, R)})
                              for k in range(1, R)) for j in range(n)]

    def start(self):
        def go():
            if self.relay:
                for j, cps in enumerate(self.own):
                    cps[self.ways[j]].start()
                for j, cps in enumerate(self.own):
                    cps[1 - self.ways[j]].start()
            else:
                for cps in self.own:
                    run(*cps)
        when(self.cond, go)

    def forward(self):
        if self.relay:
            def go():
                for j in range(self.n):
                    self.own[j][self.ways[j]].wait_recv()
                    self.fwd[j].start()
            when(self.cond, go)

    def finish(self):
        def go():
            for j in range(self.n):
                if self.relay:
                    self.own[j][1 - self.ways[j]].wait_recv()
                    self.fwd[j].wait_recv()
                    self.fwd[j].wait_send()
                else:
                    for cp in self.own[j]:
                        cp.wait_recv()
                for cp in self.own[j]:
                    cp.wait_send()
        when(self.cond, go)


class RowReduce:
    def __init__(self, snd, group, block, recv, lanes, r, R, axis="row", base=0):
        self.block, self.recv, self.lanes, self.r, self.R = block, recv, lanes, r, R
        self.relay = R == 4
        n = len(lanes)
        if self.relay:
            X, Y, Z = lax.bitwise_xor(r, 1), lax.bitwise_xor(r, 2), lax.bitwise_xor(r, 3)
            self.one, self.two, self.mids = [], [], []
            for j, ln in enumerate(lanes):
                P, Q = (X, Y) if j == 0 else (Y, X)
                self.one.append([snd(group, base + 3 * j, block(Z, ln), recv(1, ln), {axis: P}),
                                 snd(group, base + 3 * j + 1, block(P, ln), recv(0, ln), {axis: P})])
                self.two.append(snd(group, base + 3 * j + 2, block(Q, ln), recv(2, ln), {axis: Q}))
                self.mids.append(Q)
        else:
            self.all = [snd(group, base + k - 1, block(lax.rem(r + k, R), None), recv(k - 1, None), {axis: lax.rem(r + k, R)})
                        for k in range(1, R)]

    def start(self):
        if self.relay:
            for cps in self.one:
                cps[0].start()
        else:
            run(*self.all)

    def start_near(self):
        if self.relay:
            for cps in self.one:
                cps[1].start()

    def middle(self):
        if self.relay:
            for j, ln in enumerate(self.lanes):
                self.one[j][0].wait_recv()
                ref = self.block(self.mids[j], ln)
                ref[...] = (ref[...].astype(F32) + self.recv(1, ln)[...].astype(F32)).astype(BF)
                self.two[j].start()

    def total(self):
        if self.relay:
            for cps in self.one:
                settle(cps, got=False)
                cps[1].wait_recv()
            settle(self.two)
            slots = (0, 2)
        else:
            settle(self.all)
            slots = range(self.R - 1)
        t = self.block(self.r, None)[...].astype(F32)
        for k in slots:
            t = t + self.recv(k, None)[...].astype(F32)
        return t

    def finish(self):
        self.block(self.r, None)[...] = self.total().astype(BF)


class LineGather:
    def __init__(self, snd, group, n, place, c, C):
        self.C, self.c, self.n = C, c, n
        m = (C - 1) * n
        self.up = [[snd(group, k * n + j, place(j, c - k), place(j, c - k), {"col": c + 1}) for j in range(n)] for k in range(C - 1)]
        self.dn = [[snd(group, m + k * n + j, place(j, c + k), place(j, c + k), {"col": c - 1}) for j in range(n)] for k in range(C - 1)]

    def up_ok(self, k):
        return (self.c >= k) & (self.c < self.C - 1)

    def dn_ok(self, k):
        return (self.c + k <= self.C - 1) & (self.c > 0)

    def start(self):
        pl.when(self.up_ok(0))(lambda: run(*self.up[0]))
        pl.when(self.dn_ok(0))(lambda: run(*self.dn[0]))

    def step(self, k):
        def got(cps, nxt, ok):
            def go():
                for j in range(self.n):
                    cps[j].wait_recv()
                    if nxt is not None:
                        pl.when(ok)(lambda: nxt[j].start())
            return go
        more = k < self.C - 1
        pl.when(self.c >= k)(got(self.up[k - 1], self.up[k] if more else None, self.up_ok(k) if more else None))
        pl.when(self.c + k <= self.C - 1)(got(self.dn[k - 1], self.dn[k] if more else None, self.dn_ok(k) if more else None))

    def forward(self, k):
        def on(cps, nxt):
            def go():
                for j in range(self.n):
                    cps[j].wait_recv()
                    nxt[j].start()
            return go
        pl.when(self.up_ok(k))(on(self.up[k - 1], self.up[k]))
        pl.when(self.dn_ok(k))(on(self.dn[k - 1], self.dn[k]))

    def land(self):
        for k in range(1, self.C):
            pl.when(self.c == self.C - 1)(lambda: settle(self.up[k - 1], sent=False))
            pl.when(self.c == 0)(lambda: settle(self.dn[k - 1], sent=False))

    def drain(self):
        for k in range(self.C - 1):
            pl.when(self.up_ok(k))(lambda: settle(self.up[k], got=False))
            pl.when(self.dn_ok(k))(lambda: settle(self.dn[k], got=False))


def layer_call(R, C, S, fb, nh, fc, pb, qw, args):
    HB = R // S
    QT = SEQ_LEN // HB
    FF = fc * C
    fh, ph = fc // 2, pb // 2
    fq = fh // 3 // 128 * 128
    fp = fh - fq
    upw, uqw, dpw, dqw = fp, fq, fq, fp
    hb = nh * HD
    fbp = -(-fb // 128) * 128
    hp = -(-fb // 32) * 16
    CH = 256
    FH = FF // 2
    relay = R == 4
    NR = 3 if relay else R - 1
    PT = nh + 1
    V = pltpu.VMEM
    small = (nh, L, L)
    any_in = ["x", "cot", "wq", "wp", "wu", "wd"]
    vmem_in = ["doc", "taps", "g1", "s1", "g2", "s2", "qb", "ub", "pb", "db"]
    names_in = any_in + vmem_in
    outs = dict(
        out=((fb, S * SEQ_LEN), BF), gin=((fb, S * SEQ_LEN), F32), gqw=((fb, qw), F32), gup=((fb, fc), F32),
        gdn=((fb, fc), F32), gpj=((pb, fb), F32), sve=((8, fbp), F32), svu=((1, fc), F32), svl=((PT, D), F32))
    bufs = dict(
        xg=((D, SEQ_LEN), BF), wg=((R, fb, qw), BF), ms=((8, SEQ_LEN), F32), mt=((8, SEQ_LEN), F32),
        rs=((8, fbp), F32), rp=((R, 8, fbp), F32), cs=((8, fc), F32), cp=((C, 8, fc), F32),
        cg=((D, QT), BF), wpf=((R, D, fb), BF), wuf=((D, FF), BF), wdf=((D, FF), BF),
        qkv=((3 * hb, SEQ_LEN), BF), k1=((nh, L, SEQ_LEN), F32), k3=((nh, L, SEQ_LEN), F32), k2=(small, F32),
        ql=(small, F32), kl=(small, F32), sm=(small, F32), mix=(small, F32), nv=((ITERS + 1,) + small, F32),
        np_=((ITERS,) + small, F32), n1=((ITERS,) + small, F32), n2=((ITERS,) + small, F32), n3=((ITERS,) + small, F32),
        docb=((SEQ_LEN, 128), F32), band=((nh, 128, 384), F32), gband=((nh, 128, 384), F32), acc=((hb, SEQ_LEN), F32), att=((hb, SEQ_LEN), BF), attq=((D, QT), BF),
        resT=((D, QT), F32), prow=((8, D), F32), hidden=((QT, D), F32), hid=((QT, D), BF), nm1=((QT, D), F32),
        sc1=((QT, 1), F32), act=((QT, FF), BF), dact=((QT, FF), F32), res2=((QT, D), F32), gdown=((QT, D), BF),
        gpre=((QT, FF), BF), gattoT=((D, QT), BF), outT=((D, QT), BF), gatt=((hb, SEQ_LEN), BF),
        hid_o=((QT, D), BF), gdown_o=((QT, D), BF), gattoT_o=((D, QT), BF), att_o=((C * ph, QT), BF),
        act_o=((QT, C * fh), BF), gpre_o=((QT, C * fh), BF),
        gu=((D, C * fp), BF), guq=((D, C * fq), BF), gd=((D, C * fp), BF), gp=((R, C * ph, fb), BF), gdq=((D, C * fq), BF),
        ru=((NR, fb, C * fp), BF), rd=((NR, fb, C * fp), BF), rpj=((NR, C * ph, fb), BF),
        zu=((C - 1, fb, fp), BF), zd=((C - 1, fb, fp), BF), zp=((C - 1, ph, fb), BF),
        zdq=((C - 1, D, fq), BF), zuq=((C - 1, D, fq), BF), tuq=((D, fq), BF), tdq=((D, fq), BF),
        rdq=((R - 1, fb, fq), BF), ruq=((R - 1, fb, fq), BF),
        gv=(small, F32), gk=(small, F32),
        part=((D, SEQ_LEN), BF), pr=((R - 1, fb, SEQ_LEN), BF),
        gq=((R, 2, hp, qw), BF), gqo=((R, hp, qw), BF), gqr=((R, hp, qw), BF), gqz=((C - 1, hp, qw), BF),
        e0=((8, D), F32), eb=((R, 8, fbp), F32), er=((R - 1, 8, fbp), F32), e1=((8, fbp), F32), ez=((C - 1, 8, fbp), F32),
        e2=((8, fbp), F32), eo=((8, fbp), F32), u0=((C, 1, fc), F32), uz=((C - 1, 1, fc), F32), u1=((1, fc), F32),
        ur=((R - 1, 1, fc), F32), u2=((1, fc), F32), uo=((1, fc), F32), l0=((PT, D), F32), lz=((C - 1, PT, D), F32),
        l1=((PT, D), F32), lr=((R, PT, D), F32), l2=((PT, D), F32), lo=((PT, D), F32))
    NRP = 1 + 2 * (C - 1)
    sems = dict(
        x=2 * (R - 1), cot=R - 1, rowp=R - 1, colp=C - 1, meta=1, ws=S * C, wr=R, wd2=R,
        zU=4 * (C - 1), zD=2 * (C - 1), rU=C * 2 * (R - 1), rD=C * (R - 1), rQ=R - 1, rS=R - 1, zQ=2 * (C - 1), zR=2 * (C - 1),
        cU=2 * C, cD=C, cQ=2 * C,
        att=HB - 1, gatt=HB - 1, ex=5 + C, ru=max(6, R - 1), rd=max(6, R - 1), rp=max(6, R - 1), rcol=3 * (C - 1),
        zq=2 * (C - 1), rq=2 * (R - 1), part=max(6, R - 1), outx=R - 1,
        gqd=1, gqrow=R - 1, gqcol=C - 1, gqf=1, erow=R - 1, ecol=C - 1, ed=1, ucol=C - 1, urow=R - 1, ud=1, lcol=C - 1, lrow=R, ld=1, fin=3)
    local = dict(loc=21)

    late_sems = ["ru", "rd", "rp", "rcol", "zq", "rq", "part", "gqd", "gqrow", "gqcol", "gqf", "erow", "ecol", "ed", "ucol",
                 "urow", "ud", "lcol", "lrow", "ld", "fin"]
    first_sems = [g for g in sems if g not in late_sems]

    def body(*refs):
        n = len(names_in)
        i = dict(zip(names_in, refs[:n]))
        o = dict(zip(outs, refs[n:n + len(outs)]))
        k = n + len(outs)
        b = dict(zip(bufs, refs[k:k + len(bufs)]))
        k += len(bufs)
        ss = dict(zip(first_sems + list(local), refs[k:]))
        k += len(first_sems) + len(local)
        rs = dict(zip(sems, refs[k:]))
        free = [ss[g].at[j] for g in ("rU", "rD", "zU", "zD", "zQ", "zR", "cU", "cD", "cQ", "rQ", "rS", "x") for j in range(sems[g])]
        for g in late_sems:
            ss[g] = Pool(free[:sems[g]])
            free = free[sems[g]:]
        d = lax.axis_index("dp")
        r = lax.axis_index("row")
        c = lax.axis_index("col")
        a, h = r // HB, lax.rem(r, HB)
        core = {"dp": 1 - d}

        def snd(group, slot, src, dst, dev):
            return remote(src, dst, ss[group].at[slot], rs[group].at[slot], dev)

        def loc(slot, src, dst):
            return pltpu.make_async_copy(src, dst, ss["loc"].at[slot])

        def fr(ref, q):
            return ref.at[pl.ds(al(q * fb, fb), fb), :]

        def peer(k):
            return lax.rem(r + k, R)

        def cpeer(k):
            return lax.rem(c + k, C)

        own = c == h
        bar = pltpu.get_barrier_semaphore()
        for k in range(1, R):
            pl.semaphore_signal(bar, inc=1, device_id={"row": peer(k)}, device_id_type=MESH)
        for k in range(1, C):
            pl.semaphore_signal(bar, inc=1, device_id={"col": cpeer(k)}, device_id_type=MESH)
        pl.semaphore_signal(bar, inc=1, device_id=core, device_id_type=MESH)
        for q in range(R):
            @pl.when(jnp.logical_not(own & (r == q)))
            def _():
                pl.semaphore_signal(bar, inc=1, device_id={"row": q, "col": h}, device_id_type=MESH)
        half = fb // 2

        def xcols(q, part=None):
            rows = slice(None) if part is None else pl.ds(part * half, half)
            return i["x"].at[rows, pl.ds(al(q // HB * SEQ_LEN, SEQ_LEN), SEQ_LEN)]

        x_loc = loc(0, xcols(r), fr(b["xg"], r))
        x_loc.start()

        def cols_of(col, first, width):
            return pl.ds(al(d * (FF // 2) + col * fh + first, 128), width)

        def wide(ref, row, col, first, width):
            return ref.at[pl.ds(al(row * fb, fb), fb), cols_of(col, first, width)]

        def narrow(ref, row, col):
            return ref.at[row, pl.ds(al(col * pb + d * ph, ph), ph), :]

        bulk_loc = [loc(1, i["wu"].at[:, pl.ds(al(d * fh, fh), fh)], wide(b["wuf"], r, c, 0, fh)),
                    loc(2, i["wd"].at[:, pl.ds(al(d * fh, fh), fh)], wide(b["wdf"], r, c, 0, fh)),
                    loc(3, i["wp"].at[pl.ds(al(d * ph, ph), ph), :], narrow(b["wpf"], r, c))]
        run(*bulk_loc)
        cot_rows = min(fb, 64)
        stage = []
        for s in range(S):
            for f in range(0, fb, cot_rows):
                m = len(stage)
                buf = b["k1"].at[m] if m < nh else b["k3"].at[m - nh]
                stage.append((s, f, m, loc(4 + m, i["cot"].at[f:f + cot_rows, s * SEQ_LEN:(s + 1) * SEQ_LEN], buf.at[0:cot_rows, :])))
        run(*[t[3] for t in stage])
        b["ms"][...] = jnp.zeros((8, SEQ_LEN), F32)
        b["ms"][0:1, :] = i["doc"][...].astype(F32)
        b["ms"][1:1 + nh, 0:CONV] = i["taps"][...]
        b["ms"][1 + nh:2 + nh, 0:qw] = i["qb"][...].astype(F32).reshape(1, qw)
        b["rs"][...] = jnp.zeros((8, fbp), F32)
        for j, name in enumerate(("g1", "s1", "g2", "s2")):
            b["rs"][j:j + 1, 0:fb] = i[name][...]
        b["rs"][4:5, 0:fb] = i["pb"][...].astype(F32).reshape(1, fb)
        b["rs"][5:6, 0:fb] = i["db"][...].astype(F32).reshape(1, fb)
        b["cs"][...] = jnp.zeros((8, fc), F32)
        b["cs"][0:1, :] = i["ub"][...].astype(F32).reshape(1, fc)
        for cp in bulk_loc:
            cp.wait()
        x_loc.wait()
        pl.semaphore_wait(bar, R - 1 + C - 1 + 1 + S * C - jnp.where(own, 1, 0))

        dst_row, dst_col = lax.rem(r, S) * HB + c, r // S
        meta_self = (dst_row == r) & (dst_col == c)
        meta_out = snd("meta", 0, b["ms"], b["mt"], {"row": dst_row, "col": dst_col})
        meta_in = snd("meta", 0, b["ms"], b["mt"], {"row": c * S + a, "col": h})
        meta_loc = loc(17, b["ms"], b["mt"])
        pl.when(jnp.logical_not(meta_self))(meta_out.start)
        pl.when(meta_self)(meta_loc.start)

        def place_u(col):
            return lambda j, row: narrow(b["wpf"], row, col) if j else wide(b["wuf"], row, col, 0, upw)

        def place_d(col):
            return lambda j, row: wide(b["wdf"], row, col, 0, dpw)

        zU = LineGather(snd, "zU", 2, lambda j, col: place_u(col)(j, r), c, C)
        zD = LineGather(snd, "zD", 1, lambda j, col: place_d(col)(j, r), c, C)
        at_cols = [(None, c)]
        for k in range(1, C):
            at_cols += [(c >= k, c - k), (c + k <= C - 1, c + k)]
        rU = [RowGather(snd, "rU", col * 2 * (R - 1), (0, 1), place_u(col), r, R, cond) for cond, col in at_cols]
        rD = [RowGather(snd, "rD", col * (R - 1), (1,), place_d(col), r, R, cond) for cond, col in at_cols]
        rQ = RowGather(snd, "rQ", 0, (0,), lambda j, row: wide(b["wuf"], row, c, upw, uqw), r, R)
        rS = RowGather(snd, "rS", 0, (1,), lambda j, row: wide(b["wdf"], row, c, dpw, dqw), r, R)
        rQ.start()
        zQ = LineGather(snd, "zQ", 1, lambda j, col: b["wuf"].at[:, cols_of(col, upw, uqw)], c, C)
        zR = LineGather(snd, "zR", 1, lambda j, col: b["wdf"].at[:, cols_of(col, dpw, dqw)], c, C)
        zU.start()
        zD.start()
        if relay:
            xg = RowGather(snd, "x", 0, (0, 1), lambda j, q: b["xg"].at[pl.ds(al(q * fb + j * half, half), half), :], r, R)
            xg.start()
        else:
            xs = [snd("x", k - 1, xcols(peer(k)), fr(b["xg"], r), {"row": peer(k)}) for k in range(1, R)]
            run(*xs)
        par = lax.rem(r, 2) == d
        w_out = []
        for ap in range(S):
            for cq in range(C):
                t = ap * HB + c
                go = par & jnp.logical_not((t == r) & (c == cq))
                cp = remote(i["wq"], b["wg"].at[r], ss["ws"].at[ap * C + cq], rs["wr"].at[r], {"row": t, "col": cq})
                w_out.append((go, cp))
        for go, cp in w_out:
            pl.when(go)(cp.start)
        w_loc = loc(16, i["wq"], b["wg"].at[r])
        pl.when(own & par)(w_loc.start)
        def cot_at(s, cols):
            return b["gpre"].at[pl.ds(al(s // 3 * fb, fb), fb), cols]

        for s, f, m, cp in stage:
            cp.wait()
            buf = b["k1"].at[m] if m < nh else b["k3"].at[m - nh]
            b["gpre"][s // 3 * fb + f:s // 3 * fb + f + cot_rows, s % 3 * SEQ_LEN:(s % 3 + 1) * SEQ_LEN] = buf[0:cot_rows, :].astype(BF)

        def cot_src(q):
            s = q // HB
            return cot_at(s, pl.ds(al(lax.rem(s, 3) * SEQ_LEN + lax.rem(q, HB) * QT, QT), QT))

        zU.step(1)
        if relay:
            xg.forward()
        rQ.forward()
        rS.start()
        zD.forward(1)
        pl.when(jnp.logical_not(meta_self))(meta_in.wait_recv)
        pl.when(meta_self)(meta_loc.wait)
        doc_row = b["mt"][0:1, :]
        rowb = jnp.broadcast_to(doc_row, (8, SEQ_LEN)).astype(BF)
        pick = pick_mat()
        land_row = nt(rowb, pick)[0:1]
        land_col = nt(pick, rowb)[:, 0:1]
        for hh in range(nh):
            b["band"][hh] = band(b["mt"][1 + hh:2 + hh, 0:384])
        one = jnp.where(iota((8, 128), 0) == 0, 1.0, 0.0).astype(BF)
        b["docb"][...] = tn(rowb, one)
        for k in range(2, C - 1):
            zU.step(k)
            zD.forward(k)
        rQ.finish()
        zQ.start()
        rS.forward()
        if relay:
            xg.finish()
        else:
            settle(xs)
        for m in range(2 * C - 3):
            rU[m].start()
        gs = [snd("cot", k - 1, cot_src(peer(k)), fr(b["cg"], r), {"row": peer(k)}) for k in range(1, R)]
        g_loc = loc(18, cot_src(r), fr(b["cg"], r))
        ps = [snd("rowp", k - 1, b["rs"], b["rp"].at[r], {"row": peer(k)}) for k in range(1, R)]
        p_loc = loc(19, b["rs"], b["rp"].at[r])
        cs = [snd("colp", k - 1, b["cs"], b["cp"].at[c], {"col": cpeer(k)}) for k in range(1, C)]
        c_loc = loc(20, b["cs"], b["cp"].at[c])
        run(*ps, p_loc, *cs, c_loc)
        w_fwd = [snd("wd2", q, b["wg"].at[q], b["wg"].at[q], core) for q in range(R)]
        for q in range(R):
            mine_q = (q % 2) == d
            here_q = own & (r == q)
            w_in = remote(i["wq"], b["wg"].at[q], ss["ws"].at[0], rs["wr"].at[q], {"row": q, "col": h})
            pl.when(mine_q & here_q)(w_loc.wait)
            pl.when(mine_q & jnp.logical_not(here_q))(w_in.wait_recv)
            pl.when(mine_q)(w_fwd[q].start)
        for q in range(R):
            pl.when((q % 2) != d)(w_fwd[q].wait_recv)
        qb = jnp.where(iota((8, qw), 0) == 1 + nh, b["mt"][:, 0:qw], 0.0).astype(BF)
        acc = tn(qb, jnp.ones((8, SEQ_LEN), BF))
        for q in range(R):
            acc = acc + tn(b["wg"][q], b["xg"][q * fb:(q + 1) * fb, :])
        b["qkv"][...] = acc.astype(BF)

        def scores(hh):
            head_scores(hh, b["qkv"], doc_row, land_row, land_col, b["k1"], b["k3"], b["k2"], b["ql"], b["kl"], b["sm"])

        for hh in range(nh):
            scores(hh)
        zQ.forward(1)
        rS.finish()
        zR.start()
        zU.step(C - 1)
        for m in range(2 * C - 3, NRP):
            rU[m].start()
        newton(nh, b["k2"], b["nv"], b["np_"], b["n1"], b["n2"], b["n3"])
        for k in range(2, C - 1):
            zQ.forward(k)
        for m in range(3):
            rU[m].forward()
        conv_fwd(nh, b["qkv"], b["docb"], doc_row, b["band"], b["acc"])
        for hh in range(nh):
            head_out(hh, b["k1"], b["nv"][ITERS, hh], b["sm"], b["mix"], b["acc"], b["att"])

        def group(k):
            return lax.rem(h + k, HB)

        def hrows(ref, q):
            return ref.at[pl.ds(al(q * hb, hb), hb), :]

        def tcols(ref, q):
            return ref.at[:, pl.ds(al(q * QT, QT), QT)]

        at = [snd("att", k - 1, tcols(b["att"], group(k)), hrows(b["attq"], h), {"row": a * HB + group(k)})
              for k in range(1, HB)]
        run(*at)
        at_loc = loc(0, tcols(b["att"], h), hrows(b["attq"], h))
        at_loc.start()
        for m in range(3, NRP):
            rU[m].forward()
        zD.land()
        for m in range(NRP):
            rD[m].start()
        zR.forward(1)
        for cp in ps + cs:
            cp.wait()
        for cp in (p_loc, c_loc):
            cp.wait()
        prow = jnp.zeros((8, D), F32)
        for q in range(R):
            piece = jnp.concatenate([b["rp"][q], jnp.zeros((8, D - fbp), F32)], axis=1)
            prow = prow + (pltpu.roll(piece, q * fb, 1) if q else piece)
        b["prow"][...] = prow
        def cross(group, slot, cond, *refs):
            cps = [snd(group, slot + j, ref, ref, core) for j, ref in enumerate(refs)]
            when(cond, lambda: run(*cps))
            return cond, cps

        crossed, later = [], []
        for m, (cond, col) in enumerate(at_cols):
            rU[m].finish()
            crossed.append(cross("cU", 2 * col, cond, b["wuf"].at[:, cols_of(col, 0, upw)],
                                 b["wpf"].at[:, pl.ds(al(col * pb + d * ph, ph), ph), :]))
        zQ.land()
        for k in range(2, C - 1):
            zR.forward(k)
        for m, (cond, col) in enumerate(at_cols):
            crossed.append(cross("cQ", 2 * col, cond, b["wuf"].at[:, cols_of(col, upw, uqw)]))
        settle(at)
        at_loc.wait()
        for cond, cps in crossed:
            when(cond, lambda: settle(cps))

        for q in range(R):
            t = tn(b["wpf"][q], b["attq"][...])
            b["resT"][q * fb:(q + 1) * fb, :] = t + b["xg"][q * fb:(q + 1) * fb, pl.ds(al(h * QT, QT), QT)].astype(F32)
        res1 = b["resT"][...].T + b["prow"][4:5, :]
        hidden, nm1, sc1 = norm_forward(res1, b["prow"][0:1, :], b["prow"][1:2, :])
        b["hidden"][...] = hidden
        b["nm1"][...] = nm1
        b["sc1"][...] = sc1
        b["hid"][...] = hidden.astype(BF)
        ex_hid = snd("ex", 0, b["hid"], b["hid_o"], core)
        ex_hid.start()

        def up(j, _):
            cols = pl.ds(al(j * fh, 128), fh)
            bias = b["cp"][lax.rem(j, C), 0:1, pl.ds(al(j // C * fh, 128), fh)]
            pre = nn(b["hid"][...], b["wuf"][:, cols]) + bias
            cdf, pdf = gauss(pre)
            b["act"][:, cols] = (pre * cdf).astype(BF)
            b["dact"][:, cols] = cdf + pre * pdf
            return 0

        lax.fori_loop(0, C, up, 0)
        for m in range(2 * C - 3):
            rD[m].forward()
        lax.fori_loop(C, 2 * C, up, 0)
        for m in range(2 * C - 3, NRP):
            rD[m].forward()
        run(*gs, g_loc)
        zR.land()
        for m, (cond, col) in enumerate(at_cols):
            later.append(cross("cQ", 2 * col + 1, cond, b["wdf"].at[:, cols_of(col, dpw, dqw)]))
        other_half = pl.ds(al((1 - d) * FH, 128), FH)
        ex_act = [snd("ex", 3, b["act"].at[:, other_half], b["act_o"], core)]
        run(*ex_act)
        for m, (cond, col) in enumerate(at_cols):
            rD[m].finish()
            later.append(cross("cD", col, cond, b["wdf"].at[:, cols_of(col, 0, dpw)]))
        for cond, cps in later:
            when(cond, lambda: settle(cps))
        for line in (zU, zD, zQ, zR):
            line.drain()

        def down(j, _):
            cols = pl.ds(al(j * CH, CH), CH)
            b["res2"][:, cols] = b["hidden"][:, cols] + nt(b["act"][...], b["wdf"][cols, :]) + b["prow"][5:6, cols]
            return 0

        lax.fori_loop(0, D // CH, down, 0)
        gain2 = b["prow"][2:3, :]
        out, nm2, sc2 = norm_forward(b["res2"][...], gain2, b["prow"][3:4, :])
        settle(gs)
        g_loc.wait()
        ups = b["cg"][...].astype(F32).T
        e0 = b["e0"]
        e0[...] = jnp.zeros((8, D), F32)
        e0[2:3, :] = tsum(ups * nm2)
        e0[5:6, :] = tsum(ups)
        gres2 = norm_backward(ups, gain2, nm2, sc2)
        b["res2"][...] = gres2
        b["gdown"][...] = gres2.astype(BF)
        e0[4:5, :] = tsum(b["gdown"][...].astype(F32))
        ex_gdown = snd("ex", 1, b["gdown"], b["gdown_o"], core)
        ex_gdown.start()
        b["outT"][...] = out.T.astype(BF)
        ox = [snd("outx", k - 1, fr(b["outT"], peer(k)), tcols(o["out"], a * HB + h), {"row": peer(k)}) for k in range(1, R)]
        o_loc = loc(1, fr(b["outT"], r), tcols(o["out"], a * HB + h))
        run(*ox, o_loc)

        def gact(j, _):
            cols = pl.ds(al(j * fh, 128), fh)
            g = nn(b["gdown"][...], b["wdf"][:, cols])
            gp = (g * b["dact"][:, cols]).astype(BF)
            b["gpre"][:, cols] = gp
            b["u0"][lax.rem(j, C), 0:1, pl.ds(al(j // C * fh, 128), fh)] = tsum(gp.astype(F32))
            return 0

        lax.fori_loop(0, C, gact, 0)
        def grad_block(q, mine, mine_w, other, other_w, dst, dst_q):
            to = slice(q * fh, (q + 1) * fh)
            t = tn(b[mine][...], b[mine_w][:, cols_of(q, 0, fh)]) + tn(b[other][...], b[other_w][:, to])
            b[dst][:, q * fp:(q + 1) * fp] = t[:, :fp].astype(BF)
            b[dst_q][:, q * fq:(q + 1) * fq] = t[:, fp:].astype(BF)

        def along_col(group, base, block, buf):
            line = RowReduce(snd, group, block, lambda k, ln: buf.at[k], (None,), c, C, "col", base)
            line.start()
            line.start_near()
            return line

        def scatter_q(base, src, buf):
            return along_col("zq", base, lambda q, ln: src.at[:, pl.ds(al(q * fq, fq), fq)], buf)

        def half_block(ref):
            return lambda q, ln: ref.at[q] if ln is None else ref.at[q, ln, :]

        def block_of(ref):
            return lambda q, ln: ref.at[pl.ds(al(q * fb, fb), fb), slice(None) if ln is None else ln]

        def recv_of(ref):
            return lambda k, ln: ref.at[k, :, slice(None) if ln is None else ln]

        settle(ex_act)
        settle([ex_gdown])
        for q in range(C):
            grad_block(q, "gdown", "act", "gdown_o", "act_o", "gd", "gdq")

        def lanes(n):
            return slice(0, n // 2), slice(n // 2, n)

        red_d = RowReduce(snd, "rd", block_of(b["gd"]), recv_of(b["rd"]), lanes(C * fp), r, R)
        red_d.start()
        zqd = scatter_q(0, b["gdq"], b["zdq"])

        lax.fori_loop(C, 2 * C, gact, 0)
        ex_gpre = [snd("ex", 4, b["gpre"].at[:, other_half], b["gpre_o"], core)]
        run(*ex_gpre)
        def ghid_step(j, _):
            cols = pl.ds(al(j * CH, CH), CH)
            b["hidden"][:, cols] = b["res2"][:, cols] + nt(b["gpre"][...], b["wuf"][cols, :])
            return 0

        lax.fori_loop(0, D // CH, ghid_step, 0)
        ghid = b["hidden"][...]
        nm1 = b["nm1"][...]
        e0[0:1, :] = tsum(ghid * nm1)
        e0[1:2, :] = tsum(ghid)
        gres1 = norm_backward(ghid, b["prow"][0:1, :], nm1, b["sc1"][...])
        e0[3:4, :] = tsum(gres1.astype(BF).astype(F32))
        b["resT"][...] = gres1.T
        b["gattoT"][...] = b["resT"][...].astype(BF)
        ga = jnp.zeros((D, QT), F32)
        for q in range(R):
            ga = ga + nn(b["wpf"][q], b["gattoT"][q * fb:(q + 1) * fb, :])
        b["cg"][...] = ga.astype(BF)
        gt = [snd("gatt", k - 1, hrows(b["cg"], group(k)), tcols(b["gatt"], h), {"row": a * HB + group(k)})
              for k in range(1, HB)]
        run(*gt)
        gt_loc = loc(2, hrows(b["cg"], h), tcols(b["gatt"], h))
        gt_loc.start()
        red_d.start_near()
        b["eb"][...] = jnp.zeros((R, 8, fbp), F32)
        for q in range(R):
            b["eb"][q, :, 0:fb] = e0[:, q * fb:(q + 1) * fb]
        er = [snd("erow", k - 1, b["eb"].at[peer(k)], b["er"].at[k - 1], {"row": peer(k)}) for k in range(1, R)]
        uc = [snd("ucol", k - 1, b["u0"].at[cpeer(k)], b["uz"].at[k - 1], {"col": cpeer(k)}) for k in range(1, C)]
        run(*er, *uc)
        ex_att = [snd("ex", 2, b["gattoT"], b["gattoT_o"], core)] + [
            snd("ex", 5 + q, b["attq"].at[pl.ds(al(q * pb + (1 - d) * ph, ph), ph), :],
                b["att_o"].at[q * ph:(q + 1) * ph, :], core) for q in range(C)]
        run(*ex_att)
        settle([ex_hid])
        settle(ex_gpre)
        for q in range(C):
            grad_block(q, "hid", "gpre", "hid_o", "gpre_o", "gu", "guq")
        zqu = scatter_q(C - 1, b["guq"], b["zuq"])
        own_rows = pl.ds(al(r * fb, fb), fb)
        red_u = RowReduce(snd, "ru", block_of(b["gu"]), recv_of(b["ru"]), lanes(C * fp), r, R)
        settle(ex_att)
        for q in range(C):
            rows = pl.ds(al(q * pb + d * ph, ph), ph)
            tp = slice(q * ph, (q + 1) * ph)
            for p in range(R):
                f = slice(p * fb, (p + 1) * fb)
                b["gp"][p, tp, :] = (nt(b["attq"][rows, :], b["gattoT"][f, :])
                                     + nt(b["att_o"][tp, :], b["gattoT_o"][f, :])).astype(BF)
        red_p = RowReduce(snd, "rp", half_block(b["gp"]), half_block(b["rpj"]), lanes(C * ph), r, R)
        red_p.start()
        red_p.start_near()
        red_u.start()
        def total(own_part, buf, m):
            t = own_part.astype(F32)
            for k in range(m):
                t = t + buf[k].astype(F32)
            return t

        def pcol(ref, n):
            return lambda q, ln: ref.at[own_rows, pl.ds(al(q * n, n), n)]


        def whole(first, buf, m):
            for k in range(m):
                first = first + buf[k]
            return first

        settle(gt)
        gt_loc.wait()
        conv_bwd(nh, b["qkv"], b["gatt"], b["docb"], doc_row, b["band"], b["acc"], b["gband"])
        for hh in range(nh):
            head_bwd1(hh, b["qkv"], b["gatt"], b["k1"], b["k3"], b["sm"], b["mix"], b["nv"][ITERS, hh], b["gv"], b["k1"], b["k3"], b["acc"])
        red_d.middle()
        newton_bwd(nh, b["k2"], b["nv"], b["np_"], b["n1"], b["n2"], b["n3"], b["gv"], b["gk"])
        red_u.start_near()
        red_p.middle()
        zqd.middle()
        for hh in range(nh):
            head_bwd2(hh, b["qkv"], b["k2"], b["gk"], b["ql"], b["kl"], b["k1"], b["k3"], b["acc"], b["qkv"])

        for q in range(R):
            t = nt(b["xg"][q * fb:(q + 1) * fb, :], b["qkv"][...])
            for e in range(2):
                part = t[e * half:(e + 1) * half]
                if hp > half:
                    part = jnp.concatenate([part, jnp.zeros((hp - half, qw), F32)], axis=0)
                b["gq"][q, e] = part.astype(BF)
        gqd = [snd("gqd", 0, b["gq"].at[:, 1 - d], b["gqo"], core)]
        run(*gqd)
        settle(gqd)
        for q in range(R):
            b["gq"][q, d] = (b["gq"][q, d].astype(F32) + b["gqo"][q].astype(F32)).astype(BF)
        gqs = [snd("gqrow", k - 1, b["gq"].at[peer(k), d], b["gqr"].at[r], {"row": peer(k)}) for k in range(1, R)]
        run(*gqs)
        b["gqr"][r] = b["gq"][r, d]
        l0 = b["l0"]
        l0[...] = jnp.zeros((PT, D), F32)
        l0[0:1, 0:qw] = nt(jnp.ones((8, SEQ_LEN), BF), b["qkv"][...])[0:1]
        for hh in range(nh):
            l0[1 + hh:2 + hh, 0:384] = tap_row(b["gband"][hh])
        lcl = [snd("lcol", k - 1, l0, b["lz"].at[k - 1], {"col": cpeer(k)}) for k in range(1, C)]
        run(*lcl)
        red_u.middle()
        zqu.middle()
        for q in range(R):
            f = slice(q * fb, (q + 1) * fb)
            b["part"][f, :] = nn(b["wg"][q], b["qkv"][...]).astype(BF)
            mine_cols = pl.ds(al(h * QT, QT), QT)
            b["part"][f, mine_cols] = (nn(b["wg"][q], b["qkv"][:, mine_cols]) + b["resT"][f, :]).astype(BF)
        red_x = RowReduce(snd, "part", block_of(b["part"]), recv_of(b["pr"]), lanes(SEQ_LEN), r, R)
        if relay:
            red_x.start()
            red_x.start_near()
        else:
            pt = [snd("part", k - 1, fr(b["part"], peer(k)), b["pr"].at[k - 1], {"row": peer(k)}) for k in range(1, R)]
            run(*pt)

        red_d.finish()
        rcd = along_col("rcol", 0, pcol(b["gd"], fp), b["zd"])

        def second_q(base, line, mid, dst):
            b[mid][...] = line.total().astype(BF)
            out = [snd("rq", base + k - 1, fr(b[mid], peer(k)), b[dst].at[k - 1], {"row": peer(k)}) for k in range(1, R)]
            run(*out)
            return out

        rqd = second_q(0, zqd, "tdq", "rdq")
        rqu = second_q(R - 1, zqu, "tuq", "ruq")
        gqc = RowReduce(snd, "gqcol", lambda q, ln: b["gqr"].at[q], lambda k, ln: b["gqz"].at[k], (None,), c, C, "col")
        for k in range(1, R):
            p = lax.rem(r + R - k, R)
            snd("gqrow", k - 1, b["gq"].at[p, d], b["gqr"].at[p], {"row": p}).wait_recv()
        settle(gqs, got=False)
        for ap in range(1, S):
            for q in range(HB):
                b["gqr"][q] = (b["gqr"][q].astype(F32) + b["gqr"][ap * HB + q].astype(F32)).astype(BF)
        gqc.start()
        gqc.start_near()
        rcd.middle()
        settle(lcl)
        b["l1"][...] = whole(l0[...], b["lz"], C - 1)
        lrw = [remote(b["l1"], b["lr"].at[r], ss["lrow"].at[k - 1], rs["lrow"].at[r], {"row": peer(k)}) for k in range(1, R)]
        run(*lrw)
        b["lr"][r] = b["l1"][...]
        settle(er + uc)
        b["e1"][...] = whole(b["eb"][r], b["er"], R - 1)
        b["u1"][...] = whole(b["u0"][c], b["uz"], C - 1)
        ec = [snd("ecol", k - 1, b["e1"], b["ez"].at[k - 1], {"col": cpeer(k)}) for k in range(1, C)]
        ur = [snd("urow", k - 1, b["u1"], b["ur"].at[k - 1], {"row": peer(k)}) for k in range(1, R)]
        run(*ec, *ur)
        red_u.finish()
        rcu = along_col("rcol", 3, pcol(b["gu"], fp), b["zu"])
        red_p.finish()
        rcp = along_col("rcol", 6, lambda q, ln: b["gp"].at[r, pl.ds(al(q * ph, ph), ph), :], b["zp"])

        gqc.middle()
        rcu.middle()
        rcp.middle()
        red_x.middle()
        half_rows, half_cols = pl.ds(al(d * ph, ph), ph), pl.ds(al(d * fh, fh), fh)
        pcols, qcols2 = pl.ds(al(d * fh, 128), fp), pl.ds(al(d * fh + fp, 128), fq)
        settle(ox)
        o_loc.wait()
        settle(rqd + rqu)
        o["gdn"][:, qcols2] = total(b["tdq"][own_rows, :], b["rdq"], R - 1)
        o["gup"][:, qcols2] = total(b["tuq"][own_rows, :], b["ruq"], R - 1)
        o["gdn"][:, pcols] = rcd.total()
        o["gup"][:, pcols] = rcu.total()
        o["gpj"][half_rows, :] = rcp.total()
        fin = [snd("fin", 0, o["gdn"].at[:, half_cols], o["gdn"].at[:, half_cols], core),
               snd("fin", 1, o["gup"].at[:, half_cols], o["gup"].at[:, half_cols], core),
               snd("fin", 2, o["gpj"].at[half_rows, :], o["gpj"].at[half_rows, :], core)]
        run(*fin)
        settle(ec + ur)
        b["e2"][...] = whole(b["e1"][...], b["ez"], C - 1)
        b["u2"][...] = whole(b["u1"][...], b["ur"], R - 1)
        settle(lrw, got=False)
        for k in range(1, R):
            p = peer(k)
            remote(b["l1"], b["lr"].at[p], ss["lrow"].at[0], rs["lrow"].at[p], {"row": p}).wait_recv()
        t = b["lr"][c]
        for q in range(1, S):
            t = t + b["lr"][q * HB + c]
        b["l2"][...] = t
        sd = [snd("ed", 0, b["e2"], b["eo"], core), snd("ud", 0, b["u2"], b["uo"], core), snd("ld", 0, b["l2"], b["lo"], core)]
        run(*sd)
        gq_half = pl.ds(al(d * half, 8), half)
        o["gqw"][gq_half, :] = gqc.total()[:half]
        gqf = snd("gqf", 0, o["gqw"].at[gq_half, :], o["gqw"].at[gq_half, :], core)
        gqf.start()
        if relay:
            o["gin"][...] = red_x.total()
        elif S == 1:
            settle(pt)
            o["gin"][...] = total(b["part"][own_rows, :], b["pr"], R - 1)
        else:
            settle(pt)
            o["gin"][...] = jnp.zeros((fb, S * SEQ_LEN), F32)
            o["gin"][:, pl.ds(al(a * SEQ_LEN, SEQ_LEN), SEQ_LEN)] = b["part"][own_rows, :].astype(F32)
            for k in range(1, R):
                q = lax.rem(r + R - k, R) // HB
                cols = pl.ds(al(q * SEQ_LEN, SEQ_LEN), SEQ_LEN)
                o["gin"][:, cols] += b["pr"][k - 1].astype(F32)
        for cp in sd:
            cp.wait()
        o["sve"][...] = b["e2"][...] + b["eo"][...]
        o["svu"][...] = b["u2"][...] + b["uo"][...]
        o["svl"][...] = b["l2"][...] + b["lo"][...]
        for cp in fin:
            cp.wait()
        gqf.wait()
        for go, cp in w_out:
            pl.when(go)(cp.wait_send)
        for q in range(R):
            pl.when((q % 2) == d)(w_fwd[q].wait_send)
        pl.when(jnp.logical_not(meta_self))(meta_out.wait_send)

    def dma(n):
        return pltpu.SemaphoreType.DMA((n,))

    sem = [dma(sems[g]) for g in first_sems] + [dma(n) for n in local.values()] + [dma(n) for n in sems.values()]
    limit = (59 if R == 4 else 61) << 20
    res = pl.pallas_call(
        body,
        out_shape=[pltpu.VMEM(*s) for s in outs.values()],
        in_specs=[pl.BlockSpec(memory_space=pl.ANY)] * len(any_in) + [pl.BlockSpec(memory_space=pltpu.VMEM)] * len(vmem_in),
        out_specs=[pl.BlockSpec(memory_space=pltpu.VMEM)] * len(outs),
        scratch_shapes=[pltpu.VMEM(*s) for s in bufs.values()] + sem,
        compiler_params=pltpu.CompilerParams(collective_id=0, has_side_effects=True, vmem_limit_bytes=limit),
        name="encoder_layer",
    )(*[args[n] for n in names_in])
    return dict(zip(outs, res))


def finish_call(nh, fb, fc, qw, res):
    big = ["gin", "gqw", "gup", "gdn", "gpj"]
    shapes = [struct(res[n].shape, F32) for n in big]
    rows = [fb] * 6 + [fc, qw]

    def body(*refs):
        src = refs[:5]
        out_ref, e_ref, u_ref, l_ref = refs[5:9]
        dst = refs[9:14]
        o_ref, t_ref = refs[14:16]
        vecs = refs[16:24]
        sem = refs[24]
        cps = [pltpu.make_async_copy(s, t, sem.at[j]) for j, (s, t) in enumerate(zip(src, dst))]
        run(*cps)
        o_ref[...] = out_ref[...].astype(F32)
        for j in range(6):
            vecs[j][...] = e_ref[j:j + 1, 0:fb]
        vecs[6][...] = u_ref[0, :]
        vecs[7][...] = l_ref[0, 0:qw]
        t_ref[...] = l_ref[1:1 + nh, 0:CONV]
        for cp in cps:
            cp.wait()

    A, V = pl.BlockSpec(memory_space=pl.ANY), pl.BlockSpec(memory_space=pltpu.VMEM)
    outs = shapes + [struct(res["out"].shape, F32), struct((nh, CONV), F32)] + [struct((1, n), F32) for n in rows[:6]] + [struct((n,), F32) for n in rows[6:]]
    return pl.pallas_call(
        body, out_shape=outs, in_specs=[V] * 9, out_specs=[A] * 5 + [V] * 10,
        scratch_shapes=[pltpu.SemaphoreType.DMA((5,))], name="outputs",
        compiler_params=pltpu.CompilerParams(vmem_limit_bytes=8 << 20),
    )(*[pltpu.with_memory_space_constraint(res[n], pltpu.VMEM) for n in big + ["out", "sve", "svu", "svl"]])


def make_shards(R, C):
    def shards(inputs, doc_ids, qkv_weight, qkv_bias, proj_weight, proj_bias, first_gain, first_shift,
               ffn_up, ffn_up_bias, ffn_down, ffn_down_bias, second_gain, second_shift, conv_kernel, cotangent):
        S = inputs.shape[1] // SEQ_LEN
        fb = inputs.shape[0]
        nh = conv_kernel.shape[0]
        qw = qkv_weight.shape[1]
        fc = ffn_up.shape[1]
        res = layer_call(R, C, S, fb, nh, fc, proj_weight.shape[0], qw, dict(
            x=inputs, cot=cotangent, wq=qkv_weight, wp=proj_weight, wu=ffn_up, wd=ffn_down, doc=doc_ids[None],
            taps=conv_kernel, g1=first_gain[None], s1=first_shift[None], g2=second_gain[None], s2=second_shift[None],
            qb=qkv_bias, ub=ffn_up_bias, pb=proj_bias, db=ffn_down_bias))
        gin, gqw, gup, gdn, gpj, out, taps, g1, b1, g2, pbias, dbias, b2, ubias, qbias = finish_call(nh, fb, fc, qw, res)
        return (out, gin, gqw, qbias, gpj, pbias.reshape(fb), g1.reshape(fb), b1.reshape(fb), gup,
                ubias, gdn, dbias.reshape(fb), g2.reshape(fb), b2.reshape(fb), taps)
    return shards


def solution(mesh):
    in_specs = (P("row", ("dp", "col")), P(("dp", "row")), P("row", "col"), P("col"), P("col", "row"), P("row"),
                P("row"), P("row"), P("row", "col"), P("col"), P("row", "col"), P("row"), P("row"), P("row"),
                P("col", None), P("row", ("dp", "col")))
    out_specs = (P("row", ("dp", "col")), P("row", ("dp", "col")), P("row", "col"), P("col"), P("col", "row"), P("row"),
                 P("row"), P("row"), P("row", "col"), P("col"), P("row", "col"), P("row"), P("row"), P("row"),
                 P("col", None))
    fn = make_shards(mesh.shape["row"], mesh.shape["col"])
    return jax.shard_map(fn, mesh=mesh, in_specs=in_specs, out_specs=out_specs, check_vma=False)
```

```python
from types import SimpleNamespace as Names

import jax
import jax.numpy as jnp
from jax import lax
from jax.experimental import pallas as pl
from jax.experimental.pallas import tpu as pltpu
from jax.sharding import PartitionSpec as P

D = 768
HEAD_DIM = 64
SEQ_LEN = 1024
EPSILON = 1e-05
F32=jnp.float32; BF=jnp.bfloat16
HD=64; SEQ=1024; SEG=16; CONV=33; ITERS=6; L=64
NEG=-1e9

def dg(a,b,ca,cb):
    return lax.dot_general(a,b,(((ca,),(cb,)),((),())),preferred_element_type=F32)
def nn(a,b): return dg(a,b,1,0)
def nt(a,b): return dg(a,b,1,1)
def tn(a,b): return dg(a,b,0,0)
def split(x):
    hi=x.astype(BF); lo=(x-hi.astype(F32)).astype(BF)
    return hi,lo
def cat(hl): return jnp.concatenate(hl,axis=0)
def halves(x):
    n=x.shape[0]//2
    return x[:n]+x[n:]
def nn2(a,b): return halves(nn(cat(split(a)),b))
def nt2(a,b): return halves(nt(cat(split(a)),b))
def nn3(a,b):
    ah,al=split(a); bh,bl=split(b)
    return halves(nn(cat((ah,al)),bh))+nn(ah,bl)
def nt3(a,b):
    ah,al=split(a); bh,bl=split(b)
    return halves(nt(cat((ah,al)),bh))+nt(ah,bl)

def iota(shape,dim): return lax.broadcasted_iota(jnp.int32,shape,dim)
def avg_mat():
    return jnp.where((iota((L,SEQ),1)//SEG)==iota((L,SEQ),0),F32(1.0/SEG),F32(0)).astype(BF)
def pick_mat():
    return jnp.where(iota((L,SEQ),1)==iota((L,SEQ),0)*SEG,F32(1),F32(0)).astype(BF)

def skew(x,left):
    W=x.shape[1]
    j=iota(x.shape,0)
    for bit in range(7):
        m=1<<bit
        x=jnp.where((j&m)!=0,pltpu.roll(x,(W-m) if left else m,1),x)
    return x

def band(w_row):
    return skew(jnp.broadcast_to(pltpu.roll(w_row,128-CONV//2,1),(128,384)),False)

def span(bt):
    return max(bt-1,0),min(bt+2,SEQ//128)

def same_doc(docb_ref,doc_row,bt):
    lo,hi=span(bt)
    col=docb_ref[bt*128:(bt+1)*128,:]
    return jnp.concatenate([col==doc_row[:,n*128:(n+1)*128] for n in range(lo,hi)],axis=1)

def conv_fwd(nh,qkv_ref,docb_ref,doc_row,band_ref,acc_ref):
    for bt in range(SEQ//128):
        lo,hi=span(bt)
        same=same_doc(docb_ref,doc_row,bt)
        off=(lo-bt+1)*128
        for h in range(nh):
            b=h*3*HD+2*HD
            ct=jnp.where(same,band_ref[h,:,off:off+(hi-lo)*128],0.0)
            o=nt(qkv_ref[b:b+HD,lo*128:hi*128],cat(split(ct)))
            acc_ref[h*HD:(h+1)*HD,bt*128:(bt+1)*128]=o[:,:128]+o[:,128:]

def head_scores(h,qkv_ref,doc_row,land_row,land_col,k1_ref,k3_ref,k2_ref,ql_ref,kl_ref,sum_ref):
    b=h*3*HD
    q=qkv_ref[b:b+HD,:]; k=qkv_ref[b+HD:b+2*HD,:]; v=qkv_ref[b+2*HD:b+3*HD,:]
    at=avg_mat()
    ql=nt(at,q); kl=nt(at,k)
    ql_ref[h]=ql; kl_ref[h]=kl
    keep=land_col==doc_row
    s1=jnp.where(keep,nn2(kl,q)*0.125,NEG)
    e1=jnp.exp(s1-jnp.max(s1,axis=0,keepdims=True))
    k1_ref[h]=e1/jnp.sum(e1,axis=0,keepdims=True)
    s3=jnp.where(keep,nn2(ql,k)*0.125,NEG)
    e3=jnp.exp(s3-jnp.max(s3,axis=1,keepdims=True))
    k3=e3/jnp.sum(e3,axis=1,keepdims=True)
    k3_ref[h]=k3
    s2=jnp.where(land_col==land_row,nt3(ql,kl)*0.125,NEG)
    e2=jnp.exp(s2-jnp.max(s2,axis=1,keepdims=True))
    k2_ref[h]=e2/jnp.sum(e2,axis=1,keepdims=True)
    sum_ref[h]=nt2(k3,v)

def eye(): return jnp.where(iota((L,L),0)==iota((L,L),1),F32(1),F32(0))

def newton(nh,k2_ref,v_ref,p_ref,n1_ref,n2_ref,n3_ref):
    for h in range(nh):
        v_ref[0,h]=k2_ref[h].T*(1.0/L)
    def step(i,_):
        I=eye()
        P=[nn3(k2_ref[h],v_ref[i,h]) for h in range(nh)]
        N1=[7.0*I-P[h] for h in range(nh)]
        N2=[15.0*I-nn3(P[h],N1[h]) for h in range(nh)]
        N3=[13.0*I-nn3(P[h],N2[h]) for h in range(nh)]
        for h in range(nh):
            p_ref[i,h]=P[h]; n1_ref[i,h]=N1[h]; n2_ref[i,h]=N2[h]; n3_ref[i,h]=N3[h]
            v_ref[i+1,h]=nn3(0.25*v_ref[i,h],N3[h])
        return 0
    lax.fori_loop(0,ITERS,step,0)

def head_out(h,k1_ref,inv,sum_ref,mix_ref,acc_ref,att_ref):
    mixed=nn3(inv,sum_ref[h])
    mix_ref[h]=mixed
    mt=mixed.T
    k1=k1_ref[h]
    res=nn3(mt,k1)
    att_ref[h*HD:(h+1)*HD,:]=(res+acc_ref[h*HD:(h+1)*HD,:]).astype(BF)

def newton_bwd(nh,k2_ref,v_ref,p_ref,n1_ref,n2_ref,n3_ref,gv_ref,gk_ref):
    for h in range(nh):
        gk_ref[h]=jnp.zeros((L,L),F32)
    def step(j,_):
        i=ITERS-1-j
        H=range(nh)
        gV=[gv_ref[h] for h in H]; V=[v_ref[i,h] for h in H]
        VT=[V[h].T for h in H]; PT=[p_ref[i,h].T for h in H]
        gN3=[0.25*nn3(VT[h],gV[h]) for h in H]
        gVn=[0.25*nt3(gV[h],n3_ref[i,h]) for h in H]
        gN2=[-nn3(PT[h],gN3[h]) for h in H]
        gN1=[-nn3(PT[h],gN2[h]) for h in H]
        gP=[-nt3(gN3[h],n2_ref[i,h])-nt3(gN2[h],n1_ref[i,h])-gN1[h] for h in H]
        for h in H:
            gk_ref[h]+=nt3(gP[h],V[h])
            gv_ref[h]=gVn[h]+nn3(k2_ref[h].T,gP[h])
        return 0
    lax.fori_loop(0,ITERS,step,0)
    for h in range(nh):
        gk_ref[h]+=gv_ref[h].T*(1.0/L)

def conv_bwd(nh,qkv_ref,g_ref,docb_ref,doc_row,band_ref,gacc_ref,gband_ref):
    for bt in range(SEQ//128):
        lo,hi=span(bt)
        same=same_doc(docb_ref,doc_row,bt)
        off=(lo-bt+1)*128
        for h in range(nh):
            b=h*3*HD+2*HD
            lanes=slice(off,off+(hi-lo)*128)
            ct=jnp.where(same,band_ref[h,:,lanes],0.0)
            g=g_ref[h*HD:(h+1)*HD,bt*128:(bt+1)*128]
            gv=nn(jnp.concatenate([g,g],axis=1),cat(split(ct)))
            gb=jnp.where(same,tn(g,qkv_ref[b:b+HD,lo*128:hi*128]),0.0)
            rows=slice(h*HD,(h+1)*HD)
            if bt==0:
                gband_ref[h]=jnp.zeros((128,384),F32)
                gacc_ref[rows,0:256]=gv
            else:
                gacc_ref[rows,lo*128:(bt+1)*128]+=gv[:,:256]
                if hi>bt+1:
                    gacc_ref[rows,(bt+1)*128:hi*128]=gv[:,256:]
            gband_ref[h,:,lanes]+=gb

def tap_row(gband):
    x=skew(gband,True)
    return pltpu.roll(jnp.sum(x,axis=0,keepdims=True),384-(128-CONV//2),1)

def head_bwd1(h,qkv_ref,g_ref,k1_ref,k3_ref,sum_ref,mix_ref,inv,gv_ref,gs1_ref,gs3_ref,gacc_ref):
    b=h*3*HD
    v=qkv_ref[b+2*HD:b+3*HD,:]
    g=g_ref[h*HD:(h+1)*HD,:]
    k1=k1_ref[h]
    gmix=nt2(k1,g)
    gk1=nn2(mix_ref[h],g)
    gs1_ref[h]=k1*(gk1-jnp.sum(k1*gk1,axis=0,keepdims=True))
    gv_ref[h]=nt3(gmix,sum_ref[h])
    gsum=nn3(inv.T,gmix)
    k3=k3_ref[h]
    gk3=nn2(gsum,v)
    gs3_ref[h]=k3*(gk3-jnp.sum(k3*gk3,axis=1,keepdims=True))
    gacc_ref[h*HD:(h+1)*HD,:]+=nn3(gsum.T,k3)

def head_bwd2(h,qkv_ref,k2_ref,gk_ref,ql_ref,kl_ref,gs1_ref,gs3_ref,gacc_ref,out_ref):
    b=h*3*HD
    q=qkv_ref[b:b+HD,:]; k=qkv_ref[b+HD:b+2*HD,:]
    k2=k2_ref[h]; gk2=gk_ref[h]
    gs2=k2*(gk2-jnp.sum(k2*gk2,axis=1,keepdims=True))
    ql=ql_ref[h]; kl=kl_ref[h]
    gs1=gs1_ref[h]; gs3=gs3_ref[h]
    gkl=nt2(gs1,q)+nn3(gs2.T,ql)
    gql=nt2(gs3,k)+nn3(gs2,kl)
    at=avg_mat()
    gq=(nn3(kl.T,gs1)+nn2(gql.T,at))*0.125
    gk=(nn3(ql.T,gs3)+nn2(gkl.T,at))*0.125
    out_ref[b:b+HD,:]=gq.astype(BF)
    out_ref[b+HD:b+2*HD,:]=gk.astype(BF)
    out_ref[b+2*HD:b+3*HD,:]=gacc_ref[h*HD:(h+1)*HD,:].astype(BF)

MESH = pl.DeviceIdType.MESH


def struct(shape, dtype):
    return jax.ShapeDtypeStruct(shape, dtype)


def remote(src, dst, ss, rs, dev):
    return pltpu.make_async_remote_copy(
        src_ref=src, dst_ref=dst, send_sem=ss, recv_sem=rs, device_id=dev, device_id_type=MESH
    )


def run(*copies):
    for cp in copies:
        cp.start()


def settle(cps, sent=True, got=True):
    for cp in cps:
        if sent:
            cp.wait_send()
        if got:
            cp.wait_recv()


def when(cond, fn):
    if cond is None:
        fn()
    else:
        pl.when(cond)(fn)


def al(x, n):
    return pl.multiple_of(x, n)


def gauss(x):
    e = jnp.exp(-0.5 * x * x)
    t = 1.0 / (1.0 + jnp.abs(x) * 0.23164190)
    p = t * 0.5307027145 - 0.7265760135
    p = (p * t + 0.7107068705) * t - 0.1422483680
    q = (p * t + 0.1274147960) * t * e
    return jnp.where(x >= 0, 1.0 - q, q), e * 0.3989422804014327


def norm_forward(residual, gain, shift):
    average = jnp.mean(residual, axis=1, keepdims=True)
    spread = jnp.mean(residual * residual, axis=1, keepdims=True) - average * average
    scaling = lax.rsqrt(spread + EPSILON)
    normed = (residual - average) * scaling
    return normed * gain + shift, normed, scaling


def norm_backward(upstream, gain, normed, scaling):
    scaled = upstream * gain
    mean_scaled = jnp.mean(scaled, axis=1, keepdims=True)
    crossed = jnp.mean(scaled * normed, axis=1, keepdims=True)
    return scaling * (scaled - mean_scaled - normed * crossed)


def tsum(x):
    return jnp.sum(x, axis=0, keepdims=True)


class Pool:
    def __init__(self, entries):
        self.at = entries


class RowGather:
    def __init__(self, snd, group, base, ways, place, r, R, cond=None):
        n = len(ways)
        self.cond, self.n, self.relay, self.ways = cond, n, R == 4, ways
        if self.relay:
            X, Y = lax.bitwise_xor(r, 1), lax.bitwise_xor(r, 2)
            self.own = []
            self.fwd = []
            for j in range(n):
                mine = place(j, r)
                self.own.append((snd(group, base + 2 * j, mine, mine, {"row": X}),
                                 snd(group, base + 2 * j + 1, mine, mine, {"row": Y})))
                src = place(j, Y if ways[j] else X)
                self.fwd.append(snd(group, base + 2 * n + j, src, src, {"row": X if ways[j] else Y}))
        else:
            self.own = [tuple(snd(group, base + j * (R - 1) + k - 1, place(j, r), place(j, r), {"row": lax.rem(r + k, R)})
                              for k in range(1, R)) for j in range(n)]

    def start(self):
        def go():
            if self.relay:
                for j, cps in enumerate(self.own):
                    cps[self.ways[j]].start()
                for j, cps in enumerate(self.own):
                    cps[1 - self.ways[j]].start()
            else:
                for cps in self.own:
                    run(*cps)
        when(self.cond, go)

    def forward(self):
        if self.relay:
            def go():
                for j in range(self.n):
                    self.own[j][self.ways[j]].wait_recv()
                    self.fwd[j].start()
            when(self.cond, go)

    def finish(self):
        def go():
            for j in range(self.n):
                if self.relay:
                    self.own[j][1 - self.ways[j]].wait_recv()
                    self.fwd[j].wait_recv()
                    self.fwd[j].wait_send()
                else:
                    for cp in self.own[j]:
                        cp.wait_recv()
                for cp in self.own[j]:
                    cp.wait_send()
        when(self.cond, go)


class RowReduce:
    def __init__(self, snd, group, block, recv, lanes, r, R, axis="row", base=0):
        self.block, self.recv, self.lanes, self.r, self.R = block, recv, lanes, r, R
        self.relay = R == 4
        n = len(lanes)
        if self.relay:
            X, Y, Z = lax.bitwise_xor(r, 1), lax.bitwise_xor(r, 2), lax.bitwise_xor(r, 3)
            self.one, self.two, self.mids = [], [], []
            for j, ln in enumerate(lanes):
                P, Q = (X, Y) if j == 0 else (Y, X)
                self.one.append([snd(group, base + 3 * j, block(Z, ln), recv(1, ln), {axis: P}),
                                 snd(group, base + 3 * j + 1, block(P, ln), recv(0, ln), {axis: P})])
                self.two.append(snd(group, base + 3 * j + 2, block(Q, ln), recv(2, ln), {axis: Q}))
                self.mids.append(Q)
        else:
            self.all = [snd(group, base + k - 1, block(lax.rem(r + k, R), None), recv(k - 1, None), {axis: lax.rem(r + k, R)})
                        for k in range(1, R)]

    def start(self):
        if self.relay:
            for cps in self.one:
                cps[0].start()
        else:
            run(*self.all)

    def start_near(self):
        if self.relay:
            for cps in self.one:
                cps[1].start()

    def middle(self):
        if self.relay:
            for j, ln in enumerate(self.lanes):
                self.one[j][0].wait_recv()
                ref = self.block(self.mids[j], ln)
                ref[...] = (ref[...].astype(F32) + self.recv(1, ln)[...].astype(F32)).astype(BF)
                self.two[j].start()

    def total(self):
        if self.relay:
            for cps in self.one:
                settle(cps, got=False)
                cps[1].wait_recv()
            settle(self.two)
            slots = (0, 2)
        else:
            settle(self.all)
            slots = range(self.R - 1)
        t = self.block(self.r, None)[...].astype(F32)
        for k in slots:
            t = t + self.recv(k, None)[...].astype(F32)
        return t

    def finish(self):
        self.block(self.r, None)[...] = self.total().astype(BF)


class LineGather:
    def __init__(self, snd, group, n, place, c, C):
        self.C, self.c, self.n = C, c, n
        m = (C - 1) * n
        self.up = [[snd(group, k * n + j, place(j, c - k), place(j, c - k), {"col": c + 1}) for j in range(n)] for k in range(C - 1)]
        self.dn = [[snd(group, m + k * n + j, place(j, c + k), place(j, c + k), {"col": c - 1}) for j in range(n)] for k in range(C - 1)]

    def up_ok(self, k):
        return (self.c >= k) & (self.c < self.C - 1)

    def dn_ok(self, k):
        return (self.c + k <= self.C - 1) & (self.c > 0)

    def start(self):
        pl.when(self.up_ok(0))(lambda: run(*self.up[0]))
        pl.when(self.dn_ok(0))(lambda: run(*self.dn[0]))

    def step(self, k):
        def got(cps, nxt, ok):
            def go():
                for j in range(self.n):
                    cps[j].wait_recv()
                    if nxt is not None:
                        pl.when(ok)(lambda: nxt[j].start())
            return go
        more = k < self.C - 1
        pl.when(self.c >= k)(got(self.up[k - 1], self.up[k] if more else None, self.up_ok(k) if more else None))
        pl.when(self.c + k <= self.C - 1)(got(self.dn[k - 1], self.dn[k] if more else None, self.dn_ok(k) if more else None))

    def forward(self, k):
        def on(cps, nxt):
            def go():
                for j in range(self.n):
                    cps[j].wait_recv()
                    nxt[j].start()
            return go
        pl.when(self.up_ok(k))(on(self.up[k - 1], self.up[k]))
        pl.when(self.dn_ok(k))(on(self.dn[k - 1], self.dn[k]))

    def land(self):
        for k in range(1, self.C):
            pl.when(self.c == self.C - 1)(lambda: settle(self.up[k - 1], sent=False))
            pl.when(self.c == 0)(lambda: settle(self.dn[k - 1], sent=False))

    def drain(self):
        for k in range(self.C - 1):
            pl.when(self.up_ok(k))(lambda: settle(self.up[k], got=False))
            pl.when(self.dn_ok(k))(lambda: settle(self.dn[k], got=False))


def layer_call(R, C, S, fb, nh, fc, pb, qw, args):
    HB = R // S
    QT = SEQ_LEN // HB
    FF = fc * C
    fh, ph = fc // 2, pb // 2
    fq = fh // 3 // 128 * 128
    fp = fh - fq
    upw, uqw, dpw, dqw = fp, fq, fq, fp
    hb = nh * HD
    fbp = -(-fb // 128) * 128
    hp = -(-fb // 32) * 16
    CH = 256
    FH = FF // 2
    relay = R == 4
    NR = 3 if relay else R - 1
    PT = nh + 1
    V = pltpu.VMEM
    small = (nh, L, L)
    any_in = ["x", "cot", "wq", "wp", "wu", "wd"]
    vmem_in = ["doc", "taps", "g1", "s1", "g2", "s2", "qb", "ub", "pb", "db"]
    names_in = any_in + vmem_in
    outs = dict(
        out=((fb, S * SEQ_LEN), BF), gin=((fb, S * SEQ_LEN), F32), gqw=((fb, qw), F32), gup=((fb, fc), F32),
        gdn=((fb, fc), F32), gpj=((pb, fb), F32), sve=((8, fbp), F32), svu=((1, fc), F32), svl=((PT, D), F32))
    bufs = dict(
        xg=((D, SEQ_LEN), BF), wg=((R, fb, qw), BF), ms=((8, SEQ_LEN), F32), mt=((8, SEQ_LEN), F32),
        rs=((8, fbp), F32), rp=((R, 8, fbp), F32), cs=((8, fc), F32), cp=((C, 8, fc), F32),
        cg=((D, QT), BF), wpf=((R, D, fb), BF), wuf=((D, FF), BF), wdf=((D, FF), BF),
        qkv=((3 * hb, SEQ_LEN), BF), k1=((nh, L, SEQ_LEN), F32), k3=((nh, L, SEQ_LEN), F32), k2=(small, F32),
        ql=(small, F32), kl=(small, F32), sm=(small, F32), mix=(small, F32), nv=((ITERS + 1,) + small, F32),
        np_=((ITERS,) + small, F32), n1=((ITERS,) + small, F32), n2=((ITERS,) + small, F32), n3=((ITERS,) + small, F32),
        docb=((SEQ_LEN, 128), F32), band=((nh, 128, 384), F32), gband=((nh, 128, 384), F32), acc=((hb, SEQ_LEN), F32), att=((hb, SEQ_LEN), BF), attq=((D, QT), BF),
        resT=((D, QT), F32), prow=((8, D), F32), hidden=((QT, D), F32), hid=((QT, D), BF), nm1=((QT, D), F32),
        sc1=((QT, 1), F32), act=((QT, FF), BF), dact=((QT, FF), F32), res2=((QT, D), F32), gdown=((QT, D), BF),
        gpre=((QT, FF), BF), gattoT=((D, QT), BF), outT=((D, QT), BF), gatt=((hb, SEQ_LEN), BF),
        hid_o=((QT, D), BF), gdown_o=((QT, D), BF), gattoT_o=((D, QT), BF), att_o=((C * ph, QT), BF),
        act_o=((QT, C * fh), BF), gpre_o=((QT, C * fh), BF),
        gu=((D, C * fp), BF), guq=((D, C * fq), BF), gd=((D, C * fp), BF), gp=((R, C * ph, fb), BF), gdq=((D, C * fq), BF),
        ru=((NR, fb, C * fp), BF), rd=((NR, fb, C * fp), BF), rpj=((NR, C * ph, fb), BF),
        zu=((C - 1, fb, fp), BF), zd=((C - 1, fb, fp), BF), zp=((C - 1, ph, fb), BF),
        zdq=((C - 1, D, fq), BF), zuq=((C - 1, D, fq), BF), tuq=((D, fq), BF), tdq=((D, fq), BF),
        rdq=((R - 1, fb, fq), BF), ruq=((R - 1, fb, fq), BF),
        gv=(small, F32), gk=(small, F32),
        part=((D, SEQ_LEN), BF), pr=((R - 1, fb, SEQ_LEN), BF),
        gq=((R, 2, hp, qw), BF), gqo=((R, hp, qw), BF), gqr=((R, hp, qw), BF), gqz=((C - 1, hp, qw), BF),
        e0=((8, D), F32), eb=((R, 8, fbp), F32), er=((R - 1, 8, fbp), F32), e1=((8, fbp), F32), ez=((C - 1, 8, fbp), F32),
        e2=((8, fbp), F32), eo=((8, fbp), F32), u0=((C, 1, fc), F32), uz=((C - 1, 1, fc), F32), u1=((1, fc), F32),
        ur=((R - 1, 1, fc), F32), u2=((1, fc), F32), uo=((1, fc), F32), l0=((PT, D), F32), lz=((C - 1, PT, D), F32),
        l1=((PT, D), F32), lr=((R, PT, D), F32), l2=((PT, D), F32), lo=((PT, D), F32))
    NRP = 1 + 2 * (C - 1)
    sems = dict(
        x=2 * (R - 1), cot=R - 1, rowp=R - 1, colp=C - 1, meta=1, ws=S * C, wr=R, wd2=R,
        zU=4 * (C - 1), zD=2 * (C - 1), rU=C * 2 * (R - 1), rD=C * (R - 1), rQ=R - 1, rS=R - 1, zQ=2 * (C - 1), zR=2 * (C - 1),
        cU=2 * C, cD=C, cQ=2 * C,
        att=HB - 1, gatt=HB - 1, ex=5 + C, ru=max(6, R - 1), rd=max(6, R - 1), rp=max(6, R - 1), rcol=3 * (C - 1),
        zq=2 * (C - 1), rq=2 * (R - 1), part=max(6, R - 1), outx=R - 1,
        gqd=1, gqrow=R - 1, gqcol=C - 1, gqf=1, erow=R - 1, ecol=C - 1, ed=1, ucol=C - 1, urow=R - 1, ud=1, lcol=C - 1, lrow=R, ld=1, fin=3)
    local = dict(loc=21)

    late_sems = ["ru", "rd", "rp", "rcol", "zq", "rq", "part", "gqd", "gqrow", "gqcol", "gqf", "erow", "ecol", "ed", "ucol",
                 "urow", "ud", "lcol", "lrow", "ld", "fin"]
    first_sems = [g for g in sems if g not in late_sems]

    def body(*refs):
        n = len(names_in)
        i = Names(**dict(zip(names_in, refs[:n])))
        o = Names(**dict(zip(outs, refs[n:n + len(outs)])))
        k = n + len(outs)
        b = Names(**dict(zip(bufs, refs[k:k + len(bufs)])))
        N = Names(**{g: g for g in list(sems) + list(local)})
        k += len(bufs)
        ss = dict(zip(first_sems + list(local), refs[k:]))
        k += len(first_sems) + len(local)
        rs = dict(zip(sems, refs[k:]))
        free = [ss[g].at[j] for g in ("rU", "rD", "zU", "zD", "zQ", "zR", "cU", "cD", "cQ", "rQ", "rS", "x") for j in range(sems[g])]
        for g in late_sems:
            ss[g] = Pool(free[:sems[g]])
            free = free[sems[g]:]
        d = lax.axis_index("dp")
        r = lax.axis_index("row")
        c = lax.axis_index("col")
        a, h = r // HB, lax.rem(r, HB)
        core = {"dp": 1 - d}

        def snd(group, slot, src, dst, dev):
            return remote(src, dst, ss[group].at[slot], rs[group].at[slot], dev)

        def loc(slot, src, dst):
            return pltpu.make_async_copy(src, dst, ss[N.loc].at[slot])

        def fr(ref, q):
            return ref.at[pl.ds(al(q * fb, fb), fb), :]

        def peer(k):
            return lax.rem(r + k, R)

        def cpeer(k):
            return lax.rem(c + k, C)

        own = c == h
        bar = pltpu.get_barrier_semaphore()
        for k in range(1, R):
            pl.semaphore_signal(bar, inc=1, device_id={"row": peer(k)}, device_id_type=MESH)
        for k in range(1, C):
            pl.semaphore_signal(bar, inc=1, device_id={"col": cpeer(k)}, device_id_type=MESH)
        pl.semaphore_signal(bar, inc=1, device_id=core, device_id_type=MESH)
        for q in range(R):
            @pl.when(jnp.logical_not(own & (r == q)))
            def _():
                pl.semaphore_signal(bar, inc=1, device_id={"row": q, "col": h}, device_id_type=MESH)
        half = fb // 2

        def xcols(q, part=None):
            rows = slice(None) if part is None else pl.ds(part * half, half)
            return i.x.at[rows, pl.ds(al(q // HB * SEQ_LEN, SEQ_LEN), SEQ_LEN)]

        x_loc = loc(0, xcols(r), fr(b.xg, r))
        x_loc.start()

        def cols_of(col, first, width):
            return pl.ds(al(d * (FF // 2) + col * fh + first, 128), width)

        def wide(ref, row, col, first, width):
            return ref.at[pl.ds(al(row * fb, fb), fb), cols_of(col, first, width)]

        def narrow(ref, row, col):
            return ref.at[row, pl.ds(al(col * pb + d * ph, ph), ph), :]

        bulk_loc = [loc(1, i.wu.at[:, pl.ds(al(d * fh, fh), fh)], wide(b.wuf, r, c, 0, fh)),
                    loc(2, i.wd.at[:, pl.ds(al(d * fh, fh), fh)], wide(b.wdf, r, c, 0, fh)),
                    loc(3, i.wp.at[pl.ds(al(d * ph, ph), ph), :], narrow(b.wpf, r, c))]
        run(*bulk_loc)
        cot_rows = min(fb, 64)
        stage = []
        for s in range(S):
            for f in range(0, fb, cot_rows):
                m = len(stage)
                buf = b.k1.at[m] if m < nh else b.k3.at[m - nh]
                stage.append((s, f, m, loc(4 + m, i.cot.at[f:f + cot_rows, s * SEQ_LEN:(s + 1) * SEQ_LEN], buf.at[0:cot_rows, :])))
        run(*[t[3] for t in stage])
        b.ms[...] = jnp.zeros((8, SEQ_LEN), F32)
        b.ms[0:1, :] = i.doc[...].astype(F32)
        b.ms[1:1 + nh, 0:CONV] = i.taps[...]
        b.ms[1 + nh:2 + nh, 0:qw] = i.qb[...].astype(F32).reshape(1, qw)
        b.rs[...] = jnp.zeros((8, fbp), F32)
        for j, name in enumerate(("g1", "s1", "g2", "s2")):
            b.rs[j:j + 1, 0:fb] = getattr(i, name)[...]
        b.rs[4:5, 0:fb] = i.pb[...].astype(F32).reshape(1, fb)
        b.rs[5:6, 0:fb] = i.db[...].astype(F32).reshape(1, fb)
        b.cs[...] = jnp.zeros((8, fc), F32)
        b.cs[0:1, :] = i.ub[...].astype(F32).reshape(1, fc)
        for cp in bulk_loc:
            cp.wait()
        x_loc.wait()
        pl.semaphore_wait(bar, R - 1 + C - 1 + 1 + S * C - jnp.where(own, 1, 0))

        dst_row, dst_col = lax.rem(r, S) * HB + c, r // S
        meta_self = (dst_row == r) & (dst_col == c)
        meta_out = snd(N.meta, 0, b.ms, b.mt, {"row": dst_row, "col": dst_col})
        meta_in = snd(N.meta, 0, b.ms, b.mt, {"row": c * S + a, "col": h})
        meta_loc = loc(17, b.ms, b.mt)
        pl.when(jnp.logical_not(meta_self))(meta_out.start)
        pl.when(meta_self)(meta_loc.start)

        def place_u(col):
            return lambda j, row: narrow(b.wpf, row, col) if j else wide(b.wuf, row, col, 0, upw)

        def place_d(col):
            return lambda j, row: wide(b.wdf, row, col, 0, dpw)

        zU = LineGather(snd, N.zU, 2, lambda j, col: place_u(col)(j, r), c, C)
        zD = LineGather(snd, N.zD, 1, lambda j, col: place_d(col)(j, r), c, C)
        at_cols = [(None, c)]
        for k in range(1, C):
            at_cols += [(c >= k, c - k), (c + k <= C - 1, c + k)]
        rU = [RowGather(snd, N.rU, col * 2 * (R - 1), (0, 1), place_u(col), r, R, cond) for cond, col in at_cols]
        rD = [RowGather(snd, N.rD, col * (R - 1), (1,), place_d(col), r, R, cond) for cond, col in at_cols]
        rQ = RowGather(snd, N.rQ, 0, (0,), lambda j, row: wide(b.wuf, row, c, upw, uqw), r, R)
        rS = RowGather(snd, N.rS, 0, (1,), lambda j, row: wide(b.wdf, row, c, dpw, dqw), r, R)
        rQ.start()
        zQ = LineGather(snd, N.zQ, 1, lambda j, col: b.wuf.at[:, cols_of(col, upw, uqw)], c, C)
        zR = LineGather(snd, N.zR, 1, lambda j, col: b.wdf.at[:, cols_of(col, dpw, dqw)], c, C)
        zU.start()
        zD.start()
        if relay:
            xg = RowGather(snd, N.x, 0, (0, 1), lambda j, q: b.xg.at[pl.ds(al(q * fb + j * half, half), half), :], r, R)
            xg.start()
        else:
            xs = [snd(N.x, k - 1, xcols(peer(k)), fr(b.xg, r), {"row": peer(k)}) for k in range(1, R)]
            run(*xs)
        par = lax.rem(r, 2) == d
        w_out = []
        for ap in range(S):
            for cq in range(C):
                t = ap * HB + c
                go = par & jnp.logical_not((t == r) & (c == cq))
                cp = remote(i.wq, b.wg.at[r], ss[N.ws].at[ap * C + cq], rs[N.wr].at[r], {"row": t, "col": cq})
                w_out.append((go, cp))
        for go, cp in w_out:
            pl.when(go)(cp.start)
        w_loc = loc(16, i.wq, b.wg.at[r])
        pl.when(own & par)(w_loc.start)
        def cot_at(s, cols):
            return b.gpre.at[pl.ds(al(s // 3 * fb, fb), fb), cols]

        for s, f, m, cp in stage:
            cp.wait()
            buf = b.k1.at[m] if m < nh else b.k3.at[m - nh]
            b.gpre[s // 3 * fb + f:s // 3 * fb + f + cot_rows, s % 3 * SEQ_LEN:(s % 3 + 1) * SEQ_LEN] = buf[0:cot_rows, :].astype(BF)

        def cot_src(q):
            s = q // HB
            return cot_at(s, pl.ds(al(lax.rem(s, 3) * SEQ_LEN + lax.rem(q, HB) * QT, QT), QT))

        zU.step(1)
        if relay:
            xg.forward()
        rQ.forward()
        rS.start()
        zD.forward(1)
        pl.when(jnp.logical_not(meta_self))(meta_in.wait_recv)
        pl.when(meta_self)(meta_loc.wait)
        doc_row = b.mt[0:1, :]
        rowb = jnp.broadcast_to(doc_row, (8, SEQ_LEN)).astype(BF)
        pick = pick_mat()
        land_row = nt(rowb, pick)[0:1]
        land_col = nt(pick, rowb)[:, 0:1]
        for hh in range(nh):
            b.band[hh] = band(b.mt[1 + hh:2 + hh, 0:384])
        one = jnp.where(iota((8, 128), 0) == 0, 1.0, 0.0).astype(BF)
        b.docb[...] = tn(rowb, one)
        for k in range(2, C - 1):
            zU.step(k)
            zD.forward(k)
        rQ.finish()
        zQ.start()
        rS.forward()
        if relay:
            xg.finish()
        else:
            settle(xs)
        for m in range(2 * C - 3):
            rU[m].start()
        gs = [snd(N.cot, k - 1, cot_src(peer(k)), fr(b.cg, r), {"row": peer(k)}) for k in range(1, R)]
        g_loc = loc(18, cot_src(r), fr(b.cg, r))
        ps = [snd(N.rowp, k - 1, b.rs, b.rp.at[r], {"row": peer(k)}) for k in range(1, R)]
        p_loc = loc(19, b.rs, b.rp.at[r])
        cs = [snd(N.colp, k - 1, b.cs, b.cp.at[c], {"col": cpeer(k)}) for k in range(1, C)]
        c_loc = loc(20, b.cs, b.cp.at[c])
        run(*ps, p_loc, *cs, c_loc)
        w_fwd = [snd(N.wd2, q, b.wg.at[q], b.wg.at[q], core) for q in range(R)]
        for q in range(R):
            mine_q = (q % 2) == d
            here_q = own & (r == q)
            w_in = remote(i.wq, b.wg.at[q], ss[N.ws].at[0], rs[N.wr].at[q], {"row": q, "col": h})
            pl.when(mine_q & here_q)(w_loc.wait)
            pl.when(mine_q & jnp.logical_not(here_q))(w_in.wait_recv)
            pl.when(mine_q)(w_fwd[q].start)
        for q in range(R):
            pl.when((q % 2) != d)(w_fwd[q].wait_recv)
        qb = jnp.where(iota((8, qw), 0) == 1 + nh, b.mt[:, 0:qw], 0.0).astype(BF)
        acc = tn(qb, jnp.ones((8, SEQ_LEN), BF))
        for q in range(R):
            acc = acc + tn(b.wg[q], b.xg[q * fb:(q + 1) * fb, :])
        b.qkv[...] = acc.astype(BF)

        def scores(hh):
            head_scores(hh, b.qkv, doc_row, land_row, land_col, b.k1, b.k3, b.k2, b.ql, b.kl, b.sm)

        for hh in range(nh):
            scores(hh)
        zQ.forward(1)
        rS.finish()
        zR.start()
        zU.step(C - 1)
        for m in range(2 * C - 3, NRP):
            rU[m].start()
        newton(nh, b.k2, b.nv, b.np_, b.n1, b.n2, b.n3)
        for k in range(2, C - 1):
            zQ.forward(k)
        for m in range(3):
            rU[m].forward()
        conv_fwd(nh, b.qkv, b.docb, doc_row, b.band, b.acc)
        for hh in range(nh):
            head_out(hh, b.k1, b.nv[ITERS, hh], b.sm, b.mix, b.acc, b.att)

        def group(k):
            return lax.rem(h + k, HB)

        def hrows(ref, q):
            return ref.at[pl.ds(al(q * hb, hb), hb), :]

        def tcols(ref, q):
            return ref.at[:, pl.ds(al(q * QT, QT), QT)]

        at = [snd(N.att, k - 1, tcols(b.att, group(k)), hrows(b.attq, h), {"row": a * HB + group(k)})
              for k in range(1, HB)]
        run(*at)
        at_loc = loc(0, tcols(b.att, h), hrows(b.attq, h))
        at_loc.start()
        for m in range(3, NRP):
            rU[m].forward()
        zD.land()
        for m in range(NRP):
            rD[m].start()
        zR.forward(1)
        for cp in ps + cs:
            cp.wait()
        for cp in (p_loc, c_loc):
            cp.wait()
        prow = jnp.zeros((8, D), F32)
        for q in range(R):
            piece = jnp.concatenate([b.rp[q], jnp.zeros((8, D - fbp), F32)], axis=1)
            prow = prow + (pltpu.roll(piece, q * fb, 1) if q else piece)
        b.prow[...] = prow
        def cross(group, slot, cond, *refs):
            cps = [snd(group, slot + j, ref, ref, core) for j, ref in enumerate(refs)]
            when(cond, lambda: run(*cps))
            return cond, cps

        crossed, later = [], []
        for m, (cond, col) in enumerate(at_cols):
            rU[m].finish()
            crossed.append(cross(N.cU, 2 * col, cond, b.wuf.at[:, cols_of(col, 0, upw)],
                                 b.wpf.at[:, pl.ds(al(col * pb + d * ph, ph), ph), :]))
        zQ.land()
        for k in range(2, C - 1):
            zR.forward(k)
        for m, (cond, col) in enumerate(at_cols):
            crossed.append(cross(N.cQ, 2 * col, cond, b.wuf.at[:, cols_of(col, upw, uqw)]))
        settle(at)
        at_loc.wait()
        for cond, cps in crossed:
            when(cond, lambda: settle(cps))

        for q in range(R):
            t = tn(b.wpf[q], b.attq[...])
            b.resT[q * fb:(q + 1) * fb, :] = t + b.xg[q * fb:(q + 1) * fb, pl.ds(al(h * QT, QT), QT)].astype(F32)
        res1 = b.resT[...].T + b.prow[4:5, :]
        hidden, nm1, sc1 = norm_forward(res1, b.prow[0:1, :], b.prow[1:2, :])
        b.hidden[...] = hidden
        b.nm1[...] = nm1
        b.sc1[...] = sc1
        b.hid[...] = hidden.astype(BF)
        ex_hid = snd(N.ex, 0, b.hid, b.hid_o, core)
        ex_hid.start()

        def up(j, _):
            cols = pl.ds(al(j * fh, 128), fh)
            bias = b.cp[lax.rem(j, C), 0:1, pl.ds(al(j // C * fh, 128), fh)]
            pre = nn(b.hid[...], b.wuf[:, cols]) + bias
            cdf, pdf = gauss(pre)
            b.act[:, cols] = (pre * cdf).astype(BF)
            b.dact[:, cols] = cdf + pre * pdf
            return 0

        lax.fori_loop(0, C, up, 0)
        for m in range(2 * C - 3):
            rD[m].forward()
        lax.fori_loop(C, 2 * C, up, 0)
        for m in range(2 * C - 3, NRP):
            rD[m].forward()
        run(*gs, g_loc)
        zR.land()
        for m, (cond, col) in enumerate(at_cols):
            later.append(cross(N.cQ, 2 * col + 1, cond, b.wdf.at[:, cols_of(col, dpw, dqw)]))
        other_half = pl.ds(al((1 - d) * FH, 128), FH)
        ex_act = [snd(N.ex, 3, b.act.at[:, other_half], b.act_o, core)]
        run(*ex_act)
        for m, (cond, col) in enumerate(at_cols):
            rD[m].finish()
            later.append(cross(N.cD, col, cond, b.wdf.at[:, cols_of(col, 0, dpw)]))
        for cond, cps in later:
            when(cond, lambda: settle(cps))
        for line in (zU, zD, zQ, zR):
            line.drain()

        def down(j, _):
            cols = pl.ds(al(j * CH, CH), CH)
            b.res2[:, cols] = b.hidden[:, cols] + nt(b.act[...], b.wdf[cols, :]) + b.prow[5:6, cols]
            return 0

        lax.fori_loop(0, D // CH, down, 0)
        gain2 = b.prow[2:3, :]
        out, nm2, sc2 = norm_forward(b.res2[...], gain2, b.prow[3:4, :])
        settle(gs)
        g_loc.wait()
        ups = b.cg[...].astype(F32).T
        e0 = b.e0
        e0[...] = jnp.zeros((8, D), F32)
        e0[2:3, :] = tsum(ups * nm2)
        e0[5:6, :] = tsum(ups)
        gres2 = norm_backward(ups, gain2, nm2, sc2)
        b.res2[...] = gres2
        b.gdown[...] = gres2.astype(BF)
        e0[4:5, :] = tsum(b.gdown[...].astype(F32))
        ex_gdown = snd(N.ex, 1, b.gdown, b.gdown_o, core)
        ex_gdown.start()
        b.outT[...] = out.T.astype(BF)
        ox = [snd(N.outx, k - 1, fr(b.outT, peer(k)), tcols(o.out, a * HB + h), {"row": peer(k)}) for k in range(1, R)]
        o_loc = loc(1, fr(b.outT, r), tcols(o.out, a * HB + h))
        run(*ox, o_loc)

        def gact(j, _):
            cols = pl.ds(al(j * fh, 128), fh)
            g = nn(b.gdown[...], b.wdf[:, cols])
            gp = (g * b.dact[:, cols]).astype(BF)
            b.gpre[:, cols] = gp
            b.u0[lax.rem(j, C), 0:1, pl.ds(al(j // C * fh, 128), fh)] = tsum(gp.astype(F32))
            return 0

        lax.fori_loop(0, C, gact, 0)
        def grad_block(q, mine, mine_w, other, other_w, dst, dst_q):
            to = slice(q * fh, (q + 1) * fh)
            t = tn(mine[...], mine_w[:, cols_of(q, 0, fh)]) + tn(other[...], other_w[:, to])
            dst[:, q * fp:(q + 1) * fp] = t[:, :fp].astype(BF)
            dst_q[:, q * fq:(q + 1) * fq] = t[:, fp:].astype(BF)

        def along_col(group, base, block, buf):
            line = RowReduce(snd, group, block, lambda k, ln: buf.at[k], (None,), c, C, "col", base)
            line.start()
            line.start_near()
            return line

        def scatter_q(base, src, buf):
            return along_col(N.zq, base, lambda q, ln: src.at[:, pl.ds(al(q * fq, fq), fq)], buf)

        def half_block(ref):
            return lambda q, ln: ref.at[q] if ln is None else ref.at[q, ln, :]

        def block_of(ref):
            return lambda q, ln: ref.at[pl.ds(al(q * fb, fb), fb), slice(None) if ln is None else ln]

        def recv_of(ref):
            return lambda k, ln: ref.at[k, :, slice(None) if ln is None else ln]

        settle(ex_act)
        settle([ex_gdown])
        for q in range(C):
            grad_block(q, b.gdown, b.act, b.gdown_o, b.act_o, b.gd, b.gdq)

        def lanes(n):
            return slice(0, n // 2), slice(n // 2, n)

        red_d = RowReduce(snd, N.rd, block_of(b.gd), recv_of(b.rd), lanes(C * fp), r, R)
        red_d.start()
        zqd = scatter_q(0, b.gdq, b.zdq)

        lax.fori_loop(C, 2 * C, gact, 0)
        ex_gpre = [snd(N.ex, 4, b.gpre.at[:, other_half], b.gpre_o, core)]
        run(*ex_gpre)
        def ghid_step(j, _):
            cols = pl.ds(al(j * CH, CH), CH)
            b.hidden[:, cols] = b.res2[:, cols] + nt(b.gpre[...], b.wuf[cols, :])
            return 0

        lax.fori_loop(0, D // CH, ghid_step, 0)
        ghid = b.hidden[...]
        nm1 = b.nm1[...]
        e0[0:1, :] = tsum(ghid * nm1)
        e0[1:2, :] = tsum(ghid)
        gres1 = norm_backward(ghid, b.prow[0:1, :], nm1, b.sc1[...])
        e0[3:4, :] = tsum(gres1.astype(BF).astype(F32))
        b.resT[...] = gres1.T
        b.gattoT[...] = b.resT[...].astype(BF)
        ga = jnp.zeros((D, QT), F32)
        for q in range(R):
            ga = ga + nn(b.wpf[q], b.gattoT[q * fb:(q + 1) * fb, :])
        b.cg[...] = ga.astype(BF)
        gt = [snd(N.gatt, k - 1, hrows(b.cg, group(k)), tcols(b.gatt, h), {"row": a * HB + group(k)})
              for k in range(1, HB)]
        run(*gt)
        gt_loc = loc(2, hrows(b.cg, h), tcols(b.gatt, h))
        gt_loc.start()
        red_d.start_near()
        b.eb[...] = jnp.zeros((R, 8, fbp), F32)
        for q in range(R):
            b.eb[q, :, 0:fb] = e0[:, q * fb:(q + 1) * fb]
        er = [snd(N.erow, k - 1, b.eb.at[peer(k)], b.er.at[k - 1], {"row": peer(k)}) for k in range(1, R)]
        uc = [snd(N.ucol, k - 1, b.u0.at[cpeer(k)], b.uz.at[k - 1], {"col": cpeer(k)}) for k in range(1, C)]
        run(*er, *uc)
        ex_att = [snd(N.ex, 2, b.gattoT, b.gattoT_o, core)] + [
            snd(N.ex, 5 + q, b.attq.at[pl.ds(al(q * pb + (1 - d) * ph, ph), ph), :],
                b.att_o.at[q * ph:(q + 1) * ph, :], core) for q in range(C)]
        run(*ex_att)
        settle([ex_hid])
        settle(ex_gpre)
        for q in range(C):
            grad_block(q, b.hid, b.gpre, b.hid_o, b.gpre_o, b.gu, b.guq)
        zqu = scatter_q(C - 1, b.guq, b.zuq)
        own_rows = pl.ds(al(r * fb, fb), fb)
        red_u = RowReduce(snd, N.ru, block_of(b.gu), recv_of(b.ru), lanes(C * fp), r, R)
        settle(ex_att)
        for q in range(C):
            rows = pl.ds(al(q * pb + d * ph, ph), ph)
            tp = slice(q * ph, (q + 1) * ph)
            for p in range(R):
                f = slice(p * fb, (p + 1) * fb)
                b.gp[p, tp, :] = (nt(b.attq[rows, :], b.gattoT[f, :])
                                     + nt(b.att_o[tp, :], b.gattoT_o[f, :])).astype(BF)
        red_p = RowReduce(snd, N.rp, half_block(b.gp), half_block(b.rpj), lanes(C * ph), r, R)
        red_p.start()
        red_p.start_near()
        red_u.start()
        def total(own_part, buf, m):
            t = own_part.astype(F32)
            for k in range(m):
                t = t + buf[k].astype(F32)
            return t

        def pcol(ref, n):
            return lambda q, ln: ref.at[own_rows, pl.ds(al(q * n, n), n)]


        def whole(first, buf, m):
            for k in range(m):
                first = first + buf[k]
            return first

        settle(gt)
        gt_loc.wait()
        conv_bwd(nh, b.qkv, b.gatt, b.docb, doc_row, b.band, b.acc, b.gband)
        for hh in range(nh):
            head_bwd1(hh, b.qkv, b.gatt, b.k1, b.k3, b.sm, b.mix, b.nv[ITERS, hh], b.gv, b.k1, b.k3, b.acc)
        red_d.middle()
        newton_bwd(nh, b.k2, b.nv, b.np_, b.n1, b.n2, b.n3, b.gv, b.gk)
        red_u.start_near()
        red_p.middle()
        zqd.middle()
        for hh in range(nh):
            head_bwd2(hh, b.qkv, b.k2, b.gk, b.ql, b.kl, b.k1, b.k3, b.acc, b.qkv)

        for q in range(R):
            t = nt(b.xg[q * fb:(q + 1) * fb, :], b.qkv[...])
            for e in range(2):
                part = t[e * half:(e + 1) * half]
                if hp > half:
                    part = jnp.concatenate([part, jnp.zeros((hp - half, qw), F32)], axis=0)
                b.gq[q, e] = part.astype(BF)
        gqd = [snd(N.gqd, 0, b.gq.at[:, 1 - d], b.gqo, core)]
        run(*gqd)
        settle(gqd)
        for q in range(R):
            b.gq[q, d] = (b.gq[q, d].astype(F32) + b.gqo[q].astype(F32)).astype(BF)
        gqs = [snd(N.gqrow, k - 1, b.gq.at[peer(k), d], b.gqr.at[r], {"row": peer(k)}) for k in range(1, R)]
        run(*gqs)
        b.gqr[r] = b.gq[r, d]
        l0 = b.l0
        l0[...] = jnp.zeros((PT, D), F32)
        l0[0:1, 0:qw] = nt(jnp.ones((8, SEQ_LEN), BF), b.qkv[...])[0:1]
        for hh in range(nh):
            l0[1 + hh:2 + hh, 0:384] = tap_row(b.gband[hh])
        lcl = [snd(N.lcol, k - 1, l0, b.lz.at[k - 1], {"col": cpeer(k)}) for k in range(1, C)]
        run(*lcl)
        red_u.middle()
        zqu.middle()
        for q in range(R):
            f = slice(q * fb, (q + 1) * fb)
            b.part[f, :] = nn(b.wg[q], b.qkv[...]).astype(BF)
            mine_cols = pl.ds(al(h * QT, QT), QT)
            b.part[f, mine_cols] = (nn(b.wg[q], b.qkv[:, mine_cols]) + b.resT[f, :]).astype(BF)
        red_x = RowReduce(snd, N.part, block_of(b.part), recv_of(b.pr), lanes(SEQ_LEN), r, R)
        if relay:
            red_x.start()
            red_x.start_near()
        else:
            pt = [snd(N.part, k - 1, fr(b.part, peer(k)), b.pr.at[k - 1], {"row": peer(k)}) for k in range(1, R)]
            run(*pt)

        red_d.finish()
        rcd = along_col(N.rcol, 0, pcol(b.gd, fp), b.zd)

        def second_q(base, line, mid, dst):
            mid[...] = line.total().astype(BF)
            out = [snd(N.rq, base + k - 1, fr(mid, peer(k)), dst.at[k - 1], {"row": peer(k)}) for k in range(1, R)]
            run(*out)
            return out

        rqd = second_q(0, zqd, b.tdq, b.rdq)
        rqu = second_q(R - 1, zqu, b.tuq, b.ruq)
        gqc = RowReduce(snd, N.gqcol, lambda q, ln: b.gqr.at[q], lambda k, ln: b.gqz.at[k], (None,), c, C, "col")
        for k in range(1, R):
            p = lax.rem(r + R - k, R)
            snd(N.gqrow, k - 1, b.gq.at[p, d], b.gqr.at[p], {"row": p}).wait_recv()
        settle(gqs, got=False)
        for ap in range(1, S):
            for q in range(HB):
                b.gqr[q] = (b.gqr[q].astype(F32) + b.gqr[ap * HB + q].astype(F32)).astype(BF)
        gqc.start()
        gqc.start_near()
        rcd.middle()
        settle(lcl)
        b.l1[...] = whole(l0[...], b.lz, C - 1)
        lrw = [remote(b.l1, b.lr.at[r], ss[N.lrow].at[k - 1], rs[N.lrow].at[r], {"row": peer(k)}) for k in range(1, R)]
        run(*lrw)
        b.lr[r] = b.l1[...]
        settle(er + uc)
        b.e1[...] = whole(b.eb[r], b.er, R - 1)
        b.u1[...] = whole(b.u0[c], b.uz, C - 1)
        ec = [snd(N.ecol, k - 1, b.e1, b.ez.at[k - 1], {"col": cpeer(k)}) for k in range(1, C)]
        ur = [snd(N.urow, k - 1, b.u1, b.ur.at[k - 1], {"row": peer(k)}) for k in range(1, R)]
        run(*ec, *ur)
        red_u.finish()
        rcu = along_col(N.rcol, 3, pcol(b.gu, fp), b.zu)
        red_p.finish()
        rcp = along_col(N.rcol, 6, lambda q, ln: b.gp.at[r, pl.ds(al(q * ph, ph), ph), :], b.zp)

        gqc.middle()
        rcu.middle()
        rcp.middle()
        red_x.middle()
        half_rows, half_cols = pl.ds(al(d * ph, ph), ph), pl.ds(al(d * fh, fh), fh)
        pcols, qcols2 = pl.ds(al(d * fh, 128), fp), pl.ds(al(d * fh + fp, 128), fq)
        settle(ox)
        o_loc.wait()
        settle(rqd + rqu)
        o.gdn[:, qcols2] = total(b.tdq[own_rows, :], b.rdq, R - 1)
        o.gup[:, qcols2] = total(b.tuq[own_rows, :], b.ruq, R - 1)
        o.gdn[:, pcols] = rcd.total()
        o.gup[:, pcols] = rcu.total()
        o.gpj[half_rows, :] = rcp.total()
        fin = [snd(N.fin, 0, o.gdn.at[:, half_cols], o.gdn.at[:, half_cols], core),
               snd(N.fin, 1, o.gup.at[:, half_cols], o.gup.at[:, half_cols], core),
               snd(N.fin, 2, o.gpj.at[half_rows, :], o.gpj.at[half_rows, :], core)]
        run(*fin)
        settle(ec + ur)
        b.e2[...] = whole(b.e1[...], b.ez, C - 1)
        b.u2[...] = whole(b.u1[...], b.ur, R - 1)
        settle(lrw, got=False)
        for k in range(1, R):
            p = peer(k)
            remote(b.l1, b.lr.at[p], ss[N.lrow].at[0], rs[N.lrow].at[p], {"row": p}).wait_recv()
        t = b.lr[c]
        for q in range(1, S):
            t = t + b.lr[q * HB + c]
        b.l2[...] = t
        sd = [snd(N.ed, 0, b.e2, b.eo, core), snd(N.ud, 0, b.u2, b.uo, core), snd(N.ld, 0, b.l2, b.lo, core)]
        run(*sd)
        gq_half = pl.ds(al(d * half, 8), half)
        o.gqw[gq_half, :] = gqc.total()[:half]
        gqf = snd(N.gqf, 0, o.gqw.at[gq_half, :], o.gqw.at[gq_half, :], core)
        gqf.start()
        if relay:
            o.gin[...] = red_x.total()
        elif S == 1:
            settle(pt)
            o.gin[...] = total(b.part[own_rows, :], b.pr, R - 1)
        else:
            settle(pt)
            o.gin[...] = jnp.zeros((fb, S * SEQ_LEN), F32)
            o.gin[:, pl.ds(al(a * SEQ_LEN, SEQ_LEN), SEQ_LEN)] = b.part[own_rows, :].astype(F32)
            for k in range(1, R):
                q = lax.rem(r + R - k, R) // HB
                cols = pl.ds(al(q * SEQ_LEN, SEQ_LEN), SEQ_LEN)
                o.gin[:, cols] += b.pr[k - 1].astype(F32)
        for cp in sd:
            cp.wait()
        o.sve[...] = b.e2[...] + b.eo[...]
        o.svu[...] = b.u2[...] + b.uo[...]
        o.svl[...] = b.l2[...] + b.lo[...]
        for cp in fin:
            cp.wait()
        gqf.wait()
        for go, cp in w_out:
            pl.when(go)(cp.wait_send)
        for q in range(R):
            pl.when((q % 2) == d)(w_fwd[q].wait_send)
        pl.when(jnp.logical_not(meta_self))(meta_out.wait_send)

    def dma(n):
        return pltpu.SemaphoreType.DMA((n,))

    sem = [dma(sems[g]) for g in first_sems] + [dma(n) for n in local.values()] + [dma(n) for n in sems.values()]
    limit = (59 if R == 4 else 61) << 20
    res = pl.pallas_call(
        body,
        out_shape=[pltpu.VMEM(*s) for s in outs.values()],
        in_specs=[pl.BlockSpec(memory_space=pl.ANY)] * len(any_in) + [pl.BlockSpec(memory_space=pltpu.VMEM)] * len(vmem_in),
        out_specs=[pl.BlockSpec(memory_space=pltpu.VMEM)] * len(outs),
        scratch_shapes=[pltpu.VMEM(*s) for s in bufs.values()] + sem,
        compiler_params=pltpu.CompilerParams(collective_id=0, has_side_effects=True, vmem_limit_bytes=limit),
        name="encoder_layer",
    )(*[args[n] for n in names_in])
    return dict(zip(outs, res))


def finish_call(nh, fb, fc, qw, res):
    big = ["gin", "gqw", "gup", "gdn", "gpj"]
    shapes = [struct(res[n].shape, F32) for n in big]
    rows = [fb] * 6 + [fc, qw]

    def body(*refs):
        src = refs[:5]
        out_ref, e_ref, u_ref, l_ref = refs[5:9]
        dst = refs[9:14]
        o_ref, t_ref = refs[14:16]
        vecs = refs[16:24]
        sem = refs[24]
        cps = [pltpu.make_async_copy(s, t, sem.at[j]) for j, (s, t) in enumerate(zip(src, dst))]
        run(*cps)
        o_ref[...] = out_ref[...].astype(F32)
        for j in range(6):
            vecs[j][...] = e_ref[j:j + 1, 0:fb]
        vecs[6][...] = u_ref[0, :]
        vecs[7][...] = l_ref[0, 0:qw]
        t_ref[...] = l_ref[1:1 + nh, 0:CONV]
        for cp in cps:
            cp.wait()

    A, V = pl.BlockSpec(memory_space=pl.ANY), pl.BlockSpec(memory_space=pltpu.VMEM)
    outs = shapes + [struct(res["out"].shape, F32), struct((nh, CONV), F32)] + [struct((1, n), F32) for n in rows[:6]] + [struct((n,), F32) for n in rows[6:]]
    return pl.pallas_call(
        body, out_shape=outs, in_specs=[V] * 9, out_specs=[A] * 5 + [V] * 10,
        scratch_shapes=[pltpu.SemaphoreType.DMA((5,))], name="outputs",
        compiler_params=pltpu.CompilerParams(vmem_limit_bytes=8 << 20),
    )(*[pltpu.with_memory_space_constraint(res[n], pltpu.VMEM) for n in big + ["out", "sve", "svu", "svl"]])


def make_shards(R, C):
    def shards(inputs, doc_ids, qkv_weight, qkv_bias, proj_weight, proj_bias, first_gain, first_shift,
               ffn_up, ffn_up_bias, ffn_down, ffn_down_bias, second_gain, second_shift, conv_kernel, cotangent):
        S = inputs.shape[1] // SEQ_LEN
        fb = inputs.shape[0]
        nh = conv_kernel.shape[0]
        qw = qkv_weight.shape[1]
        fc = ffn_up.shape[1]
        res = layer_call(R, C, S, fb, nh, fc, proj_weight.shape[0], qw, dict(
            x=inputs, cot=cotangent, wq=qkv_weight, wp=proj_weight, wu=ffn_up, wd=ffn_down, doc=doc_ids[None],
            taps=conv_kernel, g1=first_gain[None], s1=first_shift[None], g2=second_gain[None], s2=second_shift[None],
            qb=qkv_bias, ub=ffn_up_bias, pb=proj_bias, db=ffn_down_bias))
        gin, gqw, gup, gdn, gpj, out, taps, g1, b1, g2, pbias, dbias, b2, ubias, qbias = finish_call(nh, fb, fc, qw, res)
        return (out, gin, gqw, qbias, gpj, pbias.reshape(fb), g1.reshape(fb), b1.reshape(fb), gup,
                ubias, gdn, dbias.reshape(fb), g2.reshape(fb), b2.reshape(fb), taps)
    return shards


def solution(mesh):
    in_specs = (P("row", ("dp", "col")), P(("dp", "row")), P("row", "col"), P("col"), P("col", "row"), P("row"),
                P("row"), P("row"), P("row", "col"), P("col"), P("row", "col"), P("row"), P("row"), P("row"),
                P("col", None), P("row", ("dp", "col")))
    out_specs = (P("row", ("dp", "col")), P("row", ("dp", "col")), P("row", "col"), P("col"), P("col", "row"), P("row"),
                 P("row"), P("row"), P("row", "col"), P("col"), P("row", "col"), P("row"), P("row"), P("row"),
                 P("col", None))
    fn = make_shards(mesh.shape["row"], mesh.shape["col"])
    return jax.shard_map(fn, mesh=mesh, in_specs=in_specs, out_specs=out_specs, check_vma=False)
```
